32 devices in a mesh: fsdp: 8 (over z, core), expert: 4 (over y, x).
Axes of the slice: x: 2, y: 2, z: 4, core: 2. Of those that a mesh axis runs over, the one named last changes fastest.
Arguments:
- tokens: bfloat16 [4096, 1536], P(('fsdp', 'expert')), may hold values from -6 to 6
- lengths: int32 [32, 4], P(('fsdp', 'expert')), may hold values from 1 to 64, 128 in all within a row
- routes: int32 [2, 4096, 8], P(None, ('fsdp', 'expert')), may hold values from 0 to 19, all different within a row; in each aligned block of 128 rows (0 to 127, 128 to 255, ..., all dimensions but the last counted through in order) at most 80 rows name the same one
- gates: float32 [2, 4096, 8], P(None, ('fsdp', 'expert')), may hold values from 0.04 to 0.4
- cotangent: bfloat16 [4096, 1536], P(('fsdp', 'expert')), may hold values from -6 to 6
- norm_attn: bfloat16 [2, 1536], P(None, ('fsdp', 'expert')), may hold values from 0.5 to 1.5
- norm_ffn: bfloat16 [2, 1536], P(None, ('fsdp', 'expert')), may hold values from 0.5 to 1.5
- query: bfloat16 [2, 1536, 1536], P(None, ('fsdp', 'expert')), may hold values from -0.15625 to 0.15625
- key: bfloat16 [2, 1536, 512], P(None, ('fsdp', 'expert')), may hold values from -0.15625 to 0.15625
- value: bfloat16 [2, 1536, 512], P(None, ('fsdp', 'expert')), may hold values from -0.15625 to 0.15625
- output: bfloat16 [2, 1536, 1536], P(None, ('fsdp', 'expert')), may hold values from -0.625 to 0.625
- w_gate: bfloat16 [2, 1536, 20, 512], P(None, 'fsdp', 'expert'), may hold values from -0.15625 to 0.15625
- w_up: bfloat16 [2, 1536, 20, 512], P(None, 'fsdp', 'expert'), may hold values from -0.15625 to 0.15625
- w_down: bfloat16 [2, 1536, 20, 512], P(None, 'fsdp', 'expert'), may hold values from -0.75 to 0.75
Outputs:
- result: bfloat16 [4096, 1536], P(('fsdp', 'expert'))
- grad_tokens: float32 [4096, 1536], P(('fsdp', 'expert'))
- grad_norm_attn: float32 [2, 1536], P(None, ('fsdp', 'expert'))
- grad_norm_ffn: float32 [2, 1536], P(None, ('fsdp', 'expert'))
- grad_query: float32 [2, 1536, 1536], P(None, ('fsdp', 'expert'))
- grad_key: float32 [2, 1536, 512], P(None, ('fsdp', 'expert'))
- grad_value: float32 [2, 1536, 512], P(None, ('fsdp', 'expert'))
- grad_output: float32 [2, 1536, 1536], P(None, ('fsdp', 'expert'))
- grad_w_gate: float32 [2, 1536, 20, 512], P(None, 'fsdp', 'expert')
- grad_w_up: float32 [2, 1536, 20, 512], P(None, 'fsdp', 'expert')
- grad_w_down: float32 [2, 1536, 20, 512], P(None, 'fsdp', 'expert')
The draws below stay inside these ranges and needn't reach their ends.
Inputs may be any that keep to these rules, and one draw needn't show every extreme that they name: `lengths`: every row sums to 128, and the largest entry of every row is 64. `routes`: the 8 experts of a token in a layer differ. Among the 128 rows of one device in one layer, no expert is named by more than 80 rows, and in every layer some expert is named by exactly 80 rows of some device.
All inputs are finite; a program needn't handle non-finite values.
Results may differ from the reference program's by a relative error of at most 0.025.
Values may be sent and summed in bfloat16 or wider, within the bound.
No kernel may reach another device: no remote copies, remote signals or barrier semaphores. Data moves between devices by JAX's collectives and lax.ppermute only.
A program may use at most 512 MiB of HBM per device.

```python
import math
import jax
import jax.numpy as jnp
import numpy as np
from jax import lax

MODEL_DIMENSION = 1536
QUERY_HEADS = 24
KEY_VALUE_HEADS = 8
HEAD_DIMENSION = 64
FF = 512
TOPK = 8
DECODER_LAYERS = 2
SEQ_DEV = 4
TOK_DEV = 128
EXPERTS = 20
MOST_LEN = 64
CAP = 80
TOKENS = 4096
N_FSDP = 8
N_EXPERT = 4


def steps_of(stream_key, extent, shards, smallest, high):
    factor_of = 1.0
    for position, parts in shards:
        steps = jax.random.uniform(jax.random.fold_in(jax.random.fold_in(stream_key, 6), position), (parts,), jnp.float32, smallest / len(shards), high / len(shards))
        factor_of = factor_of * jnp.repeat(jnp.exp(steps), extent[position] // parts).reshape((-1,) + (1,) * (len(extent) - 1 - position))
    return factor_of


def profile(number_of, total, limit, lean):
    weights = [(1 << 20) // math.isqrt(standing ** lean) + 1 for standing in range(2, number_of + 1)]
    rest, given = total - limit - (number_of - 1), [1] * (number_of - 1)
    while rest > 0:
        free = [i for i in range(number_of - 1) if given[i] < limit]
        pool, remaining = sum([weights[i] for i in free]), rest
        for i in free:
            addition = min(limit - given[i], max(1, remaining * weights[i] // pool), rest)
            given[i] = given[i] + addition
            rest = rest - addition
    return np.array([limit] + given)


def ragged(stream_key, amount, total, limit, lean):
    if amount == 2:
        one = jax.random.randint(stream_key, (), max(1, total - limit), min(limit, total - 1) + 1)
        return jnp.stack([one, total - one])
    sizes = jnp.asarray(profile(amount, total, limit, lean), jnp.int32)
    pairs = (amount - 1) // 2
    donor, receiver = sizes[1:1 + 2 * pairs:2], sizes[2:2 + 2 * pairs:2]
    slack = jnp.minimum(donor - 1, limit - receiver)
    moved = jax.random.randint(jax.random.fold_in(stream_key, 1), (pairs,), 0, 1 << 20) % (slack + 1)
    sizes = sizes.at[1:1 + 2 * pairs:2].set(donor - moved).at[2:2 + 2 * pairs:2].set(receiver + moved)
    return sizes[jax.random.permutation(jax.random.fold_in(stream_key, 2), amount)]


def deal_out(rng, own, number, rows, count, top, reach, skew):
    sequence = jax.random.permutation(rng, count)
    packed, ordinary = load_shares(count, rows * top, reach, skew, True), load_shares(count, rows * top, reach, skew, False)
    places = jnp.arange(count)

    def named(tallies, rotation):
        used = int((tallies > 0).sum())
        fixed = max(1, used // 4)
        shifted = fixed + (places - fixed + rotation * (used - fixed)) % max(1, count - fixed)
        return jnp.zeros((count,), jnp.int32).at[sequence[jnp.where(places < fixed, places, shifted)]].set(jnp.asarray(tallies, jnp.int32))

    tallies = jnp.where(number % 4 == 0, named(packed, number // 4), named(ordinary, number - number // 4 - 1))
    mixed = jax.random.permutation(jax.random.fold_in(own, 3), count)
    giver, sink = mixed[0:count // 2 * 2:2], mixed[1:count // 2 * 2:2]
    margin = jnp.minimum(tallies[giver] - 1, reach - tallies[sink]) // 2
    margin = jnp.where((giver == sequence[0]) | (sink == sequence[0]) | (tallies[sink] == 0), 0, jnp.maximum(margin, 0))
    shifted = jax.random.randint(jax.random.fold_in(own, 4), (count // 2,), 0, 1 << 20) % (margin + 1)
    tallies = tallies.at[giver].add(-shifted).at[sink].add(shifted)
    items = jnp.searchsorted(jnp.cumsum(tallies), jnp.arange(rows * top), side="right").astype(jnp.int32)
    grid = items.reshape(top, rows).T
    grid = grid[jax.random.permutation(jax.random.fold_in(own, 1), rows)]
    rotation = jax.random.randint(jax.random.fold_in(own, 2), (rows, 1), 0, top)
    return jnp.take_along_axis(grid, (jnp.arange(top)[None, :] + rotation) % top, axis=1)


def load_shares(count, total, most, lean, full):
    portions = [(1 << 20) // math.isqrt(grade ** lean) + 1 for grade in range(1, count + 1)]
    largest = most if full else min(most, max(-(-total // count), total * portions[0] // sum(portions)))
    least = 1 if total - largest >= count - 1 else 0
    given, spare = [largest] + [least] * (count - 1), total - largest - least * (count - 1)
    while spare > 0:
        candidates = [i for i in range(1, count) if given[i] < largest] or [i for i in range(1, count) if given[i] < most]
        mass, remaining = sum([portions[i] for i in candidates]), spare
        for i in candidates:
            addition = min(most - given[i], max(1, remaining * portions[i] // mass), spare)
            given[i] = given[i] + addition
            spare = spare - addition
    return np.array(given)


def bell_draw(stream_key, dims, scale, most, pieces=(), held_as=jnp.bfloat16):
    factor_of = steps_of(stream_key, dims, pieces, -0.22, 0.18) if pieces else 1.0
    values = jax.random.normal(stream_key, dims, jnp.float32) * scale * factor_of
    return jnp.minimum(jnp.maximum(values, -most), most).astype(held_as)


def setup_inputs(seed: int = 0) -> dict:
    arg_keys = jax.random.split(jax.random.key(seed), 15)
    tokens = bell_draw(arg_keys[0], (TOKENS, MODEL_DIMENSION), 1.0, 6.0, ((0, 32),))
    lengths = jax.vmap(lambda own: ragged(own, SEQ_DEV, TOK_DEV, MOST_LEN, 2))(jax.random.split(arg_keys[1], (N_FSDP * N_EXPERT))).reshape((N_FSDP * N_EXPERT, SEQ_DEV)).astype(jnp.int32)
    routes_keys = jax.random.split(jax.random.fold_in(arg_keys[2], 1), DECODER_LAYERS * TOKENS // TOK_DEV)
    routes_turns = jax.random.permutation(jax.random.fold_in(arg_keys[2], 3), DECODER_LAYERS * TOKENS // TOK_DEV)
    routes = jax.vmap(lambda own, number: deal_out(jax.random.fold_in(arg_keys[2], 2), own, number, TOK_DEV, EXPERTS, TOPK, CAP, 2))(routes_keys, routes_turns).reshape((DECODER_LAYERS, TOKENS, TOPK))
    gates = jnp.clip(jnp.exp(math.log(0.4) - 2.3025851 * jax.random.uniform(arg_keys[3], (DECODER_LAYERS, TOKENS, TOPK), jnp.float32) ** steps_of(arg_keys[3], (DECODER_LAYERS, TOKENS, TOPK), ((1, 32),), -0.2, 0.2)), 0.04, 0.4)
    cotangent = bell_draw(arg_keys[4], (TOKENS, MODEL_DIMENSION), 1.0, 6.0, ((0, 32),))
    norm_attn = jnp.clip(1.0 + 0.1 * jax.random.normal(arg_keys[5], (DECODER_LAYERS, MODEL_DIMENSION), jnp.float32), 0.5, 1.5).astype(jnp.bfloat16)
    norm_ffn = jnp.clip(1.0 + 0.1 * jax.random.normal(arg_keys[6], (DECODER_LAYERS, MODEL_DIMENSION), jnp.float32), 0.5, 1.5).astype(jnp.bfloat16)
    query = bell_draw(arg_keys[7], (DECODER_LAYERS, MODEL_DIMENSION, QUERY_HEADS * HEAD_DIMENSION), MODEL_DIMENSION ** -0.5, 0.15625, ((1, 32),))
    key = bell_draw(arg_keys[8], (DECODER_LAYERS, MODEL_DIMENSION, KEY_VALUE_HEADS * HEAD_DIMENSION), MODEL_DIMENSION ** -0.5, 0.15625, ((1, 32),))
    value = bell_draw(arg_keys[9], (DECODER_LAYERS, MODEL_DIMENSION, KEY_VALUE_HEADS * HEAD_DIMENSION), MODEL_DIMENSION ** -0.5, 0.15625, ((1, 32),))
    output = bell_draw(arg_keys[10], (DECODER_LAYERS, QUERY_HEADS * HEAD_DIMENSION, MODEL_DIMENSION), (MODEL_DIMENSION // 16) ** -0.5, 0.625, ((1, 32),))
    w_gate = bell_draw(arg_keys[11], (DECODER_LAYERS, MODEL_DIMENSION, EXPERTS, FF), MODEL_DIMENSION ** -0.5, 0.15625, ((1, 8), (2, 4)))
    w_up = bell_draw(arg_keys[12], (DECODER_LAYERS, MODEL_DIMENSION, EXPERTS, FF), MODEL_DIMENSION ** -0.5, 0.15625, ((1, 8), (2, 4)))
    w_down = bell_draw(arg_keys[13], (DECODER_LAYERS, MODEL_DIMENSION, EXPERTS, FF), (FF // 8) ** -0.5, 0.75, ((1, 8), (2, 4)))
    return dict(tokens=tokens, lengths=lengths, routes=routes, gates=gates, cotangent=cotangent, norm_attn=norm_attn, norm_ffn=norm_ffn, query=query, key=key, value=value, output=output, w_gate=w_gate, w_up=w_up, w_down=w_down)


NORM_EPS = 1e-06
MASKED = -1000000000.0
FULL_ACCURACY = lax.Precision.HIGHEST

@jax.custom_vjp
def reduced_input(v):
    return lax.optimization_barrier(v.astype(jnp.bfloat16)).astype(jnp.float32)

@jax.custom_vjp
def reduced_gradient(v):
    return v

def low_keep(v):
    return (reduced_input(v), None)

def low_pass(kept, grad):
    return (grad,)

def back_keep(v):
    return (v, None)

def back_low(kept, grad):
    return (reduced_input(grad),)
reduced_input.defvjp(low_keep, low_pass)
reduced_gradient.defvjp(back_keep, back_low)

def positions(length_row, count_of_rows):
    ends = jnp.cumsum(length_row).astype(jnp.int32)
    token_order = jnp.arange(count_of_rows, dtype=jnp.int32)
    passed = token_order[:, None] >= ends[None, :]
    segment = lax.optimization_barrier(jnp.sum(passed.astype(jnp.int32), axis=1)).astype(jnp.int32)
    before = lax.optimization_barrier(jnp.sum(jnp.where(passed, length_row[None, :], 0), axis=1)).astype(jnp.int32)
    return (segment, token_order - before)

def rope_tables(seq_place, head_width):
    half_width = head_width // 2
    freq_table = jnp.exp(jnp.arange(half_width, dtype=jnp.float32) * (-2.0 * math.log(10000.0) / head_width))
    angles = seq_place.astype(jnp.float32)[:, None] * freq_table[None, :]
    return (jnp.cos(angles), jnp.sin(angles))

def apply_rotation(vector, cosine_table, sine_table):
    half_width = vector.shape[-1] // 2
    former = vector[..., :half_width]
    latter = vector[..., half_width:]
    cos_wide = cosine_table[:, None, :]
    sin_wide = sine_table[:, None, :]
    return jnp.concatenate([former * cos_wide - latter * sin_wide, latter * cos_wide + former * sin_wide], axis=-1)

def rms_norm(vector, norm_gain):
    return vector * lax.rsqrt(lax.optimization_barrier(jnp.mean(vector * vector, axis=-1, keepdims=True)) + NORM_EPS) * norm_gain

def attend_block(block_rows, length_row, norm_gain, w_query, key_matrix, value_matrix, w_output):
    count_of_rows = block_rows.shape[0]
    segment, seq_place = positions(length_row, count_of_rows)
    cosine_table, sine_table = rope_tables(seq_place, HEAD_DIMENSION)
    normalized_input = reduced_input(rms_norm(block_rows, norm_gain))
    query_unrotated = reduced_gradient(jnp.dot(normalized_input, w_query, precision=FULL_ACCURACY)).reshape(count_of_rows, QUERY_HEADS, HEAD_DIMENSION)
    key_unrotated = reduced_gradient(jnp.dot(normalized_input, key_matrix, precision=FULL_ACCURACY)).reshape(count_of_rows, KEY_VALUE_HEADS, HEAD_DIMENSION)
    value_rows = reduced_input(reduced_gradient(jnp.dot(normalized_input, value_matrix, precision=FULL_ACCURACY))).reshape(count_of_rows, KEY_VALUE_HEADS, HEAD_DIMENSION)
    rotated_query = reduced_input(apply_rotation(query_unrotated, cosine_table, sine_table)).reshape(count_of_rows, KEY_VALUE_HEADS, QUERY_HEADS // KEY_VALUE_HEADS, HEAD_DIMENSION)
    turned_k = reduced_input(apply_rotation(key_unrotated, cosine_table, sine_table))
    scores = reduced_gradient(jnp.einsum('qhgd,khd->hgqk', rotated_query, turned_k, precision=FULL_ACCURACY) * HEAD_DIMENSION ** (-0.5))
    token_order = jnp.arange(count_of_rows, dtype=jnp.int32)
    allowed = (segment[:, None] == segment[None, :]) & (token_order[:, None] >= token_order[None, :])
    scores = jnp.where(allowed, scores, MASKED)
    attn_probs = reduced_input(jax.nn.softmax(scores, axis=-1))
    mixed_heads = reduced_input(reduced_gradient(jnp.einsum('hgqk,khd->qhgd', attn_probs, value_rows, precision=FULL_ACCURACY)))
    mixed_heads = mixed_heads.reshape(count_of_rows, QUERY_HEADS * HEAD_DIMENSION)
    return reduced_gradient(jnp.dot(mixed_heads, w_output, precision=FULL_ACCURACY))

def expert_group(normalized_input, group_routes, group_gates, w_gate, w_up, w_down):
    count_of_rows = normalized_input.shape[0]
    local_routes = group_routes.reshape(N_EXPERT, TOK_DEV * TOPK)
    onehot = (local_routes[:, :, None] == jnp.arange(EXPERTS, dtype=jnp.int32)[None, None, :]).astype(jnp.int32)
    slot_index = (lax.optimization_barrier(jnp.sum(jnp.cumsum(onehot, axis=1) * onehot, axis=2)) - 1).astype(jnp.int32)
    source_index = jnp.arange(N_EXPERT, dtype=jnp.int32)[:, None]
    buffer_rows = N_EXPERT * CAP
    places = (local_routes * buffer_rows + source_index * CAP + slot_index).reshape(-1).astype(jnp.int32)
    token_ids = (jnp.arange(count_of_rows * TOPK, dtype=jnp.int32) // TOPK).astype(jnp.int32)
    owners = jnp.full((EXPERTS * buffer_rows,), count_of_rows, jnp.int32).at[places].set(token_ids)
    taken = reduced_gradient(jnp.take(normalized_input, owners, axis=0, mode='fill', fill_value=0.0))
    taken = taken.reshape(EXPERTS, buffer_rows, normalized_input.shape[1])
    gate_e = jnp.moveaxis(w_gate, 1, 0)
    up_e = jnp.moveaxis(w_up, 1, 0)
    down_e = jnp.moveaxis(w_down, 1, 0)
    gate_pre = reduced_gradient(jnp.einsum('erd,edf->erf', taken, gate_e, precision=FULL_ACCURACY))
    up_pre = reduced_gradient(jnp.einsum('erd,edf->erf', taken, up_e, precision=FULL_ACCURACY))
    hidden = reduced_input(gate_pre * jax.nn.sigmoid(gate_pre) * up_pre)
    produced = reduced_input(reduced_gradient(jnp.einsum('erf,edf->erd', hidden, down_e, precision=FULL_ACCURACY)))
    produced = produced.reshape(EXPERTS * buffer_rows, normalized_input.shape[1])
    picked = jnp.take(produced, places, axis=0).reshape(count_of_rows, TOPK, normalized_input.shape[1])
    return lax.optimization_barrier(jnp.sum(picked * group_gates[:, :, None], axis=1))

def layer_forward(residual, lengths, layer_routes, layer_gates, params):
    gain_attn, gain_ffn, w_query, key_matrix, value_matrix, w_output, w_gate, w_up, w_down = params
    model_width = residual.shape[1]
    blocks = residual.reshape(-1, TOK_DEV, model_width)

    def attend(block_item):
        return attend_block(block_item[0], block_item[1], gain_attn, w_query, key_matrix, value_matrix, w_output)
    attn_out = lax.map(jax.checkpoint(attend), (blocks, lengths))
    middle = residual + attn_out.reshape(residual.shape)
    normalized_input = reduced_input(rms_norm(middle, gain_ffn))
    group_rows = N_EXPERT * TOK_DEV
    normed_groups = normalized_input.reshape(-1, group_rows, model_width)
    route_groups = layer_routes.reshape(-1, group_rows, TOPK)
    gate_groups = layer_gates.reshape(-1, group_rows, TOPK)

    def mix(group_item):
        return expert_group(group_item[0], group_item[1], group_item[2], w_gate, w_up, w_down)
    moe_out = lax.map(jax.checkpoint(mix), (normed_groups, route_groups, gate_groups))
    return middle + moe_out.reshape(residual.shape)

def reference(tokens, lengths, routes, gates, cotangent, norm_attn, norm_ffn, query, key, value, output, w_gate, w_up, w_down):
    start_state = tokens.astype(jnp.float32)
    weights = (norm_attn.astype(jnp.float32), norm_ffn.astype(jnp.float32), query.astype(jnp.float32), key.astype(jnp.float32), value.astype(jnp.float32), output.astype(jnp.float32), w_gate.astype(jnp.float32), w_up.astype(jnp.float32), w_down.astype(jnp.float32))

    def forward(state, params):
        for layer_idx in range(DECODER_LAYERS):
            layer_params = tuple((entry[layer_idx] for entry in params))
            state = layer_forward(state, lengths, routes[layer_idx], gates[layer_idx], layer_params)
        return state
    final_state, pullback = jax.vjp(forward, start_state, weights)
    grad_start, grad_weights = pullback(cotangent.astype(jnp.float32))
    return (final_state.astype(jnp.bfloat16), grad_start, grad_weights[0], grad_weights[1], grad_weights[2], grad_weights[3], grad_weights[4], grad_weights[5], grad_weights[6], grad_weights[7], grad_weights[8])
```

```python
import math

import jax
import jax.numpy as jnp
from jax import lax
from jax.sharding import PartitionSpec as P

QUERY_HEADS = 24
KEY_VALUE_HEADS = 8
HEAD_DIMENSION = 64
CORES = 2

NORM_EPS = 1e-06
MASKED = -1000000000.0
AXES = ("fsdp", "expert")


class Place:
    def __init__(self):
        self.planes = lax.axis_size("fsdp") // CORES
        self.columns = lax.axis_size("expert")
        fsdp = lax.axis_index("fsdp")
        self.plane = fsdp // CORES
        self.core = fsdp % CORES
        self.column = lax.axis_index("expert")

    def hop(self, value, up=0, flip=0, swap=0):
        pairs = []
        for plane in range(self.planes):
            for core in range(CORES):
                for column in range(self.columns):
                    source = (plane * CORES + core) * self.columns + column
                    target = ((plane + up) % self.planes * CORES + (core ^ swap)) * self.columns
                    pairs.append((source, target + (column ^ flip)))
        return lax.ppermute(value, AXES, pairs)


def spread(place, block):
    if place.columns != 4:
        return [block] + [place.hop(block, flip=m) for m in range(1, place.columns)]
    half = block.shape[1] // 2
    one = place.hop(block, flip=1)
    two = place.hop(block, flip=2)
    head = place.hop(one[:, :half], flip=2)
    tail = place.hop(two[:, half:], flip=1)
    return [block, one, two, jnp.concatenate([head, tail], axis=1)]


def gather_tokens(place, block):
    own = block[None]
    others = jnp.stack([place.hop(block, up=k) for k in range(1, place.planes)])
    near = spread(place, own)
    far = spread(place, others)
    return [jnp.concatenate([a, b], axis=0) for a, b in zip(near, far)]


def fold(place, parts):
    wide = lambda value: value.astype(jnp.float32)
    if place.columns != 4:
        total = wide(parts[0])
        for m in range(1, place.columns):
            total = total + wide(place.hop(parts[m], flip=m))
        return total
    half = parts[0].shape[1] // 2
    head = place.hop(parts[3][:, :half], flip=2)
    tail = place.hop(parts[3][:, half:], flip=1)
    one_tail = place.hop(parts[1][:, half:], flip=1)
    two_head = place.hop(parts[2][:, :half], flip=2)
    one_head = place.hop((wide(parts[1][:, :half]) + wide(head)).astype(parts[1].dtype), flip=1)
    two_tail = place.hop((wide(parts[2][:, half:]) + wide(tail)).astype(parts[2].dtype), flip=2)
    upper = wide(parts[0][:, :half]) + wide(one_head) + wide(two_head)
    lower = wide(parts[0][:, half:]) + wide(one_tail) + wide(two_tail)
    return jnp.concatenate([upper, lower], axis=1)


def scatter_sums(place, parts):
    far = fold(place, [part[1:] for part in parts]).astype(parts[0].dtype)
    arrived = [place.hop(far[k - 1], up=-k) for k in range(1, place.planes)]
    total = fold(place, [part[:1] for part in parts])[0]
    for piece in arrived:
        total = total + piece.astype(jnp.float32)
    return total


def gather_gates(place, routes, gates, expert_count):
    names = jnp.arange(expert_count, dtype=jnp.int32)
    chosen = routes[:, None, :, :] == names[None, :, None, None]
    table = jnp.sum(jnp.where(chosen, gates[:, None, :, :], 0.0), axis=3)
    line = jnp.stack([table] + [place.hop(table, up=k) for k in range(1, place.planes)])
    owned = expert_count // place.columns
    found = []
    for m in range(place.columns):
        start = (place.column ^ m) * owned
        piece = lax.dynamic_slice_in_dim(line, start, owned, axis=2)
        found.append(place.hop(piece, flip=m) if m else piece)
    return found


def gather_experts(place, weights):
    rows, experts, hidden = weights[0].shape
    share = hidden // place.planes

    def cut(plane):
        pieces = [lax.dynamic_slice_in_dim(w, plane * share, share, axis=2) for w in weights]
        return jnp.stack([p.reshape(rows, experts * share) for p in pieces])

    own = [cut(place.plane)]
    for k in range(1, place.planes):
        own.append(place.hop(cut((place.plane + k) % place.planes), up=k))
    own = jnp.stack(own)
    sibling = place.hop(own, swap=1)
    both = jnp.concatenate([own, sibling])
    shard = jnp.arange(place.planes * CORES)
    index = ((shard % CORES) ^ place.core) * place.planes
    index = index + (place.plane - shard // CORES) % place.planes
    return [
        jnp.take(both[:, i], index, axis=0).reshape(-1, experts * share)
        for i in range(len(weights))
    ]


def scatter_experts(place, grads, experts):
    features, width = grads[0].shape
    rows = features // (place.planes * CORES)
    share = width // experts
    shape = (place.planes, CORES, rows, width)
    stacked = jnp.stack([g.reshape(shape) for g in grads], axis=1)
    mine = lax.dynamic_index_in_dim(stacked, place.core, axis=2, keepdims=False)
    others = lax.dynamic_index_in_dim(stacked, 1 - place.core, axis=2, keepdims=False)
    arrived = place.hop(others.astype(jnp.bfloat16), swap=1)
    total = (mine + arrived.astype(jnp.float32)).astype(jnp.bfloat16)
    pieces = [lax.dynamic_index_in_dim(total, place.plane, axis=0, keepdims=False)]
    for k in range(1, place.planes):
        target = (place.plane + k) % place.planes
        piece = lax.dynamic_index_in_dim(total, target, axis=0, keepdims=False)
        pieces.append(place.hop(piece, up=k))
    index = (place.plane - jnp.arange(place.planes)) % place.planes
    ordered = jnp.take(jnp.stack(pieces), index, axis=0)
    ordered = ordered.reshape(place.planes, len(grads), rows, experts, share)
    ordered = jnp.transpose(ordered, (1, 2, 3, 0, 4)).reshape(len(grads), rows, experts, -1)
    return [ordered[i].astype(jnp.float32) for i in range(len(grads))]


def positions(length_row, count_of_rows):
    ends = jnp.cumsum(length_row)
    token_order = jnp.arange(count_of_rows, dtype=jnp.int32)
    passed = token_order[:, None] >= ends[None, :]
    segment = jnp.sum(passed.astype(jnp.int32), axis=1)
    before = jnp.sum(jnp.where(passed, length_row[None, :], 0), axis=1)
    return (segment, token_order - before)


def rope_tables(seq_place, head_width):
    half_width = head_width // 2
    freq_table = jnp.exp(
        jnp.arange(half_width, dtype=jnp.float32) * (-2.0 * math.log(10000.0) / head_width)
    )
    angles = seq_place.astype(jnp.float32)[:, None] * freq_table[None, :]
    return (jnp.cos(angles), jnp.sin(angles))


def apply_rotation(vector, cosine_table, sine_table):
    half_width = vector.shape[-1] // 2
    former = vector[..., :half_width]
    latter = vector[..., half_width:]
    cos_wide = cosine_table[:, None, :]
    sin_wide = sine_table[:, None, :]
    return jnp.concatenate(
        [former * cos_wide - latter * sin_wide, latter * cos_wide + former * sin_wide], axis=-1
    )


def reverse_rotation(vector, cosine_table, sine_table):
    return apply_rotation(vector, cosine_table, -sine_table)


def rms_forward(residual, norm_gain):
    inverse = lax.rsqrt(jnp.mean(residual * residual, axis=-1, keepdims=True) + NORM_EPS)
    return (inverse, (residual * inverse * norm_gain).astype(jnp.bfloat16))


def rms_backward(residual, inverse, norm_gain, upstream):
    gain_grad = jnp.sum(upstream * residual * inverse, axis=0)
    scaled = upstream * norm_gain
    inner = jnp.mean(scaled * residual, axis=-1, keepdims=True)
    return (gain_grad, inverse * scaled - residual * inverse * inverse * inverse * inner)


def score_block(rotated_query, turned_k, allowed):
    scores = jnp.einsum(
        "qhgd,khd->hgqk", rotated_query, turned_k, preferred_element_type=jnp.float32
    ) * HEAD_DIMENSION ** (-0.5)
    return jnp.where(allowed, scores, MASKED)


def attend_forward(residual, allowed, tables, gain, matrices):
    w_in, w_output = matrices
    count_of_rows = residual.shape[0]
    query_width = QUERY_HEADS * HEAD_DIMENSION
    key_width = KEY_VALUE_HEADS * HEAD_DIMENSION
    inverse, normalized_input = rms_forward(residual, gain)
    projected = jnp.dot(normalized_input, w_in, preferred_element_type=jnp.float32)
    query_unrotated = projected[:, :query_width].reshape(count_of_rows, QUERY_HEADS, -1)
    key_unrotated = projected[:, query_width : query_width + key_width]
    key_unrotated = key_unrotated.reshape(count_of_rows, KEY_VALUE_HEADS, -1)
    value_rows = projected[:, query_width + key_width :].astype(jnp.bfloat16)
    value_rows = value_rows.reshape(count_of_rows, KEY_VALUE_HEADS, -1)
    rotated_query = (
        apply_rotation(query_unrotated, *tables)
        .astype(jnp.bfloat16)
        .reshape(count_of_rows, KEY_VALUE_HEADS, QUERY_HEADS // KEY_VALUE_HEADS, HEAD_DIMENSION)
    )
    turned_k = apply_rotation(key_unrotated, *tables).astype(jnp.bfloat16)
    scores = score_block(rotated_query, turned_k, allowed)
    row_top = jnp.max(scores, axis=-1, keepdims=True)
    exp_scores = jnp.exp(scores - row_top)
    row_total = jnp.sum(exp_scores, axis=-1, keepdims=True)
    attn_probs = (exp_scores / row_total).astype(jnp.bfloat16)
    log_total = row_top + jnp.log(row_total)
    mixed_heads = jnp.einsum(
        "hgqk,khd->qhgd", attn_probs, value_rows, preferred_element_type=jnp.float32
    )
    mixed_heads = mixed_heads.astype(jnp.bfloat16).reshape(count_of_rows, query_width)
    attn_out = jnp.dot(mixed_heads, w_output, preferred_element_type=jnp.float32)
    return (
        residual + attn_out,
        (inverse, normalized_input, rotated_query, turned_k, value_rows, log_total, mixed_heads),
    )


def attend_backward(residual, allowed, tables, gain, matrices, stash, upstream):
    w_in, w_output = matrices
    inverse, normalized_input, rotated_query, turned_k, value_rows, log_total, mixed_heads = stash
    count_of_rows = residual.shape[0]
    branch_grad = upstream.astype(jnp.bfloat16)
    grad_wo = jnp.einsum("td,te->de", mixed_heads, branch_grad, preferred_element_type=jnp.float32)
    mixed_gradient = jnp.einsum(
        "te,de->td", branch_grad, w_output, preferred_element_type=jnp.float32
    )
    mixed_gradient = mixed_gradient.astype(jnp.bfloat16).reshape(
        count_of_rows, KEY_VALUE_HEADS, QUERY_HEADS // KEY_VALUE_HEADS, HEAD_DIMENSION
    )
    attn_probs = jnp.exp(score_block(rotated_query, turned_k, allowed) - log_total)
    value_rows_gradient = jnp.einsum(
        "hgqk,qhgd->khd",
        attn_probs.astype(jnp.bfloat16),
        mixed_gradient,
        preferred_element_type=jnp.float32,
    )
    value_rows_gradient = value_rows_gradient.astype(jnp.bfloat16).reshape(count_of_rows, -1)
    grad_probs = jnp.einsum(
        "qhgd,khd->hgqk", mixed_gradient, value_rows, preferred_element_type=jnp.float32
    )
    grad_scores = attn_probs * (
        grad_probs - jnp.sum(attn_probs * grad_probs, axis=-1, keepdims=True)
    )
    grad_scores = grad_scores.astype(jnp.bfloat16)
    grad_tq = jnp.einsum(
        "hgqk,khd->qhgd", grad_scores, turned_k, preferred_element_type=jnp.float32
    ) * HEAD_DIMENSION ** (-0.5)
    turned_key_gradient = jnp.einsum(
        "hgqk,qhgd->khd", grad_scores, rotated_query, preferred_element_type=jnp.float32
    ) * HEAD_DIMENSION ** (-0.5)
    grad_query = reverse_rotation(
        grad_tq.reshape(count_of_rows, QUERY_HEADS, HEAD_DIMENSION), *tables
    )
    grad_query = grad_query.astype(jnp.bfloat16).reshape(count_of_rows, -1)
    grad_key = reverse_rotation(turned_key_gradient, *tables).astype(jnp.bfloat16)
    grad_key = grad_key.reshape(count_of_rows, -1)
    grad_in = jnp.concatenate([grad_query, grad_key, value_rows_gradient], axis=1)
    grad_w_in = jnp.einsum("td,te->de", normalized_input, grad_in, preferred_element_type=jnp.float32)
    grad_normed = jnp.einsum("te,de->td", grad_in, w_in, preferred_element_type=jnp.float32)
    gain_grad, residual_grad = rms_backward(residual, inverse, gain, grad_normed)
    return (upstream + residual_grad, gain_grad, grad_w_in, grad_wo)


def widen(gate_columns, share):
    return jnp.repeat(gate_columns, share, axis=1)


def experts_forward(place, middle, gain, gate_parts, weights):
    w_gate, w_up, w_down = weights
    share = w_gate.shape[1] // gate_parts[0].shape[1]
    model_width = middle.shape[1]
    inverse, normalized_input = rms_forward(middle, gain)
    chunks = gather_tokens(place, normalized_input)
    parts, kept = [], []
    for chunk, gate_columns in zip(chunks, gate_parts):
        rows = chunk.reshape(-1, model_width)
        gate_pre = jnp.dot(rows, w_gate, preferred_element_type=jnp.float32)
        up_pre = jnp.dot(rows, w_up, preferred_element_type=jnp.float32)
        weighed = gate_pre * jax.nn.sigmoid(gate_pre) * up_pre * widen(gate_columns, share)
        weighed = weighed.astype(jnp.bfloat16)
        produced = lax.dot_general(
            weighed, w_down, (((1,), (1,)), ((), ())), preferred_element_type=jnp.float32
        )
        parts.append(produced.astype(jnp.bfloat16).reshape(chunk.shape))
        kept.append((rows, gate_pre, up_pre, weighed))
    return (middle + scatter_sums(place, parts), (inverse, kept))


def experts_backward(place, middle, gain, gate_parts, weights, stash, upstream, chunks):
    w_gate, w_up, w_down = weights
    share = w_gate.shape[1] // gate_parts[0].shape[1]
    model_width = middle.shape[1]
    inverse, kept = stash
    parts, gate_grads, up_grads, row_grads = [], [], [], []
    for chunk, gate_columns, (rows, gate_pre, up_pre, weighed) in zip(chunks, gate_parts, kept):
        grads = chunk.reshape(-1, model_width)
        hidden_grad = jnp.dot(grads, w_down, preferred_element_type=jnp.float32)
        hidden_grad = hidden_grad * widen(gate_columns, share)
        gate_sig = jax.nn.sigmoid(gate_pre)
        gate_grad = hidden_grad * up_pre * gate_sig * (1.0 + gate_pre * (1.0 - gate_sig))
        gate_grad = gate_grad.astype(jnp.bfloat16)
        up_grad = (hidden_grad * gate_pre * gate_sig).astype(jnp.bfloat16)
        back = (((1,), (1,)), ((), ()))
        produced = lax.dot_general(gate_grad, w_gate, back, preferred_element_type=jnp.float32)
        produced = produced + lax.dot_general(
            up_grad, w_up, back, preferred_element_type=jnp.float32
        )
        parts.append(produced.astype(jnp.bfloat16).reshape(chunk.shape))
        gate_grads.append(gate_grad)
        up_grads.append(up_grad)
        row_grads.append(grads)
    normed_grad = scatter_sums(place, parts)
    rows = jnp.concatenate([entry[0] for entry in kept])
    weighed = jnp.concatenate([entry[3] for entry in kept])
    outer = (((0,), (0,)), ((), ()))
    weight_grads = [
        lax.dot_general(a, b, outer, preferred_element_type=jnp.float32)
        for a, b in (
            (rows, jnp.concatenate(gate_grads)),
            (rows, jnp.concatenate(up_grads)),
            (jnp.concatenate(row_grads), weighed),
        )
    ]
    gain_grad, middle_grad = rms_backward(middle, inverse, gain, normed_grad)
    return (upstream + middle_grad, gain_grad, weight_grads)


def shards(
    tokens,
    lengths,
    routes,
    gates,
    cotangent,
    norm_attn,
    norm_ffn,
    query,
    key,
    value,
    output,
    w_gate,
    w_up,
    w_down,
):
    place = Place()
    token_rows = tokens.shape[0]
    layer_count, _, experts, _ = w_gate.shape
    expert_count = experts * place.columns
    in_width = query.shape[2] + key.shape[2] + value.shape[2]
    segment, seq_place = positions(lengths[0], token_rows)
    tables = rope_tables(seq_place, HEAD_DIMENSION)
    token_order = jnp.arange(token_rows, dtype=jnp.int32)
    allowed = (segment[:, None] == segment[None, :]) & (
        token_order[:, None] >= token_order[None, :]
    )
    gains = jnp.concatenate([norm_attn, norm_ffn]).T
    packs = []
    for l in range(layer_count):
        pack = [query[l], key[l], value[l], output[l]]
        if l == 0:
            pack.append(jnp.pad(gains, ((0, 0), (0, 128 - gains.shape[1]))))
        packs.append(jnp.concatenate(pack, axis=1))
    full = lax.all_gather(packs[0], AXES, axis=0, tiled=True)
    gains = full[:, in_width + output.shape[2] :].T[: 2 * layer_count].astype(jnp.float32)
    gate_rows = gather_gates(place, routes, gates, expert_count)
    gate_parts = [
        [
            jnp.transpose(piece[:, l], (0, 2, 1)).reshape(-1, experts)
            for piece in gate_rows
        ]
        for l in range(layer_count)
    ]
    expert_weights = gather_experts(place, [w_gate[0], w_up[0], w_down[0]])
    last_grads = None

    residual = tokens.astype(jnp.float32)
    matrices, weights, stored = [], [], []
    for l in range(layer_count):
        matrices.append((full[:, :in_width], full[:, in_width : in_width + output.shape[2]]))
        weights.append(expert_weights)
        layer_input = residual
        middle, attn_stash = attend_forward(layer_input, allowed, tables, gains[l], matrices[l])
        if l + 1 < layer_count:
            held, pack, *shares = lax.optimization_barrier(
                (middle, packs[l + 1], w_gate[l + 1], w_up[l + 1], w_down[l + 1])
            )
            middle = held
            full = lax.all_gather(pack, AXES, axis=0, tiled=True)
            expert_weights = gather_experts(place, shares)
        residual, moe_stash = experts_forward(
            place, middle, gains[layer_count + l], gate_parts[l], weights[l]
        )
        if l + 2 == layer_count or layer_count == 1:
            held, last = lax.optimization_barrier((residual, cotangent))
            residual = held
            last_grads = gather_tokens(place, last)
        stored.append((layer_input, middle, attn_stash, moe_stash))
    result = residual.astype(jnp.bfloat16)

    upstream = cotangent.astype(jnp.float32)
    in_grads, out_grads = [None] * layer_count, [None] * layer_count
    gain_grads = [None] * (2 * layer_count)
    expert_grads = [None] * layer_count
    for l in reversed(range(layer_count)):
        layer_input, middle, attn_stash, moe_stash = stored[l]
        chunks = last_grads
        if l + 1 < layer_count:
            chunks = gather_tokens(place, upstream.astype(jnp.bfloat16))
        upstream, gain_grads[layer_count + l], weight_grads = experts_backward(
            place,
            middle,
            gains[layer_count + l],
            gate_parts[l],
            weights[l],
            moe_stash,
            upstream,
            chunks,
        )
        expert_grads[l] = scatter_experts(place, weight_grads, experts)
        upstream, gain_grads[l], grad_w_in, grad_wo = attend_backward(
            layer_input, allowed, tables, gains[l], matrices[l], attn_stash, upstream
        )
        summed = lax.psum_scatter(
            jnp.concatenate([grad_w_in, grad_wo], axis=1).astype(jnp.bfloat16),
            AXES,
            scatter_dimension=0,
            tiled=True,
        ).astype(jnp.float32)
        in_grads[l], out_grads[l] = summed[:, :in_width], summed[:, in_width:]
    gain_sums = lax.psum_scatter(jnp.stack(gain_grads), AXES, scatter_dimension=1, tiled=True)
    in_grads = jnp.stack(in_grads)
    key_start, value_start = query.shape[2], query.shape[2] + key.shape[2]
    return (
        result,
        upstream,
        gain_sums[:layer_count],
        gain_sums[layer_count:],
        in_grads[:, :, :key_start],
        in_grads[:, :, key_start:value_start],
        in_grads[:, :, value_start:],
        jnp.stack(out_grads),
        jnp.stack([entry[0] for entry in expert_grads]),
        jnp.stack([entry[1] for entry in expert_grads]),
        jnp.stack([entry[2] for entry in expert_grads]),
    )


def solution(mesh):
    rows = P(AXES, None)
    layered = P(None, AXES, None)
    expert = P(None, "fsdp", "expert", None)
    gain = P(None, AXES)
    return jax.shard_map(
        shards,
        mesh=mesh,
        in_specs=(rows, rows, layered, layered, rows, gain, gain)
        + (layered,) * 4
        + (expert,) * 3,
        out_specs=(rows, rows, gain, gain) + (layered,) * 4 + (expert,) * 3,
        check_vma=False,
    )
```

```python
import functools
import math

import jax
import jax.numpy as jnp
from jax import lax
from jax.experimental import pallas as pl
from jax.experimental.pallas import tpu as pltpu
from jax.sharding import PartitionSpec as P

QUERY_HEADS = 24
KEY_VALUE_HEADS = 8
HEAD_DIMENSION = 64
CORES = 2

NORM_EPS = 1e-06
MASKED = -1000000000.0
AXES = ("fsdp", "expert")


class Place:
    def __init__(self):
        self.planes = lax.axis_size("fsdp") // CORES
        self.columns = lax.axis_size("expert")
        fsdp = lax.axis_index("fsdp")
        self.plane = fsdp // CORES
        self.core = fsdp % CORES
        self.column = lax.axis_index("expert")

    def hop(self, value, up=0, flip=0, swap=0):
        pairs = []
        for plane in range(self.planes):
            for core in range(CORES):
                for column in range(self.columns):
                    source = (plane * CORES + core) * self.columns + column
                    target = ((plane + up) % self.planes * CORES + (core ^ swap)) * self.columns
                    pairs.append((source, target + (column ^ flip)))
        return lax.ppermute(value, AXES, pairs)


def spread(place, block):
    if place.columns != 4:
        return [block] + [place.hop(block, flip=m) for m in range(1, place.columns)]
    half = block.shape[1] // 2
    one = place.hop(block, flip=1)
    two = place.hop(block, flip=2)
    head = place.hop(one[:, :half], flip=2)
    tail = place.hop(two[:, half:], flip=1)
    return [block, one, two, jnp.concatenate([head, tail], axis=1)]


def gather_tokens(place, block):
    own = block[None]
    others = jnp.stack([place.hop(block, up=k) for k in range(1, place.planes)])
    near = spread(place, own)
    far = spread(place, others)
    return [jnp.concatenate([a, b], axis=0) for a, b in zip(near, far)]


def fold(place, parts):
    wide = lambda value: value.astype(jnp.float32)
    if place.columns != 4:
        total = wide(parts[0])
        for m in range(1, place.columns):
            total = total + wide(place.hop(parts[m], flip=m))
        return total
    half = parts[0].shape[1] // 2
    head = place.hop(parts[3][:, :half], flip=2)
    tail = place.hop(parts[3][:, half:], flip=1)
    one_tail = place.hop(parts[1][:, half:], flip=1)
    two_head = place.hop(parts[2][:, :half], flip=2)
    one_head = place.hop((wide(parts[1][:, :half]) + wide(head)).astype(parts[1].dtype), flip=1)
    two_tail = place.hop((wide(parts[2][:, half:]) + wide(tail)).astype(parts[2].dtype), flip=2)
    upper = wide(parts[0][:, :half]) + wide(one_head) + wide(two_head)
    lower = wide(parts[0][:, half:]) + wide(one_tail) + wide(two_tail)
    return jnp.concatenate([upper, lower], axis=1)


def scatter_sums(place, parts):
    far = fold(place, [part[1:] for part in parts]).astype(parts[0].dtype)
    arrived = [place.hop(far[k - 1], up=-k) for k in range(1, place.planes)]
    total = fold(place, [part[:1] for part in parts])[0]
    for piece in arrived:
        total = total + piece.astype(jnp.float32)
    return total


def gather_gates(place, routes, gates, expert_count):
    names = jnp.arange(expert_count, dtype=jnp.int32)
    chosen = routes[:, None, :, :] == names[None, :, None, None]
    table = jnp.sum(jnp.where(chosen, gates[:, None, :, :], 0.0), axis=3)
    line = jnp.stack([table] + [place.hop(table, up=k) for k in range(1, place.planes)])
    owned = expert_count // place.columns
    found = []
    for m in range(place.columns):
        start = (place.column ^ m) * owned
        piece = lax.dynamic_slice_in_dim(line, start, owned, axis=2)
        found.append(place.hop(piece, flip=m) if m else piece)
    return found


def gather_experts(place, weights):
    rows, experts, hidden = weights[0].shape
    share = hidden // place.planes

    def cut(plane):
        pieces = [lax.dynamic_slice_in_dim(w, plane * share, share, axis=2) for w in weights]
        return jnp.stack([p.reshape(rows, experts * share) for p in pieces])

    own = [cut(place.plane)]
    for k in range(1, place.planes):
        own.append(place.hop(cut((place.plane + k) % place.planes), up=k))
    own = jnp.stack(own)
    sibling = place.hop(own, swap=1)
    both = jnp.concatenate([own, sibling])
    shard = jnp.arange(place.planes * CORES)
    index = ((shard % CORES) ^ place.core) * place.planes
    index = index + (place.plane - shard // CORES) % place.planes
    return [
        jnp.take(both[:, i], index, axis=0).reshape(-1, experts * share)
        for i in range(len(weights))
    ]


def scatter_experts(place, grads, experts):
    features, width = grads[0].shape
    rows = features // (place.planes * CORES)
    share = width // experts
    shape = (place.planes, CORES, rows, width)
    stacked = jnp.stack([g.reshape(shape) for g in grads], axis=1)
    mine = lax.dynamic_index_in_dim(stacked, place.core, axis=2, keepdims=False)
    others = lax.dynamic_index_in_dim(stacked, 1 - place.core, axis=2, keepdims=False)
    arrived = place.hop(others.astype(jnp.bfloat16), swap=1)
    total = (mine + arrived.astype(jnp.float32)).astype(jnp.bfloat16)
    pieces = [lax.dynamic_index_in_dim(total, place.plane, axis=0, keepdims=False)]
    for k in range(1, place.planes):
        target = (place.plane + k) % place.planes
        piece = lax.dynamic_index_in_dim(total, target, axis=0, keepdims=False)
        pieces.append(place.hop(piece, up=k))
    index = (place.plane - jnp.arange(place.planes)) % place.planes
    ordered = jnp.take(jnp.stack(pieces), index, axis=0)
    ordered = ordered.reshape(place.planes, len(grads), rows, experts, share)
    ordered = jnp.transpose(ordered, (1, 2, 3, 0, 4)).reshape(len(grads), rows, experts, -1)
    return [ordered[i].astype(jnp.float32) for i in range(len(grads))]


def positions(length_row, count_of_rows):
    ends = jnp.cumsum(length_row)
    token_order = jnp.arange(count_of_rows, dtype=jnp.int32)
    passed = token_order[:, None] >= ends[None, :]
    segment = jnp.sum(passed.astype(jnp.int32), axis=1)
    before = jnp.sum(jnp.where(passed, length_row[None, :], 0), axis=1)
    return (segment, token_order - before)


def rope_tables(seq_place, head_width):
    half_width = head_width // 2
    freq_table = jnp.exp(
        jnp.arange(half_width, dtype=jnp.float32) * (-2.0 * math.log(10000.0) / head_width)
    )
    angles = seq_place.astype(jnp.float32)[:, None] * freq_table[None, :]
    return (jnp.cos(angles), jnp.sin(angles))


def apply_rotation(vector, cosine_table, sine_table):
    half_width = vector.shape[-1] // 2
    former = vector[..., :half_width]
    latter = vector[..., half_width:]
    cos_wide = cosine_table[:, None, :]
    sin_wide = sine_table[:, None, :]
    return jnp.concatenate(
        [former * cos_wide - latter * sin_wide, latter * cos_wide + former * sin_wide], axis=-1
    )


def reverse_rotation(vector, cosine_table, sine_table):
    return apply_rotation(vector, cosine_table, -sine_table)


def rms_forward(residual, norm_gain):
    inverse = lax.rsqrt(jnp.mean(residual * residual, axis=-1, keepdims=True) + NORM_EPS)
    return (inverse, (residual * inverse * norm_gain).astype(jnp.bfloat16))


def rms_backward(residual, inverse, norm_gain, upstream):
    gain_grad = jnp.sum(upstream * residual * inverse, axis=0)
    scaled = upstream * norm_gain
    inner = jnp.mean(scaled * residual, axis=-1, keepdims=True)
    return (gain_grad, inverse * scaled - residual * inverse * inverse * inverse * inner)


def score_block(rotated_query, turned_k, allowed):
    scores = jnp.einsum(
        "qhgd,khd->hgqk", rotated_query, turned_k, preferred_element_type=jnp.float32
    ) * HEAD_DIMENSION ** (-0.5)
    return jnp.where(allowed, scores, MASKED)


def attend_forward(residual, allowed, tables, gain, matrices):
    w_in, w_output = matrices
    count_of_rows = residual.shape[0]
    query_width = QUERY_HEADS * HEAD_DIMENSION
    key_width = KEY_VALUE_HEADS * HEAD_DIMENSION
    inverse, normalized_input = rms_forward(residual, gain)
    projected = jnp.dot(normalized_input, w_in, preferred_element_type=jnp.float32)
    query_unrotated = projected[:, :query_width].reshape(count_of_rows, QUERY_HEADS, -1)
    key_unrotated = projected[:, query_width : query_width + key_width]
    key_unrotated = key_unrotated.reshape(count_of_rows, KEY_VALUE_HEADS, -1)
    value_rows = projected[:, query_width + key_width :].astype(jnp.bfloat16)
    value_rows = value_rows.reshape(count_of_rows, KEY_VALUE_HEADS, -1)
    rotated_query = (
        apply_rotation(query_unrotated, *tables)
        .astype(jnp.bfloat16)
        .reshape(count_of_rows, KEY_VALUE_HEADS, QUERY_HEADS // KEY_VALUE_HEADS, HEAD_DIMENSION)
    )
    turned_k = apply_rotation(key_unrotated, *tables).astype(jnp.bfloat16)
    scores = score_block(rotated_query, turned_k, allowed)
    row_top = jnp.max(scores, axis=-1, keepdims=True)
    exp_scores = jnp.exp(scores - row_top)
    row_total = jnp.sum(exp_scores, axis=-1, keepdims=True)
    attn_probs = (exp_scores / row_total).astype(jnp.bfloat16)
    log_total = row_top + jnp.log(row_total)
    mixed_heads = jnp.einsum(
        "hgqk,khd->qhgd", attn_probs, value_rows, preferred_element_type=jnp.float32
    )
    mixed_heads = mixed_heads.astype(jnp.bfloat16).reshape(count_of_rows, query_width)
    attn_out = jnp.dot(mixed_heads, w_output, preferred_element_type=jnp.float32)
    return (
        residual + attn_out,
        (inverse, normalized_input, rotated_query, turned_k, value_rows, log_total, mixed_heads),
    )


def attend_backward(residual, allowed, tables, gain, matrices, stash, upstream):
    w_in, w_output = matrices
    inverse, normalized_input, rotated_query, turned_k, value_rows, log_total, mixed_heads = stash
    count_of_rows = residual.shape[0]
    branch_grad = upstream.astype(jnp.bfloat16)
    grad_wo = jnp.einsum("td,te->de", mixed_heads, branch_grad, preferred_element_type=jnp.float32)
    mixed_gradient = jnp.einsum(
        "te,de->td", branch_grad, w_output, preferred_element_type=jnp.float32
    )
    mixed_gradient = mixed_gradient.astype(jnp.bfloat16).reshape(
        count_of_rows, KEY_VALUE_HEADS, QUERY_HEADS // KEY_VALUE_HEADS, HEAD_DIMENSION
    )
    attn_probs = jnp.exp(score_block(rotated_query, turned_k, allowed) - log_total)
    value_rows_gradient = jnp.einsum(
        "hgqk,qhgd->khd",
        attn_probs.astype(jnp.bfloat16),
        mixed_gradient,
        preferred_element_type=jnp.float32,
    )
    value_rows_gradient = value_rows_gradient.astype(jnp.bfloat16).reshape(count_of_rows, -1)
    grad_probs = jnp.einsum(
        "qhgd,khd->hgqk", mixed_gradient, value_rows, preferred_element_type=jnp.float32
    )
    grad_scores = attn_probs * (
        grad_probs - jnp.sum(attn_probs * grad_probs, axis=-1, keepdims=True)
    )
    grad_scores = grad_scores.astype(jnp.bfloat16)
    grad_tq = jnp.einsum(
        "hgqk,khd->qhgd", grad_scores, turned_k, preferred_element_type=jnp.float32
    ) * HEAD_DIMENSION ** (-0.5)
    turned_key_gradient = jnp.einsum(
        "hgqk,qhgd->khd", grad_scores, rotated_query, preferred_element_type=jnp.float32
    ) * HEAD_DIMENSION ** (-0.5)
    grad_query = reverse_rotation(
        grad_tq.reshape(count_of_rows, QUERY_HEADS, HEAD_DIMENSION), *tables
    )
    grad_query = grad_query.astype(jnp.bfloat16).reshape(count_of_rows, -1)
    grad_key = reverse_rotation(turned_key_gradient, *tables).astype(jnp.bfloat16)
    grad_key = grad_key.reshape(count_of_rows, -1)
    grad_in = jnp.concatenate([grad_query, grad_key, value_rows_gradient], axis=1)
    grad_w_in = jnp.einsum("td,te->de", normalized_input, grad_in, preferred_element_type=jnp.float32)
    grad_normed = jnp.einsum("te,de->td", grad_in, w_in, preferred_element_type=jnp.float32)
    gain_grad, residual_grad = rms_backward(residual, inverse, gain, grad_normed)
    return (upstream + residual_grad, gain_grad, grad_w_in, grad_wo)


def widen(gate_columns, share):
    return jnp.repeat(gate_columns, share, axis=1)


def experts_forward(place, middle, gain, gate_parts, weights):
    w_gate, w_up, w_down = weights
    share = w_gate.shape[1] // gate_parts[0].shape[1]
    model_width = middle.shape[1]
    inverse, normalized_input = rms_forward(middle, gain)
    chunks = gather_tokens(place, normalized_input)
    parts, kept = [], []
    for chunk, gate_columns in zip(chunks, gate_parts):
        rows = chunk.reshape(-1, model_width)
        gate_pre = jnp.dot(rows, w_gate, preferred_element_type=jnp.float32)
        up_pre = jnp.dot(rows, w_up, preferred_element_type=jnp.float32)
        weighed = gate_pre * jax.nn.sigmoid(gate_pre) * up_pre * widen(gate_columns, share)
        weighed = weighed.astype(jnp.bfloat16)
        produced = lax.dot_general(
            weighed, w_down, (((1,), (1,)), ((), ())), preferred_element_type=jnp.float32
        )
        parts.append(produced.astype(jnp.bfloat16).reshape(chunk.shape))
        kept.append((rows, gate_pre, up_pre, weighed))
    return (middle + scatter_sums(place, parts), (inverse, kept))


def experts_backward(place, middle, gain, gate_parts, weights, stash, upstream, chunks):
    w_gate, w_up, w_down = weights
    share = w_gate.shape[1] // gate_parts[0].shape[1]
    model_width = middle.shape[1]
    inverse, kept = stash
    parts, gate_grads, up_grads, row_grads = [], [], [], []
    for chunk, gate_columns, (rows, gate_pre, up_pre, weighed) in zip(chunks, gate_parts, kept):
        grads = chunk.reshape(-1, model_width)
        hidden_grad = jnp.dot(grads, w_down, preferred_element_type=jnp.float32)
        hidden_grad = hidden_grad * widen(gate_columns, share)
        gate_sig = jax.nn.sigmoid(gate_pre)
        gate_grad = hidden_grad * up_pre * gate_sig * (1.0 + gate_pre * (1.0 - gate_sig))
        gate_grad = gate_grad.astype(jnp.bfloat16)
        up_grad = (hidden_grad * gate_pre * gate_sig).astype(jnp.bfloat16)
        back = (((1,), (1,)), ((), ()))
        produced = lax.dot_general(gate_grad, w_gate, back, preferred_element_type=jnp.float32)
        produced = produced + lax.dot_general(
            up_grad, w_up, back, preferred_element_type=jnp.float32
        )
        parts.append(produced.astype(jnp.bfloat16).reshape(chunk.shape))
        gate_grads.append(gate_grad)
        up_grads.append(up_grad)
        row_grads.append(grads)
    normed_grad = scatter_sums(place, parts)
    rows = jnp.concatenate([entry[0] for entry in kept])
    weighed = jnp.concatenate([entry[3] for entry in kept])
    outer = (((0,), (0,)), ((), ()))
    weight_grads = [
        lax.dot_general(a, b, outer, preferred_element_type=jnp.float32)
        for a, b in (
            (rows, jnp.concatenate(gate_grads)),
            (rows, jnp.concatenate(up_grads)),
            (jnp.concatenate(row_grads), weighed),
        )
    ]
    gain_grad, middle_grad = rms_backward(middle, inverse, gain, normed_grad)
    return (upstream + middle_grad, gain_grad, weight_grads)


def shards(
    tokens,
    lengths,
    routes,
    gates,
    cotangent,
    norm_attn,
    norm_ffn,
    query,
    key,
    value,
    output,
    w_gate,
    w_up,
    w_down,
):
    place = Place()
    token_rows = tokens.shape[0]
    layer_count, _, experts, _ = w_gate.shape
    expert_count = experts * place.columns
    in_width = query.shape[2] + key.shape[2] + value.shape[2]
    segment, seq_place = positions(lengths[0], token_rows)
    tables = rope_tables(seq_place, HEAD_DIMENSION)
    token_order = jnp.arange(token_rows, dtype=jnp.int32)
    allowed = (segment[:, None] == segment[None, :]) & (
        token_order[:, None] >= token_order[None, :]
    )
    gains = jnp.concatenate([norm_attn, norm_ffn]).T
    packs = []
    for l in range(layer_count):
        pack = [query[l], key[l], value[l], output[l]]
        if l == 0:
            pack.append(jnp.pad(gains, ((0, 0), (0, 128 - gains.shape[1]))))
        packs.append(jnp.concatenate(pack, axis=1))
    full = lax.all_gather(packs[0], AXES, axis=0, tiled=True)
    gains = full[:, in_width + output.shape[2] :].T[: 2 * layer_count].astype(jnp.float32)
    gate_rows = gather_gates(place, routes, gates, expert_count)
    gate_parts = [
        [
            jnp.transpose(piece[:, l], (0, 2, 1)).reshape(-1, experts)
            for piece in gate_rows
        ]
        for l in range(layer_count)
    ]
    expert_weights = gather_experts(place, [w_gate[0], w_up[0], w_down[0]])
    last_grads = None

    residual = tokens.astype(jnp.float32)
    matrices, weights, stored = [], [], []
    for l in range(layer_count):
        matrices.append((full[:, :in_width], full[:, in_width : in_width + output.shape[2]]))
        weights.append(expert_weights)
        layer_input = residual
        middle, attn_stash = attend_forward(layer_input, allowed, tables, gains[l], matrices[l])
        if l + 1 < layer_count:
            held, pack, *shares = lax.optimization_barrier(
                (middle, packs[l + 1], w_gate[l + 1], w_up[l + 1], w_down[l + 1])
            )
            middle = held
            full = lax.all_gather(pack, AXES, axis=0, tiled=True)
            expert_weights = gather_experts(place, shares)
        residual, moe_stash = experts_forward(
            place, middle, gains[layer_count + l], gate_parts[l], weights[l]
        )
        if l + 2 == layer_count or layer_count == 1:
            held, last = lax.optimization_barrier((residual, cotangent))
            residual = held
            last_grads = gather_tokens(place, last)
        stored.append((layer_input, middle, attn_stash, moe_stash))
    result = residual.astype(jnp.bfloat16)

    upstream = cotangent.astype(jnp.float32)
    in_grads, out_grads = [None] * layer_count, [None] * layer_count
    gain_grads = [None] * (2 * layer_count)
    expert_grads = [None] * layer_count
    for l in reversed(range(layer_count)):
        layer_input, middle, attn_stash, moe_stash = stored[l]
        chunks = last_grads
        if l + 1 < layer_count:
            chunks = gather_tokens(place, upstream.astype(jnp.bfloat16))
        upstream, gain_grads[layer_count + l], weight_grads = experts_backward(
            place,
            middle,
            gains[layer_count + l],
            gate_parts[l],
            weights[l],
            moe_stash,
            upstream,
            chunks,
        )
        expert_grads[l] = scatter_experts(place, weight_grads, experts)
        upstream, gain_grads[l], grad_w_in, grad_wo = attend_backward(
            layer_input, allowed, tables, gains[l], matrices[l], attn_stash, upstream
        )
        summed = lax.psum_scatter(
            jnp.concatenate([grad_w_in, grad_wo], axis=1).astype(jnp.bfloat16),
            AXES,
            scatter_dimension=0,
            tiled=True,
        ).astype(jnp.float32)
        in_grads[l], out_grads[l] = summed[:, :in_width], summed[:, in_width:]
    gain_sums = lax.psum_scatter(jnp.stack(gain_grads), AXES, scatter_dimension=1, tiled=True)
    in_grads = jnp.stack(in_grads)
    key_start, value_start = query.shape[2], query.shape[2] + key.shape[2]
    return (
        result,
        upstream,
        gain_sums[:layer_count],
        gain_sums[layer_count:],
        in_grads[:, :, :key_start],
        in_grads[:, :, key_start:value_start],
        in_grads[:, :, value_start:],
        jnp.stack(out_grads),
        jnp.stack([entry[0] for entry in expert_grads]),
        jnp.stack([entry[1] for entry in expert_grads]),
        jnp.stack([entry[2] for entry in expert_grads]),
    )


HEADS_PER_TURN = 6
LANES = 128
EXTRA = 128
HALF = 64
TILE = 256
MIB = 1 << 20


def any_spec():
    return pl.BlockSpec(memory_space=pl.ANY)


def whole_spec():
    return pl.BlockSpec(memory_space=pltpu.VMEM)


def scalar_spec():
    return pl.BlockSpec(memory_space=pltpu.SMEM)


def shape_of(*dims, dtype=jnp.bfloat16):
    return jax.ShapeDtypeStruct(dims, dtype)


class Copies:
    def __init__(self, semaphores, first=0):
        self.semaphores = semaphores
        self.used = first
        self.open = []

    def start(self, source, target):
        copy = pltpu.make_async_copy(source, target, self.semaphores.at[self.used])
        self.used += 1
        copy.start()
        self.open.append(copy)

    def wait(self):
        for copy in self.open:
            copy.wait()
        self.open = []


def shard_row(where, swapped, m, k, rows):
    plane = lax.rem(where[0] - k + 4, 4)
    fsdp = plane * CORES + (where[1] ^ swapped)
    return pl.multiple_of((fsdp * 4 + (where[2] ^ m)) * rows, 16)


def load_matrices(copies, where, pieces, full, rows, cut):
    at = 0
    for swapped in range(CORES):
        for first, count in ((0, 1), (1, 3)):
            for m, low, high in ((0, 0, None), (1, 0, None), (2, 0, None), (3, 0, cut), (3, cut, None)):
                piece = pieces[at]
                at += 1
                high = full.shape[1] if high is None else high
                for n in range(count):
                    row = shard_row(where, swapped, m, first + n, rows)
                    copies.start(
                        piece.at[pl.ds(n * rows, rows), :],
                        full.at[pl.ds(row, rows), pl.ds(low, high - low)],
                    )


MATRIX_PIECES = 20
MATRIX_COPIES = 40


def half_swap(x):
    lane = lax.broadcasted_iota(jnp.int32, x.shape, 1)
    return jnp.where(lane % 64 < 32, pltpu.roll(x, 96, 1), pltpu.roll(x, 32, 1))


def both_sides(pair, side):
    lane = lax.broadcasted_iota(jnp.int32, pair.shape, 1)
    wide = pair.astype(jnp.float32)
    here = jnp.where(lane // 64 == side, wide, 0.0)
    there = pltpu.roll(here, 64, 1)
    here, there = here.astype(jnp.bfloat16), there.astype(jnp.bfloat16)
    return (here, there) if side == 0 else (there, here)


def merge_sides(even, odd, side):
    lane = lax.broadcasted_iota(jnp.int32, even.shape, 1)
    if side == 0:
        return jnp.where(lane < 64, even + pltpu.roll(odd, 64, 1), 0.0)
    return jnp.where(lane < 64, 0.0, odd + pltpu.roll(even, 64, 1))


def contract(a, b, dims):
    return lax.dot_general(a, b, (dims, ((), ())), preferred_element_type=jnp.float32)


PLAIN = ((1,), (0,))
ACROSS = ((1,), (1,))
OUTER = ((0,), (0,))


def read_sum(base, terms):
    if not terms:
        return base[...].astype(jnp.float32)
    halves = []
    for side in range(2):
        rows = pl.ds(side * HALF, HALF)
        total = base[rows, :].astype(jnp.float32)
        for term in terms:
            part = term[side][...] if isinstance(term, tuple) else term[rows, :]
            total = total + part.astype(jnp.float32)
        halves.append(total)
    return jnp.concatenate(halves, axis=0)


def attend_forward_kernel(terms, width, where, base, *refs):
    refs = list(refs)
    extra = [refs.pop(0) for _ in range(terms)]
    cosine, sine, allowed = refs[:3]
    pieces = refs[3 : 3 + MATRIX_PIECES]
    refs = refs[3 + MATRIX_PIECES :]
    h_out, m_out, nf_out, na_out, q_out, k_out, v_out, o_out, lse_out, gain_out = refs[:10]
    full, proj, mixed, semaphores = refs[10:]
    copies = Copies(semaphores)
    load_matrices(copies, where, pieces, full, full.shape[0] // 32, pieces[3].shape[1])
    h = read_sum(base, group_terms(extra))
    h_out[...] = h
    inverse = lax.rsqrt(jnp.mean(h * h, axis=1, keepdims=True) + NORM_EPS)
    model = h.shape[1]
    in_width = width
    key_start = model
    value_start = model + (in_width - model) // 2
    copies.wait()
    gains = full[:, pl.ds(in_width + model, EXTRA)].astype(jnp.float32).T
    gain_out[...] = gains[:8]
    na_out[...] = (h * inverse * gains[0:1]).astype(jnp.bfloat16)
    step = 512

    @pl.loop(0, in_width // step)
    def _(i):
        columns = pl.ds(pl.multiple_of(i * step, step), step)
        proj[:, columns] = contract(na_out[...], full[:, columns], PLAIN)

    cos, sin = cosine[...], sine[...]

    @pl.loop(0, key_start // LANES)
    def _(i):
        columns = pl.ds(pl.multiple_of(i * LANES, LANES), LANES)
        x = proj[:, columns]
        q_out[:, columns] = (x * cos + half_swap(x) * sin).astype(jnp.bfloat16)

    @pl.loop(0, (value_start - key_start) // LANES)
    def _(i):
        start = pl.multiple_of(i * LANES, LANES)
        x = proj[:, pl.ds(key_start + start, LANES)]
        k_out[:, pl.ds(start, LANES)] = (x * cos + half_swap(x) * sin).astype(jnp.bfloat16)

    v_out[...] = proj[:, value_start:in_width].astype(jnp.bfloat16)
    lse_out[...] = jnp.zeros_like(lse_out)
    open_keys = allowed[...] > 0.5
    lane = lax.broadcasted_iota(jnp.int32, open_keys.shape, 1)

    @pl.loop(0, KEY_VALUE_HEADS // 2)
    def _(turn):
        pair = pl.ds(pl.multiple_of(turn * LANES, LANES), LANES)
        keys = [both_sides(k_out[:, pair], side) for side in range(2)]
        values = [both_sides(v_out[:, pair], side) for side in range(2)]
        lse = lse_out[...]
        for group in range(HEADS_PER_TURN // 2):
            columns = pl.ds(
                pl.multiple_of(turn * (HEADS_PER_TURN * 64) + group * LANES, LANES), LANES
            )
            total = jnp.zeros((h.shape[0], LANES), jnp.float32)
            for side in range(2):
                head = group * 2 + side
                scores = contract(q_out[:, columns], keys[head // 3][side], ACROSS)
                scores = jnp.where(open_keys, scores * HEAD_DIMENSION ** (-0.5), MASKED)
                top = jnp.max(scores, axis=1, keepdims=True)
                weights = jnp.exp(scores - top)
                row_total = jnp.sum(weights, axis=1, keepdims=True)
                probs = (weights / row_total).astype(jnp.bfloat16)
                lse = jnp.where(lane == turn * HEADS_PER_TURN + head, top + jnp.log(row_total), lse)
                total = total + contract(probs, values[head // 3][side], PLAIN)
            o_out[:, columns] = total.astype(jnp.bfloat16)
        lse_out[...] = lse

    @pl.loop(0, model // step)
    def _(i):
        columns = pl.ds(pl.multiple_of(i * step, step), step)
        weights = full[:, pl.ds(pl.multiple_of(in_width + i * step, step), step)]
        mixed[:, columns] = contract(o_out[...], weights, PLAIN)

    m = h_out[...] + mixed[...]
    m_out[...] = m
    inverse = lax.rsqrt(jnp.mean(m * m, axis=1, keepdims=True) + NORM_EPS)
    nf_out[...] = (m * inverse * gain_out[1:2]).astype(jnp.bfloat16)


def group_terms(extra):
    if not extra:
        return []
    whole, halves = extra[:4], extra[4:]
    return list(whole) + [(halves[i], halves[i + 1]) for i in range(0, len(halves), 2)]


def attend_forward_fast(where, base, extra, tables, pieces, in_width, after=()):
    rows, model = base.shape
    bf, f32 = jnp.bfloat16, jnp.float32
    key_width = (in_width - model) // 2
    total = in_width + model + EXTRA
    shapes = [
        shape_of(rows, model, dtype=f32),
        shape_of(rows, model, dtype=f32),
        shape_of(rows, model),
        shape_of(rows, model),
        shape_of(rows, model),
        shape_of(rows, key_width),
        shape_of(rows, key_width),
        shape_of(rows, model),
        shape_of(rows, LANES, dtype=f32),
        shape_of(8, model, dtype=f32),
    ]

    def body(*refs):
        used = 2 + len(extra) + 3 + MATRIX_PIECES
        attend_forward_kernel(
            len(extra), in_width, *refs[:used], *refs[used + len(after) :]
        )

    return pl.pallas_call(
        body,
        name="attend_forward",
        out_shape=shapes,
        in_specs=[scalar_spec()]
        + [whole_spec()] * (4 + len(extra))
        + [any_spec()] * (MATRIX_PIECES + len(after)),
        out_specs=[whole_spec()] * len(shapes),
        scratch_shapes=[
            pltpu.VMEM((model, total), bf),
            pltpu.VMEM((rows, in_width), f32),
            pltpu.VMEM((rows, model), f32),
            pltpu.SemaphoreType.DMA((MATRIX_COPIES,)),
        ],
        compiler_params=pltpu.CompilerParams(vmem_limit_bytes=44 * MIB),
        cost_estimate=pl.CostEstimate(
            flops=2 * rows * model * total, bytes_accessed=2 * model * total, transcendentals=0
        ),
    )(where, base, *extra, *tables, *pieces, *after)


def attend_backward_kernel(terms, width, where, base, upstream, *refs):
    refs = list(refs)
    extra = [refs.pop(0) for _ in range(terms)]
    h_in, m_in, na, q, k, v, o, lse_in, gains, cosine, sine, allowed = refs[:12]
    pieces = refs[12 : 12 + MATRIX_PIECES]
    refs = refs[12 + MATRIX_PIECES :]
    gh_out, gh_low, mine, other = refs[:4]
    full, sums, mixed, grad_in, turned, semaphores = refs[4:]
    rows, model = h_in.shape
    in_width = width
    key_start = model
    value_start = model + (in_width - model) // 2
    shard = full.shape[0] // 32
    copies = Copies(semaphores)
    load_matrices(copies, where, pieces, full, shard, pieces[3].shape[1])
    gnf = read_sum(base, group_terms(extra))
    m = m_in[...]
    inverse = lax.rsqrt(jnp.mean(m * m, axis=1, keepdims=True) + NORM_EPS)
    gain_ffn = jnp.sum(gnf * m * inverse, axis=0, keepdims=True)
    scaled = gnf * gains[1:2]
    inner = jnp.mean(scaled * m, axis=1, keepdims=True)
    gm = upstream[...].astype(jnp.float32)
    gm = gm + inverse * scaled - m * (inverse * inverse * inverse) * inner
    gh_out[...] = gm
    gh_low[...] = gm.astype(jnp.bfloat16)
    copies.wait()
    step = 512

    @pl.loop(0, model // step)
    def _(i):
        row = pl.ds(pl.multiple_of(i * step, step), step)
        mixed[:, row] = contract(gh_low[...], full[row, in_width : in_width + model], ACROSS).astype(
            jnp.bfloat16
        )

    open_keys = allowed[...] > 0.5
    lane = lax.broadcasted_iota(jnp.int32, open_keys.shape, 1)
    cos, sin = cosine[...], sine[...]
    scale = HEAD_DIMENSION ** (-0.5)

    @pl.loop(0, KEY_VALUE_HEADS // 2)
    def _(turn):
        start = pl.multiple_of(turn * LANES, LANES)
        pair = pl.ds(start, LANES)
        keys = [both_sides(k[:, pair], side) for side in range(2)]
        values = [both_sides(v[:, pair], side) for side in range(2)]
        zero = jnp.zeros((rows, LANES), jnp.float32)
        grad_k = [[zero, zero], [zero, zero]]
        grad_v = [[zero, zero], [zero, zero]]
        lse = lse_in[...]
        for group in range(HEADS_PER_TURN // 2):
            columns = pl.ds(
                pl.multiple_of(turn * (HEADS_PER_TURN * 64) + group * LANES, LANES), LANES
            )
            grad_q = zero
            for side in range(2):
                head = group * 2 + side
                kv = head // 3
                top = jnp.sum(
                    jnp.where(lane == turn * HEADS_PER_TURN + head, lse, 0.0), axis=1, keepdims=True
                )
                scores = contract(q[:, columns], keys[kv][side], ACROSS) * scale
                probs = jnp.exp(jnp.where(open_keys, scores, MASKED) - top)
                go = mixed[:, columns]
                grad_v[kv][side] = grad_v[kv][side] + contract(
                    probs.astype(jnp.bfloat16), go, OUTER
                )
                grad_p = contract(go, values[kv][side], ACROSS)
                grad_s = probs * (grad_p - jnp.sum(probs * grad_p, axis=1, keepdims=True))
                grad_s = grad_s.astype(jnp.bfloat16)
                grad_q = grad_q + contract(grad_s, keys[kv][side], PLAIN)
                grad_k[kv][side] = grad_k[kv][side] + contract(grad_s, q[:, columns], OUTER)
            grad_q = grad_q * scale
            grad_in[:, columns] = (grad_q * cos - half_swap(grad_q) * sin).astype(jnp.bfloat16)
        key_grad = merge_sides(*grad_k[0], 0) + merge_sides(*grad_k[1], 1)
        key_grad = key_grad * scale
        key_grad = key_grad * cos - half_swap(key_grad) * sin
        value_grad = merge_sides(*grad_v[0], 0) + merge_sides(*grad_v[1], 1)
        grad_in[:, pl.ds(key_start + start, LANES)] = key_grad.astype(jnp.bfloat16)
        grad_in[:, pl.ds(value_start + start, LANES)] = value_grad.astype(jnp.bfloat16)

    turned[...] = jnp.zeros_like(turned)

    @pl.loop(0, in_width // step)
    def _(i):
        columns = pl.ds(pl.multiple_of(i * step, step), step)
        turned[...] += contract(grad_in[:, columns], full[:, columns], ACROSS)

    grad_na = turned[...]
    h = h_in[...]
    inverse = lax.rsqrt(jnp.mean(h * h, axis=1, keepdims=True) + NORM_EPS)
    gain_attn = jnp.sum(grad_na * h * inverse, axis=0, keepdims=True)
    scaled = grad_na * gains[0:1]
    inner = jnp.mean(scaled * h, axis=1, keepdims=True)
    band = 384

    @pl.loop(0, model // band)
    def _(i):
        start = pl.multiple_of(i * band, band)
        row = pl.ds(start, band)
        sums[row, in_width : in_width + model] = contract(o[:, row], gh_low[...], OUTER).astype(
            jnp.bfloat16
        )
        sums[row, :in_width] = contract(na[:, row], grad_in[...], OUTER).astype(jnp.bfloat16)

    both = jnp.concatenate([gain_attn, gain_ffn, jnp.zeros((EXTRA - 2, model), jnp.float32)], axis=0)
    sums[:, pl.ds(in_width + model, EXTRA)] = both.T.astype(jnp.bfloat16)
    for m_index in range(4):
        for n in range(4):
            for swapped, target in ((1, other), (0, mine)):
                row = shard_row(where, swapped, m_index, n, shard)
                copies.start(
                    sums.at[pl.ds(row, shard), :],
                    target.at[pl.ds((m_index * 4 + n) * shard, shard), :],
                )
    gh = gh_out[...] + inverse * scaled - h * (inverse * inverse * inverse) * inner
    gh_out[...] = gh
    gh_low[...] = gh.astype(jnp.bfloat16)
    copies.wait()


def attend_backward_fast(where, base, upstream, extra, stash, tables, pieces, in_width, after=()):
    rows, model = upstream.shape
    bf, f32 = jnp.bfloat16, jnp.float32
    total = in_width + model + EXTRA
    shapes = [
        shape_of(rows, model, dtype=f32),
        shape_of(rows, model),
        shape_of(model // 2, total),
        shape_of(model // 2, total),
    ]

    def body(*refs):
        used = 3 + len(extra) + 12 + MATRIX_PIECES
        attend_backward_kernel(len(extra), in_width, *refs[:used], *refs[used + len(after) :])

    return pl.pallas_call(
        body,
        name="attend_backward",
        out_shape=shapes,
        in_specs=[scalar_spec()]
        + [whole_spec()] * (2 + len(extra) + 12)
        + [any_spec()] * (MATRIX_PIECES + len(after)),
        out_specs=[whole_spec()] * 2 + [any_spec()] * 2,
        scratch_shapes=[
            pltpu.VMEM((model, total), bf),
            pltpu.VMEM((model, total), bf),
            pltpu.VMEM((rows, model), bf),
            pltpu.VMEM((rows, in_width), bf),
            pltpu.VMEM((rows, model), f32),
            pltpu.SemaphoreType.DMA((MATRIX_COPIES + 32,)),
        ],
        compiler_params=pltpu.CompilerParams(vmem_limit_bytes=56 * MIB),
        cost_estimate=pl.CostEstimate(
            flops=4 * rows * model * total, bytes_accessed=4 * model * total, transcendentals=0
        ),
    )(where, base, upstream, *extra, *stash, *tables, *pieces, *after)


def load_experts(copies, where, pieces, targets):
    at = 0
    for swapped in range(CORES):
        for k in range(4):
            piece = pieces[at]
            at += 1
            _, experts, rows, share = piece.shape
            fsdp = lax.rem(where[0] - k + 4, 4) * CORES + (where[1] ^ swapped)
            row = pl.ds(pl.multiple_of(fsdp * rows, 16), rows)
            for i, target in enumerate(targets):
                for e in range(experts):
                    copies.start(piece.at[i, e], target.at[row, pl.ds(e * share, share)])


def widen_tile(columns, share, width):
    lane = lax.broadcasted_iota(jnp.int32, (columns.shape[0], width), 1)
    wide = jnp.broadcast_to(columns[:, 0:1], lane.shape)
    for e in range(1, width // share):
        wide = jnp.where(lane >= e * share, columns[:, e : e + 1], wide)
    return wide


def start_rows(copies, pieces, rows_ref):
    at = 0
    for piece in pieces:
        rows = piece.shape[0]
        copies.start(piece, rows_ref.at[pl.ds(at, rows), :])
        at += rows


def part_rows(n):
    return [n] + [n // 2] * 6


def experts_forward_kernel(where, gates, *refs):
    pieces, weights = refs[:5], refs[5:13]
    parts, x_out, g_out, u_out = refs[13:20], *refs[20:23]
    x, y, g, u, w_gate, w_up, w_down, semaphores = refs[23:]
    copies = Copies(semaphores)
    start_rows(copies, pieces, x)
    load_experts(copies, where, weights, (w_gate, w_up, w_down))
    share = weights[0].shape[3]
    width = w_gate.shape[1]
    copies.wait()
    copies.start(x, x_out)

    @pl.loop(0, x.shape[0] // TILE)
    def _(i):
        row = pl.ds(pl.multiple_of(i * TILE, TILE), TILE)
        gate_pre = contract(x[row, :], w_gate[...], PLAIN)
        up_pre = contract(x[row, :], w_up[...], PLAIN)
        g[row, :] = gate_pre
        u[row, :] = up_pre
        wide = widen_tile(gates[row, :], share, width)
        weighed = (gate_pre * jax.nn.sigmoid(gate_pre) * up_pre * wide).astype(jnp.bfloat16)
        y[row, :] = contract(weighed, w_down[...], ACROSS).astype(jnp.bfloat16)

    copies.start(g, g_out)
    copies.start(u, u_out)
    at = 0
    for part in parts:
        copies.start(y.at[pl.ds(at, part.shape[0]), :], part)
        at += part.shape[0]
    copies.wait()


def experts_forward_fast(where, gates, pieces, weights, after=()):
    n, model = pieces[0].shape
    _, experts, _, share = weights[0].shape
    rows, width = 4 * n, experts * share
    bf, f32 = jnp.bfloat16, jnp.float32
    shapes = [shape_of(r, model) for r in part_rows(n)]
    shapes += [shape_of(rows, model)] + [shape_of(rows, width, dtype=f32)] * 2

    def body(*refs):
        experts_forward_kernel(*refs[:15], *refs[15 + len(after) :])

    return pl.pallas_call(
        body,
        name="experts_forward",
        out_shape=shapes,
        in_specs=[scalar_spec(), whole_spec()] + [any_spec()] * (13 + len(after)),
        out_specs=[any_spec()] * len(shapes),
        scratch_shapes=[
            pltpu.VMEM((rows, model), bf),
            pltpu.VMEM((rows, model), bf),
            pltpu.VMEM((rows, width), f32),
            pltpu.VMEM((rows, width), f32),
        ]
        + [pltpu.VMEM((model, width), bf)] * 3
        + [pltpu.SemaphoreType.DMA((5 + 24 * experts + 10,))],
        compiler_params=pltpu.CompilerParams(vmem_limit_bytes=48 * MIB),
        cost_estimate=pl.CostEstimate(
            flops=6 * rows * model * width, bytes_accessed=8 * rows * model, transcendentals=0
        ),
    )(where, gates, *pieces, *weights, *after)


def experts_backward_kernel(where, gates, *refs):
    pieces, g_in, u_in, weights = refs[:5], refs[5], refs[6], refs[7:15]
    parts, r_out, gg_out, gu_out, p_out = refs[15:22], *refs[22:26]
    x, y, g, u, gg, gu, p, w_gate, w_up, w_down, semaphores = refs[26:]
    copies = Copies(semaphores)
    start_rows(copies, pieces, x)
    load_experts(copies, where, weights, (w_gate, w_up, w_down))
    copies.start(g_in, g)
    copies.start(u_in, u)
    share = weights[0].shape[3]
    width = w_gate.shape[1]
    copies.wait()
    copies.start(x, r_out)

    @pl.loop(0, x.shape[0] // TILE)
    def _(i):
        row = pl.ds(pl.multiple_of(i * TILE, TILE), TILE)
        wide = widen_tile(gates[row, :], share, width)
        hidden_grad = contract(x[row, :], w_down[...], PLAIN) * wide
        gate_pre, up_pre = g[row, :], u[row, :]
        sig = jax.nn.sigmoid(gate_pre)
        active = gate_pre * sig
        p[row, :] = (active * up_pre * wide).astype(jnp.bfloat16)
        gate_grad = hidden_grad * up_pre * sig * (1.0 + gate_pre * (1.0 - sig))
        gg[row, :] = gate_grad.astype(jnp.bfloat16)
        gu[row, :] = (hidden_grad * active).astype(jnp.bfloat16)
        back = contract(gg[row, :], w_gate[...], ACROSS)
        back = back + contract(gu[row, :], w_up[...], ACROSS)
        y[row, :] = back.astype(jnp.bfloat16)

    at = 0
    for part in parts:
        copies.start(y.at[pl.ds(at, part.shape[0]), :], part)
        at += part.shape[0]
    copies.start(gg, gg_out)
    copies.start(gu, gu_out)
    copies.start(p, p_out)
    copies.wait()


def experts_backward_fast(where, gates, pieces, stash, weights, after=()):
    n, model = pieces[0].shape
    _, experts, _, share = weights[0].shape
    rows, width = 4 * n, experts * share
    bf, f32 = jnp.bfloat16, jnp.float32
    shapes = [shape_of(r, model) for r in part_rows(n)]
    shapes += [shape_of(rows, model)] + [shape_of(rows, width)] * 3

    def body(*refs):
        experts_backward_kernel(*refs[:17], *refs[17 + len(after) :])

    return pl.pallas_call(
        body,
        name="experts_backward",
        out_shape=shapes,
        in_specs=[scalar_spec(), whole_spec()] + [any_spec()] * (15 + len(after)),
        out_specs=[any_spec()] * len(shapes),
        scratch_shapes=[
            pltpu.VMEM((rows, model), bf),
            pltpu.VMEM((rows, model), bf),
            pltpu.VMEM((rows, width), f32),
            pltpu.VMEM((rows, width), f32),
            pltpu.VMEM((rows, width), bf),
            pltpu.VMEM((rows, width), bf),
            pltpu.VMEM((rows, width), bf),
        ]
        + [pltpu.VMEM((model, width), bf)] * 3
        + [pltpu.SemaphoreType.DMA((5 + 24 * experts + 13,))],
        compiler_params=pltpu.CompilerParams(vmem_limit_bytes=52 * MIB),
        cost_estimate=pl.CostEstimate(
            flops=6 * rows * model * width, bytes_accessed=12 * rows * model, transcendentals=0
        ),
    )(where, gates, *pieces, *stash, *weights, *after)


def weight_grads_kernel(experts, where, *refs):
    sources, mine, other = refs[:10], refs[10], refs[11]
    x, r, gg, gu, p, out, semaphores = refs[12:]
    copies = Copies(semaphores)
    for target, near, far in zip((x, r, gg, gu, p), sources[:5], sources[5:]):
        start_rows(copies, (near, far), target)
    copies.wait()
    band = x.shape[1] // 4
    rows = band // CORES
    share = gg.shape[1] // experts

    @pl.loop(0, 4)
    def _(z):
        columns = pl.ds(pl.multiple_of(z * band, band), band)
        k = lax.rem(z - where[0] + 4, 4)
        for i, (a, b) in enumerate(((x, gg), (x, gu), (r, p))):
            grads = contract(a[:, columns], b[...], OUTER).astype(jnp.bfloat16)
            for core in range(CORES):
                for e in range(experts):
                    out[core, k, i, e] = grads[
                        core * rows : (core + 1) * rows, e * share : (e + 1) * share
                    ]

    copies.start(out.at[1 - where[1]], other)
    copies.start(out.at[where[1]], mine)
    copies.wait()


def weight_grads_fast(where, near, far, experts, after=()):
    model, width = near[0].shape[1], near[2].shape[1]
    count = near[0].shape[0] + far[0].shape[0]
    rows, share = model // 8, width // experts
    bf = jnp.bfloat16

    def body(*refs):
        weight_grads_kernel(experts, *refs[:11], *refs[11 + len(after) :])

    return pl.pallas_call(
        body,
        name="weight_grads",
        out_shape=[shape_of(4, 3, experts, rows, share)] * 2,
        in_specs=[scalar_spec()] + [any_spec()] * (10 + len(after)),
        out_specs=[any_spec()] * 2,
        scratch_shapes=[
            pltpu.VMEM((count, model), bf),
            pltpu.VMEM((count, model), bf),
            pltpu.VMEM((count, width), bf),
            pltpu.VMEM((count, width), bf),
            pltpu.VMEM((count, width), bf),
            pltpu.VMEM((CORES, 4, 3, experts, rows, share), bf),
            pltpu.SemaphoreType.DMA((12,)),
        ],
        compiler_params=pltpu.CompilerParams(vmem_limit_bytes=56 * MIB),
        cost_estimate=pl.CostEstimate(
            flops=6 * count * model * width, bytes_accessed=8 * count * model, transcendentals=0
        ),
    )(where, *near, *far, *after)


def cut_kernel(layer, where, w_gate, w_up, w_down, *refs):
    outs, semaphores = refs[:4], refs[4]
    copies = Copies(semaphores)
    share = outs[0].shape[3]
    for k, out in enumerate(outs):
        columns = pl.ds(pl.multiple_of(lax.rem(where[0] + k, 4) * share, share), share)
        for i, w in enumerate((w_gate, w_up, w_down)):
            copies.start(w.at[layer, :, :, columns], out.at[i])
    copies.wait()


def cut_experts(where, weights, layer, after=()):
    _, experts, rows, hidden = weights[0].shape

    def body(*refs):
        cut_kernel(layer, *refs[:4], *refs[4 + len(after) :])

    return pl.pallas_call(
        body,
        name="cut_experts",
        out_shape=[shape_of(3, experts, rows, hidden // 4)] * 4,
        in_specs=[scalar_spec()] + [any_spec()] * (3 + len(after)),
        out_specs=[any_spec()] * 4,
        scratch_shapes=[pltpu.SemaphoreType.DMA((12,))],
    )(where, *weights, *after)


def join_kernel(layer, where, *refs):
    pieces, outs = refs[:4], refs[-3:]
    i = pl.program_id(0)
    share = pieces[0].shape[3]
    for index, out in enumerate(outs):

        @pl.when(i == index)
        def _():
            for k, piece in enumerate(pieces):
                columns = pl.ds(pl.multiple_of(lax.rem(where[0] - k + 4, 4) * share, share), share)
                out[0, :, :, columns] = piece[0].astype(jnp.float32)


def join_experts(where, pieces, layer, layers, earlier=None):
    mats, experts, rows, share = pieces[0].shape
    shape = shape_of(layers, experts, rows, 4 * share, dtype=jnp.float32)
    given = [] if earlier is None else list(earlier)

    return pl.pallas_call(
        functools.partial(join_kernel, layer),
        name="join_experts",
        grid=(mats,),
        out_shape=[shape] * mats,
        in_specs=[scalar_spec()]
        + [pl.BlockSpec((1, experts, rows, share), lambda i: (i, 0, 0, 0))] * 4
        + [any_spec()] * len(given),
        out_specs=[pl.BlockSpec((1, experts, rows, 4 * share), lambda i: (layer, 0, 0, 0))] * mats,
        input_output_aliases={5 + j: j for j in range(len(given))},
        compiler_params=pltpu.CompilerParams(vmem_limit_bytes=40 * MIB),
    )(where, *pieces, *given)


def spread_pieces(place, block, axis=0):
    half = block.shape[axis] // 2 // 128 * 128 if axis else block.shape[axis] // 2
    one = place.hop(block, flip=1)
    two = place.hop(block, flip=2)
    head = place.hop(lax.slice_in_dim(one, 0, half, axis=axis), flip=2)
    tail = place.hop(lax.slice_in_dim(two, half, None, axis=axis), flip=1)
    return [block, one, two, head, tail]


def up_hops(place, block):
    return jnp.concatenate([place.hop(block, up=k) for k in range(1, 4)])


def gather_pieces(place, block, axis=0):
    far = up_hops(place, block)
    return spread_pieces(place, block, axis), spread_pieces(place, far, axis)


def add_low(a, b):
    return (a.astype(jnp.float32) + b.astype(jnp.float32)).astype(a.dtype)


def fold_pieces(place, parts):
    own, one_head, one_tail, two_head, two_tail, last_head, last_tail = parts
    head = place.hop(last_head, flip=2)
    tail = place.hop(last_tail, flip=1)
    one_tail = place.hop(one_tail, flip=1)
    two_head = place.hop(two_head, flip=2)
    one_head = place.hop(add_low(one_head, head), flip=1)
    two_tail = place.hop(add_low(two_tail, tail), flip=2)
    return own, one_head, one_tail, two_head, two_tail


def add_pieces(own, one_head, one_tail, two_head, two_tail, axis=0):
    wide = lambda value: value.astype(jnp.float32)
    one = jnp.concatenate([one_head, one_tail], axis=axis)
    two = jnp.concatenate([two_head, two_tail], axis=axis)
    return wide(own) + wide(one) + wide(two)


def blocks_kernel(own, one_head, one_tail, two_head, two_tail, *outs):
    half = one_head.shape[0]
    rows = outs[0].shape[0]
    step = HALF
    for start in range(0, own.shape[0], step):
        first, second = (one_head, two_head) if start < half else (one_tail, two_tail)
        at = pl.ds(start % half, step)
        total = own[pl.ds(start, step), :].astype(jnp.float32)
        total = total + first[at, :].astype(jnp.float32) + second[at, :].astype(jnp.float32)
        outs[start // rows][pl.ds(start % rows, step), :] = total.astype(jnp.bfloat16)


def sum_blocks(own, *halves):
    rows, model = own.shape
    return pl.pallas_call(
        blocks_kernel,
        name="sum_blocks",
        out_shape=[shape_of(rows // 3, model)] * 3,
        in_specs=[whole_spec()] * 5,
        out_specs=[whole_spec()] * 3,
    )(own, *halves)


def scatter_pieces(place, near, far):
    blocks = sum_blocks(*fold_pieces(place, far))
    arrived = [place.hop(blocks[k - 1], up=-k) for k in range(1, 4)]
    own, one_head, one_tail, two_head, two_tail = fold_pieces(place, near)
    return [own, *arrived, one_head, one_tail, two_head, two_tail]


def total_of(base, extra):
    total = base.astype(jnp.float32)
    for block in extra[:4]:
        total = total + block.astype(jnp.float32)
    for head, tail in (extra[4:6], extra[6:8]):
        total = total + jnp.concatenate([head, tail]).astype(jnp.float32)
    return total


def gather_matrices(place, pack):
    near, far = gather_pieces(place, pack, axis=1)
    own = near + far
    return own + [place.hop(piece, swap=1) for piece in own]


def scatter_matrices(place, mine, other, cut):
    arrived = place.hop(other, swap=1)
    total = add_low(mine, arrived)
    rows = mine.shape[0] // 16
    chunks = [total[m * 4 * rows : (m + 1) * 4 * rows] for m in range(4)]

    def parts(first, last):
        piece = [chunk[first * rows : last * rows] for chunk in chunks]
        found = [piece[0]]
        for m in range(1, 4):
            found += [piece[m][:, :cut], piece[m][:, cut:]]
        return found

    far = add_pieces(*fold_pieces(place, parts(1, 4)), axis=1).astype(jnp.bfloat16)
    arrived = [
        place.hop(far[(k - 1) * rows : k * rows], up=-k) for k in range(1, 4)
    ]
    final = add_pieces(*fold_pieces(place, parts(0, 1)), axis=1)
    for block in arrived:
        final = final + block.astype(jnp.float32)
    return final


def tables_of(length_row, rows):
    order = jnp.arange(rows, dtype=jnp.int32)
    index = jnp.arange(length_row.shape[0], dtype=jnp.int32)
    ends = jnp.sum(jnp.where(index[:, None] <= index[None, :], length_row[:, None], 0), axis=0)
    passed = order[:, None] >= ends[None, :]
    segment = jnp.sum(passed.astype(jnp.int32), axis=1)
    begin = jnp.sum(jnp.where(passed, length_row[None, :], 0), axis=1)
    cosine, sine = rope_tables(order - begin, HEAD_DIMENSION)
    allowed = (segment[:, None] == segment[None, :]) & (order[:, None] >= order[None, :])
    return (
        jnp.concatenate([cosine] * 4, axis=1),
        jnp.concatenate([-sine, sine] * 2, axis=1),
        allowed.astype(jnp.float32),
    )


def tie(value, *events):
    flat, tree = jax.tree.flatten(value)
    held = lax.optimization_barrier((*flat, *events))
    return jax.tree.unflatten(tree, held[: len(flat)])


def gate_rows_of(place, routes, gates, expert_count):
    found = gather_gates(place, routes, gates, expert_count)
    owned = expert_count // place.columns
    order = jnp.stack(found)
    order = jnp.transpose(order, (2, 0, 1, 4, 3))
    order = jnp.pad(order, ((0, 0),) * 4 + ((0, 8 - owned),))
    return [
        (layer[:, :1].reshape(-1, 8), layer[:, 1:].reshape(-1, 8)) for layer in order
    ]


def shards_fast(
    tokens,
    lengths,
    routes,
    gates,
    cotangent,
    norm_attn,
    norm_ffn,
    query,
    key,
    value,
    output,
    w_gate,
    w_up,
    w_down,
):
    place = Place()
    where = jnp.stack([place.plane, place.core, place.column]).astype(jnp.int32)
    rows, model = tokens.shape
    layer_count, _, experts, _ = w_gate.shape
    expert_count = experts * place.columns
    in_width = query.shape[2] + key.shape[2] + value.shape[2]
    packs = []
    for l in range(layer_count):
        gains = jnp.stack([norm_attn[l], norm_ffn[l]], axis=1)
        gains = jnp.pad(gains, ((0, 0), (0, EXTRA - 2)))
        packs.append(jnp.concatenate([query[l], key[l], value[l], output[l], gains], axis=1))
    cut = packs[0].shape[1] // 2 // 128 * 128
    weights = [jnp.transpose(w, (0, 2, 1, 3)) for w in (w_gate, w_up, w_down)]
    tables = tables_of(lengths[0], rows)

    def bring_experts(layer, after):
        cuts = cut_experts(where, weights, layer, after=after)
        own = [cuts[0]] + [place.hop(cuts[k], up=k) for k in range(1, 4)]
        return own + [place.hop(piece, swap=1) for piece in own]

    matrices = [gather_matrices(place, packs[0])]
    bank = [bring_experts(0, (matrices[0][5],))]
    gate_rows = gate_rows_of(place, routes, gates, expert_count)

    base, extra = tokens.astype(jnp.float32), []
    stored = []
    last = None
    for l in range(layer_count):
        outs = attend_forward_fast(where, base, extra, tables, matrices[l], in_width)
        h, m, nf = outs[:3]
        near, far = gather_pieces(place, nf)
        if l + 1 < layer_count:
            matrices.append(gather_matrices(place, tie(packs[l + 1], nf)))
        y_near = experts_forward_fast(where, gate_rows[l][0], near, bank[l])
        y_far = experts_forward_fast(where, gate_rows[l][1], far, bank[l])
        if l + 1 < layer_count:
            bank.append(bring_experts(l + 1, (y_far[0],)))
        else:
            last = gather_pieces(place, tie(cotangent, y_far[0]))
        base, extra = m, scatter_pieces(place, y_near[:7], y_far[:7])
        stored.append((h, outs, y_near[7:], y_far[7:]))
    result = total_of(base, extra).astype(jnp.bfloat16)

    upstream = cotangent.astype(jnp.float32)
    zero = jnp.zeros((rows, model), jnp.bfloat16)
    sums = [None] * layer_count
    joined = None
    for l in reversed(range(layer_count)):
        h, outs, kept_near, kept_far = stored[l]
        near, far = last
        b_near = experts_backward_fast(where, gate_rows[l][0], near, kept_near[1:], bank[l])
        b_far = experts_backward_fast(where, gate_rows[l][1], far, kept_far[1:], bank[l])
        extra = scatter_pieces(place, b_near[:7], b_far[:7])
        mine, other = weight_grads_fast(
            where, (kept_near[0], *b_near[7:]), (kept_far[0], *b_far[7:]), experts
        )
        arrived = place.hop(other, swap=1)
        total = [add_low(mine[k], arrived[k]) for k in range(4)]
        pieces = [total[0]] + [place.hop(total[k], up=k) for k in range(1, 4)]
        m, na, q, k, v, o, lse, gains = outs[1], *outs[3:]
        upstream, low, mine, other = attend_backward_fast(
            where,
            zero,
            upstream,
            extra,
            (h, m, na, q, k, v, o, lse, gains),
            tables,
            matrices[l],
            in_width,
        )
        if l:
            last = gather_pieces(place, low)
        sums[l] = scatter_matrices(place, mine, other, cut)
        joined = join_experts(where, pieces, l, layer_count, joined)
    sums = jnp.stack(sums)
    gain_sums = sums[:, :, in_width + model :]
    starts = (0, query.shape[2], query.shape[2] + key.shape[2], in_width, in_width + model)
    return (
        result,
        upstream,
        gain_sums[:, :, 0],
        gain_sums[:, :, 1],
        *[sums[:, :, a:b] for a, b in zip(starts, starts[1:])],
        *[jnp.transpose(grads, (0, 2, 1, 3)) for grads in joined],
    )


def solution(mesh):
    rows = P(AXES, None)
    layered = P(None, AXES, None)
    expert = P(None, "fsdp", "expert", None)
    gain = P(None, AXES)
    regular = mesh.shape["fsdp"] == 8 and mesh.shape["expert"] == 4
    return jax.shard_map(
        shards_fast if regular else shards,
        mesh=mesh,
        in_specs=(rows, rows, layered, layered, rows, gain, gain)
        + (layered,) * 4
        + (expert,) * 3,
        out_specs=(rows, rows, gain, gain) + (layered,) * 4 + (expert,) * 3,
        check_vma=False,
    )
```

```python
import functools
import math

import jax
import jax.numpy as jnp
from jax import lax
from jax.experimental import pallas as pl
from jax.experimental.pallas import tpu as pltpu
from jax.sharding import PartitionSpec as P

QUERY_HEADS = 24
KEY_VALUE_HEADS = 8
HEAD_DIMENSION = 64
CORES = 2

NORM_EPS = 1e-06
MASKED = -1000000000.0
AXES = ("fsdp", "expert")


class Place:
    def __init__(self):
        self.planes = lax.axis_size("fsdp") // CORES
        self.columns = lax.axis_size("expert")
        fsdp = lax.axis_index("fsdp")
        self.plane = fsdp // CORES
        self.core = fsdp % CORES
        self.column = lax.axis_index("expert")

    def hop(self, value, up=0, flip=0, swap=0):
        pairs = []
        for plane in range(self.planes):
            for core in range(CORES):
                for column in range(self.columns):
                    source = (plane * CORES + core) * self.columns + column
                    target = ((plane + up) % self.planes * CORES + (core ^ swap)) * self.columns
                    pairs.append((source, target + (column ^ flip)))
        return lax.ppermute(value, AXES, pairs)


def spread(place, block):
    if place.columns != 4:
        return [block] + [place.hop(block, flip=m) for m in range(1, place.columns)]
    half = block.shape[1] // 2
    one = place.hop(block, flip=1)
    two = place.hop(block, flip=2)
    head = place.hop(one[:, :half], flip=2)
    tail = place.hop(two[:, half:], flip=1)
    return [block, one, two, jnp.concatenate([head, tail], axis=1)]


def gather_tokens(place, block):
    own = block[None]
    others = jnp.stack([place.hop(block, up=k) for k in range(1, place.planes)])
    near = spread(place, own)
    far = spread(place, others)
    return [jnp.concatenate([a, b], axis=0) for a, b in zip(near, far)]


def fold(place, parts):
    wide = lambda value: value.astype(jnp.float32)
    if place.columns != 4:
        total = wide(parts[0])
        for m in range(1, place.columns):
            total = total + wide(place.hop(parts[m], flip=m))
        return total
    half = parts[0].shape[1] // 2
    head = place.hop(parts[3][:, :half], flip=2)
    tail = place.hop(parts[3][:, half:], flip=1)
    one_tail = place.hop(parts[1][:, half:], flip=1)
    two_head = place.hop(parts[2][:, :half], flip=2)
    one_head = place.hop((wide(parts[1][:, :half]) + wide(head)).astype(parts[1].dtype), flip=1)
    two_tail = place.hop((wide(parts[2][:, half:]) + wide(tail)).astype(parts[2].dtype), flip=2)
    upper = wide(parts[0][:, :half]) + wide(one_head) + wide(two_head)
    lower = wide(parts[0][:, half:]) + wide(one_tail) + wide(two_tail)
    return jnp.concatenate([upper, lower], axis=1)


def scatter_sums(place, parts):
    far = fold(place, [part[1:] for part in parts]).astype(parts[0].dtype)
    arrived = [place.hop(far[k - 1], up=-k) for k in range(1, place.planes)]
    total = fold(place, [part[:1] for part in parts])[0]
    for piece in arrived:
        total = total + piece.astype(jnp.float32)
    return total


def gates_line(place, routes, gates, expert_count):
    names = jnp.arange(expert_count, dtype=jnp.int32)
    chosen = routes[:, None, :, :] == names[None, :, None, None]
    table = jnp.sum(jnp.where(chosen, gates[:, None, :, :], 0.0), axis=3)
    return jnp.stack([table] + [place.hop(table, up=k) for k in range(1, place.planes)])


def spread_gates(place, line):
    owned = line.shape[2] // place.columns
    found = []
    for m in range(place.columns):
        start = (place.column ^ m) * owned
        piece = lax.dynamic_slice_in_dim(line, start, owned, axis=2)
        found.append(place.hop(piece, flip=m) if m else piece)
    return found


def gather_gates(place, routes, gates, expert_count):
    return spread_gates(place, gates_line(place, routes, gates, expert_count))


def gather_experts(place, weights):
    rows, experts, hidden = weights[0].shape
    share = hidden // place.planes

    def cut(plane):
        pieces = [lax.dynamic_slice_in_dim(w, plane * share, share, axis=2) for w in weights]
        return jnp.stack([p.reshape(rows, experts * share) for p in pieces])

    own = [cut(place.plane)]
    for k in range(1, place.planes):
        own.append(place.hop(cut((place.plane + k) % place.planes), up=k))
    own = jnp.stack(own)
    sibling = place.hop(own, swap=1)
    both = jnp.concatenate([own, sibling])
    shard = jnp.arange(place.planes * CORES)
    index = ((shard % CORES) ^ place.core) * place.planes
    index = index + (place.plane - shard // CORES) % place.planes
    return [
        jnp.take(both[:, i], index, axis=0).reshape(-1, experts * share)
        for i in range(len(weights))
    ]


def scatter_experts(place, grads, experts):
    features, width = grads[0].shape
    rows = features // (place.planes * CORES)
    share = width // experts
    shape = (place.planes, CORES, rows, width)
    stacked = jnp.stack([g.reshape(shape) for g in grads], axis=1)
    mine = lax.dynamic_index_in_dim(stacked, place.core, axis=2, keepdims=False)
    others = lax.dynamic_index_in_dim(stacked, 1 - place.core, axis=2, keepdims=False)
    arrived = place.hop(others.astype(jnp.bfloat16), swap=1)
    total = (mine + arrived.astype(jnp.float32)).astype(jnp.bfloat16)
    pieces = [lax.dynamic_index_in_dim(total, place.plane, axis=0, keepdims=False)]
    for k in range(1, place.planes):
        target = (place.plane + k) % place.planes
        piece = lax.dynamic_index_in_dim(total, target, axis=0, keepdims=False)
        pieces.append(place.hop(piece, up=k))
    index = (place.plane - jnp.arange(place.planes)) % place.planes
    ordered = jnp.take(jnp.stack(pieces), index, axis=0)
    ordered = ordered.reshape(place.planes, len(grads), rows, experts, share)
    ordered = jnp.transpose(ordered, (1, 2, 3, 0, 4)).reshape(len(grads), rows, experts, -1)
    return [ordered[i].astype(jnp.float32) for i in range(len(grads))]


def positions(length_row, count_of_rows):
    ends = jnp.cumsum(length_row)
    token_order = jnp.arange(count_of_rows, dtype=jnp.int32)
    passed = token_order[:, None] >= ends[None, :]
    segment = jnp.sum(passed.astype(jnp.int32), axis=1)
    before = jnp.sum(jnp.where(passed, length_row[None, :], 0), axis=1)
    return (segment, token_order - before)


def rope_tables(seq_place, head_width):
    half_width = head_width // 2
    freq_table = jnp.exp(
        jnp.arange(half_width, dtype=jnp.float32) * (-2.0 * math.log(10000.0) / head_width)
    )
    angles = seq_place.astype(jnp.float32)[:, None] * freq_table[None, :]
    return (jnp.cos(angles), jnp.sin(angles))


def apply_rotation(vector, cosine_table, sine_table):
    half_width = vector.shape[-1] // 2
    former = vector[..., :half_width]
    latter = vector[..., half_width:]
    cos_wide = cosine_table[:, None, :]
    sin_wide = sine_table[:, None, :]
    return jnp.concatenate(
        [former * cos_wide - latter * sin_wide, latter * cos_wide + former * sin_wide], axis=-1
    )


def reverse_rotation(vector, cosine_table, sine_table):
    return apply_rotation(vector, cosine_table, -sine_table)


def rms_forward(residual, norm_gain):
    inverse = lax.rsqrt(jnp.mean(residual * residual, axis=-1, keepdims=True) + NORM_EPS)
    return (inverse, (residual * inverse * norm_gain).astype(jnp.bfloat16))


def rms_backward(residual, inverse, norm_gain, upstream):
    gain_grad = jnp.sum(upstream * residual * inverse, axis=0)
    scaled = upstream * norm_gain
    inner = jnp.mean(scaled * residual, axis=-1, keepdims=True)
    return (gain_grad, inverse * scaled - residual * inverse * inverse * inverse * inner)


def score_block(rotated_query, turned_k, allowed):
    scores = jnp.einsum(
        "qhgd,khd->hgqk", rotated_query, turned_k, preferred_element_type=jnp.float32
    ) * HEAD_DIMENSION ** (-0.5)
    return jnp.where(allowed, scores, MASKED)


def attend_forward(residual, allowed, tables, gain, matrices):
    w_in, w_output = matrices
    count_of_rows = residual.shape[0]
    query_width = QUERY_HEADS * HEAD_DIMENSION
    key_width = KEY_VALUE_HEADS * HEAD_DIMENSION
    inverse, normalized_input = rms_forward(residual, gain)
    projected = jnp.dot(normalized_input, w_in, preferred_element_type=jnp.float32)
    query_unrotated = projected[:, :query_width].reshape(count_of_rows, QUERY_HEADS, -1)
    key_unrotated = projected[:, query_width : query_width + key_width]
    key_unrotated = key_unrotated.reshape(count_of_rows, KEY_VALUE_HEADS, -1)
    value_rows = projected[:, query_width + key_width :].astype(jnp.bfloat16)
    value_rows = value_rows.reshape(count_of_rows, KEY_VALUE_HEADS, -1)
    rotated_query = (
        apply_rotation(query_unrotated, *tables)
        .astype(jnp.bfloat16)
        .reshape(count_of_rows, KEY_VALUE_HEADS, QUERY_HEADS // KEY_VALUE_HEADS, HEAD_DIMENSION)
    )
    turned_k = apply_rotation(key_unrotated, *tables).astype(jnp.bfloat16)
    scores = score_block(rotated_query, turned_k, allowed)
    row_top = jnp.max(scores, axis=-1, keepdims=True)
    exp_scores = jnp.exp(scores - row_top)
    row_total = jnp.sum(exp_scores, axis=-1, keepdims=True)
    attn_probs = (exp_scores / row_total).astype(jnp.bfloat16)
    log_total = row_top + jnp.log(row_total)
    mixed_heads = jnp.einsum(
        "hgqk,khd->qhgd", attn_probs, value_rows, preferred_element_type=jnp.float32
    )
    mixed_heads = mixed_heads.astype(jnp.bfloat16).reshape(count_of_rows, query_width)
    attn_out = jnp.dot(mixed_heads, w_output, preferred_element_type=jnp.float32)
    return (
        residual + attn_out,
        (inverse, normalized_input, rotated_query, turned_k, value_rows, log_total, mixed_heads),
    )


def attend_backward(residual, allowed, tables, gain, matrices, stash, upstream):
    w_in, w_output = matrices
    inverse, normalized_input, rotated_query, turned_k, value_rows, log_total, mixed_heads = stash
    count_of_rows = residual.shape[0]
    branch_grad = upstream.astype(jnp.bfloat16)
    grad_wo = jnp.einsum("td,te->de", mixed_heads, branch_grad, preferred_element_type=jnp.float32)
    mixed_gradient = jnp.einsum(
        "te,de->td", branch_grad, w_output, preferred_element_type=jnp.float32
    )
    mixed_gradient = mixed_gradient.astype(jnp.bfloat16).reshape(
        count_of_rows, KEY_VALUE_HEADS, QUERY_HEADS // KEY_VALUE_HEADS, HEAD_DIMENSION
    )
    attn_probs = jnp.exp(score_block(rotated_query, turned_k, allowed) - log_total)
    value_rows_gradient = jnp.einsum(
        "hgqk,qhgd->khd",
        attn_probs.astype(jnp.bfloat16),
        mixed_gradient,
        preferred_element_type=jnp.float32,
    )
    value_rows_gradient = value_rows_gradient.astype(jnp.bfloat16).reshape(count_of_rows, -1)
    grad_probs = jnp.einsum(
        "qhgd,khd->hgqk", mixed_gradient, value_rows, preferred_element_type=jnp.float32
    )
    grad_scores = attn_probs * (
        grad_probs - jnp.sum(attn_probs * grad_probs, axis=-1, keepdims=True)
    )
    grad_scores = grad_scores.astype(jnp.bfloat16)
    grad_tq = jnp.einsum(
        "hgqk,khd->qhgd", grad_scores, turned_k, preferred_element_type=jnp.float32
    ) * HEAD_DIMENSION ** (-0.5)
    turned_key_gradient = jnp.einsum(
        "hgqk,qhgd->khd", grad_scores, rotated_query, preferred_element_type=jnp.float32
    ) * HEAD_DIMENSION ** (-0.5)
    grad_query = reverse_rotation(
        grad_tq.reshape(count_of_rows, QUERY_HEADS, HEAD_DIMENSION), *tables
    )
    grad_query = grad_query.astype(jnp.bfloat16).reshape(count_of_rows, -1)
    grad_key = reverse_rotation(turned_key_gradient, *tables).astype(jnp.bfloat16)
    grad_key = grad_key.reshape(count_of_rows, -1)
    grad_in = jnp.concatenate([grad_query, grad_key, value_rows_gradient], axis=1)
    grad_w_in = jnp.einsum("td,te->de", normalized_input, grad_in, preferred_element_type=jnp.float32)
    grad_normed = jnp.einsum("te,de->td", grad_in, w_in, preferred_element_type=jnp.float32)
    gain_grad, residual_grad = rms_backward(residual, inverse, gain, grad_normed)
    return (upstream + residual_grad, gain_grad, grad_w_in, grad_wo)


def widen(gate_columns, share):
    return jnp.repeat(gate_columns, share, axis=1)


def experts_forward(place, middle, gain, gate_parts, weights):
    w_gate, w_up, w_down = weights
    share = w_gate.shape[1] // gate_parts[0].shape[1]
    model_width = middle.shape[1]
    inverse, normalized_input = rms_forward(middle, gain)
    chunks = gather_tokens(place, normalized_input)
    parts, kept = [], []
    for chunk, gate_columns in zip(chunks, gate_parts):
        rows = chunk.reshape(-1, model_width)
        gate_pre = jnp.dot(rows, w_gate, preferred_element_type=jnp.float32)
        up_pre = jnp.dot(rows, w_up, preferred_element_type=jnp.float32)
        weighed = gate_pre * jax.nn.sigmoid(gate_pre) * up_pre * widen(gate_columns, share)
        weighed = weighed.astype(jnp.bfloat16)
        produced = lax.dot_general(
            weighed, w_down, (((1,), (1,)), ((), ())), preferred_element_type=jnp.float32
        )
        parts.append(produced.astype(jnp.bfloat16).reshape(chunk.shape))
        kept.append((rows, gate_pre, up_pre, weighed))
    return (middle + scatter_sums(place, parts), (inverse, kept))


def experts_backward(place, middle, gain, gate_parts, weights, stash, upstream, chunks):
    w_gate, w_up, w_down = weights
    share = w_gate.shape[1] // gate_parts[0].shape[1]
    model_width = middle.shape[1]
    inverse, kept = stash
    parts, gate_grads, up_grads, row_grads = [], [], [], []
    for chunk, gate_columns, (rows, gate_pre, up_pre, weighed) in zip(chunks, gate_parts, kept):
        grads = chunk.reshape(-1, model_width)
        hidden_grad = jnp.dot(grads, w_down, preferred_element_type=jnp.float32)
        hidden_grad = hidden_grad * widen(gate_columns, share)
        gate_sig = jax.nn.sigmoid(gate_pre)
        gate_grad = hidden_grad * up_pre * gate_sig * (1.0 + gate_pre * (1.0 - gate_sig))
        gate_grad = gate_grad.astype(jnp.bfloat16)
        up_grad = (hidden_grad * gate_pre * gate_sig).astype(jnp.bfloat16)
        back = (((1,), (1,)), ((), ()))
        produced = lax.dot_general(gate_grad, w_gate, back, preferred_element_type=jnp.float32)
        produced = produced + lax.dot_general(
            up_grad, w_up, back, preferred_element_type=jnp.float32
        )
        parts.append(produced.astype(jnp.bfloat16).reshape(chunk.shape))
        gate_grads.append(gate_grad)
        up_grads.append(up_grad)
        row_grads.append(grads)
    normed_grad = scatter_sums(place, parts)
    rows = jnp.concatenate([entry[0] for entry in kept])
    weighed = jnp.concatenate([entry[3] for entry in kept])
    outer = (((0,), (0,)), ((), ()))
    weight_grads = [
        lax.dot_general(a, b, outer, preferred_element_type=jnp.float32)
        for a, b in (
            (rows, jnp.concatenate(gate_grads)),
            (rows, jnp.concatenate(up_grads)),
            (jnp.concatenate(row_grads), weighed),
        )
    ]
    gain_grad, middle_grad = rms_backward(middle, inverse, gain, normed_grad)
    return (upstream + middle_grad, gain_grad, weight_grads)


def shards(
    tokens,
    lengths,
    routes,
    gates,
    cotangent,
    norm_attn,
    norm_ffn,
    query,
    key,
    value,
    output,
    w_gate,
    w_up,
    w_down,
):
    place = Place()
    token_rows = tokens.shape[0]
    layer_count, _, experts, _ = w_gate.shape
    expert_count = experts * place.columns
    in_width = query.shape[2] + key.shape[2] + value.shape[2]
    segment, seq_place = positions(lengths[0], token_rows)
    tables = rope_tables(seq_place, HEAD_DIMENSION)
    token_order = jnp.arange(token_rows, dtype=jnp.int32)
    allowed = (segment[:, None] == segment[None, :]) & (
        token_order[:, None] >= token_order[None, :]
    )
    gains = jnp.concatenate([norm_attn, norm_ffn]).T
    packs = []
    for l in range(layer_count):
        pack = [query[l], key[l], value[l], output[l]]
        if l == 0:
            pack.append(jnp.pad(gains, ((0, 0), (0, 128 - gains.shape[1]))))
        packs.append(jnp.concatenate(pack, axis=1))
    full = lax.all_gather(packs[0], AXES, axis=0, tiled=True)
    gains = full[:, in_width + output.shape[2] :].T[: 2 * layer_count].astype(jnp.float32)
    gate_rows = gather_gates(place, routes, gates, expert_count)
    gate_parts = [
        [
            jnp.transpose(piece[:, l], (0, 2, 1)).reshape(-1, experts)
            for piece in gate_rows
        ]
        for l in range(layer_count)
    ]
    expert_weights = gather_experts(place, [w_gate[0], w_up[0], w_down[0]])
    last_grads = None

    residual = tokens.astype(jnp.float32)
    matrices, weights, stored = [], [], []
    for l in range(layer_count):
        matrices.append((full[:, :in_width], full[:, in_width : in_width + output.shape[2]]))
        weights.append(expert_weights)
        layer_input = residual
        middle, attn_stash = attend_forward(layer_input, allowed, tables, gains[l], matrices[l])
        if l + 1 < layer_count:
            held, pack, *shares = lax.optimization_barrier(
                (middle, packs[l + 1], w_gate[l + 1], w_up[l + 1], w_down[l + 1])
            )
            middle = held
            full = lax.all_gather(pack, AXES, axis=0, tiled=True)
            expert_weights = gather_experts(place, shares)
        residual, moe_stash = experts_forward(
            place, middle, gains[layer_count + l], gate_parts[l], weights[l]
        )
        if l + 2 == layer_count or layer_count == 1:
            held, last = lax.optimization_barrier((residual, cotangent))
            residual = held
            last_grads = gather_tokens(place, last)
        stored.append((layer_input, middle, attn_stash, moe_stash))
    result = residual.astype(jnp.bfloat16)

    upstream = cotangent.astype(jnp.float32)
    in_grads, out_grads = [None] * layer_count, [None] * layer_count
    gain_grads = [None] * (2 * layer_count)
    expert_grads = [None] * layer_count
    for l in reversed(range(layer_count)):
        layer_input, middle, attn_stash, moe_stash = stored[l]
        chunks = last_grads
        if l + 1 < layer_count:
            chunks = gather_tokens(place, upstream.astype(jnp.bfloat16))
        upstream, gain_grads[layer_count + l], weight_grads = experts_backward(
            place,
            middle,
            gains[layer_count + l],
            gate_parts[l],
            weights[l],
            moe_stash,
            upstream,
            chunks,
        )
        expert_grads[l] = scatter_experts(place, weight_grads, experts)
        upstream, gain_grads[l], grad_w_in, grad_wo = attend_backward(
            layer_input, allowed, tables, gains[l], matrices[l], attn_stash, upstream
        )
        summed = lax.psum_scatter(
            jnp.concatenate([grad_w_in, grad_wo], axis=1).astype(jnp.bfloat16),
            AXES,
            scatter_dimension=0,
            tiled=True,
        ).astype(jnp.float32)
        in_grads[l], out_grads[l] = summed[:, :in_width], summed[:, in_width:]
    gain_sums = lax.psum_scatter(jnp.stack(gain_grads), AXES, scatter_dimension=1, tiled=True)
    in_grads = jnp.stack(in_grads)
    key_start, value_start = query.shape[2], query.shape[2] + key.shape[2]
    return (
        result,
        upstream,
        gain_sums[:layer_count],
        gain_sums[layer_count:],
        in_grads[:, :, :key_start],
        in_grads[:, :, key_start:value_start],
        in_grads[:, :, value_start:],
        jnp.stack(out_grads),
        jnp.stack([entry[0] for entry in expert_grads]),
        jnp.stack([entry[1] for entry in expert_grads]),
        jnp.stack([entry[2] for entry in expert_grads]),
    )


HEADS_PER_TURN = 6
LANES = 128
EXTRA = 128
HALF = 64
TILE = 256
MIB = 1 << 20
COST_PART = 16


def cost(flops):
    return pl.CostEstimate(flops=flops // COST_PART, bytes_accessed=0, transcendentals=0)


def any_spec():
    return pl.BlockSpec(memory_space=pl.ANY)


def whole_spec():
    return pl.BlockSpec(memory_space=pltpu.VMEM)


def scalar_spec():
    return pl.BlockSpec(memory_space=pltpu.SMEM)


def shape_of(*dims, dtype=jnp.bfloat16):
    return jax.ShapeDtypeStruct(dims, dtype)


class Copies:
    def __init__(self, semaphores, first=0):
        self.semaphores = semaphores
        self.used = first
        self.open = []

    def start(self, source, target):
        copy = pltpu.make_async_copy(source, target, self.semaphores.at[self.used])
        self.used += 1
        copy.start()
        self.open.append(copy)

    def wait(self):
        for copy in self.open:
            copy.wait()
        self.open = []


def shard_row(where, swapped, m, k, rows):
    plane = lax.rem(where[0] - k + 4, 4)
    fsdp = plane * CORES + (where[1] ^ swapped)
    return pl.multiple_of((fsdp * 4 + (where[2] ^ m)) * rows, 16)


MATRIX_PIECES = 10
MATRIX_COPIES = 40


def load_matrices(copies, where, pieces, full):
    rows, cut = pieces[0].shape[0] // 4, pieces[3].shape[1]
    spans = ((0, 0, full.shape[1]),) * 3 + ((3, 0, cut), (3, cut, full.shape[1] - cut))
    for swapped in range(CORES):
        for index, (m, low, width) in enumerate(spans):
            piece = pieces[swapped * 5 + index]
            for k in range(4):
                row = shard_row(where, swapped, m or index, k, rows)
                copies.start(
                    piece.at[pl.ds(k * rows, rows), :], full.at[pl.ds(row, rows), pl.ds(low, width)]
                )


def half_swap(x):
    lane = lax.broadcasted_iota(jnp.int32, x.shape, 1)
    return jnp.where(lane % 64 < 32, pltpu.roll(x, 96, 1), pltpu.roll(x, 32, 1))


def both_sides(pair, side):
    lane = lax.broadcasted_iota(jnp.int32, pair.shape, 1)
    wide = pair.astype(jnp.float32)
    here = jnp.where(lane // 64 == side, wide, 0.0)
    there = pltpu.roll(here, 64, 1)
    here, there = here.astype(jnp.bfloat16), there.astype(jnp.bfloat16)
    return (here, there) if side == 0 else (there, here)


def merge_sides(even, odd, side):
    lane = lax.broadcasted_iota(jnp.int32, even.shape, 1)
    if side == 0:
        return jnp.where(lane < 64, even + pltpu.roll(odd, 64, 1), 0.0)
    return jnp.where(lane < 64, 0.0, odd + pltpu.roll(even, 64, 1))


def contract(a, b, dims):
    return lax.dot_general(a, b, (dims, ((), ())), preferred_element_type=jnp.float32)


PLAIN = ((1,), (0,))
ACROSS = ((1,), (1,))
OUTER = ((0,), (0,))


def read_sum(base, extra):
    if not extra:
        return base[...].astype(jnp.float32)
    *blocks, one_head, two_tail, by_one, by_two = extra
    top = pl.ds(0, HALF)
    halves = []
    for side, terms in enumerate(((one_head, by_two), (two_tail, by_one))):
        rows = pl.ds(side * HALF, HALF)
        total = base[rows, :].astype(jnp.float32)
        for block in blocks:
            total = total + block[rows, :].astype(jnp.float32)
        for term in terms:
            total = total + term[top, :].astype(jnp.float32)
        halves.append(total)
    return jnp.concatenate(halves, axis=0)


def attend_forward_kernel(terms, width, where, base, *refs):
    refs = list(refs)
    extra = [refs.pop(0) for _ in range(terms)]
    cosine, sine, allowed = refs[:3]
    pieces = refs[3 : 3 + MATRIX_PIECES]
    refs = refs[3 + MATRIX_PIECES :]
    h_out, m_out, nf_out, na_out, q_out, k_out, v_out, o_out, lse_out, gain_out = refs[:10]
    full, proj, mixed, semaphores = refs[10:]
    copies = Copies(semaphores)
    load_matrices(copies, where, pieces, full)
    h = read_sum(base, extra)
    h_out[...] = h
    inverse = lax.rsqrt(jnp.mean(h * h, axis=1, keepdims=True) + NORM_EPS)
    model = h.shape[1]
    in_width = width
    key_start = model
    value_start = model + (in_width - model) // 2
    copies.wait()
    gains = full[:, pl.ds(in_width + model, EXTRA)].astype(jnp.float32).T
    gain_out[...] = gains[:8]
    na_out[...] = (h * inverse * gains[0:1]).astype(jnp.bfloat16)
    step = 512

    @pl.loop(0, in_width // step)
    def _(i):
        columns = pl.ds(pl.multiple_of(i * step, step), step)
        proj[:, columns] = contract(na_out[...], full[:, columns], PLAIN)

    cos, sin = cosine[...], sine[...]

    @pl.loop(0, key_start // LANES)
    def _(i):
        columns = pl.ds(pl.multiple_of(i * LANES, LANES), LANES)
        x = proj[:, columns]
        q_out[:, columns] = (x * cos + half_swap(x) * sin).astype(jnp.bfloat16)

    @pl.loop(0, (value_start - key_start) // LANES)
    def _(i):
        start = pl.multiple_of(i * LANES, LANES)
        x = proj[:, pl.ds(key_start + start, LANES)]
        k_out[:, pl.ds(start, LANES)] = (x * cos + half_swap(x) * sin).astype(jnp.bfloat16)

    v_out[...] = proj[:, value_start:in_width].astype(jnp.bfloat16)
    lse_out[...] = jnp.zeros_like(lse_out)
    open_keys = allowed[...] > 0.5
    lane = lax.broadcasted_iota(jnp.int32, open_keys.shape, 1)

    @pl.loop(0, KEY_VALUE_HEADS // 2)
    def _(turn):
        pair = pl.ds(pl.multiple_of(turn * LANES, LANES), LANES)
        keys = [both_sides(k_out[:, pair], side) for side in range(2)]
        values = [both_sides(v_out[:, pair], side) for side in range(2)]
        lse = lse_out[...]
        for group in range(HEADS_PER_TURN // 2):
            columns = pl.ds(
                pl.multiple_of(turn * (HEADS_PER_TURN * 64) + group * LANES, LANES), LANES
            )
            total = jnp.zeros((h.shape[0], LANES), jnp.float32)
            for side in range(2):
                head = group * 2 + side
                scores = contract(q_out[:, columns], keys[head // 3][side], ACROSS)
                scores = jnp.where(open_keys, scores * HEAD_DIMENSION ** (-0.5), MASKED)
                top = jnp.max(scores, axis=1, keepdims=True)
                weights = jnp.exp(scores - top)
                row_total = jnp.sum(weights, axis=1, keepdims=True)
                probs = (weights / row_total).astype(jnp.bfloat16)
                lse = jnp.where(lane == turn * HEADS_PER_TURN + head, top + jnp.log(row_total), lse)
                total = total + contract(probs, values[head // 3][side], PLAIN)
            o_out[:, columns] = total.astype(jnp.bfloat16)
        lse_out[...] = lse

    @pl.loop(0, model // step)
    def _(i):
        columns = pl.ds(pl.multiple_of(i * step, step), step)
        weights = full[:, pl.ds(pl.multiple_of(in_width + i * step, step), step)]
        mixed[:, columns] = contract(o_out[...], weights, PLAIN)

    m = h_out[...] + mixed[...]
    m_out[...] = m
    inverse = lax.rsqrt(jnp.mean(m * m, axis=1, keepdims=True) + NORM_EPS)
    nf_out[...] = (m * inverse * gain_out[1:2]).astype(jnp.bfloat16)


def attend_forward_fast(where, base, extra, tables, pieces, in_width, after=()):
    rows, model = base.shape
    bf, f32 = jnp.bfloat16, jnp.float32
    key_width = (in_width - model) // 2
    total = in_width + model + EXTRA
    shapes = [
        shape_of(rows, model, dtype=f32),
        shape_of(rows, model, dtype=f32),
        shape_of(rows, model),
        shape_of(rows, model),
        shape_of(rows, model),
        shape_of(rows, key_width),
        shape_of(rows, key_width),
        shape_of(rows, model),
        shape_of(rows, LANES, dtype=f32),
        shape_of(8, model, dtype=f32),
    ]

    def body(*refs):
        used = 2 + len(extra) + 3 + MATRIX_PIECES
        attend_forward_kernel(len(extra), in_width, *refs[:used], *refs[used + len(after) :])

    return pl.pallas_call(
        body,
        name="attend_forward",
        out_shape=shapes,
        in_specs=[scalar_spec()]
        + [whole_spec()] * (4 + len(extra))
        + [any_spec()] * (MATRIX_PIECES + len(after)),
        out_specs=[whole_spec()] * len(shapes),
        scratch_shapes=[
            pltpu.VMEM((model, total), bf),
            pltpu.VMEM((rows, in_width), f32),
            pltpu.VMEM((rows, model), f32),
            pltpu.SemaphoreType.DMA((MATRIX_COPIES,)),
        ],
        compiler_params=pltpu.CompilerParams(vmem_limit_bytes=44 * MIB),
        cost_estimate=cost(2 * rows * model * total),
    )(where, base, *extra, *tables, *pieces, *after)


def attend_backward_kernel(terms, width, where, base, upstream, *refs):
    refs = list(refs)
    extra = [refs.pop(0) for _ in range(terms)]
    h_in, m_in, na, q, k, v, o, lse_in, gains, cosine, sine, allowed = refs[:12]
    pieces = refs[12 : 12 + MATRIX_PIECES]
    outs, refs = refs[12 + MATRIX_PIECES : -6], refs[-6:]
    gh_out, gh_low = outs[:2]
    full, sums, mixed, grad_in, turned, semaphores = refs
    rows, model = h_in.shape
    in_width = width
    key_start = model
    value_start = model + (in_width - model) // 2
    shard = full.shape[0] // 32
    copies = Copies(semaphores)
    load_matrices(copies, where, pieces, full)
    gnf = read_sum(base, extra)
    m = m_in[...]
    inverse = lax.rsqrt(jnp.mean(m * m, axis=1, keepdims=True) + NORM_EPS)
    gain_ffn = jnp.sum(gnf * m * inverse, axis=0, keepdims=True)
    scaled = gnf * gains[1:2]
    inner = jnp.mean(scaled * m, axis=1, keepdims=True)
    gm = upstream[...].astype(jnp.float32)
    gm = gm + inverse * scaled - m * (inverse * inverse * inverse) * inner
    gh_out[...] = gm
    gh_low[...] = gm.astype(jnp.bfloat16)
    copies.wait()
    step = 512

    @pl.loop(0, model // step)
    def _(i):
        row = pl.ds(pl.multiple_of(i * step, step), step)
        mixed[:, row] = contract(gh_low[...], full[row, in_width : in_width + model], ACROSS).astype(
            jnp.bfloat16
        )

    open_keys = allowed[...] > 0.5
    lane = lax.broadcasted_iota(jnp.int32, open_keys.shape, 1)
    cos, sin = cosine[...], sine[...]
    scale = HEAD_DIMENSION ** (-0.5)

    @pl.loop(0, KEY_VALUE_HEADS // 2)
    def _(turn):
        start = pl.multiple_of(turn * LANES, LANES)
        pair = pl.ds(start, LANES)
        keys = [both_sides(k[:, pair], side) for side in range(2)]
        values = [both_sides(v[:, pair], side) for side in range(2)]
        zero = jnp.zeros((rows, LANES), jnp.float32)
        grad_k = [[zero, zero], [zero, zero]]
        grad_v = [[zero, zero], [zero, zero]]
        lse = lse_in[...]
        for group in range(HEADS_PER_TURN // 2):
            columns = pl.ds(
                pl.multiple_of(turn * (HEADS_PER_TURN * 64) + group * LANES, LANES), LANES
            )
            grad_q = zero
            for side in range(2):
                head = group * 2 + side
                kv = head // 3
                top = jnp.sum(
                    jnp.where(lane == turn * HEADS_PER_TURN + head, lse, 0.0), axis=1, keepdims=True
                )
                scores = contract(q[:, columns], keys[kv][side], ACROSS) * scale
                probs = jnp.exp(jnp.where(open_keys, scores, MASKED) - top)
                go = mixed[:, columns]
                grad_v[kv][side] = grad_v[kv][side] + contract(
                    probs.astype(jnp.bfloat16), go, OUTER
                )
                grad_p = contract(go, values[kv][side], ACROSS)
                grad_s = probs * (grad_p - jnp.sum(probs * grad_p, axis=1, keepdims=True))
                grad_s = grad_s.astype(jnp.bfloat16)
                grad_q = grad_q + contract(grad_s, keys[kv][side], PLAIN)
                grad_k[kv][side] = grad_k[kv][side] + contract(grad_s, q[:, columns], OUTER)
            grad_q = grad_q * scale
            grad_in[:, columns] = (grad_q * cos - half_swap(grad_q) * sin).astype(jnp.bfloat16)
        key_grad = merge_sides(*grad_k[0], 0) + merge_sides(*grad_k[1], 1)
        key_grad = key_grad * scale
        key_grad = key_grad * cos - half_swap(key_grad) * sin
        value_grad = merge_sides(*grad_v[0], 0) + merge_sides(*grad_v[1], 1)
        grad_in[:, pl.ds(key_start + start, LANES)] = key_grad.astype(jnp.bfloat16)
        grad_in[:, pl.ds(value_start + start, LANES)] = value_grad.astype(jnp.bfloat16)

    turned[...] = jnp.zeros_like(turned)

    @pl.loop(0, in_width // step)
    def _(i):
        columns = pl.ds(pl.multiple_of(i * step, step), step)
        turned[...] += contract(grad_in[:, columns], full[:, columns], ACROSS)

    grad_na = turned[...]
    h = h_in[...]
    inverse = lax.rsqrt(jnp.mean(h * h, axis=1, keepdims=True) + NORM_EPS)
    gain_attn = jnp.sum(grad_na * h * inverse, axis=0, keepdims=True)
    scaled = grad_na * gains[0:1]
    inner = jnp.mean(scaled * h, axis=1, keepdims=True)
    band = 384

    @pl.loop(0, model // band)
    def _(i):
        start = pl.multiple_of(i * band, band)
        row = pl.ds(start, band)
        sums[row, in_width : in_width + model] = contract(o[:, row], gh_low[...], OUTER).astype(
            jnp.bfloat16
        )
        sums[row, :in_width] = contract(na[:, row], grad_in[...], OUTER).astype(jnp.bfloat16)

    both = jnp.concatenate([gain_attn, gain_ffn, jnp.zeros((EXTRA - 2, model), jnp.float32)], axis=0)
    sums[:, pl.ds(in_width + model, EXTRA)] = both.T.astype(jnp.bfloat16)
    if len(outs) == 3:
        copies.start(sums, outs[2])
    else:
        for swapped in (1, 0):
            for first, count in ((1, 3), (0, 1)):
                target = outs[2 + 2 * (1 - swapped) + (1 - first)]
                for m_index in range(4):
                    for n in range(count):
                        row = shard_row(where, swapped, m_index, first + n, shard)
                        copies.start(
                            sums.at[pl.ds(row, shard), :],
                            target.at[pl.ds((m_index * count + n) * shard, shard), :],
                        )
    gh = gh_out[...] + inverse * scaled - h * (inverse * inverse * inverse) * inner
    gh_out[...] = gh
    gh_low[...] = gh.astype(jnp.bfloat16)
    copies.wait()


def attend_backward_fast(
    split, where, base, upstream, extra, stash, tables, pieces, in_width, after=()
):
    rows, model = upstream.shape
    bf, f32 = jnp.bfloat16, jnp.float32
    total = in_width + model + EXTRA
    shapes = [
        shape_of(rows, model, dtype=f32),
        shape_of(rows, model),
    ]
    if split:
        shapes += [shape_of(model // 8 * part, total) for part in (3, 1, 3, 1)]
    else:
        shapes += [shape_of(model, total)]

    def body(*refs):
        used = 3 + len(extra) + 12 + MATRIX_PIECES
        attend_backward_kernel(len(extra), in_width, *refs[:used], *refs[used + len(after) :])

    return pl.pallas_call(
        body,
        name="attend_backward",
        out_shape=shapes,
        in_specs=[scalar_spec()]
        + [whole_spec()] * (2 + len(extra) + 12)
        + [any_spec()] * (MATRIX_PIECES + len(after)),
        out_specs=[whole_spec()] * 2 + [any_spec()] * (len(shapes) - 2),
        scratch_shapes=[
            pltpu.VMEM((model, total), bf),
            pltpu.VMEM((model, total), bf),
            pltpu.VMEM((rows, model), bf),
            pltpu.VMEM((rows, in_width), bf),
            pltpu.VMEM((rows, model), f32),
            pltpu.SemaphoreType.DMA((MATRIX_COPIES + 32,)),
        ],
        compiler_params=pltpu.CompilerParams(vmem_limit_bytes=56 * MIB),
        cost_estimate=cost(4 * rows * model * total),
    )(where, base, upstream, *extra, *stash, *tables, *pieces, *after)


SHARES = ((0, 0, 3), (1, 0, 3), (3, 0, 3), (2, 0, 1), (2, 1, 2))
WEIGHT_PIECES = CORES * len(SHARES)


def load_experts(copies, where, pieces, targets):
    at = 0
    for swapped in range(CORES):
        for k, first, count in SHARES:
            piece = pieces[at]
            at += 1
            _, experts, rows, share = piece.shape
            fsdp = lax.rem(where[0] - k + 4, 4) * CORES + (where[1] ^ swapped)
            row = pl.ds(pl.multiple_of(fsdp * rows, 16), rows)
            for i, target in enumerate(targets[first : first + count]):
                for e in range(experts):
                    copies.start(piece.at[i, e], target.at[row, pl.ds(e * share, share)])


def widen_tile(columns, share, width):
    lane = lax.broadcasted_iota(jnp.int32, (columns.shape[0], width), 1)
    wide = jnp.broadcast_to(columns[:, 0:1], lane.shape)
    for e in range(1, width // share):
        wide = jnp.where(lane >= e * share, columns[:, e : e + 1], wide)
    return wide


def start_rows(copies, pieces, rows_ref, spans=None):
    at = 0
    for index, piece in enumerate(pieces):
        first, rows = spans[index] if spans else (0, piece.shape[0])
        if rows:
            copies.start(piece.at[pl.ds(first, rows), :], rows_ref.at[pl.ds(at, rows), :])
        at += rows


def spans_of(far):
    if far:
        return ((HALF * 2, HALF * 6),) * 3 + ((HALF * 2, HALF * 2), (0, HALF * 4))
    return ((0, HALF * 2),) * 4 + ((0, 0),)


def part_rows(n):
    return [n, n // 2, n // 2, n, n]


def start_parts(copies, y, parts):
    n = parts[0].shape[0]
    half = n // 2

    def start(first, count, part, at=0):
        copies.start(y.at[pl.ds(first, count), :], part.at[pl.ds(at, count), :])

    own, one_head, two_tail, to_one, to_two = parts
    start(0, n, own)
    start(n, half, one_head)
    start(2 * n + half, half, two_tail)
    start(n + half, half, to_one)
    start(3 * n + half, half, to_one, half)
    start(2 * n, half, to_two)
    start(3 * n, half, to_two, half)


def experts_forward_kernel(where, gates, *refs):
    pieces, weights, refs = refs[:5], refs[5 : 5 + WEIGHT_PIECES], refs[5 + WEIGHT_PIECES :]
    parts, x_out, g_out, u_out = refs[:5], *refs[5:8]
    x, y, g, u, w_gate, w_up, w_down, semaphores = refs[8:]
    copies = Copies(semaphores)
    start_rows(copies, pieces, x)
    load_experts(copies, where, weights, (w_gate, w_up, w_down))
    share = weights[0].shape[3]
    width = w_gate.shape[1]
    copies.wait()
    copies.start(x, x_out)

    @pl.loop(0, x.shape[0] // TILE)
    def _(i):
        row = pl.ds(pl.multiple_of(i * TILE, TILE), TILE)
        gate_pre = contract(x[row, :], w_gate[...], PLAIN)
        up_pre = contract(x[row, :], w_up[...], PLAIN)
        g[row, :] = gate_pre
        u[row, :] = up_pre
        wide = widen_tile(gates[row, :], share, width)
        weighed = (gate_pre * jax.nn.sigmoid(gate_pre) * up_pre * wide).astype(jnp.bfloat16)
        y[row, :] = contract(weighed, w_down[...], ACROSS).astype(jnp.bfloat16)

    start_parts(copies, y, parts)
    copies.start(g, g_out)
    copies.start(u, u_out)
    copies.wait()


def experts_forward_fast(where, gates, pieces, weights, after=()):
    n, model = pieces[0].shape
    _, experts, _, share = weights[0].shape
    rows, width = 4 * n, experts * share
    bf, f32 = jnp.bfloat16, jnp.float32
    shapes = [shape_of(r, model) for r in part_rows(n)]
    shapes += [shape_of(rows, model)] + [shape_of(rows, width, dtype=f32)] * 2

    def body(*refs):
        used = 7 + WEIGHT_PIECES
        experts_forward_kernel(*refs[:used], *refs[used + len(after) :])

    return pl.pallas_call(
        body,
        name="experts_forward",
        out_shape=shapes,
        in_specs=[scalar_spec(), whole_spec()] + [any_spec()] * (5 + WEIGHT_PIECES + len(after)),
        out_specs=[any_spec()] * len(shapes),
        scratch_shapes=[
            pltpu.VMEM((rows, model), bf),
            pltpu.VMEM((rows, model), bf),
            pltpu.VMEM((rows, width), f32),
            pltpu.VMEM((rows, width), f32),
        ]
        + [pltpu.VMEM((model, width), bf)] * 3
        + [pltpu.SemaphoreType.DMA((5 + 24 * experts + 20,))],
        compiler_params=pltpu.CompilerParams(vmem_limit_bytes=48 * MIB),
        cost_estimate=cost(6 * rows * model * width),
    )(where, gates, *pieces, *weights, *after)


def experts_backward_kernel(spans, where, gates, *refs):
    pieces, g_in, u_in = refs[:5], refs[5], refs[6]
    weights, refs = refs[7 : 7 + WEIGHT_PIECES], refs[7 + WEIGHT_PIECES :]
    parts, r_out, gg_out, gu_out, p_out = refs[:5], *refs[5:9]
    x, y, g, u, gg, gu, p, w_gate, w_up, w_down, semaphores = refs[9:]
    copies = Copies(semaphores)
    start_rows(copies, pieces, x, spans)
    load_experts(copies, where, weights, (w_gate, w_up, w_down))
    copies.start(g_in, g)
    copies.start(u_in, u)
    share = weights[0].shape[3]
    width = w_gate.shape[1]
    copies.wait()
    copies.start(x, r_out)

    @pl.loop(0, x.shape[0] // TILE)
    def _(i):
        row = pl.ds(pl.multiple_of(i * TILE, TILE), TILE)
        wide = widen_tile(gates[row, :], share, width)
        hidden_grad = contract(x[row, :], w_down[...], PLAIN) * wide
        gate_pre, up_pre = g[row, :], u[row, :]
        sig = jax.nn.sigmoid(gate_pre)
        active = gate_pre * sig
        p[row, :] = (active * up_pre * wide).astype(jnp.bfloat16)
        gate_grad = hidden_grad * up_pre * sig * (1.0 + gate_pre * (1.0 - sig))
        gg[row, :] = gate_grad.astype(jnp.bfloat16)
        gu[row, :] = (hidden_grad * active).astype(jnp.bfloat16)
        back = contract(gg[row, :], w_gate[...], ACROSS)
        back = back + contract(gu[row, :], w_up[...], ACROSS)
        y[row, :] = back.astype(jnp.bfloat16)

    start_parts(copies, y, parts)
    copies.start(gg, gg_out)
    copies.start(gu, gu_out)
    copies.start(p, p_out)
    copies.wait()


def experts_backward_fast(where, gates, pieces, stash, weights, spans=None, after=()):
    n, model = gates.shape[0] // 4, pieces[0].shape[1]
    _, experts, _, share = weights[0].shape
    rows, width = 4 * n, experts * share
    bf, f32 = jnp.bfloat16, jnp.float32
    shapes = [shape_of(r, model) for r in part_rows(n)]
    shapes += [shape_of(rows, model)] + [shape_of(rows, width)] * 3

    def body(*refs):
        used = 9 + WEIGHT_PIECES
        experts_backward_kernel(spans, *refs[:used], *refs[used + len(after) :])

    return pl.pallas_call(
        body,
        name="experts_backward",
        out_shape=shapes,
        in_specs=[scalar_spec(), whole_spec()] + [any_spec()] * (7 + WEIGHT_PIECES + len(after)),
        out_specs=[any_spec()] * len(shapes),
        scratch_shapes=[
            pltpu.VMEM((rows, model), bf),
            pltpu.VMEM((rows, model), bf),
            pltpu.VMEM((rows, width), f32),
            pltpu.VMEM((rows, width), f32),
            pltpu.VMEM((rows, width), bf),
            pltpu.VMEM((rows, width), bf),
            pltpu.VMEM((rows, width), bf),
        ]
        + [pltpu.VMEM((model, width), bf)] * 3
        + [pltpu.SemaphoreType.DMA((5 + 24 * experts + 20,))],
        compiler_params=pltpu.CompilerParams(vmem_limit_bytes=52 * MIB),
        cost_estimate=cost(6 * rows * model * width),
    )(where, gates, *pieces, *stash, *weights, *after)


def weight_grads_kernel(experts, where, *refs):
    sources, mine, other = refs[:4], refs[4], refs[5]
    x, g, out, semaphores = refs[6:]
    copies = Copies(semaphores)
    for target, near, far in zip((x, g), sources[:2], sources[2:]):
        start_rows(copies, (near, far), target)
    copies.wait()
    band = x.shape[1] // 4
    rows = band // CORES
    share = g.shape[1] // experts

    @pl.loop(0, 4)
    def _(z):
        columns = pl.ds(pl.multiple_of(z * band, band), band)
        k = lax.rem(z - where[0] + 4, 4)
        grads = contract(x[:, columns], g[...], OUTER).astype(jnp.bfloat16)
        for core in range(CORES):
            for e in range(experts):
                out[core, k, e] = grads[
                    core * rows : (core + 1) * rows, e * share : (e + 1) * share
                ]

    copies.start(out.at[1 - where[1]], other)
    copies.start(out.at[where[1]], mine)
    copies.wait()


def weight_grads_fast(where, near, far, experts, after=()):
    model, width = near[0].shape[1], near[1].shape[1]
    count = near[0].shape[0] + far[0].shape[0]
    rows, share = model // 8, width // experts
    bf = jnp.bfloat16

    def body(*refs):
        weight_grads_kernel(experts, *refs[:5], *refs[5 + len(after) :])

    return pl.pallas_call(
        body,
        name="weight_grads",
        out_shape=[shape_of(4, experts, rows, share)] * 2,
        in_specs=[scalar_spec()] + [any_spec()] * (4 + len(after)),
        out_specs=[any_spec()] * 2,
        scratch_shapes=[
            pltpu.VMEM((count, model), bf),
            pltpu.VMEM((count, width), bf),
            pltpu.VMEM((CORES, 4, experts, rows, share), bf),
            pltpu.SemaphoreType.DMA((6,)),
        ],
        compiler_params=pltpu.CompilerParams(vmem_limit_bytes=40 * MIB),
        cost_estimate=cost(2 * count * model * width),
    )(where, *near, *far, *after)


def cut_kernel(where, w_gate, w_up, w_down, *outs):
    share = outs[0].shape[3]
    matrices = (w_gate, w_up, w_down)
    for (k, first, count), out in zip(SHARES, outs):
        columns = pl.ds(pl.multiple_of(lax.rem(where[0] + k, 4) * share, share), share)
        for i in range(count):
            out[i, 0] = matrices[first + i][0, 0, :, columns]


def cut_experts(where, weights, layer):
    _, experts, rows, hidden = weights[0].shape
    share = hidden // 4
    return pl.pallas_call(
        cut_kernel,
        name="cut_experts",
        grid=(experts,),
        out_shape=[shape_of(count, experts, rows, share) for _, _, count in SHARES],
        in_specs=[scalar_spec()]
        + [pl.BlockSpec((1, 1, rows, hidden), lambda e: (layer, e, 0, 0))] * 3,
        out_specs=[
            pl.BlockSpec((count, 1, rows, share), lambda e: (0, e, 0, 0)) for _, _, count in SHARES
        ],
    )(where, *weights)


def join_kernel(layer, where, *refs):
    pieces, outs = refs[:4], refs[-3:]
    i = pl.program_id(0)
    share = pieces[0].shape[3]
    for index, out in enumerate(outs):

        @pl.when(i == index)
        def _():
            for k, piece in enumerate(pieces):
                columns = pl.ds(pl.multiple_of(lax.rem(where[0] - k + 4, 4) * share, share), share)
                out[0, :, :, columns] = piece[0].astype(jnp.float32)


def join_experts(where, pieces, layer, layers, earlier=None):
    mats, experts, rows, share = pieces[0].shape
    shape = shape_of(layers, experts, rows, 4 * share, dtype=jnp.float32)
    given = [] if earlier is None else list(earlier)

    return pl.pallas_call(
        functools.partial(join_kernel, layer),
        name="join_experts",
        grid=(mats,),
        out_shape=[shape] * mats,
        in_specs=[scalar_spec()]
        + [pl.BlockSpec((1, experts, rows, share), lambda i: (i, 0, 0, 0))] * 4
        + [any_spec()] * len(given),
        out_specs=[pl.BlockSpec((1, experts, rows, 4 * share), lambda i: (layer, 0, 0, 0))] * mats,
        input_output_aliases={5 + j: j for j in range(len(given))},
        compiler_params=pltpu.CompilerParams(vmem_limit_bytes=40 * MIB),
    )(where, *pieces, *given)


def tie(value, *events):
    flat, tree = jax.tree.flatten(value)
    held = lax.optimization_barrier((*flat, *events))
    return jax.tree.unflatten(tree, held[: len(flat)])


def spread_first(place, block):
    return [block, place.hop(block, flip=1), place.hop(block, flip=2)]


def spread_last(place, first, axis=0, cut=None):
    block, one, two = first
    cut = cut or block.shape[axis] // 2
    head = place.hop(lax.slice_in_dim(one, 0, cut, axis=axis), flip=2)
    tail = place.hop(lax.slice_in_dim(two, cut, None, axis=axis), flip=1)
    return [block, one, two, head, tail]


def spread_pieces(place, block):
    return spread_last(place, spread_first(place, block))


def up_hops(place, block):
    return [place.hop(block, up=k) for k in range(1, 4)]


def add_low(a, b):
    return (a.astype(jnp.float32) + b.astype(jnp.float32)).astype(a.dtype)


def fold_first(place, parts):
    own, one_head, two_tail, to_one, to_two = parts
    return own, one_head, two_tail, place.hop(to_one, flip=1), place.hop(to_two, flip=2)


def fold_sums(first):
    own, one_head, two_tail, by_one, by_two = first
    half = one_head.shape[0]
    return own, add_low(one_head, by_two[half:]), add_low(two_tail, by_one[half:]), by_one, by_two


def fold_start(place, parts):
    return fold_sums(fold_first(place, parts))


def fold_end(place, state):
    own, one_head, two_tail, by_one, by_two = state
    return own, place.hop(one_head, flip=1), place.hop(two_tail, flip=2), by_one, by_two


def add_pieces(own, one_head, two_tail, by_one, by_two, axis=0):
    wide = lambda value: value.astype(jnp.float32)
    half = one_head.shape[0]
    one = jnp.concatenate([one_head, by_one[:half]], axis=axis)
    two = jnp.concatenate([by_two[:half], two_tail], axis=axis)
    return wide(own) + wide(one) + wide(two)


def blocks_kernel(own, one_head, two_tail, by_one, by_two, *outs):
    half = one_head.shape[0]
    rows = outs[0].shape[0]
    step = HALF
    for start in range(0, own.shape[0], step):
        terms = (one_head, by_two) if start < half else (two_tail, by_one)
        at = pl.ds(start % half, step)
        total = own[pl.ds(start, step), :].astype(jnp.float32)
        for term in terms:
            total = total + term[at, :].astype(jnp.float32)
        outs[start // rows][pl.ds(start % rows, step), :] = total.astype(jnp.bfloat16)


def sum_blocks(own, *others):
    rows, model = own.shape
    return pl.pallas_call(
        blocks_kernel,
        name="sum_blocks",
        out_shape=[shape_of(rows // 3, model)] * 3,
        in_specs=[whole_spec()] * 5,
        out_specs=[whole_spec()] * 3,
    )(own, *others)


def down_hops(place, blocks):
    return [place.hop(blocks[k - 1], up=-k) for k in range(1, 4)]


def total_of(base, extra):
    *blocks, one_head, two_tail, by_one, by_two = extra
    total = base.astype(jnp.float32) + add_pieces(blocks[0], one_head, two_tail, by_one, by_two)
    for block in blocks[1:]:
        total = total + block.astype(jnp.float32)
    return total


def received(near_ends, arrived):
    own, one_head, two_tail, by_one, by_two = near_ends
    return [own, *arrived, one_head, two_tail, by_one, by_two]


def merge_kernel(cut, mine, arrived, own, one_head, two_tail, to_one, to_two):
    m = pl.program_id(0)
    total = (mine[...].astype(jnp.float32) + arrived[...].astype(jnp.float32)).astype(jnp.bfloat16)
    rows = total.shape[0]

    @pl.when(m == 0)
    def _():
        own[...] = total

    @pl.when(m == 1)
    def _():
        one_head[...] = total[:, :cut]
        to_one[:rows, :] = total[:, cut:]

    @pl.when(m == 2)
    def _():
        to_two[:rows, :] = total[:, :cut]
        two_tail[...] = total[:, cut:]

    @pl.when(m == 3)
    def _():
        to_two[rows:, :] = total[:, :cut]
        to_one[rows:, :] = total[:, cut:]


def merge_cores(mine, arrived, cut):
    rows, width = mine.shape[0] // 4, mine.shape[1]
    outs = [(rows, width), (rows, cut), (rows, width - cut), (2 * rows, width - cut), (2 * rows, cut)]
    return pl.pallas_call(
        functools.partial(merge_kernel, cut),
        name="merge_cores",
        grid=(4,),
        out_shape=[shape_of(*out) for out in outs],
        in_specs=[pl.BlockSpec((rows, width), lambda m: (m, 0))] * 2,
        out_specs=[pl.BlockSpec(out, lambda m: (0, 0)) for out in outs],
        compiler_params=pltpu.CompilerParams(vmem_limit_bytes=40 * MIB),
    )(mine, arrived)


def pack_kernel(*refs):
    layers = refs[0].shape[0]
    for l in range(layers):
        out = refs[l - layers]
        at = 0
        for ref in refs[:-layers]:
            width = ref.shape[2]
            out[:, at : at + width] = ref[l]
            at += width


def pack_matrices(*arrays):
    width = sum(a.shape[2] for a in arrays)
    layers, rows, _ = arrays[0].shape
    return pl.pallas_call(
        pack_kernel,
        name="pack_matrices",
        out_shape=[shape_of(rows, width)] * layers,
        in_specs=[whole_spec()] * len(arrays),
        out_specs=[whole_spec()] * layers,
    )(*arrays)


def scatter_matrices(place, other_far, other_near, mine_far, mine_near, cut, event):
    rows = mine_near.shape[0] // 4
    arrived_far = place.hop(other_far, swap=1)
    arrived_near = place.hop(other_near, swap=1)
    far = fold_first(place, merge_cores(mine_far, arrived_far, cut))
    near = fold_start(place, merge_cores(mine_near, arrived_near, cut))
    far = fold_sums(tie(far, event))
    far = add_pieces(*fold_end(place, far), axis=1).astype(jnp.bfloat16)
    arrived = down_hops(place, [far[k * rows : (k + 1) * rows] for k in range(3)])
    final = add_pieces(*fold_end(place, near), axis=1)
    for block in arrived:
        final = final + block.astype(jnp.float32)
    return final


def tables_of(length_row, rows):
    order = jnp.arange(rows, dtype=jnp.int32)
    index = jnp.arange(length_row.shape[0], dtype=jnp.int32)
    ends = jnp.sum(jnp.where(index[:, None] <= index[None, :], length_row[:, None], 0), axis=0)
    passed = order[:, None] >= ends[None, :]
    segment = jnp.sum(passed.astype(jnp.int32), axis=1)
    begin = jnp.sum(jnp.where(passed, length_row[None, :], 0), axis=1)
    cosine, sine = rope_tables(order - begin, HEAD_DIMENSION)
    allowed = (segment[:, None] == segment[None, :]) & (order[:, None] >= order[None, :])
    return (
        jnp.concatenate([cosine] * 4, axis=1),
        jnp.concatenate([-sine, sine] * 2, axis=1),
        allowed.astype(jnp.float32),
    )


def gate_rows_of(place, line):
    order = jnp.stack(spread_gates(place, line))
    order = jnp.transpose(order, (2, 0, 1, 4, 3))
    order = jnp.pad(order, ((0, 0),) * 4 + ((0, 8 - order.shape[4]),))
    return [
        (layer[:, :1].reshape(-1, 8), layer[:, 1:].reshape(-1, 8)) for layer in order
    ]


def shards_fast(
    tokens,
    lengths,
    routes,
    gates,
    cotangent,
    norm_attn,
    norm_ffn,
    query,
    key,
    value,
    output,
    w_gate,
    w_up,
    w_down,
):
    place = Place()
    where = jnp.stack([place.plane, place.core, place.column]).astype(jnp.int32)
    rows, model = tokens.shape
    layer_count, _, experts, _ = w_gate.shape
    expert_count = experts * place.columns
    in_width = query.shape[2] + key.shape[2] + value.shape[2]
    gains = jnp.stack([norm_attn, norm_ffn], axis=2)
    gains = jnp.pad(gains, ((0, 0), (0, 0), (0, EXTRA - 2)))
    packs = pack_matrices(query, key, value, output, gains)
    cut = packs[0].shape[1] // 2 // 128 * 128
    weights = [jnp.transpose(w, (0, 2, 1, 3)) for w in (w_gate, w_up, w_down)]
    tables = tables_of(lengths[0], rows)

    def share_cores(shares):
        return list(shares) + [place.hop(piece, swap=1) for piece in shares]

    def line_of(block):
        return jnp.concatenate([block] + up_hops(place, block))

    cuts = [cut_experts(where, weights, l) for l in range(layer_count)]
    gate_line = gates_line(place, routes, gates, expert_count)
    line = jnp.concatenate([packs[0]] + tie(up_hops(place, packs[0]), cuts[0][0], gate_line))
    first = spread_first(place, line)
    gate_rows = gate_rows_of(place, gate_line)
    cuts[0] = tie(cuts[0], line)
    shares = [cuts[0][0], place.hop(cuts[0][1], up=1), place.hop(cuts[0][2], up=3)]
    first = tie(first, shares[1], shares[2], gate_rows[0][0], gate_rows[-1][0], cuts[-1][0])
    shares.append(place.hop(tie(cuts[0][3], first[0]), up=2))
    matrices = [share_cores(tie(spread_last(place, first, axis=1, cut=cut), shares[3]))]
    shares.append(place.hop(tie(cuts[0][4], matrices[0][0]), up=2))

    base, extra = tokens.astype(jnp.float32), []
    stored = []
    for l in range(layer_count):
        more = l + 1 < layer_count
        after = [rows for pair in gate_rows for rows in pair] if l == 0 else []
        outs = attend_forward_fast(where, base, extra, tables, matrices[l], in_width, after=after)
        h, m, nf = outs[:3]
        nf, last_share = tie((nf, shares[4]))
        bank_l = share_cores(shares[:4] + [last_share])
        ups = up_hops(place, nf)
        near = spread_pieces(place, nf)
        far = jnp.concatenate(tie(ups, near[3], near[4]))
        far = spread_first(place, far)
        y_near = experts_forward_fast(where, gate_rows[l][0], near, bank_l)
        near_state = fold_start(place, y_near[:5])
        line = line_of(tie(packs[l + 1] if more else cotangent, y_near[0]))
        far = spread_last(place, tie(far, y_near[0]))
        passing = spread_first(place, tie(line, far[3], far[4]))
        y_far = experts_forward_fast(
            where, gate_rows[l][1], far, bank_l, after=(near_state[1], near_state[2])
        )
        stored.append((h, outs, y_near[5:], y_far[5:], bank_l))
        if more:
            y_far, passing = tie((y_far, passing))
            far_state = fold_start(place, y_far[:5])
            ready = tie(cuts[l + 1], far[3])
            shares = [ready[0], place.hop(ready[1], up=1), None, place.hop(ready[3], up=2)]
            far_state, one, two = tie((far_state, shares[1], shares[3]), near_state[1])
            third = place.hop(tie(ready[2], far_state[1]), up=3)
            far_ends, third = tie((fold_end(place, far_state), third))
            blocks = sum_blocks(*far_ends)
            matrices.append(share_cores(spread_last(place, tie(passing, blocks[0]), 1, cut)))
            arrived = down_hops(place, blocks)
            shares = [ready[0], one, third, two]
            shares.append(place.hop(tie(ready[4], blocks[0]), up=2))
            base, extra = m, received(fold_end(place, near_state), arrived)
        else:
            last = spread_last(place, passing)

    upstream = cotangent
    zero = jnp.zeros((rows, model), jnp.bfloat16)
    sums = [None] * layer_count
    joined = None
    for l in reversed(range(layer_count)):
        h, outs, kept_near, kept_far, bank_l = stored[l]
        m, na, q, k, v, o, lse, gains = outs[1], *outs[3:]

        spans = (spans_of(False), spans_of(True)) if l + 1 == layer_count else (None, None)

        def run_near(after=()):
            return experts_backward_fast(
                where, gate_rows[l][0], near, kept_near[1:], bank_l, spans[0], after=after
            )

        def run_far(after=()):
            return experts_backward_fast(
                where, gate_rows[l][1], far, kept_far[1:], bank_l, spans[1], after=after
            )

        if l + 1 == layer_count:
            near = far = last
            b_near = run_near(after=(y_far[0],))
            near_state_b = fold_start(place, b_near[:5])
            b_far = run_far(after=(b_near[0],))
            far_first = fold_first(place, b_far[:5])
        else:
            ups = up_hops(place, low)
            near = spread_pieces(place, low)
            far = jnp.concatenate(tie(ups, near[3], near[4]))
            far = spread_first(place, far)
            total = tie(held_total(), far[0])
            came = [place.hop(total[1], up=1), place.hop(total[3], up=3)]
            b_near = run_near()
            near_state_b = fold_start(place, b_near[:5])
            far, came = tie((far, came), b_near[0])
            far = spread_last(place, far)
            came.insert(1, place.hop(tie(total[2], far[0]), up=2))
            b_far = run_far(after=(near_state_b[1], near_state_b[2]))
            result_ends = fold_end(place, tie(result_state, far[3], far[4]))
            b_far, came, result_ends = tie((b_far, came, result_ends))
            far_first = fold_first(place, b_far[:5])
            arrived = down_hops(place, sum_blocks(*result_ends))
            far_first = tie(far_first, *arrived)
            result = total_of(stored[-1][1][1], received(result_near, arrived)).astype(jnp.bfloat16)
            joined = join_experts(where, [total[0], *came], l + 1, layer_count, joined)

        def weight_grads(i, after):
            pick = lambda kept, found: ((kept[0], found[6 + i]) if i < 2 else (found[5], found[8]))
            return weight_grads_fast(
                where, pick(kept_near, b_near), pick(kept_far, b_far), experts, after=after
            )

        near_ends = fold_end(place, near_state_b)
        grads = [weight_grads(0, (b_far[0],))]
        grads.append(weight_grads(1, (grads[0][0],)))
        far_state_b = fold_sums(tie(far_first, grads[1][0]))
        if l == 0:
            grads.append(weight_grads(2, (far_state_b[1], far_state_b[2])))
        far_ends = tie(fold_end(place, far_state_b), grads[-1][0], near_ends[1], near_ends[2])
        blocks = sum_blocks(*far_ends)
        arrived = down_hops(place, blocks)
        if l:
            grads.append(weight_grads(2, (far_ends[0],)))

        def total_grads():
            swapped = [place.hop(other, swap=1) for _, other in grads]
            return [
                jnp.stack([add_low(grads[i][0][k], swapped[i][k]) for i in range(3)])
                for k in range(4)
            ]

        if l == 0:
            total = total_grads()
            ready = tie(total, *arrived)
            came = [place.hop(ready[1], up=1), place.hop(ready[3], up=3)]
        if l + 1 == layer_count:
            result_state = fold_start(place, tie(y_far[:5], blocks[0]))
        upstream, low, *partial = attend_backward_fast(
            l == 0,
            where,
            zero,
            upstream,
            received(near_ends, arrived),
            (h, m, na, q, k, v, o, lse, gains),
            tables,
            matrices[l],
            in_width,
            after=() if l else (*total, joined[0]),
        )
        if l + 1 == layer_count:
            held_total = total_grads
            result_near = fold_end(place, near_state)
            low, result_state = tie((low, result_state), *result_near)
        if l == 0:
            partial, came = tie((partial, came), sums[-1])
            came.insert(1, place.hop(tie(total[2], upstream), up=2))
            sums[l] = scatter_matrices(place, *partial, cut, came[1])
            joined = join_experts(where, [total[0], *came], l, layer_count, joined)
        else:
            sums[l] = lax.psum_scatter(
                partial[0], AXES, scatter_dimension=0, tiled=True
            ).astype(jnp.float32)
    sums = jnp.stack(sums)
    gain_sums = sums[:, :, in_width + model :]
    starts = (0, query.shape[2], query.shape[2] + key.shape[2], in_width, in_width + model)
    return (
        result,
        upstream,
        gain_sums[:, :, 0],
        gain_sums[:, :, 1],
        *[sums[:, :, a:b] for a, b in zip(starts, starts[1:])],
        *[jnp.transpose(grads, (0, 2, 1, 3)) for grads in joined],
    )


def solution(mesh):
    rows = P(AXES, None)
    layered = P(None, AXES, None)
    expert = P(None, "fsdp", "expert", None)
    gain = P(None, AXES)
    regular = mesh.shape["fsdp"] == 8 and mesh.shape["expert"] == 4
    return jax.shard_map(
        shards_fast if regular else shards,
        mesh=mesh,
        in_specs=(rows, rows, layered, layered, rows, gain, gain)
        + (layered,) * 4
        + (expert,) * 3,
        out_specs=(rows, rows, gain, gain) + (layered,) * 4 + (expert,) * 3,
        check_vma=False,
    )
```

```python
import functools
import math

import jax
import jax.numpy as jnp
from jax import lax
from jax.experimental import pallas as pl
from jax.experimental.pallas import tpu as pltpu
from jax.sharding import PartitionSpec as P

QUERY_HEADS = 24
KEY_VALUE_HEADS = 8
HEAD_DIMENSION = 64
CORES = 2

NORM_EPS = 1e-06
MASKED = -1000000000.0
AXES = ("fsdp", "expert")


class Place:
    def __init__(self):
        self.planes = lax.axis_size("fsdp") // CORES
        self.columns = lax.axis_size("expert")
        fsdp = lax.axis_index("fsdp")
        self.plane = fsdp // CORES
        self.core = fsdp % CORES
        self.column = lax.axis_index("expert")

    def hop(self, value, up=0, flip=0, swap=0):
        pairs = []
        for plane in range(self.planes):
            for core in range(CORES):
                for column in range(self.columns):
                    source = (plane * CORES + core) * self.columns + column
                    target = ((plane + up) % self.planes * CORES + (core ^ swap)) * self.columns
                    pairs.append((source, target + (column ^ flip)))
        return lax.ppermute(value, AXES, pairs)


def spread(place, block):
    if place.columns != 4:
        return [block] + [place.hop(block, flip=m) for m in range(1, place.columns)]
    half = block.shape[1] // 2
    one = place.hop(block, flip=1)
    two = place.hop(block, flip=2)
    head = place.hop(one[:, :half], flip=2)
    tail = place.hop(two[:, half:], flip=1)
    return [block, one, two, jnp.concatenate([head, tail], axis=1)]


def gather_tokens(place, block):
    own = block[None]
    others = jnp.stack([place.hop(block, up=k) for k in range(1, place.planes)])
    near = spread(place, own)
    far = spread(place, others)
    return [jnp.concatenate([a, b], axis=0) for a, b in zip(near, far)]


def fold(place, parts):
    wide = lambda value: value.astype(jnp.float32)
    if place.columns != 4:
        total = wide(parts[0])
        for m in range(1, place.columns):
            total = total + wide(place.hop(parts[m], flip=m))
        return total
    half = parts[0].shape[1] // 2
    head = place.hop(parts[3][:, :half], flip=2)
    tail = place.hop(parts[3][:, half:], flip=1)
    one_tail = place.hop(parts[1][:, half:], flip=1)
    two_head = place.hop(parts[2][:, :half], flip=2)
    one_head = place.hop((wide(parts[1][:, :half]) + wide(head)).astype(parts[1].dtype), flip=1)
    two_tail = place.hop((wide(parts[2][:, half:]) + wide(tail)).astype(parts[2].dtype), flip=2)
    upper = wide(parts[0][:, :half]) + wide(one_head) + wide(two_head)
    lower = wide(parts[0][:, half:]) + wide(one_tail) + wide(two_tail)
    return jnp.concatenate([upper, lower], axis=1)


def scatter_sums(place, parts):
    far = fold(place, [part[1:] for part in parts]).astype(parts[0].dtype)
    arrived = [place.hop(far[k - 1], up=-k) for k in range(1, place.planes)]
    total = fold(place, [part[:1] for part in parts])[0]
    for piece in arrived:
        total = total + piece.astype(jnp.float32)
    return total


def gate_table(routes, gates, expert_count):
    names = jnp.arange(expert_count, dtype=jnp.int32)
    chosen = routes[:, None, :, :] == names[None, :, None, None]
    return jnp.sum(jnp.where(chosen, gates[:, None, :, :], 0.0), axis=3)


def spread_gates(place, table):
    axis = table.ndim - 2
    owned = table.shape[axis] // place.columns
    found = []
    for m in range(place.columns):
        start = (place.column ^ m) * owned
        piece = lax.dynamic_slice_in_dim(table, start, owned, axis=axis)
        found.append(place.hop(piece, flip=m) if m else piece)
    return found


def gather_gates(place, routes, gates, expert_count):
    table = gate_table(routes, gates, expert_count)
    line = jnp.stack([table] + [place.hop(table, up=k) for k in range(1, place.planes)])
    return spread_gates(place, line)


def gather_experts(place, weights):
    rows, experts, hidden = weights[0].shape
    share = hidden // place.planes

    def cut(plane):
        pieces = [lax.dynamic_slice_in_dim(w, plane * share, share, axis=2) for w in weights]
        return jnp.stack([p.reshape(rows, experts * share) for p in pieces])

    own = [cut(place.plane)]
    for k in range(1, place.planes):
        own.append(place.hop(cut((place.plane + k) % place.planes), up=k))
    own = jnp.stack(own)
    sibling = place.hop(own, swap=1)
    both = jnp.concatenate([own, sibling])
    shard = jnp.arange(place.planes * CORES)
    index = ((shard % CORES) ^ place.core) * place.planes
    index = index + (place.plane - shard // CORES) % place.planes
    return [
        jnp.take(both[:, i], index, axis=0).reshape(-1, experts * share)
        for i in range(len(weights))
    ]


def scatter_experts(place, grads, experts):
    features, width = grads[0].shape
    rows = features // (place.planes * CORES)
    share = width // experts
    shape = (place.planes, CORES, rows, width)
    stacked = jnp.stack([g.reshape(shape) for g in grads], axis=1)
    mine = lax.dynamic_index_in_dim(stacked, place.core, axis=2, keepdims=False)
    others = lax.dynamic_index_in_dim(stacked, 1 - place.core, axis=2, keepdims=False)
    arrived = place.hop(others.astype(jnp.bfloat16), swap=1)
    total = (mine + arrived.astype(jnp.float32)).astype(jnp.bfloat16)
    pieces = [lax.dynamic_index_in_dim(total, place.plane, axis=0, keepdims=False)]
    for k in range(1, place.planes):
        target = (place.plane + k) % place.planes
        piece = lax.dynamic_index_in_dim(total, target, axis=0, keepdims=False)
        pieces.append(place.hop(piece, up=k))
    index = (place.plane - jnp.arange(place.planes)) % place.planes
    ordered = jnp.take(jnp.stack(pieces), index, axis=0)
    ordered = ordered.reshape(place.planes, len(grads), rows, experts, share)
    ordered = jnp.transpose(ordered, (1, 2, 3, 0, 4)).reshape(len(grads), rows, experts, -1)
    return [ordered[i].astype(jnp.float32) for i in range(len(grads))]


def positions(length_row, count_of_rows):
    ends = jnp.cumsum(length_row)
    token_order = jnp.arange(count_of_rows, dtype=jnp.int32)
    passed = token_order[:, None] >= ends[None, :]
    segment = jnp.sum(passed.astype(jnp.int32), axis=1)
    before = jnp.sum(jnp.where(passed, length_row[None, :], 0), axis=1)
    return (segment, token_order - before)


def rope_tables(seq_place, head_width):
    half_width = head_width // 2
    freq_table = jnp.exp(
        jnp.arange(half_width, dtype=jnp.float32) * (-2.0 * math.log(10000.0) / head_width)
    )
    angles = seq_place.astype(jnp.float32)[:, None] * freq_table[None, :]
    return (jnp.cos(angles), jnp.sin(angles))


def apply_rotation(vector, cosine_table, sine_table):
    half_width = vector.shape[-1] // 2
    former = vector[..., :half_width]
    latter = vector[..., half_width:]
    cos_wide = cosine_table[:, None, :]
    sin_wide = sine_table[:, None, :]
    return jnp.concatenate(
        [former * cos_wide - latter * sin_wide, latter * cos_wide + former * sin_wide], axis=-1
    )


def reverse_rotation(vector, cosine_table, sine_table):
    return apply_rotation(vector, cosine_table, -sine_table)


def rms_forward(residual, norm_gain):
    inverse = lax.rsqrt(jnp.mean(residual * residual, axis=-1, keepdims=True) + NORM_EPS)
    return (inverse, (residual * inverse * norm_gain).astype(jnp.bfloat16))


def rms_backward(residual, inverse, norm_gain, upstream):
    gain_grad = jnp.sum(upstream * residual * inverse, axis=0)
    scaled = upstream * norm_gain
    inner = jnp.mean(scaled * residual, axis=-1, keepdims=True)
    return (gain_grad, inverse * scaled - residual * inverse * inverse * inverse * inner)


def score_block(rotated_query, turned_k, allowed):
    scores = jnp.einsum(
        "qhgd,khd->hgqk", rotated_query, turned_k, preferred_element_type=jnp.float32
    ) * HEAD_DIMENSION ** (-0.5)
    return jnp.where(allowed, scores, MASKED)


def attend_forward(residual, allowed, tables, gain, matrices):
    w_in, w_output = matrices
    count_of_rows = residual.shape[0]
    query_width = QUERY_HEADS * HEAD_DIMENSION
    key_width = KEY_VALUE_HEADS * HEAD_DIMENSION
    inverse, normalized_input = rms_forward(residual, gain)
    projected = jnp.dot(normalized_input, w_in, preferred_element_type=jnp.float32)
    query_unrotated = projected[:, :query_width].reshape(count_of_rows, QUERY_HEADS, -1)
    key_unrotated = projected[:, query_width : query_width + key_width]
    key_unrotated = key_unrotated.reshape(count_of_rows, KEY_VALUE_HEADS, -1)
    value_rows = projected[:, query_width + key_width :].astype(jnp.bfloat16)
    value_rows = value_rows.reshape(count_of_rows, KEY_VALUE_HEADS, -1)
    rotated_query = (
        apply_rotation(query_unrotated, *tables)
        .astype(jnp.bfloat16)
        .reshape(count_of_rows, KEY_VALUE_HEADS, QUERY_HEADS // KEY_VALUE_HEADS, HEAD_DIMENSION)
    )
    turned_k = apply_rotation(key_unrotated, *tables).astype(jnp.bfloat16)
    scores = score_block(rotated_query, turned_k, allowed)
    row_top = jnp.max(scores, axis=-1, keepdims=True)
    exp_scores = jnp.exp(scores - row_top)
    row_total = jnp.sum(exp_scores, axis=-1, keepdims=True)
    attn_probs = (exp_scores / row_total).astype(jnp.bfloat16)
    log_total = row_top + jnp.log(row_total)
    mixed_heads = jnp.einsum(
        "hgqk,khd->qhgd", attn_probs, value_rows, preferred_element_type=jnp.float32
    )
    mixed_heads = mixed_heads.astype(jnp.bfloat16).reshape(count_of_rows, query_width)
    attn_out = jnp.dot(mixed_heads, w_output, preferred_element_type=jnp.float32)
    return (
        residual + attn_out,
        (inverse, normalized_input, rotated_query, turned_k, value_rows, log_total, mixed_heads),
    )


def attend_backward(residual, allowed, tables, gain, matrices, stash, upstream):
    w_in, w_output = matrices
    inverse, normalized_input, rotated_query, turned_k, value_rows, log_total, mixed_heads = stash
    count_of_rows = residual.shape[0]
    branch_grad = upstream.astype(jnp.bfloat16)
    grad_wo = jnp.einsum("td,te->de", mixed_heads, branch_grad, preferred_element_type=jnp.float32)
    mixed_gradient = jnp.einsum(
        "te,de->td", branch_grad, w_output, preferred_element_type=jnp.float32
    )
    mixed_gradient = mixed_gradient.astype(jnp.bfloat16).reshape(
        count_of_rows, KEY_VALUE_HEADS, QUERY_HEADS // KEY_VALUE_HEADS, HEAD_DIMENSION
    )
    attn_probs = jnp.exp(score_block(rotated_query, turned_k, allowed) - log_total)
    value_rows_gradient = jnp.einsum(
        "hgqk,qhgd->khd",
        attn_probs.astype(jnp.bfloat16),
        mixed_gradient,
        preferred_element_type=jnp.float32,
    )
    value_rows_gradient = value_rows_gradient.astype(jnp.bfloat16).reshape(count_of_rows, -1)
    grad_probs = jnp.einsum(
        "qhgd,khd->hgqk", mixed_gradient, value_rows, preferred_element_type=jnp.float32
    )
    grad_scores = attn_probs * (
        grad_probs - jnp.sum(attn_probs * grad_probs, axis=-1, keepdims=True)
    )
    grad_scores = grad_scores.astype(jnp.bfloat16)
    grad_tq = jnp.einsum(
        "hgqk,khd->qhgd", grad_scores, turned_k, preferred_element_type=jnp.float32
    ) * HEAD_DIMENSION ** (-0.5)
    turned_key_gradient = jnp.einsum(
        "hgqk,qhgd->khd", grad_scores, rotated_query, preferred_element_type=jnp.float32
    ) * HEAD_DIMENSION ** (-0.5)
    grad_query = reverse_rotation(
        grad_tq.reshape(count_of_rows, QUERY_HEADS, HEAD_DIMENSION), *tables
    )
    grad_query = grad_query.astype(jnp.bfloat16).reshape(count_of_rows, -1)
    grad_key = reverse_rotation(turned_key_gradient, *tables).astype(jnp.bfloat16)
    grad_key = grad_key.reshape(count_of_rows, -1)
    grad_in = jnp.concatenate([grad_query, grad_key, value_rows_gradient], axis=1)
    grad_w_in = jnp.einsum("td,te->de", normalized_input, grad_in, preferred_element_type=jnp.float32)
    grad_normed = jnp.einsum("te,de->td", grad_in, w_in, preferred_element_type=jnp.float32)
    gain_grad, residual_grad = rms_backward(residual, inverse, gain, grad_normed)
    return (upstream + residual_grad, gain_grad, grad_w_in, grad_wo)


def widen(gate_columns, share):
    return jnp.repeat(gate_columns, share, axis=1)


def experts_forward(place, middle, gain, gate_parts, weights):
    w_gate, w_up, w_down = weights
    share = w_gate.shape[1] // gate_parts[0].shape[1]
    model_width = middle.shape[1]
    inverse, normalized_input = rms_forward(middle, gain)
    chunks = gather_tokens(place, normalized_input)
    parts, kept = [], []
    for chunk, gate_columns in zip(chunks, gate_parts):
        rows = chunk.reshape(-1, model_width)
        gate_pre = jnp.dot(rows, w_gate, preferred_element_type=jnp.float32)
        up_pre = jnp.dot(rows, w_up, preferred_element_type=jnp.float32)
        weighed = gate_pre * jax.nn.sigmoid(gate_pre) * up_pre * widen(gate_columns, share)
        weighed = weighed.astype(jnp.bfloat16)
        produced = lax.dot_general(
            weighed, w_down, (((1,), (1,)), ((), ())), preferred_element_type=jnp.float32
        )
        parts.append(produced.astype(jnp.bfloat16).reshape(chunk.shape))
        kept.append((rows, gate_pre, up_pre, weighed))
    return (middle + scatter_sums(place, parts), (inverse, kept))


def experts_backward(place, middle, gain, gate_parts, weights, stash, upstream, chunks):
    w_gate, w_up, w_down = weights
    share = w_gate.shape[1] // gate_parts[0].shape[1]
    model_width = middle.shape[1]
    inverse, kept = stash
    parts, gate_grads, up_grads, row_grads = [], [], [], []
    for chunk, gate_columns, (rows, gate_pre, up_pre, weighed) in zip(chunks, gate_parts, kept):
        grads = chunk.reshape(-1, model_width)
        hidden_grad = jnp.dot(grads, w_down, preferred_element_type=jnp.float32)
        hidden_grad = hidden_grad * widen(gate_columns, share)
        gate_sig = jax.nn.sigmoid(gate_pre)
        gate_grad = hidden_grad * up_pre * gate_sig * (1.0 + gate_pre * (1.0 - gate_sig))
        gate_grad = gate_grad.astype(jnp.bfloat16)
        up_grad = (hidden_grad * gate_pre * gate_sig).astype(jnp.bfloat16)
        back = (((1,), (1,)), ((), ()))
        produced = lax.dot_general(gate_grad, w_gate, back, preferred_element_type=jnp.float32)
        produced = produced + lax.dot_general(
            up_grad, w_up, back, preferred_element_type=jnp.float32
        )
        parts.append(produced.astype(jnp.bfloat16).reshape(chunk.shape))
        gate_grads.append(gate_grad)
        up_grads.append(up_grad)
        row_grads.append(grads)
    normed_grad = scatter_sums(place, parts)
    rows = jnp.concatenate([entry[0] for entry in kept])
    weighed = jnp.concatenate([entry[3] for entry in kept])
    outer = (((0,), (0,)), ((), ()))
    weight_grads = [
        lax.dot_general(a, b, outer, preferred_element_type=jnp.float32)
        for a, b in (
            (rows, jnp.concatenate(gate_grads)),
            (rows, jnp.concatenate(up_grads)),
            (jnp.concatenate(row_grads), weighed),
        )
    ]
    gain_grad, middle_grad = rms_backward(middle, inverse, gain, normed_grad)
    return (upstream + middle_grad, gain_grad, weight_grads)


def shards(
    tokens,
    lengths,
    routes,
    gates,
    cotangent,
    norm_attn,
    norm_ffn,
    query,
    key,
    value,
    output,
    w_gate,
    w_up,
    w_down,
):
    place = Place()
    token_rows = tokens.shape[0]
    layer_count, _, experts, _ = w_gate.shape
    expert_count = experts * place.columns
    in_width = query.shape[2] + key.shape[2] + value.shape[2]
    segment, seq_place = positions(lengths[0], token_rows)
    tables = rope_tables(seq_place, HEAD_DIMENSION)
    token_order = jnp.arange(token_rows, dtype=jnp.int32)
    allowed = (segment[:, None] == segment[None, :]) & (
        token_order[:, None] >= token_order[None, :]
    )
    gains = jnp.concatenate([norm_attn, norm_ffn]).T
    packs = []
    for l in range(layer_count):
        pack = [query[l], key[l], value[l], output[l]]
        if l == 0:
            pack.append(jnp.pad(gains, ((0, 0), (0, 128 - gains.shape[1]))))
        packs.append(jnp.concatenate(pack, axis=1))
    full = lax.all_gather(packs[0], AXES, axis=0, tiled=True)
    gains = full[:, in_width + output.shape[2] :].T[: 2 * layer_count].astype(jnp.float32)
    gate_rows = gather_gates(place, routes, gates, expert_count)
    gate_parts = [
        [
            jnp.transpose(piece[:, l], (0, 2, 1)).reshape(-1, experts)
            for piece in gate_rows
        ]
        for l in range(layer_count)
    ]
    expert_weights = gather_experts(place, [w_gate[0], w_up[0], w_down[0]])
    last_grads = None

    residual = tokens.astype(jnp.float32)
    matrices, weights, stored = [], [], []
    for l in range(layer_count):
        matrices.append((full[:, :in_width], full[:, in_width : in_width + output.shape[2]]))
        weights.append(expert_weights)
        layer_input = residual
        middle, attn_stash = attend_forward(layer_input, allowed, tables, gains[l], matrices[l])
        if l + 1 < layer_count:
            held, pack, *shares = lax.optimization_barrier(
                (middle, packs[l + 1], w_gate[l + 1], w_up[l + 1], w_down[l + 1])
            )
            middle = held
            full = lax.all_gather(pack, AXES, axis=0, tiled=True)
            expert_weights = gather_experts(place, shares)
        residual, moe_stash = experts_forward(
            place, middle, gains[layer_count + l], gate_parts[l], weights[l]
        )
        if l + 2 == layer_count or layer_count == 1:
            held, last = lax.optimization_barrier((residual, cotangent))
            residual = held
            last_grads = gather_tokens(place, last)
        stored.append((layer_input, middle, attn_stash, moe_stash))
    result = residual.astype(jnp.bfloat16)

    upstream = cotangent.astype(jnp.float32)
    in_grads, out_grads = [None] * layer_count, [None] * layer_count
    gain_grads = [None] * (2 * layer_count)
    expert_grads = [None] * layer_count
    for l in reversed(range(layer_count)):
        layer_input, middle, attn_stash, moe_stash = stored[l]
        chunks = last_grads
        if l + 1 < layer_count:
            chunks = gather_tokens(place, upstream.astype(jnp.bfloat16))
        upstream, gain_grads[layer_count + l], weight_grads = experts_backward(
            place,
            middle,
            gains[layer_count + l],
            gate_parts[l],
            weights[l],
            moe_stash,
            upstream,
            chunks,
        )
        expert_grads[l] = scatter_experts(place, weight_grads, experts)
        upstream, gain_grads[l], grad_w_in, grad_wo = attend_backward(
            layer_input, allowed, tables, gains[l], matrices[l], attn_stash, upstream
        )
        summed = lax.psum_scatter(
            jnp.concatenate([grad_w_in, grad_wo], axis=1).astype(jnp.bfloat16),
            AXES,
            scatter_dimension=0,
            tiled=True,
        ).astype(jnp.float32)
        in_grads[l], out_grads[l] = summed[:, :in_width], summed[:, in_width:]
    gain_sums = lax.psum_scatter(jnp.stack(gain_grads), AXES, scatter_dimension=1, tiled=True)
    in_grads = jnp.stack(in_grads)
    key_start, value_start = query.shape[2], query.shape[2] + key.shape[2]
    return (
        result,
        upstream,
        gain_sums[:layer_count],
        gain_sums[layer_count:],
        in_grads[:, :, :key_start],
        in_grads[:, :, key_start:value_start],
        in_grads[:, :, value_start:],
        jnp.stack(out_grads),
        jnp.stack([entry[0] for entry in expert_grads]),
        jnp.stack([entry[1] for entry in expert_grads]),
        jnp.stack([entry[2] for entry in expert_grads]),
    )


HEADS_PER_TURN = 6
LANES = 128
EXTRA = 128
HALF = 64
TILE = 256
MIB = 1 << 20
COST_PART = 16


def cost(flops):
    return pl.CostEstimate(flops=flops // COST_PART, bytes_accessed=0, transcendentals=0)


def any_spec():
    return pl.BlockSpec(memory_space=pl.ANY)


def whole_spec():
    return pl.BlockSpec(memory_space=pltpu.VMEM)


def scalar_spec():
    return pl.BlockSpec(memory_space=pltpu.SMEM)


def shape_of(*dims, dtype=jnp.bfloat16):
    return jax.ShapeDtypeStruct(dims, dtype)


class Copies:
    def __init__(self, semaphores, first=0):
        self.semaphores = semaphores
        self.used = first
        self.open = []

    def start(self, source, target):
        copy = pltpu.make_async_copy(source, target, self.semaphores.at[self.used])
        self.used += 1
        copy.start()
        self.open.append(copy)

    def wait(self):
        for copy in self.open:
            copy.wait()
        self.open = []


def shard_row(where, swapped, m, k, rows):
    plane = lax.rem(where[0] - k + 4, 4)
    fsdp = plane * CORES + (where[1] ^ swapped)
    return pl.multiple_of((fsdp * 4 + (where[2] ^ m)) * rows, 16)


MATRIX_PIECES = 10
MATRIX_COPIES = 40


def load_matrices(copies, where, pieces, full):
    rows, cut = pieces[0].shape[0] // 4, pieces[3].shape[1]
    spans = ((0, 0, full.shape[1]),) * 3 + ((3, 0, cut), (3, cut, full.shape[1] - cut))
    for swapped in range(CORES):
        for index, (m, low, width) in enumerate(spans):
            piece = pieces[swapped * 5 + index]
            for k in range(4):
                row = shard_row(where, swapped, m or index, k, rows)
                copies.start(
                    piece.at[pl.ds(k * rows, rows), :], full.at[pl.ds(row, rows), pl.ds(low, width)]
                )


def half_swap(x):
    lane = lax.broadcasted_iota(jnp.int32, x.shape, 1)
    return jnp.where(lane % 64 < 32, pltpu.roll(x, 96, 1), pltpu.roll(x, 32, 1))


def both_sides(pair, side):
    lane = lax.broadcasted_iota(jnp.int32, pair.shape, 1)
    wide = pair.astype(jnp.float32)
    here = jnp.where(lane // 64 == side, wide, 0.0)
    there = pltpu.roll(here, 64, 1)
    here, there = here.astype(jnp.bfloat16), there.astype(jnp.bfloat16)
    return (here, there) if side == 0 else (there, here)


def merge_sides(even, odd, side):
    lane = lax.broadcasted_iota(jnp.int32, even.shape, 1)
    if side == 0:
        return jnp.where(lane < 64, even + pltpu.roll(odd, 64, 1), 0.0)
    return jnp.where(lane < 64, 0.0, odd + pltpu.roll(even, 64, 1))


def contract(a, b, dims):
    return lax.dot_general(a, b, (dims, ((), ())), preferred_element_type=jnp.float32)


PLAIN = ((1,), (0,))
ACROSS = ((1,), (1,))
OUTER = ((0,), (0,))


def read_sum(base, extra):
    total = base[...].astype(jnp.float32)
    for term in extra:
        total = total + term[pl.ds(0, total.shape[0]), :].astype(jnp.float32)
    return total


def attend_forward_kernel(terms, width, where, base, *refs):
    refs = list(refs)
    extra = [refs.pop(0) for _ in range(terms)]
    cosine, sine, allowed = refs[:3]
    pieces = refs[3 : 3 + MATRIX_PIECES]
    refs = refs[3 + MATRIX_PIECES :]
    h_out, m_out, nf_out, na_out, q_out, k_out, v_out, o_out, lse_out, gain_out = refs[:10]
    full, proj, mixed, semaphores = refs[10:]
    copies = Copies(semaphores)
    load_matrices(copies, where, pieces, full)
    h = read_sum(base, extra)
    h_out[...] = h
    inverse = lax.rsqrt(jnp.mean(h * h, axis=1, keepdims=True) + NORM_EPS)
    model = h.shape[1]
    in_width = width
    key_start = model
    value_start = model + (in_width - model) // 2
    copies.wait()
    gains = full[:, pl.ds(in_width + model, EXTRA)].astype(jnp.float32).T
    gain_out[...] = gains[:8]
    na_out[...] = (h * inverse * gains[0:1]).astype(jnp.bfloat16)
    step = 512

    @pl.loop(0, in_width // step)
    def _(i):
        columns = pl.ds(pl.multiple_of(i * step, step), step)
        proj[:, columns] = contract(na_out[...], full[:, columns], PLAIN)

    cos, sin = cosine[...], sine[...]

    @pl.loop(0, key_start // LANES)
    def _(i):
        columns = pl.ds(pl.multiple_of(i * LANES, LANES), LANES)
        x = proj[:, columns]
        q_out[:, columns] = (x * cos + half_swap(x) * sin).astype(jnp.bfloat16)

    @pl.loop(0, (value_start - key_start) // LANES)
    def _(i):
        start = pl.multiple_of(i * LANES, LANES)
        x = proj[:, pl.ds(key_start + start, LANES)]
        k_out[:, pl.ds(start, LANES)] = (x * cos + half_swap(x) * sin).astype(jnp.bfloat16)

    v_out[...] = proj[:, value_start:in_width].astype(jnp.bfloat16)
    lse_out[...] = jnp.zeros_like(lse_out)
    open_keys = allowed[...] > 0.5
    lane = lax.broadcasted_iota(jnp.int32, open_keys.shape, 1)

    @pl.loop(0, KEY_VALUE_HEADS // 2)
    def _(turn):
        pair = pl.ds(pl.multiple_of(turn * LANES, LANES), LANES)
        keys = [both_sides(k_out[:, pair], side) for side in range(2)]
        values = [both_sides(v_out[:, pair], side) for side in range(2)]
        lse = lse_out[...]
        for group in range(HEADS_PER_TURN // 2):
            columns = pl.ds(
                pl.multiple_of(turn * (HEADS_PER_TURN * 64) + group * LANES, LANES), LANES
            )
            total = jnp.zeros((h.shape[0], LANES), jnp.float32)
            for side in range(2):
                head = group * 2 + side
                scores = contract(q_out[:, columns], keys[head // 3][side], ACROSS)
                scores = jnp.where(open_keys, scores * HEAD_DIMENSION ** (-0.5), MASKED)
                top = jnp.max(scores, axis=1, keepdims=True)
                weights = jnp.exp(scores - top)
                row_total = jnp.sum(weights, axis=1, keepdims=True)
                probs = (weights / row_total).astype(jnp.bfloat16)
                lse = jnp.where(lane == turn * HEADS_PER_TURN + head, top + jnp.log(row_total), lse)
                total = total + contract(probs, values[head // 3][side], PLAIN)
            o_out[:, columns] = total.astype(jnp.bfloat16)
        lse_out[...] = lse

    @pl.loop(0, model // step)
    def _(i):
        columns = pl.ds(pl.multiple_of(i * step, step), step)
        weights = full[:, pl.ds(pl.multiple_of(in_width + i * step, step), step)]
        mixed[:, columns] = contract(o_out[...], weights, PLAIN)

    m = h_out[...] + mixed[...]
    m_out[...] = m
    inverse = lax.rsqrt(jnp.mean(m * m, axis=1, keepdims=True) + NORM_EPS)
    nf_out[...] = (m * inverse * gain_out[1:2]).astype(jnp.bfloat16)


def attend_forward_fast(where, base, extra, tables, pieces, in_width, after=()):
    rows, model = base.shape
    bf, f32 = jnp.bfloat16, jnp.float32
    key_width = (in_width - model) // 2
    total = in_width + model + EXTRA
    shapes = [
        shape_of(rows, model, dtype=f32),
        shape_of(rows, model, dtype=f32),
        shape_of(rows, model),
        shape_of(rows, model),
        shape_of(rows, model),
        shape_of(rows, key_width),
        shape_of(rows, key_width),
        shape_of(rows, model),
        shape_of(rows, LANES, dtype=f32),
        shape_of(8, model, dtype=f32),
    ]

    def body(*refs):
        used = 2 + len(extra) + 3 + MATRIX_PIECES
        attend_forward_kernel(len(extra), in_width, *refs[:used], *refs[used + len(after) :])

    return pl.pallas_call(
        body,
        name="attend_forward",
        out_shape=shapes,
        in_specs=[scalar_spec()]
        + [whole_spec()] * (4 + len(extra))
        + [any_spec()] * (MATRIX_PIECES + len(after)),
        out_specs=[whole_spec()] * len(shapes),
        scratch_shapes=[
            pltpu.VMEM((model, total), bf),
            pltpu.VMEM((rows, in_width), f32),
            pltpu.VMEM((rows, model), f32),
            pltpu.SemaphoreType.DMA((MATRIX_COPIES,)),
        ],
        compiler_params=pltpu.CompilerParams(vmem_limit_bytes=44 * MIB),
        cost_estimate=cost(2 * rows * model * total),
    )(where, base, *extra, *tables, *pieces, *after)


def attend_backward_kernel(groups, terms, width, where, base, upstream, *refs):
    refs = list(refs)
    extra = [refs.pop(0) for _ in range(terms)]
    h_in, m_in, na, q, k, v, o, lse_in, gains, cosine, sine, allowed = refs[:12]
    pieces = refs[12 : 12 + MATRIX_PIECES]
    outs, refs = refs[12 + MATRIX_PIECES : -6], refs[-6:]
    gh_out, gh_low = outs[:2]
    full, sums, mixed, grad_in, turned, semaphores = refs
    rows, model = h_in.shape
    in_width = width
    key_start = model
    value_start = model + (in_width - model) // 2
    shard = full.shape[0] // 32
    copies = Copies(semaphores)
    load_matrices(copies, where, pieces, full)
    gnf = read_sum(base, extra)
    m = m_in[...]
    inverse = lax.rsqrt(jnp.mean(m * m, axis=1, keepdims=True) + NORM_EPS)
    gain_ffn = jnp.sum(gnf * m * inverse, axis=0, keepdims=True)
    scaled = gnf * gains[1:2]
    inner = jnp.mean(scaled * m, axis=1, keepdims=True)
    gm = upstream[...].astype(jnp.float32)
    gm = gm + inverse * scaled - m * (inverse * inverse * inverse) * inner
    gh_out[...] = gm
    gh_low[...] = gm.astype(jnp.bfloat16)
    copies.wait()
    step = 512

    @pl.loop(0, model // step)
    def _(i):
        row = pl.ds(pl.multiple_of(i * step, step), step)
        mixed[:, row] = contract(gh_low[...], full[row, in_width : in_width + model], ACROSS).astype(
            jnp.bfloat16
        )

    open_keys = allowed[...] > 0.5
    lane = lax.broadcasted_iota(jnp.int32, open_keys.shape, 1)
    cos, sin = cosine[...], sine[...]
    scale = HEAD_DIMENSION ** (-0.5)

    @pl.loop(0, KEY_VALUE_HEADS // 2)
    def _(turn):
        start = pl.multiple_of(turn * LANES, LANES)
        pair = pl.ds(start, LANES)
        keys = [both_sides(k[:, pair], side) for side in range(2)]
        values = [both_sides(v[:, pair], side) for side in range(2)]
        zero = jnp.zeros((rows, LANES), jnp.float32)
        grad_k = [[zero, zero], [zero, zero]]
        grad_v = [[zero, zero], [zero, zero]]
        lse = lse_in[...]
        for group in range(HEADS_PER_TURN // 2):
            columns = pl.ds(
                pl.multiple_of(turn * (HEADS_PER_TURN * 64) + group * LANES, LANES), LANES
            )
            grad_q = zero
            for side in range(2):
                head = group * 2 + side
                kv = head // 3
                top = jnp.sum(
                    jnp.where(lane == turn * HEADS_PER_TURN + head, lse, 0.0), axis=1, keepdims=True
                )
                scores = contract(q[:, columns], keys[kv][side], ACROSS) * scale
                probs = jnp.exp(jnp.where(open_keys, scores, MASKED) - top)
                go = mixed[:, columns]
                grad_v[kv][side] = grad_v[kv][side] + contract(
                    probs.astype(jnp.bfloat16), go, OUTER
                )
                grad_p = contract(go, values[kv][side], ACROSS)
                grad_s = probs * (grad_p - jnp.sum(probs * grad_p, axis=1, keepdims=True))
                grad_s = grad_s.astype(jnp.bfloat16)
                grad_q = grad_q + contract(grad_s, keys[kv][side], PLAIN)
                grad_k[kv][side] = grad_k[kv][side] + contract(grad_s, q[:, columns], OUTER)
            grad_q = grad_q * scale
            grad_in[:, columns] = (grad_q * cos - half_swap(grad_q) * sin).astype(jnp.bfloat16)
        key_grad = merge_sides(*grad_k[0], 0) + merge_sides(*grad_k[1], 1)
        key_grad = key_grad * scale
        key_grad = key_grad * cos - half_swap(key_grad) * sin
        value_grad = merge_sides(*grad_v[0], 0) + merge_sides(*grad_v[1], 1)
        grad_in[:, pl.ds(key_start + start, LANES)] = key_grad.astype(jnp.bfloat16)
        grad_in[:, pl.ds(value_start + start, LANES)] = value_grad.astype(jnp.bfloat16)

    turned[...] = jnp.zeros_like(turned)

    @pl.loop(0, in_width // step)
    def _(i):
        columns = pl.ds(pl.multiple_of(i * step, step), step)
        turned[...] += contract(grad_in[:, columns], full[:, columns], ACROSS)

    grad_na = turned[...]
    h = h_in[...]
    inverse = lax.rsqrt(jnp.mean(h * h, axis=1, keepdims=True) + NORM_EPS)
    gain_attn = jnp.sum(grad_na * h * inverse, axis=0, keepdims=True)
    scaled = grad_na * gains[0:1]
    inner = jnp.mean(scaled * h, axis=1, keepdims=True)
    band = 384

    @pl.loop(0, model // band)
    def _(i):
        start = pl.multiple_of(i * band, band)
        row = pl.ds(start, band)
        sums[row, in_width : in_width + model] = contract(o[:, row], gh_low[...], OUTER).astype(
            jnp.bfloat16
        )
        sums[row, :in_width] = contract(na[:, row], grad_in[...], OUTER).astype(jnp.bfloat16)

    both = jnp.concatenate([gain_attn, gain_ffn, jnp.zeros((EXTRA - 2, model), jnp.float32)], axis=0)
    sums[:, pl.ds(in_width + model, EXTRA)] = both.T.astype(jnp.bfloat16)
    at = 2
    for swapped in (1, 0):
        for first, count in groups:
            for m_index in range(4):
                for n in range(count):
                    row = shard_row(where, swapped, m_index, first + n, shard)
                    copies.start(
                        sums.at[pl.ds(row, shard), :],
                        outs[at].at[pl.ds((m_index * count + n) * shard, shard), :],
                    )
            at += 1
    gh = gh_out[...] + inverse * scaled - h * (inverse * inverse * inverse) * inner
    gh_out[...] = gh
    gh_low[...] = gh.astype(jnp.bfloat16)
    copies.wait()


def attend_backward_fast(
    groups, where, base, upstream, extra, stash, tables, pieces, in_width, after=()
):
    rows, model = upstream.shape
    bf, f32 = jnp.bfloat16, jnp.float32
    total = in_width + model + EXTRA
    shapes = [
        shape_of(rows, model, dtype=f32),
        shape_of(rows, model),
    ]
    shapes += [shape_of(model // 8 * count, total) for _, count in groups] * CORES

    def body(*refs):
        used = 3 + len(extra) + 12 + MATRIX_PIECES
        attend_backward_kernel(
            groups, len(extra), in_width, *refs[:used], *refs[used + len(after) :]
        )

    return pl.pallas_call(
        body,
        name="attend_backward",
        out_shape=shapes,
        in_specs=[scalar_spec()]
        + [whole_spec()] * (2 + len(extra) + 12)
        + [any_spec()] * (MATRIX_PIECES + len(after)),
        out_specs=[whole_spec()] * 2 + [any_spec()] * (len(shapes) - 2),
        scratch_shapes=[
            pltpu.VMEM((model, total), bf),
            pltpu.VMEM((model, total), bf),
            pltpu.VMEM((rows, model), bf),
            pltpu.VMEM((rows, in_width), bf),
            pltpu.VMEM((rows, model), f32),
            pltpu.SemaphoreType.DMA((MATRIX_COPIES + 32,)),
        ],
        compiler_params=pltpu.CompilerParams(vmem_limit_bytes=56 * MIB),
        cost_estimate=cost(4 * rows * model * total),
    )(where, base, upstream, *extra, *stash, *tables, *pieces, *after)


SHARES = ((0, 0, 3), (1, 0, 3), (2, 0, 3), (3, 0, 3))
WEIGHT_PIECES = CORES * len(SHARES)


def load_experts(copies, where, pieces, targets):
    at = 0
    for swapped in range(CORES):
        for k, first, count in SHARES:
            piece = pieces[at]
            at += 1
            _, experts, rows, share = piece.shape
            fsdp = lax.rem(where[0] - k + 4, 4) * CORES + (where[1] ^ swapped)
            row = pl.ds(pl.multiple_of(fsdp * rows, 16), rows)
            for i, target in enumerate(targets[first : first + count]):
                for e in range(experts):
                    copies.start(piece.at[i, e], target.at[row, pl.ds(e * share, share)])


def widen_tile(columns, share, width):
    lane = lax.broadcasted_iota(jnp.int32, (columns.shape[0], width), 1)
    wide = jnp.broadcast_to(columns[:, 0:1], lane.shape)
    for e in range(1, width // share):
        wide = jnp.where(lane >= e * share, columns[:, e : e + 1], wide)
    return wide


def start_rows(copies, pieces, rows_ref):
    at = 0
    for piece in pieces:
        rows = piece.shape[0]
        copies.start(piece, rows_ref.at[pl.ds(at, rows), :])
        at += rows


def part_rows(n):
    return [n, n // 2, n // 2, n, n]


def start_parts(copies, y, parts):
    n = parts[0].shape[0]
    half = n // 2

    def start(first, count, part, at=0):
        copies.start(y.at[pl.ds(first, count), :], part.at[pl.ds(at, count), :])

    own, one_head, two_tail, to_one, to_two = parts
    start(0, n, own)
    start(n, half, one_head)
    start(2 * n + half, half, two_tail)
    start(n + half, half, to_one)
    start(3 * n + half, half, to_one, half)
    start(2 * n, half, to_two)
    start(3 * n, half, to_two, half)


def experts_forward_kernel(where, gates, *refs):
    pieces, weights, refs = refs[:5], refs[5 : 5 + WEIGHT_PIECES], refs[5 + WEIGHT_PIECES :]
    parts, x_out, g_out, u_out = refs[:5], *refs[5:8]
    x, y, g, u, w_gate, w_up, w_down, semaphores = refs[8:]
    copies = Copies(semaphores)
    start_rows(copies, pieces, x)
    load_experts(copies, where, weights, (w_gate, w_up, w_down))
    share = weights[0].shape[3]
    width = w_gate.shape[1]
    copies.wait()
    copies.start(x, x_out)

    @pl.loop(0, x.shape[0] // TILE)
    def _(i):
        row = pl.ds(pl.multiple_of(i * TILE, TILE), TILE)
        gate_pre = contract(x[row, :], w_gate[...], PLAIN)
        up_pre = contract(x[row, :], w_up[...], PLAIN)
        g[row, :] = gate_pre
        u[row, :] = up_pre
        wide = widen_tile(gates[row, :], share, width)
        weighed = (gate_pre * jax.nn.sigmoid(gate_pre) * up_pre * wide).astype(jnp.bfloat16)
        y[row, :] = contract(weighed, w_down[...], ACROSS).astype(jnp.bfloat16)

    start_parts(copies, y, parts)
    copies.start(g, g_out)
    copies.start(u, u_out)
    copies.wait()


def experts_forward_fast(where, gates, pieces, weights, after=()):
    n, model = pieces[0].shape
    _, experts, _, share = weights[0].shape
    rows, width = 4 * n, experts * share
    bf, f32 = jnp.bfloat16, jnp.float32
    shapes = [shape_of(r, model) for r in part_rows(n)]
    shapes += [shape_of(rows, model)] + [shape_of(rows, width, dtype=f32)] * 2

    def body(*refs):
        used = 7 + WEIGHT_PIECES
        experts_forward_kernel(*refs[:used], *refs[used + len(after) :])

    return pl.pallas_call(
        body,
        name="experts_forward",
        out_shape=shapes,
        in_specs=[scalar_spec(), whole_spec()] + [any_spec()] * (5 + WEIGHT_PIECES + len(after)),
        out_specs=[any_spec()] * len(shapes),
        scratch_shapes=[
            pltpu.VMEM((rows, model), bf),
            pltpu.VMEM((rows, model), bf),
            pltpu.VMEM((rows, width), f32),
            pltpu.VMEM((rows, width), f32),
        ]
        + [pltpu.VMEM((model, width), bf)] * 3
        + [pltpu.SemaphoreType.DMA((5 + 24 * experts + 20,))],
        compiler_params=pltpu.CompilerParams(vmem_limit_bytes=48 * MIB),
        cost_estimate=cost(6 * rows * model * width),
    )(where, gates, *pieces, *weights, *after)


def experts_backward_kernel(where, gates, *refs):
    pieces, g_in, u_in = refs[:5], refs[5], refs[6]
    weights, refs = refs[7 : 7 + WEIGHT_PIECES], refs[7 + WEIGHT_PIECES :]
    parts, r_out, gg_out, gu_out, p_out = refs[:5], *refs[5:9]
    x, y, g, u, gg, gu, p, w_gate, w_up, w_down, semaphores = refs[9:]
    copies = Copies(semaphores)
    start_rows(copies, pieces, x)
    load_experts(copies, where, weights, (w_gate, w_up, w_down))
    copies.start(g_in, g)
    copies.start(u_in, u)
    share = weights[0].shape[3]
    width = w_gate.shape[1]
    copies.wait()
    copies.start(x, r_out)

    @pl.loop(0, x.shape[0] // TILE)
    def _(i):
        row = pl.ds(pl.multiple_of(i * TILE, TILE), TILE)
        wide = widen_tile(gates[row, :], share, width)
        hidden_grad = contract(x[row, :], w_down[...], PLAIN) * wide
        gate_pre, up_pre = g[row, :], u[row, :]
        sig = jax.nn.sigmoid(gate_pre)
        active = gate_pre * sig
        p[row, :] = (active * up_pre * wide).astype(jnp.bfloat16)
        gate_grad = hidden_grad * up_pre * sig * (1.0 + gate_pre * (1.0 - sig))
        gg[row, :] = gate_grad.astype(jnp.bfloat16)
        gu[row, :] = (hidden_grad * active).astype(jnp.bfloat16)
        back = contract(gg[row, :], w_gate[...], ACROSS)
        back = back + contract(gu[row, :], w_up[...], ACROSS)
        y[row, :] = back.astype(jnp.bfloat16)

    start_parts(copies, y, parts)
    copies.start(gg, gg_out)
    copies.start(gu, gu_out)
    copies.start(p, p_out)
    copies.wait()


def experts_backward_fast(where, gates, pieces, stash, weights, after=()):
    n, model = gates.shape[0] // 4, pieces[0].shape[1]
    _, experts, _, share = weights[0].shape
    rows, width = 4 * n, experts * share
    bf, f32 = jnp.bfloat16, jnp.float32
    shapes = [shape_of(r, model) for r in part_rows(n)]
    shapes += [shape_of(rows, model)] + [shape_of(rows, width)] * 3

    def body(*refs):
        used = 9 + WEIGHT_PIECES
        experts_backward_kernel(*refs[:used], *refs[used + len(after) :])

    return pl.pallas_call(
        body,
        name="experts_backward",
        out_shape=shapes,
        in_specs=[scalar_spec(), whole_spec()] + [any_spec()] * (7 + WEIGHT_PIECES + len(after)),
        out_specs=[any_spec()] * len(shapes),
        scratch_shapes=[
            pltpu.VMEM((rows, model), bf),
            pltpu.VMEM((rows, model), bf),
            pltpu.VMEM((rows, width), f32),
            pltpu.VMEM((rows, width), f32),
            pltpu.VMEM((rows, width), bf),
            pltpu.VMEM((rows, width), bf),
            pltpu.VMEM((rows, width), bf),
        ]
        + [pltpu.VMEM((model, width), bf)] * 3
        + [pltpu.SemaphoreType.DMA((5 + 24 * experts + 20,))],
        compiler_params=pltpu.CompilerParams(vmem_limit_bytes=52 * MIB),
        cost_estimate=cost(6 * rows * model * width),
    )(where, gates, *pieces, *stash, *weights, *after)


def weight_grads_kernel(experts, where, *refs):
    sources, mine, other = refs[:4], refs[4], refs[5]
    x, g, out, semaphores = refs[6:]
    copies = Copies(semaphores)
    for target, near, far in zip((x, g), sources[:2], sources[2:]):
        start_rows(copies, (near, far), target)
    copies.wait()
    band = x.shape[1] // 4
    rows = band // CORES
    share = g.shape[1] // experts

    @pl.loop(0, 4)
    def _(z):
        columns = pl.ds(pl.multiple_of(z * band, band), band)
        k = lax.rem(z - where[0] + 4, 4)
        grads = contract(x[:, columns], g[...], OUTER).astype(jnp.bfloat16)
        for core in range(CORES):
            for e in range(experts):
                out[core, k, e] = grads[
                    core * rows : (core + 1) * rows, e * share : (e + 1) * share
                ]

    copies.start(out.at[1 - where[1]], other)
    copies.start(out.at[where[1]], mine)
    copies.wait()


def weight_grads_fast(where, near, far, experts, after=()):
    model, width = near[0].shape[1], near[1].shape[1]
    count = near[0].shape[0] + far[0].shape[0]
    rows, share = model // 8, width // experts
    bf = jnp.bfloat16

    def body(*refs):
        weight_grads_kernel(experts, *refs[:5], *refs[5 + len(after) :])

    return pl.pallas_call(
        body,
        name="weight_grads",
        out_shape=[shape_of(4, experts, rows, share)] * 2,
        in_specs=[scalar_spec()] + [any_spec()] * (4 + len(after)),
        out_specs=[any_spec()] * 2,
        scratch_shapes=[
            pltpu.VMEM((count, model), bf),
            pltpu.VMEM((count, width), bf),
            pltpu.VMEM((CORES, 4, experts, rows, share), bf),
            pltpu.SemaphoreType.DMA((6,)),
        ],
        compiler_params=pltpu.CompilerParams(vmem_limit_bytes=40 * MIB),
        cost_estimate=cost(2 * count * model * width),
    )(where, *near, *far, *after)


def cut_kernel(where, w_gate, w_up, w_down, *outs):
    share = outs[0].shape[3]
    matrices = (w_gate, w_up, w_down)
    for (k, first, count), out in zip(SHARES, outs):
        columns = pl.ds(pl.multiple_of(lax.rem(where[0] + k, 4) * share, share), share)
        for i in range(count):
            out[i, 0] = matrices[first + i][0, 0, :, columns]


def cut_experts(where, weights, layer):
    _, experts, rows, hidden = weights[0].shape
    share = hidden // 4
    return pl.pallas_call(
        cut_kernel,
        name="cut_experts",
        grid=(experts,),
        out_shape=[shape_of(count, experts, rows, share) for _, _, count in SHARES],
        in_specs=[scalar_spec()]
        + [pl.BlockSpec((1, 1, rows, hidden), lambda e: (layer, e, 0, 0))] * 3,
        out_specs=[
            pl.BlockSpec((count, 1, rows, share), lambda e: (0, e, 0, 0)) for _, _, count in SHARES
        ],
    )(where, *weights)


def merge_grads_kernel(*refs):
    mine, arrived, outs = refs[:3], refs[3:6], refs[6:]
    for i in range(3):
        for k, out in enumerate(outs):
            total = mine[i][k, 0].astype(jnp.float32) + arrived[i][k, 0].astype(jnp.float32)
            out[i, 0] = total.astype(jnp.bfloat16)


def merge_grads(mine, arrived):
    planes, experts, rows, share = mine[0].shape
    return pl.pallas_call(
        merge_grads_kernel,
        name="merge_grads",
        grid=(experts,),
        out_shape=[shape_of(3, experts, rows, share)] * planes,
        in_specs=[pl.BlockSpec((planes, 1, rows, share), lambda e: (0, e, 0, 0))] * 6,
        out_specs=[pl.BlockSpec((3, 1, rows, share), lambda e: (0, e, 0, 0))] * planes,
    )(*mine, *arrived)


def join_kernel(layer, where, *refs):
    pieces, outs = refs[:4], refs[-3:]
    i = pl.program_id(0)
    share = pieces[0].shape[3]
    for index, out in enumerate(outs):

        @pl.when(i == index)
        def _():
            for k, piece in enumerate(pieces):
                columns = pl.ds(pl.multiple_of(lax.rem(where[0] - k + 4, 4) * share, share), share)
                out[0, :, :, columns] = piece[0].astype(jnp.float32)


def join_experts(where, pieces, layer, layers, earlier=None):
    mats, experts, rows, share = pieces[0].shape
    shape = shape_of(layers, experts, rows, 4 * share, dtype=jnp.float32)
    given = [] if earlier is None else list(earlier)

    return pl.pallas_call(
        functools.partial(join_kernel, layer),
        name="join_experts",
        grid=(mats,),
        out_shape=[shape] * mats,
        in_specs=[scalar_spec()]
        + [pl.BlockSpec((1, experts, rows, share), lambda i: (i, 0, 0, 0))] * 4
        + [any_spec()] * len(given),
        out_specs=[pl.BlockSpec((1, experts, rows, 4 * share), lambda i: (layer, 0, 0, 0))] * mats,
        input_output_aliases={5 + j: j for j in range(len(given))},
        compiler_params=pltpu.CompilerParams(vmem_limit_bytes=40 * MIB),
    )(where, *pieces, *given)


def tie(value, *events):
    flat, tree = jax.tree.flatten(value)
    held = lax.optimization_barrier((*flat, *events))
    return jax.tree.unflatten(tree, held[: len(flat)])


def spread_first(place, block):
    return [block, place.hop(block, flip=1), place.hop(block, flip=2)]


def spread_last(place, first, axis=0, cut=None):
    block, one, two = first
    cut = cut or block.shape[axis] // 2
    head = place.hop(lax.slice_in_dim(one, 0, cut, axis=axis), flip=2)
    tail = place.hop(lax.slice_in_dim(two, cut, None, axis=axis), flip=1)
    return [block, one, two, head, tail]


def spread_pieces(place, block):
    return spread_last(place, spread_first(place, block))


def up_hops(place, block):
    return [place.hop(block, up=k) for k in range(1, 4)]


def add_low(a, b):
    return (a.astype(jnp.float32) + b.astype(jnp.float32)).astype(a.dtype)


def fold_first(place, parts):
    own, one_head, two_tail, to_one, to_two = parts
    return own, one_head, two_tail, place.hop(to_one, flip=1), place.hop(to_two, flip=2)


def fold_sums(first):
    own, one_head, two_tail, by_one, by_two = first
    half = one_head.shape[0]
    return own, add_low(one_head, by_two[half:]), add_low(two_tail, by_one[half:]), by_one, by_two


def fold_start(place, parts):
    return fold_sums(fold_first(place, parts))


def fold_end(place, state):
    own, one_head, two_tail, by_one, by_two = state
    return own, place.hop(one_head, flip=1), place.hop(two_tail, flip=2), by_one, by_two


def add_pieces(own, one_head, two_tail, by_one, by_two, axis=0):
    wide = lambda value: value.astype(jnp.float32)
    half = one_head.shape[0]
    one = jnp.concatenate([one_head, by_one[:half]], axis=axis)
    two = jnp.concatenate([by_two[:half], two_tail], axis=axis)
    return wide(own) + wide(one) + wide(two)


def blocks_kernel(sides, own, one_head, two_tail, by_one, by_two, *outs):
    half = one_head.shape[0]
    for side, out in zip(sides, outs):
        terms = (two_tail, by_one) if side else (one_head, by_two)
        total = own[side * half : (side + 1) * half, :].astype(jnp.float32)
        for term in terms:
            total = total + term[:half, :].astype(jnp.float32)
        out[...] = total.astype(jnp.bfloat16)


def sum_blocks(ends, sides):
    half, model = ends[1].shape
    return pl.pallas_call(
        functools.partial(blocks_kernel, sides),
        name="sum_blocks",
        out_shape=[shape_of(half, model)] * len(sides),
        in_specs=[whole_spec()] * 5,
        out_specs=[whole_spec()] * len(sides),
    )(*ends)


def down_hops(place, blocks, first=1):
    return [place.hop(block, up=-first - n) for n, block in enumerate(blocks)]


def total_of(base, extra):
    total = base.astype(jnp.float32)
    for term in extra:
        total = total + term[: base.shape[0]].astype(jnp.float32)
    return total


def received(near_ends, arrived):
    own, one_head, _, _, by_two = near_ends
    return [own, *arrived, one_head, by_two]


def merge_kernel(cut, mine, arrived, own, one_head, two_tail, to_one, to_two):
    m = pl.program_id(0)
    total = (mine[...].astype(jnp.float32) + arrived[...].astype(jnp.float32)).astype(jnp.bfloat16)
    rows = total.shape[0]

    @pl.when(m == 0)
    def _():
        own[...] = total

    @pl.when(m == 1)
    def _():
        one_head[...] = total[:, :cut]
        to_one[:rows, :] = total[:, cut:]

    @pl.when(m == 2)
    def _():
        to_two[:rows, :] = total[:, :cut]
        two_tail[...] = total[:, cut:]

    @pl.when(m == 3)
    def _():
        to_two[rows:, :] = total[:, :cut]
        to_one[rows:, :] = total[:, cut:]


def merge_cores(mine, arrived, cut):
    rows, width = mine.shape[0] // 4, mine.shape[1]
    outs = [(rows, width), (rows, cut), (rows, width - cut), (2 * rows, width - cut), (2 * rows, cut)]
    return pl.pallas_call(
        functools.partial(merge_kernel, cut),
        name="merge_cores",
        grid=(4,),
        out_shape=[shape_of(*out) for out in outs],
        in_specs=[pl.BlockSpec((rows, width), lambda m: (m, 0))] * 2,
        out_specs=[pl.BlockSpec(out, lambda m: (0, 0)) for out in outs],
        compiler_params=pltpu.CompilerParams(vmem_limit_bytes=40 * MIB),
    )(mine, arrived)


def pack_kernel(*refs):
    layers = refs[0].shape[0]
    for l in range(layers):
        out = refs[l - layers]
        at = 0
        for ref in refs[:-layers]:
            width = ref.shape[2]
            out[:, at : at + width] = ref[l]
            at += width


def pack_matrices(*arrays):
    width = sum(a.shape[2] for a in arrays)
    layers, rows, _ = arrays[0].shape
    return pl.pallas_call(
        pack_kernel,
        name="pack_matrices",
        out_shape=[shape_of(rows, width)] * layers,
        in_specs=[whole_spec()] * len(arrays),
        out_specs=[whole_spec()] * layers,
    )(*arrays)


def sum_down(place, total, own):
    rows = own.shape[0]
    total = total.astype(jnp.bfloat16)
    for block in down_hops(place, [total[k * rows : (k + 1) * rows] for k in range(3)]):
        own = own + block.astype(jnp.float32)
    return own


def tables_of(length_row, rows):
    order = jnp.arange(rows, dtype=jnp.int32)
    index = jnp.arange(length_row.shape[0], dtype=jnp.int32)
    ends = jnp.sum(jnp.where(index[:, None] <= index[None, :], length_row[:, None], 0), axis=0)
    passed = order[:, None] >= ends[None, :]
    segment = jnp.sum(passed.astype(jnp.int32), axis=1)
    begin = jnp.sum(jnp.where(passed, length_row[None, :], 0), axis=1)
    cosine, sine = rope_tables(order - begin, HEAD_DIMENSION)
    allowed = (segment[:, None] == segment[None, :]) & (order[:, None] >= order[None, :])
    return (
        jnp.concatenate([cosine] * 4, axis=1),
        jnp.concatenate([-sine, sine] * 2, axis=1),
        allowed.astype(jnp.float32),
    )


def gate_rows_of(found):
    order = jnp.transpose(jnp.stack(found), (2, 1, 0, 4, 3))
    order = jnp.pad(order, ((0, 0),) * 4 + ((0, 8 - order.shape[4]),))
    return [
        (layer[:, :2].reshape(-1, 8), layer[:, 2:].reshape(-1, 8)) for layer in order
    ]


def shards_fast(
    tokens,
    lengths,
    routes,
    gates,
    cotangent,
    norm_attn,
    norm_ffn,
    query,
    key,
    value,
    output,
    w_gate,
    w_up,
    w_down,
):
    place = Place()
    where = jnp.stack([place.plane, place.core, place.column]).astype(jnp.int32)
    rows, model = tokens.shape
    layer_count, _, experts, _ = w_gate.shape
    expert_count = experts * place.columns
    in_width = query.shape[2] + key.shape[2] + value.shape[2]
    gains = jnp.stack([norm_attn, norm_ffn], axis=2)
    gains = jnp.pad(gains, ((0, 0), (0, 0), (0, EXTRA - 2)))
    packs = pack_matrices(query, key, value, output, gains)
    cut = packs[0].shape[1] // 2 // 128 * 128
    weights = [jnp.transpose(w, (0, 2, 1, 3)) for w in (w_gate, w_up, w_down)]
    tables = tables_of(lengths[0], rows)

    def line_of(block):
        return jnp.concatenate([block] + up_hops(place, block))

    cuts = [cut_experts(where, weights, l) for l in range(layer_count)]
    table = gate_table(*tie((routes, gates), packs[0]), expert_count)
    found = jnp.stack(spread_gates(place, table))
    found = [found] + up_hops(place, found)
    line = jnp.concatenate([packs[0]] + tie(up_hops(place, packs[0]), *[cut[0] for cut in cuts], found[0]))
    first = spread_first(place, line)
    gate_rows = gate_rows_of(found)
    cuts[0] = tie(cuts[0], line)
    own_swaps = [place.hop(tie(cut[0], line), swap=1) for cut in cuts]
    two = place.hop(cuts[0][2], up=2)
    swapped = [place.hop(line, swap=1)]
    events = (gate_rows[0][0], gate_rows[-1][0], swapped[0], *own_swaps)
    first = tie(first, two, *events)
    one = place.hop(tie(cuts[0][1], first[0]), up=1)
    swapped += [place.hop(piece, swap=1) for piece in first[1:]]
    last_two = tie(spread_last(place, first, axis=1, cut=cut)[3:], one, *swapped[1:])
    matrices = [[*first, *last_two, *swapped, *[place.hop(p, swap=1) for p in last_two]]]
    shares = [cuts[0][0], one, two, place.hop(tie(cuts[0][3], last_two[0]), up=3)]
    share_swaps = [own_swaps[0], place.hop(one, swap=1), place.hop(two, swap=1)]

    def run_forward(l, which, pieces, bank, after=()):
        return experts_forward_fast(where, gate_rows[l][which], pieces, bank, after=after)

    def run_backward(l, which, pieces, stash, bank, after=()):
        return experts_backward_fast(where, gate_rows[l][which], pieces, stash, bank, after=after)

    def pairs_of(block, *events):
        ups = up_hops(place, block)
        near = spread_first(place, jnp.concatenate([block, ups[0]]))
        return near, ups[1:]

    base, extra = tokens.astype(jnp.float32), []
    stored = []
    for l in range(layer_count):
        more = l + 1 < layer_count
        after = [rows for pair in gate_rows for rows in pair] if l == 0 else []
        after += share_swaps
        outs = attend_forward_fast(where, base, extra, tables, matrices[l], in_width, after=after)
        h, m, nf = outs[:3]
        nf, late = tie((nf, shares[4 - len(shares) + len(share_swaps) :]))
        share_swaps += [place.hop(piece, swap=1) for piece in late]
        bank_l = [*shares[: 4 - len(late)], *late, *share_swaps]
        near, far = pairs_of(nf)
        near = spread_last(place, near)
        far = spread_first(place, jnp.concatenate(tie(far, near[3], near[4])))
        line = up_hops(place, tie(packs[l + 1] if more else cotangent, far[0]))
        y_near = run_forward(l, 0, near, bank_l)
        y_near, far, line[0], line[2] = tie((y_near, far, line[0], line[2]))
        far = spread_last(place, far)
        if more:
            near_first = fold_first(place, tie(y_near[:5], far[3]))
            y_far = run_forward(l, 1, far, bank_l, after=(y_near[0],))
            y_far, near_first, line[1] = tie((y_far, near_first, line[1]))
            one = place.hop(tie(cuts[l + 1][1], line[1]), up=1)
            far_first = fold_first(place, y_far[:5])
            near_ends = fold_end(place, fold_sums(near_first))
            far_first, one = tie((far_first, one))
            far_state = fold_sums(far_first)
            one_swap = place.hop(one, swap=1)
            far_ends, one_swap = tie((fold_end(place, far_state), one_swap), *near_ends[1:3])
            line = jnp.concatenate([packs[l + 1], *line])
            passing = spread_first(place, tie(line, far_ends[1], far_ends[2]))
            line_swap = place.hop(line, swap=1)
            arrived = down_hops(place, sum_blocks(near_ends, (1,)))
            blocks = sum_blocks(far_ends, (0, 1))
            arrived += down_hops(place, blocks, 2)
            passing = tie(passing, *arrived)
            two = place.hop(tie(cuts[l + 1][2], arrived[0], arrived[1], arrived[2]), up=2)
            swapped = [line_swap] + [place.hop(piece, swap=1) for piece in passing[1:]]
            last_two = tie(spread_last(place, passing, 1, cut)[3:], *swapped[1:])
            share_swaps = [own_swaps[l + 1], one_swap]
            ends = [place.hop(p, swap=1) for p in last_two]
            matrices.append([*passing, *last_two, *swapped, *ends])
            shares = [cuts[l + 1][0], one, two]
            shares.append(place.hop(tie(cuts[l + 1][3], last_two[0]), up=3))
            base, extra = m, received(near_ends, arrived)
        else:
            last_near = jnp.concatenate(tie([cotangent, line[0]], far[3], far[4]))
            last_near = spread_first(place, last_near)
            y_far = run_forward(l, 1, far, bank_l, after=(y_near[0],))
            y_far, last_near, line = tie((y_far, last_near, line))
            last_near = spread_last(place, last_near)
            last_far = spread_first(place, jnp.concatenate(tie(line[1:], *last_near[3:])))
        stored.append((h, outs, y_near, y_far, bank_l))

    upstream = cotangent
    zero = jnp.zeros((rows, model), jnp.bfloat16)
    sums = [None] * layer_count
    joined = None
    for l in reversed(range(layer_count)):
        h, outs, kept_near, kept_far, bank_l = stored[l]
        m, na, q, k, v, o, lse, gains = outs[1], *outs[3:]
        top = l + 1 == layer_count

        if top:
            b_near = run_backward(l, 0, last_near, kept_near[6:], bank_l, (y_far[0],))
            b_near, last_far = tie((b_near, last_far))
            far = spread_last(place, last_far)
            near_first = fold_first(place, tie(b_near[:5], far[3], far[4]))
            b_far = run_backward(l, 1, far, kept_far[6:], bank_l, (b_near[0],))
            b_far, near_first = tie((b_far, near_first))
            far_first = fold_first(place, b_far[:5])
        else:
            near, far = pairs_of(low)
            near = spread_last(place, near)
            far = spread_first(place, jnp.concatenate(tie(far, near[3], near[4])))
            b_near = run_backward(l, 0, near, kept_near[6:], bank_l)
            b_near, far = tie((b_near, far))
            far = spread_last(place, far)
            result_blocks = sum_blocks(tie(result_ends, b_near[0]), (0, 1))
            result_arrived = down_hops(place, result_blocks, 2)
            other_sum = place.hop(tie(other_one, b_near[0]), swap=1)
            merged = merge_cores(mine_one, other_sum, cut)
            held, merged = tie((held, merged), far[3], far[4])
            came = [place.hop(tie(held[1], result_blocks[0]), up=1), came[0]]
            merged_first = fold_first(place, merged)
            b_far = run_backward(l, 1, far, kept_far[6:], bank_l, (b_near[0],))
            b_far, merged_first, came[0] = tie((b_far, merged_first, came[0]))
            far_first = fold_first(place, b_far[:5])
            near_first = fold_first(place, tie(b_near[:5], b_far[0]))
            came.append(place.hop(tie(held[3], came[0]), up=3))

        def weight_grads(i, after, near=(kept_near, b_near), far=(kept_far, b_far)):
            pick = lambda kept, found: ((kept[5], found[6 + i]) if i < 2 else (found[5], found[8]))
            return weight_grads_fast(where, pick(*near), pick(*far), experts, after=after)

        grads = [weight_grads(0, (b_far[0],))]
        far_state = fold_sums(tie(far_first, grads[0][0]))
        near_ends = fold_end(place, fold_sums(near_first))
        grads.append(weight_grads(1, (far_state[1], far_state[2])))
        swapped = [place.hop(grads[0][1], swap=1)]
        far_ends = fold_end(place, far_state)
        far_ends, swapped = tie((far_ends, swapped), grads[1][0], *near_ends[1:3])
        swapped.append(place.hop(grads[1][1], swap=1))
        if not top:
            far_ends, came, result_arrived = tie((far_ends, came, result_arrived))
        arrived = down_hops(place, sum_blocks(near_ends, (1,)))
        blocks = sum_blocks(far_ends, (0, 1))
        arrived += down_hops(place, blocks, 2)
        grads.append(weight_grads(2, (blocks[0],)))
        arrived, swapped = tie((arrived, swapped), grads[2][0])
        swapped.append(place.hop(tie(grads[2][1], *arrived), swap=1))
        total = merge_grads([mine for mine, _ in grads], swapped)
        if top:
            held = total
            came = [place.hop(held[2], up=2)]
            result_state = fold_start(place, tie(kept_far[:5], blocks[0]))
            result_ends = fold_end(place, tie(result_state, *arrived))
            result_first = fold_first(place, tie(kept_near[:5], *arrived))
            after = ()
            groups = ((0, 4),)
        else:
            held_came = [held[0], *came]
            merged_ends = fold_end(place, fold_sums(tie(merged_first, blocks[0])))
            one_total = add_pieces(*merged_ends, axis=1)
            shard = mine_one.shape[0] // 16
            low_total = tie(one_total[shard:].astype(jnp.bfloat16), *arrived)
            one_arrived = down_hops(place, [low_total[n * shard :][:shard] for n in range(3)])
            result_near = fold_end(place, fold_sums(tie(result_first, *arrived)))
            after = (low_total, total[0])
            groups = ((1, 3), (0, 1))
        upstream, low, *partial = attend_backward_fast(
            groups,
            where,
            zero,
            upstream,
            received(near_ends, arrived),
            (h, m, na, q, k, v, o, lse, gains),
            tables,
            matrices[l],
            in_width,
            after=after,
        )
        if top:
            low, result_ends, result_first, came = tie((low, result_ends, result_first, came))
            other_one, mine_one = partial
        else:
            partial, result_near = tie((partial, result_near))
    partial, one_arrived = tie((partial, one_arrived))
    sums[1] = one_total[:shard]
    for block in one_arrived:
        sums[1] = sums[1] + block.astype(jnp.float32)
    other_far, other_near, mine_far, mine_near = partial
    other_far, other_near = place.hop(other_far, swap=1), place.hop(other_near, swap=1)
    merged_far = merge_cores(mine_far, other_far, cut)
    merged_near = merge_cores(mine_near, other_near, cut)
    came = [place.hop(tie(total[k], upstream), up=k) for k in (1, 3)]
    far_first = fold_first(place, merged_far)
    near_first = fold_first(place, tie(merged_near, merged_far[0]))
    far_state, near_state = fold_sums(tie(far_first, *came)), fold_sums(near_first)
    came.insert(1, place.hop(tie(total[2], far_state[1]), up=2))
    far_ends, near_ends = fold_end(place, far_state), fold_end(place, near_state)
    far_total = add_pieces(*far_ends, axis=1)
    sums[0] = sum_down(place, far_total, add_pieces(*near_ends, axis=1))
    joined = join_experts(where, tie(held_came, far_state[1]), 1, layer_count, None)
    joined = join_experts(where, [total[0], *came], 0, layer_count, joined)
    last_block = down_hops(place, sum_blocks(tie(result_near, far_state[1]), (1,)))
    result = total_of(stored[-1][1][1], received(result_near, last_block + result_arrived))
    result = result.astype(jnp.bfloat16)
    sums = jnp.stack(sums)
    gain_sums = sums[:, :, in_width + model :]
    starts = (0, query.shape[2], query.shape[2] + key.shape[2], in_width, in_width + model)
    return (
        result,
        upstream,
        gain_sums[:, :, 0],
        gain_sums[:, :, 1],
        *[sums[:, :, a:b] for a, b in zip(starts, starts[1:])],
        *[jnp.transpose(grads, (0, 2, 1, 3)) for grads in joined],
    )


def solution(mesh):
    rows = P(AXES, None)
    layered = P(None, AXES, None)
    expert = P(None, "fsdp", "expert", None)
    gain = P(None, AXES)
    regular = mesh.shape["fsdp"] == 8 and mesh.shape["expert"] == 4
    return jax.shard_map(
        shards_fast if regular else shards,
        mesh=mesh,
        in_specs=(rows, rows, layered, layered, rows, gain, gain)
        + (layered,) * 4
        + (expert,) * 3,
        out_specs=(rows, rows, gain, gain) + (layered,) * 4 + (expert,) * 3,
        check_vma=False,
    )
```

```python
import functools
import math

import jax
import jax.numpy as jnp
from jax import lax
from jax.experimental import pallas as pl
from jax.experimental.pallas import tpu as pltpu
from jax.sharding import PartitionSpec as P

QUERY_HEADS = 24
KEY_VALUE_HEADS = 8
HEAD_DIMENSION = 64
CORES = 2

NORM_EPS = 1e-06
MASKED = -1000000000.0
AXES = ("fsdp", "expert")


class Place:
    def __init__(self):
        self.planes = lax.axis_size("fsdp") // CORES
        self.columns = lax.axis_size("expert")
        fsdp = lax.axis_index("fsdp")
        self.plane = fsdp // CORES
        self.core = fsdp % CORES
        self.column = lax.axis_index("expert")

    def hop(self, value, up=0, flip=0, swap=0):
        pairs = []
        for plane in range(self.planes):
            for core in range(CORES):
                for column in range(self.columns):
                    source = (plane * CORES + core) * self.columns + column
                    target = ((plane + up) % self.planes * CORES + (core ^ swap)) * self.columns
                    pairs.append((source, target + (column ^ flip)))
        return lax.ppermute(value, AXES, pairs)


def spread(place, block):
    if place.columns != 4:
        return [block] + [place.hop(block, flip=m) for m in range(1, place.columns)]
    half = block.shape[1] // 2
    one = place.hop(block, flip=1)
    two = place.hop(block, flip=2)
    head = place.hop(one[:, :half], flip=2)
    tail = place.hop(two[:, half:], flip=1)
    return [block, one, two, jnp.concatenate([head, tail], axis=1)]


def gather_tokens(place, block):
    own = block[None]
    others = jnp.stack([place.hop(block, up=k) for k in range(1, place.planes)])
    near = spread(place, own)
    far = spread(place, others)
    return [jnp.concatenate([a, b], axis=0) for a, b in zip(near, far)]


def fold(place, parts):
    wide = lambda value: value.astype(jnp.float32)
    if place.columns != 4:
        total = wide(parts[0])
        for m in range(1, place.columns):
            total = total + wide(place.hop(parts[m], flip=m))
        return total
    half = parts[0].shape[1] // 2
    head = place.hop(parts[3][:, :half], flip=2)
    tail = place.hop(parts[3][:, half:], flip=1)
    one_tail = place.hop(parts[1][:, half:], flip=1)
    two_head = place.hop(parts[2][:, :half], flip=2)
    one_head = place.hop((wide(parts[1][:, :half]) + wide(head)).astype(parts[1].dtype), flip=1)
    two_tail = place.hop((wide(parts[2][:, half:]) + wide(tail)).astype(parts[2].dtype), flip=2)
    upper = wide(parts[0][:, :half]) + wide(one_head) + wide(two_head)
    lower = wide(parts[0][:, half:]) + wide(one_tail) + wide(two_tail)
    return jnp.concatenate([upper, lower], axis=1)


def scatter_sums(place, parts):
    far = fold(place, [part[1:] for part in parts]).astype(parts[0].dtype)
    arrived = [place.hop(far[k - 1], up=-k) for k in range(1, place.planes)]
    total = fold(place, [part[:1] for part in parts])[0]
    for piece in arrived:
        total = total + piece.astype(jnp.float32)
    return total


def gate_table(routes, gates, expert_count):
    names = jnp.arange(expert_count, dtype=jnp.int32)
    chosen = routes[:, None, :, :] == names[None, :, None, None]
    return jnp.sum(jnp.where(chosen, gates[:, None, :, :], 0.0), axis=3)


def spread_gates(place, table):
    axis = table.ndim - 2
    owned = table.shape[axis] // place.columns
    found = []
    for m in range(place.columns):
        start = (place.column ^ m) * owned
        piece = lax.dynamic_slice_in_dim(table, start, owned, axis=axis)
        found.append(place.hop(piece, flip=m) if m else piece)
    return found


def gather_gates(place, routes, gates, expert_count):
    table = gate_table(routes, gates, expert_count)
    line = jnp.stack([table] + [place.hop(table, up=k) for k in range(1, place.planes)])
    return spread_gates(place, line)


def gather_experts(place, weights):
    rows, experts, hidden = weights[0].shape
    share = hidden // place.planes

    def cut(plane):
        pieces = [lax.dynamic_slice_in_dim(w, plane * share, share, axis=2) for w in weights]
        return jnp.stack([p.reshape(rows, experts * share) for p in pieces])

    own = [cut(place.plane)]
    for k in range(1, place.planes):
        own.append(place.hop(cut((place.plane + k) % place.planes), up=k))
    own = jnp.stack(own)
    sibling = place.hop(own, swap=1)
    both = jnp.concatenate([own, sibling])
    shard = jnp.arange(place.planes * CORES)
    index = ((shard % CORES) ^ place.core) * place.planes
    index = index + (place.plane - shard // CORES) % place.planes
    return [
        jnp.take(both[:, i], index, axis=0).reshape(-1, experts * share)
        for i in range(len(weights))
    ]


def scatter_experts(place, grads, experts):
    features, width = grads[0].shape
    rows = features // (place.planes * CORES)
    share = width // experts
    shape = (place.planes, CORES, rows, width)
    stacked = jnp.stack([g.reshape(shape) for g in grads], axis=1)
    mine = lax.dynamic_index_in_dim(stacked, place.core, axis=2, keepdims=False)
    others = lax.dynamic_index_in_dim(stacked, 1 - place.core, axis=2, keepdims=False)
    arrived = place.hop(others.astype(jnp.bfloat16), swap=1)
    total = (mine + arrived.astype(jnp.float32)).astype(jnp.bfloat16)
    pieces = [lax.dynamic_index_in_dim(total, place.plane, axis=0, keepdims=False)]
    for k in range(1, place.planes):
        target = (place.plane + k) % place.planes
        piece = lax.dynamic_index_in_dim(total, target, axis=0, keepdims=False)
        pieces.append(place.hop(piece, up=k))
    index = (place.plane - jnp.arange(place.planes)) % place.planes
    ordered = jnp.take(jnp.stack(pieces), index, axis=0)
    ordered = ordered.reshape(place.planes, len(grads), rows, experts, share)
    ordered = jnp.transpose(ordered, (1, 2, 3, 0, 4)).reshape(len(grads), rows, experts, -1)
    return [ordered[i].astype(jnp.float32) for i in range(len(grads))]


def positions(length_row, count_of_rows):
    ends = jnp.cumsum(length_row)
    token_order = jnp.arange(count_of_rows, dtype=jnp.int32)
    passed = token_order[:, None] >= ends[None, :]
    segment = jnp.sum(passed.astype(jnp.int32), axis=1)
    before = jnp.sum(jnp.where(passed, length_row[None, :], 0), axis=1)
    return (segment, token_order - before)


def rope_tables(seq_place, head_width):
    half_width = head_width // 2
    freq_table = jnp.exp(
        jnp.arange(half_width, dtype=jnp.float32) * (-2.0 * math.log(10000.0) / head_width)
    )
    angles = seq_place.astype(jnp.float32)[:, None] * freq_table[None, :]
    return (jnp.cos(angles), jnp.sin(angles))


def apply_rotation(vector, cosine_table, sine_table):
    half_width = vector.shape[-1] // 2
    former = vector[..., :half_width]
    latter = vector[..., half_width:]
    cos_wide = cosine_table[:, None, :]
    sin_wide = sine_table[:, None, :]
    return jnp.concatenate(
        [former * cos_wide - latter * sin_wide, latter * cos_wide + former * sin_wide], axis=-1
    )


def reverse_rotation(vector, cosine_table, sine_table):
    return apply_rotation(vector, cosine_table, -sine_table)


def rms_forward(residual, norm_gain):
    inverse = lax.rsqrt(jnp.mean(residual * residual, axis=-1, keepdims=True) + NORM_EPS)
    return (inverse, (residual * inverse * norm_gain).astype(jnp.bfloat16))


def rms_backward(residual, inverse, norm_gain, upstream):
    gain_grad = jnp.sum(upstream * residual * inverse, axis=0)
    scaled = upstream * norm_gain
    inner = jnp.mean(scaled * residual, axis=-1, keepdims=True)
    return (gain_grad, inverse * scaled - residual * inverse * inverse * inverse * inner)


def score_block(rotated_query, turned_k, allowed):
    scores = jnp.einsum(
        "qhgd,khd->hgqk", rotated_query, turned_k, preferred_element_type=jnp.float32
    ) * HEAD_DIMENSION ** (-0.5)
    return jnp.where(allowed, scores, MASKED)


def attend_forward(residual, allowed, tables, gain, matrices):
    w_in, w_output = matrices
    count_of_rows = residual.shape[0]
    query_width = QUERY_HEADS * HEAD_DIMENSION
    key_width = KEY_VALUE_HEADS * HEAD_DIMENSION
    inverse, normalized_input = rms_forward(residual, gain)
    projected = jnp.dot(normalized_input, w_in, preferred_element_type=jnp.float32)
    query_unrotated = projected[:, :query_width].reshape(count_of_rows, QUERY_HEADS, -1)
    key_unrotated = projected[:, query_width : query_width + key_width]
    key_unrotated = key_unrotated.reshape(count_of_rows, KEY_VALUE_HEADS, -1)
    value_rows = projected[:, query_width + key_width :].astype(jnp.bfloat16)
    value_rows = value_rows.reshape(count_of_rows, KEY_VALUE_HEADS, -1)
    rotated_query = (
        apply_rotation(query_unrotated, *tables)
        .astype(jnp.bfloat16)
        .reshape(count_of_rows, KEY_VALUE_HEADS, QUERY_HEADS // KEY_VALUE_HEADS, HEAD_DIMENSION)
    )
    turned_k = apply_rotation(key_unrotated, *tables).astype(jnp.bfloat16)
    scores = score_block(rotated_query, turned_k, allowed)
    row_top = jnp.max(scores, axis=-1, keepdims=True)
    exp_scores = jnp.exp(scores - row_top)
    row_total = jnp.sum(exp_scores, axis=-1, keepdims=True)
    attn_probs = (exp_scores / row_total).astype(jnp.bfloat16)
    log_total = row_top + jnp.log(row_total)
    mixed_heads = jnp.einsum(
        "hgqk,khd->qhgd", attn_probs, value_rows, preferred_element_type=jnp.float32
    )
    mixed_heads = mixed_heads.astype(jnp.bfloat16).reshape(count_of_rows, query_width)
    attn_out = jnp.dot(mixed_heads, w_output, preferred_element_type=jnp.float32)
    return (
        residual + attn_out,
        (inverse, normalized_input, rotated_query, turned_k, value_rows, log_total, mixed_heads),
    )


def attend_backward(residual, allowed, tables, gain, matrices, stash, upstream):
    w_in, w_output = matrices
    inverse, normalized_input, rotated_query, turned_k, value_rows, log_total, mixed_heads = stash
    count_of_rows = residual.shape[0]
    branch_grad = upstream.astype(jnp.bfloat16)
    grad_wo = jnp.einsum("td,te->de", mixed_heads, branch_grad, preferred_element_type=jnp.float32)
    mixed_gradient = jnp.einsum(
        "te,de->td", branch_grad, w_output, preferred_element_type=jnp.float32
    )
    mixed_gradient = mixed_gradient.astype(jnp.bfloat16).reshape(
        count_of_rows, KEY_VALUE_HEADS, QUERY_HEADS // KEY_VALUE_HEADS, HEAD_DIMENSION
    )
    attn_probs = jnp.exp(score_block(rotated_query, turned_k, allowed) - log_total)
    value_rows_gradient = jnp.einsum(
        "hgqk,qhgd->khd",
        attn_probs.astype(jnp.bfloat16),
        mixed_gradient,
        preferred_element_type=jnp.float32,
    )
    value_rows_gradient = value_rows_gradient.astype(jnp.bfloat16).reshape(count_of_rows, -1)
    grad_probs = jnp.einsum(
        "qhgd,khd->hgqk", mixed_gradient, value_rows, preferred_element_type=jnp.float32
    )
    grad_scores = attn_probs * (
        grad_probs - jnp.sum(attn_probs * grad_probs, axis=-1, keepdims=True)
    )
    grad_scores = grad_scores.astype(jnp.bfloat16)
    grad_tq = jnp.einsum(
        "hgqk,khd->qhgd", grad_scores, turned_k, preferred_element_type=jnp.float32
    ) * HEAD_DIMENSION ** (-0.5)
    turned_key_gradient = jnp.einsum(
        "hgqk,qhgd->khd", grad_scores, rotated_query, preferred_element_type=jnp.float32
    ) * HEAD_DIMENSION ** (-0.5)
    grad_query = reverse_rotation(
        grad_tq.reshape(count_of_rows, QUERY_HEADS, HEAD_DIMENSION), *tables
    )
    grad_query = grad_query.astype(jnp.bfloat16).reshape(count_of_rows, -1)
    grad_key = reverse_rotation(turned_key_gradient, *tables).astype(jnp.bfloat16)
    grad_key = grad_key.reshape(count_of_rows, -1)
    grad_in = jnp.concatenate([grad_query, grad_key, value_rows_gradient], axis=1)
    grad_w_in = jnp.einsum("td,te->de", normalized_input, grad_in, preferred_element_type=jnp.float32)
    grad_normed = jnp.einsum("te,de->td", grad_in, w_in, preferred_element_type=jnp.float32)
    gain_grad, residual_grad = rms_backward(residual, inverse, gain, grad_normed)
    return (upstream + residual_grad, gain_grad, grad_w_in, grad_wo)


def widen(gate_columns, share):
    return jnp.repeat(gate_columns, share, axis=1)


def experts_forward(place, middle, gain, gate_parts, weights):
    w_gate, w_up, w_down = weights
    share = w_gate.shape[1] // gate_parts[0].shape[1]
    model_width = middle.shape[1]
    inverse, normalized_input = rms_forward(middle, gain)
    chunks = gather_tokens(place, normalized_input)
    parts, kept = [], []
    for chunk, gate_columns in zip(chunks, gate_parts):
        rows = chunk.reshape(-1, model_width)
        gate_pre = jnp.dot(rows, w_gate, preferred_element_type=jnp.float32)
        up_pre = jnp.dot(rows, w_up, preferred_element_type=jnp.float32)
        weighed = gate_pre * jax.nn.sigmoid(gate_pre) * up_pre * widen(gate_columns, share)
        weighed = weighed.astype(jnp.bfloat16)
        produced = lax.dot_general(
            weighed, w_down, (((1,), (1,)), ((), ())), preferred_element_type=jnp.float32
        )
        parts.append(produced.astype(jnp.bfloat16).reshape(chunk.shape))
        kept.append((rows, gate_pre, up_pre, weighed))
    return (middle + scatter_sums(place, parts), (inverse, kept))


def experts_backward(place, middle, gain, gate_parts, weights, stash, upstream, chunks):
    w_gate, w_up, w_down = weights
    share = w_gate.shape[1] // gate_parts[0].shape[1]
    model_width = middle.shape[1]
    inverse, kept = stash
    parts, gate_grads, up_grads, row_grads = [], [], [], []
    for chunk, gate_columns, (rows, gate_pre, up_pre, weighed) in zip(chunks, gate_parts, kept):
        grads = chunk.reshape(-1, model_width)
        hidden_grad = jnp.dot(grads, w_down, preferred_element_type=jnp.float32)
        hidden_grad = hidden_grad * widen(gate_columns, share)
        gate_sig = jax.nn.sigmoid(gate_pre)
        gate_grad = hidden_grad * up_pre * gate_sig * (1.0 + gate_pre * (1.0 - gate_sig))
        gate_grad = gate_grad.astype(jnp.bfloat16)
        up_grad = (hidden_grad * gate_pre * gate_sig).astype(jnp.bfloat16)
        back = (((1,), (1,)), ((), ()))
        produced = lax.dot_general(gate_grad, w_gate, back, preferred_element_type=jnp.float32)
        produced = produced + lax.dot_general(
            up_grad, w_up, back, preferred_element_type=jnp.float32
        )
        parts.append(produced.astype(jnp.bfloat16).reshape(chunk.shape))
        gate_grads.append(gate_grad)
        up_grads.append(up_grad)
        row_grads.append(grads)
    normed_grad = scatter_sums(place, parts)
    rows = jnp.concatenate([entry[0] for entry in kept])
    weighed = jnp.concatenate([entry[3] for entry in kept])
    outer = (((0,), (0,)), ((), ()))
    weight_grads = [
        lax.dot_general(a, b, outer, preferred_element_type=jnp.float32)
        for a, b in (
            (rows, jnp.concatenate(gate_grads)),
            (rows, jnp.concatenate(up_grads)),
            (jnp.concatenate(row_grads), weighed),
        )
    ]
    gain_grad, middle_grad = rms_backward(middle, inverse, gain, normed_grad)
    return (upstream + middle_grad, gain_grad, weight_grads)


def shards(
    tokens,
    lengths,
    routes,
    gates,
    cotangent,
    norm_attn,
    norm_ffn,
    query,
    key,
    value,
    output,
    w_gate,
    w_up,
    w_down,
):
    place = Place()
    token_rows = tokens.shape[0]
    layer_count, _, experts, _ = w_gate.shape
    expert_count = experts * place.columns
    in_width = query.shape[2] + key.shape[2] + value.shape[2]
    segment, seq_place = positions(lengths[0], token_rows)
    tables = rope_tables(seq_place, HEAD_DIMENSION)
    token_order = jnp.arange(token_rows, dtype=jnp.int32)
    allowed = (segment[:, None] == segment[None, :]) & (
        token_order[:, None] >= token_order[None, :]
    )
    gains = jnp.concatenate([norm_attn, norm_ffn]).T
    packs = []
    for l in range(layer_count):
        pack = [query[l], key[l], value[l], output[l]]
        if l == 0:
            pack.append(jnp.pad(gains, ((0, 0), (0, 128 - gains.shape[1]))))
        packs.append(jnp.concatenate(pack, axis=1))
    full = lax.all_gather(packs[0], AXES, axis=0, tiled=True)
    gains = full[:, in_width + output.shape[2] :].T[: 2 * layer_count].astype(jnp.float32)
    gate_rows = gather_gates(place, routes, gates, expert_count)
    gate_parts = [
        [
            jnp.transpose(piece[:, l], (0, 2, 1)).reshape(-1, experts)
            for piece in gate_rows
        ]
        for l in range(layer_count)
    ]
    expert_weights = gather_experts(place, [w_gate[0], w_up[0], w_down[0]])
    last_grads = None

    residual = tokens.astype(jnp.float32)
    matrices, weights, stored = [], [], []
    for l in range(layer_count):
        matrices.append((full[:, :in_width], full[:, in_width : in_width + output.shape[2]]))
        weights.append(expert_weights)
        layer_input = residual
        middle, attn_stash = attend_forward(layer_input, allowed, tables, gains[l], matrices[l])
        if l + 1 < layer_count:
            held, pack, *shares = lax.optimization_barrier(
                (middle, packs[l + 1], w_gate[l + 1], w_up[l + 1], w_down[l + 1])
            )
            middle = held
            full = lax.all_gather(pack, AXES, axis=0, tiled=True)
            expert_weights = gather_experts(place, shares)
        residual, moe_stash = experts_forward(
            place, middle, gains[layer_count + l], gate_parts[l], weights[l]
        )
        if l + 2 == layer_count or layer_count == 1:
            held, last = lax.optimization_barrier((residual, cotangent))
            residual = held
            last_grads = gather_tokens(place, last)
        stored.append((layer_input, middle, attn_stash, moe_stash))
    result = residual.astype(jnp.bfloat16)

    upstream = cotangent.astype(jnp.float32)
    in_grads, out_grads = [None] * layer_count, [None] * layer_count
    gain_grads = [None] * (2 * layer_count)
    expert_grads = [None] * layer_count
    for l in reversed(range(layer_count)):
        layer_input, middle, attn_stash, moe_stash = stored[l]
        chunks = last_grads
        if l + 1 < layer_count:
            chunks = gather_tokens(place, upstream.astype(jnp.bfloat16))
        upstream, gain_grads[layer_count + l], weight_grads = experts_backward(
            place,
            middle,
            gains[layer_count + l],
            gate_parts[l],
            weights[l],
            moe_stash,
            upstream,
            chunks,
        )
        expert_grads[l] = scatter_experts(place, weight_grads, experts)
        upstream, gain_grads[l], grad_w_in, grad_wo = attend_backward(
            layer_input, allowed, tables, gains[l], matrices[l], attn_stash, upstream
        )
        summed = lax.psum_scatter(
            jnp.concatenate([grad_w_in, grad_wo], axis=1).astype(jnp.bfloat16),
            AXES,
            scatter_dimension=0,
            tiled=True,
        ).astype(jnp.float32)
        in_grads[l], out_grads[l] = summed[:, :in_width], summed[:, in_width:]
    gain_sums = lax.psum_scatter(jnp.stack(gain_grads), AXES, scatter_dimension=1, tiled=True)
    in_grads = jnp.stack(in_grads)
    key_start, value_start = query.shape[2], query.shape[2] + key.shape[2]
    return (
        result,
        upstream,
        gain_sums[:layer_count],
        gain_sums[layer_count:],
        in_grads[:, :, :key_start],
        in_grads[:, :, key_start:value_start],
        in_grads[:, :, value_start:],
        jnp.stack(out_grads),
        jnp.stack([entry[0] for entry in expert_grads]),
        jnp.stack([entry[1] for entry in expert_grads]),
        jnp.stack([entry[2] for entry in expert_grads]),
    )


HEADS_PER_TURN = 6
LANES = 128
EXTRA = 128
HALF = 64
MIB = 1 << 20
COST_PART = 16


def cost(flops):
    return pl.CostEstimate(flops=flops // COST_PART, bytes_accessed=0, transcendentals=0)


def any_spec():
    return pl.BlockSpec(memory_space=pl.ANY)


def whole_spec():
    return pl.BlockSpec(memory_space=pltpu.VMEM)


def scalar_spec():
    return pl.BlockSpec(memory_space=pltpu.SMEM)


def shape_of(*dims, dtype=jnp.bfloat16):
    return jax.ShapeDtypeStruct(dims, dtype)


class Copies:
    def __init__(self, semaphores, first=0):
        self.semaphores = semaphores
        self.used = first
        self.open = []

    def start(self, source, target):
        copy = pltpu.make_async_copy(source, target, self.semaphores.at[self.used])
        self.used += 1
        copy.start()
        self.open.append(copy)

    def wait(self):
        for copy in self.open:
            copy.wait()
        self.open = []


def shard_row(where, swapped, m, k, rows):
    plane = lax.rem(where[0] - k + 4, 4)
    fsdp = plane * CORES + (where[1] ^ swapped)
    return pl.multiple_of((fsdp * 4 + (where[2] ^ m)) * rows, 16)


MATRIX_PIECES = 10
MATRIX_COPIES = 40


def load_matrices(copies, where, pieces, full):
    rows, cut = pieces[0].shape[0] // 4, pieces[3].shape[1]
    spans = ((0, 0, full.shape[1]),) * 3 + ((3, 0, cut), (3, cut, full.shape[1] - cut))
    for swapped in range(CORES):
        for index, (m, low, width) in enumerate(spans):
            piece = pieces[swapped * 5 + index]
            for k in range(4):
                row = shard_row(where, swapped, m or index, k, rows)
                copies.start(
                    piece.at[pl.ds(k * rows, rows), :], full.at[pl.ds(row, rows), pl.ds(low, width)]
                )


def half_swap(x):
    lane = lax.broadcasted_iota(jnp.int32, x.shape, 1)
    return jnp.where(lane % 64 < 32, pltpu.roll(x, 96, 1), pltpu.roll(x, 32, 1))


def both_sides(pair, side):
    lane = lax.broadcasted_iota(jnp.int32, pair.shape, 1)
    wide = pair.astype(jnp.float32)
    here = jnp.where(lane // 64 == side, wide, 0.0)
    there = pltpu.roll(here, 64, 1)
    here, there = here.astype(jnp.bfloat16), there.astype(jnp.bfloat16)
    return (here, there) if side == 0 else (there, here)


def merge_sides(even, odd, side):
    lane = lax.broadcasted_iota(jnp.int32, even.shape, 1)
    if side == 0:
        return jnp.where(lane < 64, even + pltpu.roll(odd, 64, 1), 0.0)
    return jnp.where(lane < 64, 0.0, odd + pltpu.roll(even, 64, 1))


def contract(a, b, dims):
    return lax.dot_general(a, b, (dims, ((), ())), preferred_element_type=jnp.float32)


PLAIN = ((1,), (0,))
ACROSS = ((1,), (1,))
OUTER = ((0,), (0,))


def read_sum(base, extra):
    total = base[...].astype(jnp.float32)
    for term in extra:
        total = total + term[pl.ds(0, total.shape[0]), :].astype(jnp.float32)
    return total


def attend_forward_kernel(terms, width, where, base, *refs):
    refs = list(refs)
    extra = [refs.pop(0) for _ in range(terms)]
    cosine, sine, allowed = refs[:3]
    pieces = refs[3 : 3 + MATRIX_PIECES]
    refs = refs[3 + MATRIX_PIECES :]
    h_out, m_out, nf_out, na_out, q_out, k_out, v_out, o_out, lse_out, gain_out = refs[:10]
    full, proj, mixed, semaphores = refs[10:]
    copies = Copies(semaphores)
    load_matrices(copies, where, pieces, full)
    h = read_sum(base, extra)
    h_out[...] = h
    inverse = lax.rsqrt(jnp.mean(h * h, axis=1, keepdims=True) + NORM_EPS)
    model = h.shape[1]
    in_width = width
    key_start = model
    value_start = model + (in_width - model) // 2
    copies.wait()
    gains = full[:, pl.ds(in_width + model, EXTRA)].astype(jnp.float32).T
    gain_out[...] = gains[:8]
    na_out[...] = (h * inverse * gains[0:1]).astype(jnp.bfloat16)
    step = 512

    @pl.loop(0, in_width // step)
    def _(i):
        columns = pl.ds(pl.multiple_of(i * step, step), step)
        proj[:, columns] = contract(na_out[...], full[:, columns], PLAIN)

    cos, sin = cosine[...], sine[...]

    @pl.loop(0, key_start // LANES)
    def _(i):
        columns = pl.ds(pl.multiple_of(i * LANES, LANES), LANES)
        x = proj[:, columns]
        q_out[:, columns] = (x * cos + half_swap(x) * sin).astype(jnp.bfloat16)

    @pl.loop(0, (value_start - key_start) // LANES)
    def _(i):
        start = pl.multiple_of(i * LANES, LANES)
        x = proj[:, pl.ds(key_start + start, LANES)]
        k_out[:, pl.ds(start, LANES)] = (x * cos + half_swap(x) * sin).astype(jnp.bfloat16)

    v_out[...] = proj[:, value_start:in_width].astype(jnp.bfloat16)
    lse_out[...] = jnp.zeros_like(lse_out)
    open_keys = allowed[...] > 0.5
    lane = lax.broadcasted_iota(jnp.int32, open_keys.shape, 1)

    @pl.loop(0, KEY_VALUE_HEADS // 2)
    def _(turn):
        pair = pl.ds(pl.multiple_of(turn * LANES, LANES), LANES)
        keys = [both_sides(k_out[:, pair], side) for side in range(2)]
        values = [both_sides(v_out[:, pair], side) for side in range(2)]
        lse = lse_out[...]
        for group in range(HEADS_PER_TURN // 2):
            columns = pl.ds(
                pl.multiple_of(turn * (HEADS_PER_TURN * 64) + group * LANES, LANES), LANES
            )
            total = jnp.zeros((h.shape[0], LANES), jnp.float32)
            for side in range(2):
                head = group * 2 + side
                scores = contract(q_out[:, columns], keys[head // 3][side], ACROSS)
                scores = jnp.where(open_keys, scores * HEAD_DIMENSION ** (-0.5), MASKED)
                top = jnp.max(scores, axis=1, keepdims=True)
                weights = jnp.exp(scores - top)
                row_total = jnp.sum(weights, axis=1, keepdims=True)
                probs = (weights / row_total).astype(jnp.bfloat16)
                lse = jnp.where(lane == turn * HEADS_PER_TURN + head, top + jnp.log(row_total), lse)
                total = total + contract(probs, values[head // 3][side], PLAIN)
            o_out[:, columns] = total.astype(jnp.bfloat16)
        lse_out[...] = lse

    @pl.loop(0, model // step)
    def _(i):
        columns = pl.ds(pl.multiple_of(i * step, step), step)
        weights = full[:, pl.ds(pl.multiple_of(in_width + i * step, step), step)]
        mixed[:, columns] = contract(o_out[...], weights, PLAIN)

    m = h_out[...] + mixed[...]
    m_out[...] = m
    inverse = lax.rsqrt(jnp.mean(m * m, axis=1, keepdims=True) + NORM_EPS)
    nf_out[...] = (m * inverse * gain_out[1:2]).astype(jnp.bfloat16)


def attend_forward_fast(where, base, extra, tables, pieces, in_width, after=()):
    rows, model = base.shape
    bf, f32 = jnp.bfloat16, jnp.float32
    key_width = (in_width - model) // 2
    total = in_width + model + EXTRA
    shapes = [
        shape_of(rows, model, dtype=f32),
        shape_of(rows, model, dtype=f32),
        shape_of(rows, model),
        shape_of(rows, model),
        shape_of(rows, model),
        shape_of(rows, key_width),
        shape_of(rows, key_width),
        shape_of(rows, model),
        shape_of(rows, LANES, dtype=f32),
        shape_of(8, model, dtype=f32),
    ]

    def body(*refs):
        used = 2 + len(extra) + 3 + MATRIX_PIECES
        attend_forward_kernel(len(extra), in_width, *refs[:used], *refs[used + len(after) :])

    return pl.pallas_call(
        body,
        name="attend_forward",
        out_shape=shapes,
        in_specs=[scalar_spec()]
        + [whole_spec()] * (4 + len(extra))
        + [any_spec()] * (MATRIX_PIECES + len(after)),
        out_specs=[whole_spec()] * len(shapes),
        scratch_shapes=[
            pltpu.VMEM((model, total), bf),
            pltpu.VMEM((rows, in_width), f32),
            pltpu.VMEM((rows, model), f32),
            pltpu.SemaphoreType.DMA((MATRIX_COPIES,)),
        ],
        compiler_params=pltpu.CompilerParams(vmem_limit_bytes=44 * MIB),
        cost_estimate=cost(2 * rows * model * total),
    )(where, base, *extra, *tables, *pieces, *after)


def attend_backward_kernel(groups, terms, width, where, base, upstream, *refs):
    refs = list(refs)
    extra = [refs.pop(0) for _ in range(terms)]
    h_in, m_in, na, q, k, v, o, lse_in, gains, cosine, sine, allowed = refs[:12]
    pieces = refs[12 : 12 + MATRIX_PIECES]
    outs, refs = refs[12 + MATRIX_PIECES : -6], refs[-6:]
    gh_out, gh_low = outs[:2]
    full, sums, mixed, grad_in, turned, semaphores = refs
    rows, model = h_in.shape
    in_width = width
    key_start = model
    value_start = model + (in_width - model) // 2
    shard = full.shape[0] // 32
    copies = Copies(semaphores)
    load_matrices(copies, where, pieces, full)
    gnf = read_sum(base, extra)
    m = m_in[...]
    inverse = lax.rsqrt(jnp.mean(m * m, axis=1, keepdims=True) + NORM_EPS)
    gain_ffn = jnp.sum(gnf * m * inverse, axis=0, keepdims=True)
    scaled = gnf * gains[1:2]
    inner = jnp.mean(scaled * m, axis=1, keepdims=True)
    gm = upstream[...].astype(jnp.float32)
    gm = gm + inverse * scaled - m * (inverse * inverse * inverse) * inner
    gh_out[...] = gm
    gh_low[...] = gm.astype(jnp.bfloat16)
    copies.wait()
    step = 512

    @pl.loop(0, model // step)
    def _(i):
        row = pl.ds(pl.multiple_of(i * step, step), step)
        mixed[:, row] = contract(gh_low[...], full[row, in_width : in_width + model], ACROSS).astype(
            jnp.bfloat16
        )

    open_keys = allowed[...] > 0.5
    lane = lax.broadcasted_iota(jnp.int32, open_keys.shape, 1)
    cos, sin = cosine[...], sine[...]
    scale = HEAD_DIMENSION ** (-0.5)

    @pl.loop(0, KEY_VALUE_HEADS // 2)
    def _(turn):
        start = pl.multiple_of(turn * LANES, LANES)
        pair = pl.ds(start, LANES)
        keys = [both_sides(k[:, pair], side) for side in range(2)]
        values = [both_sides(v[:, pair], side) for side in range(2)]
        zero = jnp.zeros((rows, LANES), jnp.float32)
        grad_k = [[zero, zero], [zero, zero]]
        grad_v = [[zero, zero], [zero, zero]]
        lse = lse_in[...]
        for group in range(HEADS_PER_TURN // 2):
            columns = pl.ds(
                pl.multiple_of(turn * (HEADS_PER_TURN * 64) + group * LANES, LANES), LANES
            )
            grad_q = zero
            for side in range(2):
                head = group * 2 + side
                kv = head // 3
                top = jnp.sum(
                    jnp.where(lane == turn * HEADS_PER_TURN + head, lse, 0.0), axis=1, keepdims=True
                )
                scores = contract(q[:, columns], keys[kv][side], ACROSS) * scale
                probs = jnp.exp(jnp.where(open_keys, scores, MASKED) - top)
                go = mixed[:, columns]
                grad_v[kv][side] = grad_v[kv][side] + contract(
                    probs.astype(jnp.bfloat16), go, OUTER
                )
                grad_p = contract(go, values[kv][side], ACROSS)
                grad_s = probs * (grad_p - jnp.sum(probs * grad_p, axis=1, keepdims=True))
                grad_s = grad_s.astype(jnp.bfloat16)
                grad_q = grad_q + contract(grad_s, keys[kv][side], PLAIN)
                grad_k[kv][side] = grad_k[kv][side] + contract(grad_s, q[:, columns], OUTER)
            grad_q = grad_q * scale
            grad_in[:, columns] = (grad_q * cos - half_swap(grad_q) * sin).astype(jnp.bfloat16)
        key_grad = merge_sides(*grad_k[0], 0) + merge_sides(*grad_k[1], 1)
        key_grad = key_grad * scale
        key_grad = key_grad * cos - half_swap(key_grad) * sin
        value_grad = merge_sides(*grad_v[0], 0) + merge_sides(*grad_v[1], 1)
        grad_in[:, pl.ds(key_start + start, LANES)] = key_grad.astype(jnp.bfloat16)
        grad_in[:, pl.ds(value_start + start, LANES)] = value_grad.astype(jnp.bfloat16)

    turned[...] = jnp.zeros_like(turned)

    @pl.loop(0, in_width // step)
    def _(i):
        columns = pl.ds(pl.multiple_of(i * step, step), step)
        turned[...] += contract(grad_in[:, columns], full[:, columns], ACROSS)

    grad_na = turned[...]
    h = h_in[...]
    inverse = lax.rsqrt(jnp.mean(h * h, axis=1, keepdims=True) + NORM_EPS)
    gain_attn = jnp.sum(grad_na * h * inverse, axis=0, keepdims=True)
    scaled = grad_na * gains[0:1]
    inner = jnp.mean(scaled * h, axis=1, keepdims=True)
    band = 384

    @pl.loop(0, model // band)
    def _(i):
        start = pl.multiple_of(i * band, band)
        row = pl.ds(start, band)
        sums[row, in_width : in_width + model] = contract(o[:, row], gh_low[...], OUTER).astype(
            jnp.bfloat16
        )
        sums[row, :in_width] = contract(na[:, row], grad_in[...], OUTER).astype(jnp.bfloat16)

    both = jnp.concatenate([gain_attn, gain_ffn, jnp.zeros((EXTRA - 2, model), jnp.float32)], axis=0)
    sums[:, pl.ds(in_width + model, EXTRA)] = both.T.astype(jnp.bfloat16)
    at = 2
    for swapped in (1, 0):
        for first, count in groups:
            for m_index in range(4):
                for n in range(count):
                    row = shard_row(where, swapped, m_index, first + n, shard)
                    copies.start(
                        sums.at[pl.ds(row, shard), :],
                        outs[at].at[pl.ds((m_index * count + n) * shard, shard), :],
                    )
            at += 1
    gh = gh_out[...] + inverse * scaled - h * (inverse * inverse * inverse) * inner
    gh_out[...] = gh
    gh_low[...] = gh.astype(jnp.bfloat16)
    copies.wait()


def attend_backward_fast(
    groups, where, base, upstream, extra, stash, tables, pieces, in_width, after=()
):
    rows, model = upstream.shape
    bf, f32 = jnp.bfloat16, jnp.float32
    total = in_width + model + EXTRA
    shapes = [
        shape_of(rows, model, dtype=f32),
        shape_of(rows, model),
    ]
    shapes += [shape_of(model // 8 * count, total) for _, count in groups] * CORES

    def body(*refs):
        used = 3 + len(extra) + 12 + MATRIX_PIECES
        attend_backward_kernel(
            groups, len(extra), in_width, *refs[:used], *refs[used + len(after) :]
        )

    return pl.pallas_call(
        body,
        name="attend_backward",
        out_shape=shapes,
        in_specs=[scalar_spec()]
        + [whole_spec()] * (2 + len(extra) + 12)
        + [any_spec()] * (MATRIX_PIECES + len(after)),
        out_specs=[whole_spec()] * 2 + [any_spec()] * (len(shapes) - 2),
        scratch_shapes=[
            pltpu.VMEM((model, total), bf),
            pltpu.VMEM((model, total), bf),
            pltpu.VMEM((rows, model), bf),
            pltpu.VMEM((rows, in_width), bf),
            pltpu.VMEM((rows, model), f32),
            pltpu.SemaphoreType.DMA((MATRIX_COPIES + 32,)),
        ],
        compiler_params=pltpu.CompilerParams(vmem_limit_bytes=56 * MIB),
        cost_estimate=cost(4 * rows * model * total),
    )(where, base, upstream, *extra, *stash, *tables, *pieces, *after)


SHARES = ((0, 0, 3), (1, 0, 3), (2, 0, 3), (3, 0, 3))
WEIGHT_PIECES = CORES * len(SHARES)


def load_experts(copies, where, pieces, targets):
    at = 0
    for swapped in range(CORES):
        for k, first, count in SHARES:
            piece = pieces[at]
            at += 1
            _, experts, rows, share = piece.shape
            fsdp = lax.rem(where[0] - k + 4, 4) * CORES + (where[1] ^ swapped)
            row = pl.ds(pl.multiple_of(fsdp * rows, 16), rows)
            for i, target in enumerate(targets[first : first + count]):
                for e in range(experts):
                    copies.start(piece.at[i, e], target.at[row, pl.ds(e * share, share)])


def widen_tile(columns, share, width):
    lane = lax.broadcasted_iota(jnp.int32, (columns.shape[0], width), 1)
    wide = jnp.broadcast_to(columns[:, 0:1], lane.shape)
    for e in range(1, width // share):
        wide = jnp.where(lane >= e * share, columns[:, e : e + 1], wide)
    return wide


def start_rows(copies, pieces, rows_ref):
    at = 0
    for piece in pieces:
        rows = piece.shape[0]
        copies.start(piece, rows_ref.at[pl.ds(at, rows), :])
        at += rows


class Pool:
    def __init__(self, semaphores, used=0):
        self.semaphores = semaphores
        self.used = used

    def copy(self, source, target):
        self.used += 1
        return pltpu.make_async_copy(source, target, self.semaphores.at[self.used - 1])


def rows_at(ref, first, count):
    return ref.at[pl.ds(first, count), :]


def tile_loads(pool, pieces, x):
    n = pieces[0].shape[0]
    found = [[pool.copy(pieces[m], rows_at(x, m * n, n))] for m in range(3)]
    half = n // 2
    last = [pool.copy(pieces[3 + i], rows_at(x, 3 * n + i * half, half)) for i in range(2)]
    return found + [last]


def tile_slices(pool, source, target, n):
    return [[pool.copy(rows_at(source, m * n, n), rows_at(target, m * n, n))] for m in range(4)]


def tile_parts(pool, y, parts):
    n = parts[0].shape[0]
    half = n // 2
    own, one_head, two_tail, to_one, to_two = parts

    def copy(first, count, part, at=0):
        return pool.copy(rows_at(y, first, count), rows_at(part, at, count))

    return [
        [copy(0, n, own)],
        [copy(n, half, one_head), copy(n + half, half, to_one)],
        [copy(2 * n, half, to_two), copy(2 * n + half, half, two_tail)],
        [copy(3 * n, half, to_two, half), copy(3 * n + half, half, to_one, half)],
    ]


def for_tile(i, groups, act):
    for m in range(4):

        @pl.when(i == m)
        def _():
            for group in groups:
                for copy in group[m]:
                    act(copy)


def finish(groups):
    for group in groups:
        for copies in group:
            for copy in copies:
                copy.wait()


def part_rows(n):
    return [n, n // 2, n // 2, n, n]


def experts_forward_kernel(where, gates, *refs):
    pieces, weights, refs = refs[:5], refs[5 : 5 + WEIGHT_PIECES], refs[5 + WEIGHT_PIECES :]
    parts, x_out, g_out, u_out = refs[:5], *refs[5:8]
    x, y, g, u, w_gate, w_up, w_down, semaphores = refs[8:]
    n = pieces[0].shape[0]
    pool = Pool(semaphores)
    loads = tile_loads(pool, pieces, x)
    for group in loads:
        for copy in group:
            copy.start()
    copies = Copies(semaphores, pool.used)
    load_experts(copies, where, weights, (w_gate, w_up, w_down))
    pool.used = copies.used
    kept = tile_slices(pool, x, x_out, n)
    stores = [
        tile_parts(pool, y, parts),
        tile_slices(pool, g, g_out, n),
        tile_slices(pool, u, u_out, n),
    ]
    share = weights[0].shape[3]
    width = w_gate.shape[1]
    copies.wait()

    @pl.loop(0, 4)
    def _(i):
        for_tile(i, [loads], lambda copy: copy.wait())
        for_tile(i, [kept], lambda copy: copy.start())
        row = pl.ds(pl.multiple_of(i * n, n), n)
        gate_pre = contract(x[row, :], w_gate[...], PLAIN)
        up_pre = contract(x[row, :], w_up[...], PLAIN)
        g[row, :] = gate_pre
        u[row, :] = up_pre
        wide = widen_tile(gates[row, :], share, width)
        weighed = (gate_pre * jax.nn.sigmoid(gate_pre) * up_pre * wide).astype(jnp.bfloat16)
        y[row, :] = contract(weighed, w_down[...], ACROSS).astype(jnp.bfloat16)
        for_tile(i, stores, lambda copy: copy.start())

    finish([kept, *stores])


def experts_forward_fast(where, gates, pieces, weights, after=()):
    n, model = pieces[0].shape
    _, experts, _, share = weights[0].shape
    rows, width = 4 * n, experts * share
    bf, f32 = jnp.bfloat16, jnp.float32
    shapes = [shape_of(r, model) for r in part_rows(n)]
    shapes += [shape_of(rows, model)] + [shape_of(rows, width, dtype=f32)] * 2

    def body(*refs):
        used = 7 + WEIGHT_PIECES
        experts_forward_kernel(*refs[:used], *refs[used + len(after) :])

    return pl.pallas_call(
        body,
        name="experts_forward",
        out_shape=shapes,
        in_specs=[scalar_spec(), whole_spec()] + [any_spec()] * (5 + WEIGHT_PIECES + len(after)),
        out_specs=[any_spec()] * len(shapes),
        scratch_shapes=[
            pltpu.VMEM((rows, model), bf),
            pltpu.VMEM((rows, model), bf),
            pltpu.VMEM((rows, width), f32),
            pltpu.VMEM((rows, width), f32),
        ]
        + [pltpu.VMEM((model, width), bf)] * 3
        + [pltpu.SemaphoreType.DMA((24 * experts + 48,))],
        compiler_params=pltpu.CompilerParams(vmem_limit_bytes=48 * MIB),
        cost_estimate=cost(6 * rows * model * width),
    )(where, gates, *pieces, *weights, *after)


def experts_backward_kernel(where, gates, *refs):
    pieces, g_in, u_in = refs[:5], refs[5], refs[6]
    weights, refs = refs[7 : 7 + WEIGHT_PIECES], refs[7 + WEIGHT_PIECES :]
    parts, r_out, gg_out, gu_out, p_out = refs[:5], *refs[5:9]
    x, y, g, u, gg, gu, p, w_gate, w_up, w_down, semaphores = refs[9:]
    n = pieces[0].shape[0]
    pool = Pool(semaphores)
    loads = [
        tile_loads(pool, pieces, x),
        tile_slices(pool, g_in, g, n),
        tile_slices(pool, u_in, u, n),
    ]
    for group in loads[0]:
        for copy in group:
            copy.start()
    copies = Copies(semaphores, pool.used)
    load_experts(copies, where, weights, (w_gate, w_up, w_down))
    for loaded in loads[1:]:
        for group in loaded:
            for copy in group:
                copy.start()
    pool.used = copies.used
    kept = tile_slices(pool, x, r_out, n)
    stores = [
        tile_parts(pool, y, parts),
        tile_slices(pool, gg, gg_out, n),
        tile_slices(pool, gu, gu_out, n),
        tile_slices(pool, p, p_out, n),
    ]
    share = weights[0].shape[3]
    width = w_gate.shape[1]
    copies.wait()

    @pl.loop(0, 4)
    def _(i):
        for_tile(i, loads, lambda copy: copy.wait())
        for_tile(i, [kept], lambda copy: copy.start())
        row = pl.ds(pl.multiple_of(i * n, n), n)
        wide = widen_tile(gates[row, :], share, width)
        hidden_grad = contract(x[row, :], w_down[...], PLAIN) * wide
        gate_pre, up_pre = g[row, :], u[row, :]
        sig = jax.nn.sigmoid(gate_pre)
        active = gate_pre * sig
        p[row, :] = (active * up_pre * wide).astype(jnp.bfloat16)
        gate_grad = hidden_grad * up_pre * sig * (1.0 + gate_pre * (1.0 - sig))
        gg[row, :] = gate_grad.astype(jnp.bfloat16)
        gu[row, :] = (hidden_grad * active).astype(jnp.bfloat16)
        back = contract(gg[row, :], w_gate[...], ACROSS)
        back = back + contract(gu[row, :], w_up[...], ACROSS)
        y[row, :] = back.astype(jnp.bfloat16)
        for_tile(i, stores, lambda copy: copy.start())

    finish([kept, *stores])


def experts_backward_fast(where, gates, pieces, stash, weights, after=()):
    n, model = gates.shape[0] // 4, pieces[0].shape[1]
    _, experts, _, share = weights[0].shape
    rows, width = 4 * n, experts * share
    bf, f32 = jnp.bfloat16, jnp.float32
    shapes = [shape_of(r, model) for r in part_rows(n)]
    shapes += [shape_of(rows, model)] + [shape_of(rows, width)] * 3

    def body(*refs):
        used = 9 + WEIGHT_PIECES
        experts_backward_kernel(*refs[:used], *refs[used + len(after) :])

    return pl.pallas_call(
        body,
        name="experts_backward",
        out_shape=shapes,
        in_specs=[scalar_spec(), whole_spec()] + [any_spec()] * (7 + WEIGHT_PIECES + len(after)),
        out_specs=[any_spec()] * len(shapes),
        scratch_shapes=[
            pltpu.VMEM((rows, model), bf),
            pltpu.VMEM((rows, model), bf),
            pltpu.VMEM((rows, width), f32),
            pltpu.VMEM((rows, width), f32),
            pltpu.VMEM((rows, width), bf),
            pltpu.VMEM((rows, width), bf),
            pltpu.VMEM((rows, width), bf),
        ]
        + [pltpu.VMEM((model, width), bf)] * 3
        + [pltpu.SemaphoreType.DMA((24 * experts + 48,))],
        compiler_params=pltpu.CompilerParams(vmem_limit_bytes=52 * MIB),
        cost_estimate=cost(6 * rows * model * width),
    )(where, gates, *pieces, *stash, *weights, *after)


def weight_grads_kernel(experts, where, *refs):
    sources, mine, other = refs[:4], refs[4], refs[5]
    x, g, out, semaphores = refs[6:]
    copies = Copies(semaphores)
    for target, near, far in zip((x, g), sources[:2], sources[2:]):
        start_rows(copies, (near, far), target)
    copies.wait()
    band = x.shape[1] // 4
    rows = band // CORES
    share = g.shape[1] // experts

    @pl.loop(0, 4)
    def _(z):
        columns = pl.ds(pl.multiple_of(z * band, band), band)
        k = lax.rem(z - where[0] + 4, 4)
        grads = contract(x[:, columns], g[...], OUTER).astype(jnp.bfloat16)
        for core in range(CORES):
            for e in range(experts):
                out[core, k, e] = grads[
                    core * rows : (core + 1) * rows, e * share : (e + 1) * share
                ]

    copies.start(out.at[1 - where[1]], other)
    copies.start(out.at[where[1]], mine)
    copies.wait()


def weight_grads_fast(where, near, far, experts, after=()):
    model, width = near[0].shape[1], near[1].shape[1]
    count = near[0].shape[0] + far[0].shape[0]
    rows, share = model // 8, width // experts
    bf = jnp.bfloat16

    def body(*refs):
        weight_grads_kernel(experts, *refs[:5], *refs[5 + len(after) :])

    return pl.pallas_call(
        body,
        name="weight_grads",
        out_shape=[shape_of(4, experts, rows, share)] * 2,
        in_specs=[scalar_spec()] + [any_spec()] * (4 + len(after)),
        out_specs=[any_spec()] * 2,
        scratch_shapes=[
            pltpu.VMEM((count, model), bf),
            pltpu.VMEM((count, width), bf),
            pltpu.VMEM((CORES, 4, experts, rows, share), bf),
            pltpu.SemaphoreType.DMA((6,)),
        ],
        compiler_params=pltpu.CompilerParams(vmem_limit_bytes=40 * MIB),
        cost_estimate=cost(2 * count * model * width),
    )(where, *near, *far, *after)


def cut_kernel(where, w_gate, w_up, w_down, *outs):
    share = outs[0].shape[3]
    matrices = (w_gate, w_up, w_down)
    for (k, first, count), out in zip(SHARES, outs):
        columns = pl.ds(pl.multiple_of(lax.rem(where[0] + k, 4) * share, share), share)
        for i in range(count):
            out[i, 0] = matrices[first + i][0, 0, :, columns]


def cut_experts(where, weights, layer):
    _, experts, rows, hidden = weights[0].shape
    share = hidden // 4
    return pl.pallas_call(
        cut_kernel,
        name="cut_experts",
        grid=(experts,),
        out_shape=[shape_of(count, experts, rows, share) for _, _, count in SHARES],
        in_specs=[scalar_spec()]
        + [pl.BlockSpec((1, 1, rows, hidden), lambda e: (layer, e, 0, 0))] * 3,
        out_specs=[
            pl.BlockSpec((count, 1, rows, share), lambda e: (0, e, 0, 0)) for _, _, count in SHARES
        ],
    )(where, *weights)


def merge_grads_kernel(*refs):
    mine, arrived, outs = refs[:3], refs[3:6], refs[6:]
    for i in range(3):
        for k, out in enumerate(outs):
            total = mine[i][k, 0].astype(jnp.float32) + arrived[i][k, 0].astype(jnp.float32)
            out[i, 0] = total.astype(jnp.bfloat16)


def merge_grads(mine, arrived):
    planes, experts, rows, share = mine[0].shape
    return pl.pallas_call(
        merge_grads_kernel,
        name="merge_grads",
        grid=(experts,),
        out_shape=[shape_of(3, experts, rows, share)] * planes,
        in_specs=[pl.BlockSpec((planes, 1, rows, share), lambda e: (0, e, 0, 0))] * 6,
        out_specs=[pl.BlockSpec((3, 1, rows, share), lambda e: (0, e, 0, 0))] * planes,
    )(*mine, *arrived)


def join_kernel(layer, where, *refs):
    pieces, outs = refs[:4], refs[-3:]
    i = pl.program_id(0)
    share = pieces[0].shape[3]
    for index, out in enumerate(outs):

        @pl.when(i == index)
        def _():
            for k, piece in enumerate(pieces):
                columns = pl.ds(pl.multiple_of(lax.rem(where[0] - k + 4, 4) * share, share), share)
                out[0, :, :, columns] = piece[0].astype(jnp.float32)


def join_experts(where, pieces, layer, layers, earlier=None):
    mats, experts, rows, share = pieces[0].shape
    shape = shape_of(layers, experts, rows, 4 * share, dtype=jnp.float32)
    given = [] if earlier is None else list(earlier)

    return pl.pallas_call(
        functools.partial(join_kernel, layer),
        name="join_experts",
        grid=(mats,),
        out_shape=[shape] * mats,
        in_specs=[scalar_spec()]
        + [pl.BlockSpec((1, experts, rows, share), lambda i: (i, 0, 0, 0))] * 4
        + [any_spec()] * len(given),
        out_specs=[pl.BlockSpec((1, experts, rows, 4 * share), lambda i: (layer, 0, 0, 0))] * mats,
        input_output_aliases={5 + j: j for j in range(len(given))},
        compiler_params=pltpu.CompilerParams(vmem_limit_bytes=40 * MIB),
    )(where, *pieces, *given)


def tie(value, *events):
    flat, tree = jax.tree.flatten(value)
    held = lax.optimization_barrier((*flat, *events))
    return jax.tree.unflatten(tree, held[: len(flat)])


def spread_first(place, block):
    return [block, place.hop(block, flip=1), place.hop(block, flip=2)]


def spread_last(place, first, axis=0, cut=None):
    block, one, two = first
    cut = cut or block.shape[axis] // 2
    head = place.hop(lax.slice_in_dim(one, 0, cut, axis=axis), flip=2)
    tail = place.hop(lax.slice_in_dim(two, cut, None, axis=axis), flip=1)
    return [block, one, two, head, tail]


def spread_pieces(place, block):
    return spread_last(place, spread_first(place, block))


def up_hops(place, block):
    return [place.hop(block, up=k) for k in range(1, 4)]


def add_low(a, b):
    return (a.astype(jnp.float32) + b.astype(jnp.float32)).astype(a.dtype)


def fold_first(place, parts):
    own, one_head, two_tail, to_one, to_two = parts
    return own, one_head, two_tail, place.hop(to_one, flip=1), place.hop(to_two, flip=2)


def fold_sums(first):
    own, one_head, two_tail, by_one, by_two = first
    half = one_head.shape[0]
    return own, add_low(one_head, by_two[half:]), add_low(two_tail, by_one[half:]), by_one, by_two


def fold_start(place, parts):
    return fold_sums(fold_first(place, parts))


def fold_end(place, state):
    own, one_head, two_tail, by_one, by_two = state
    return own, place.hop(one_head, flip=1), place.hop(two_tail, flip=2), by_one, by_two


def add_pieces(own, one_head, two_tail, by_one, by_two, axis=0):
    wide = lambda value: value.astype(jnp.float32)
    half = one_head.shape[0]
    one = jnp.concatenate([one_head, by_one[:half]], axis=axis)
    two = jnp.concatenate([by_two[:half], two_tail], axis=axis)
    return wide(own) + wide(one) + wide(two)


def blocks_kernel(sides, own, one_head, two_tail, by_one, by_two, *outs):
    half = one_head.shape[0]
    for side, out in zip(sides, outs):
        terms = (two_tail, by_one) if side else (one_head, by_two)
        total = own[side * half : (side + 1) * half, :].astype(jnp.float32)
        for term in terms:
            total = total + term[:half, :].astype(jnp.float32)
        out[...] = total.astype(jnp.bfloat16)


def sum_blocks(ends, sides):
    half, model = ends[1].shape
    return pl.pallas_call(
        functools.partial(blocks_kernel, sides),
        name="sum_blocks",
        out_shape=[shape_of(half, model)] * len(sides),
        in_specs=[whole_spec()] * 5,
        out_specs=[whole_spec()] * len(sides),
    )(*ends)


def down_hops(place, blocks, first=1):
    return [place.hop(block, up=-first - n) for n, block in enumerate(blocks)]


def total_of(base, extra):
    total = base.astype(jnp.float32)
    for term in extra:
        total = total + term[: base.shape[0]].astype(jnp.float32)
    return total


def received(near_ends, arrived):
    own, one_head, _, _, by_two = near_ends
    return [own, *arrived, one_head, by_two]


def merge_kernel(cut, mine, arrived, own, one_head, two_tail, to_one, to_two):
    m = pl.program_id(0)
    total = (mine[...].astype(jnp.float32) + arrived[...].astype(jnp.float32)).astype(jnp.bfloat16)
    rows = total.shape[0]

    @pl.when(m == 0)
    def _():
        own[...] = total

    @pl.when(m == 1)
    def _():
        one_head[...] = total[:, :cut]
        to_one[:rows, :] = total[:, cut:]

    @pl.when(m == 2)
    def _():
        to_two[:rows, :] = total[:, :cut]
        two_tail[...] = total[:, cut:]

    @pl.when(m == 3)
    def _():
        to_two[rows:, :] = total[:, :cut]
        to_one[rows:, :] = total[:, cut:]


def merge_cores(mine, arrived, cut):
    rows, width = mine.shape[0] // 4, mine.shape[1]
    outs = [(rows, width), (rows, cut), (rows, width - cut), (2 * rows, width - cut), (2 * rows, cut)]
    return pl.pallas_call(
        functools.partial(merge_kernel, cut),
        name="merge_cores",
        grid=(4,),
        out_shape=[shape_of(*out) for out in outs],
        in_specs=[pl.BlockSpec((rows, width), lambda m: (m, 0))] * 2,
        out_specs=[pl.BlockSpec(out, lambda m: (0, 0)) for out in outs],
        compiler_params=pltpu.CompilerParams(vmem_limit_bytes=40 * MIB),
    )(mine, arrived)


def pack_kernel(*refs):
    layers = refs[0].shape[0]
    for l in range(layers):
        out = refs[l - layers]
        at = 0
        for ref in refs[:-layers]:
            width = ref.shape[2]
            out[:, at : at + width] = ref[l]
            at += width


def pack_matrices(*arrays):
    width = sum(a.shape[2] for a in arrays)
    layers, rows, _ = arrays[0].shape
    return pl.pallas_call(
        pack_kernel,
        name="pack_matrices",
        out_shape=[shape_of(rows, width)] * layers,
        in_specs=[whole_spec()] * len(arrays),
        out_specs=[whole_spec()] * layers,
    )(*arrays)


def sum_down(place, total, own):
    rows = own.shape[0]
    total = total.astype(jnp.bfloat16)
    for block in down_hops(place, [total[k * rows : (k + 1) * rows] for k in range(3)]):
        own = own + block.astype(jnp.float32)
    return own


def tables_of(length_row, rows):
    order = jnp.arange(rows, dtype=jnp.int32)
    index = jnp.arange(length_row.shape[0], dtype=jnp.int32)
    ends = jnp.sum(jnp.where(index[:, None] <= index[None, :], length_row[:, None], 0), axis=0)
    passed = order[:, None] >= ends[None, :]
    segment = jnp.sum(passed.astype(jnp.int32), axis=1)
    begin = jnp.sum(jnp.where(passed, length_row[None, :], 0), axis=1)
    cosine, sine = rope_tables(order - begin, HEAD_DIMENSION)
    allowed = (segment[:, None] == segment[None, :]) & (order[:, None] >= order[None, :])
    return (
        jnp.concatenate([cosine] * 4, axis=1),
        jnp.concatenate([-sine, sine] * 2, axis=1),
        allowed.astype(jnp.float32),
    )


def gate_rows_of(found):
    order = jnp.transpose(jnp.stack(found), (2, 1, 0, 4, 3))
    order = jnp.pad(order, ((0, 0),) * 4 + ((0, 8 - order.shape[4]),))
    return [
        (layer[:, :2].reshape(-1, 8), layer[:, 2:].reshape(-1, 8)) for layer in order
    ]


def shards_fast(
    tokens,
    lengths,
    routes,
    gates,
    cotangent,
    norm_attn,
    norm_ffn,
    query,
    key,
    value,
    output,
    w_gate,
    w_up,
    w_down,
):
    place = Place()
    where = jnp.stack([place.plane, place.core, place.column]).astype(jnp.int32)
    rows, model = tokens.shape
    layer_count, _, experts, _ = w_gate.shape
    expert_count = experts * place.columns
    in_width = query.shape[2] + key.shape[2] + value.shape[2]
    gains = jnp.stack([norm_attn, norm_ffn], axis=2)
    gains = jnp.pad(gains, ((0, 0), (0, 0), (0, EXTRA - 2)))
    packs = pack_matrices(query, key, value, output, gains)
    cut = packs[0].shape[1] // 2 // 128 * 128
    weights = [jnp.transpose(w, (0, 2, 1, 3)) for w in (w_gate, w_up, w_down)]
    tables = tables_of(lengths[0], rows)

    def line_of(block):
        return jnp.concatenate([block] + up_hops(place, block))

    cuts = [cut_experts(where, weights, l) for l in range(layer_count)]
    table = gate_table(*tie((routes, gates), packs[0]), expert_count)
    found = jnp.stack(spread_gates(place, table))
    found = [found] + up_hops(place, found)
    line = jnp.concatenate([packs[0]] + tie(up_hops(place, packs[0]), *[cut[0] for cut in cuts], found[0]))
    first = spread_first(place, line)
    cuts[0] = tie(cuts[0], line)
    own_swaps = [place.hop(tie(cut[0], line), swap=1) for cut in cuts]
    one = place.hop(cuts[0][1], up=1)
    swapped = [place.hop(line, swap=1)]
    two = place.hop(tie(cuts[0][2], line), up=2)
    first = tie(first, one, two, swapped[0], *own_swaps)
    three = place.hop(tie(cuts[0][3], first[0]), up=3)
    swapped += [place.hop(piece, swap=1) for piece in first[1:]]
    last_two = tie(spread_last(place, first, axis=1, cut=cut)[3:], three, *swapped[1:])
    matrices = [[*first, *last_two, *swapped, *[place.hop(p, swap=1) for p in last_two]]]
    shares = [cuts[0][0], one, two, three]
    share_swaps = [own_swaps[0], place.hop(one, swap=1), place.hop(two, swap=1)]

    def run_forward(l, which, pieces, bank, after=()):
        return experts_forward_fast(where, gate_rows[l][which], pieces, bank, after=after)

    def run_backward(l, which, pieces, stash, bank, after=()):
        return experts_backward_fast(where, gate_rows[l][which], pieces, stash, bank, after=after)

    def pairs_of(block, *events):
        ups = up_hops(place, block)
        near = spread_first(place, jnp.concatenate([block, ups[0]]))
        return near, ups[1:]

    base, extra = tokens.astype(jnp.float32), []
    stored = []
    for l in range(layer_count):
        more = l + 1 < layer_count
        after = list(share_swaps)
        outs = attend_forward_fast(where, base, extra, tables, matrices[l], in_width, after=after)
        h, m, nf = outs[:3]
        nf, late, found = tie((nf, shares[len(share_swaps) :], found))
        if l == 0:
            gate_rows = gate_rows_of(found)
        share_swaps += [place.hop(piece, swap=1) for piece in late]
        bank_l = [*shares[: 4 - len(late)], *late, *share_swaps]
        near, far = pairs_of(nf)
        near = spread_last(place, near)
        far = spread_first(place, jnp.concatenate(tie(far, near[3], near[4])))
        line = up_hops(place, tie(packs[l + 1] if more else cotangent, far[0]))
        y_near = run_forward(l, 0, near, bank_l)
        y_near, far, line[0], line[2] = tie((y_near, far, line[0], line[2]))
        far = spread_last(place, far)
        if more:
            near_first = fold_first(place, tie(y_near[:5], far[3], far[4]))
            y_far = run_forward(l, 1, far, bank_l, after=(y_near[0],))
            y_far, near_first, line[1] = tie((y_far, near_first, line[1]))
            one = place.hop(tie(cuts[l + 1][1], line[1]), up=1)
            far_first = fold_first(place, y_far[:5])
            near_ends = fold_end(place, fold_sums(near_first))
            far_first, one = tie((far_first, one))
            far_state = fold_sums(far_first)
            one_swap = place.hop(one, swap=1)
            far_ends, one_swap = tie((fold_end(place, far_state), one_swap), *near_ends[1:3])
            line = jnp.concatenate([packs[l + 1], *line])
            passing = spread_first(place, tie(line, far_ends[1], far_ends[2]))
            line_swap = place.hop(line, swap=1)
            arrived = down_hops(place, sum_blocks(near_ends, (1,)))
            blocks = sum_blocks(far_ends, (0, 1))
            arrived += down_hops(place, blocks, 2)
            passing = tie(passing, *arrived)
            two = place.hop(tie(cuts[l + 1][2], *arrived), up=2)
            swapped = [line_swap] + [place.hop(piece, swap=1) for piece in passing[1:]]
            last_two, two = tie((spread_last(place, passing, 1, cut)[3:], two), *swapped[1:])
            share_swaps = [own_swaps[l + 1], one_swap]
            ends = [place.hop(p, swap=1) for p in last_two]
            matrices.append([*passing, *last_two, *swapped, *ends])
            shares = [cuts[l + 1][0], one, two]
            shares.append(place.hop(tie(cuts[l + 1][3], last_two[0]), up=3))
            base, extra = m, received(near_ends, arrived)
        else:
            last_near = jnp.concatenate(tie([cotangent, line[0]], far[3], far[4]))
            last_near = spread_first(place, last_near)
            y_far = run_forward(l, 1, far, bank_l, after=(y_near[0],))
            y_far, last_near, line = tie((y_far, last_near, line))
            last_near = spread_last(place, last_near)
            last_far = spread_first(place, jnp.concatenate(tie(line[1:], *last_near[3:])))
        stored.append((h, outs, y_near, y_far, bank_l))

    upstream = cotangent
    zero = jnp.zeros((rows, model), jnp.bfloat16)
    sums = [None] * layer_count
    joined = None
    for l in reversed(range(layer_count)):
        h, outs, kept_near, kept_far, bank_l = stored[l]
        m, na, q, k, v, o, lse, gains = outs[1], *outs[3:]
        top = l + 1 == layer_count

        if top:
            b_near = run_backward(l, 0, last_near, kept_near[6:], bank_l, (y_far[0],))
            b_near, last_far = tie((b_near, last_far))
            far = spread_last(place, last_far)
            near_first = fold_first(place, tie(b_near[:5], far[3], far[4]))
            b_far = run_backward(l, 1, far, kept_far[6:], bank_l, (b_near[0],))
            b_far, near_first = tie((b_far, near_first))
            far_first = fold_first(place, b_far[:5])
        else:
            ups = up_hops(place, low)
            held = merge_grads(*held_parts)
            result_ends = fold_end(place, fold_sums(result_first))
            ups[0], held = tie((ups[0], held), *result_ends[1:3])
            near = jnp.concatenate([low, ups[0]])
            other_sum = place.hop(tie(other_one, near), swap=1)
            near = spread_last(place, spread_first(place, near))
            far = spread_first(place, jnp.concatenate(tie(ups[1:], near[3], near[4])))
            result_blocks = sum_blocks(result_ends, (0, 1))
            result_arrived = down_hops(place, tie(result_blocks, far[0]), 2)
            b_near = run_backward(l, 0, near, kept_near[6:], bank_l, (held[0],))
            b_near, far, result_arrived = tie((b_near, far, result_arrived))
            merged = merge_cores(mine_one, tie(other_sum, b_near[0]), cut)
            far = spread_last(place, far)
            came = [place.hop(tie(held[2], b_near[0]), up=2)]
            merged_first = fold_first(place, tie(merged, far[3], far[4]))
            b_far = run_backward(l, 1, far, kept_far[6:], bank_l, (b_near[0],))
            b_far, merged_first, came[0] = tie((b_far, merged_first, came[0]))
            far_first = fold_first(place, b_far[:5])
            came.insert(0, place.hop(tie(held[1], b_far[0]), up=1))
            came.append(place.hop(tie(held[3], b_far[0]), up=3))

        def weight_grads(i, after, near=(kept_near, b_near), far=(kept_far, b_far)):
            pick = lambda kept, found: ((kept[5], found[6 + i]) if i < 2 else (found[5], found[8]))
            return weight_grads_fast(where, pick(*near), pick(*far), experts, after=after)

        grads = [weight_grads(0, (b_far[0],))]
        if not top:
            grads.append(weight_grads(1, (grads[0][0], came[0])))
        far_state = fold_sums(tie(far_first, grads[-1][0]))
        if not top:
            near_first = fold_first(place, tie(b_near[:5], far_state[1], far_state[2]))
        grads.append(weight_grads(len(grads), (far_state[1], far_state[2])))
        swapped = [place.hop(other, swap=1) for _, other in grads[:-1]]
        far_ends = fold_end(place, far_state)
        far_ends, swapped = tie((far_ends, swapped), grads[-1][0])
        swapped.append(place.hop(grads[-1][1], swap=1))
        if not top:
            far_ends, came = tie((far_ends, came))
        event = far_state if top else far_ends
        near_state = fold_sums(tie(near_first, event[1], event[2]))
        near_ends = fold_end(place, near_state)
        arrived = down_hops(place, sum_blocks(near_ends, (1,)))
        blocks = sum_blocks(far_ends, (0, 1))
        arrived += down_hops(place, blocks, 2)
        if top:
            grads.append(weight_grads(2, (blocks[0],)))
            arrived, swapped = tie((arrived, swapped), grads[2][0])
            swapped.append(place.hop(tie(grads[2][1], *arrived), swap=1))
        if top:
            result_first = fold_first(place, tie(kept_far[:5], *arrived))
            result_near_first = fold_first(place, tie(kept_near[:5], *arrived))
            after = ()
            groups = ((0, 4),)
        else:
            held_came = [held[0], *came]
            total = merge_grads([mine for mine, _ in grads], swapped)
            merged_ends = fold_end(place, fold_sums(tie(merged_first, blocks[0], *near_ends[1:3])))
            one_total = add_pieces(*merged_ends, axis=1)
            shard = mine_one.shape[0] // 16
            low_total = one_total[shard:].astype(jnp.bfloat16)
            arrived = tie(arrived, total[0], low_total)
            low_total = tie(low_total, *arrived)
            one_arrived = down_hops(place, [low_total[n * shard :][:shard] for n in range(3)])
            result_near = fold_end(place, fold_sums(tie(result_near_first, *arrived)))
            after = (low_total, total[0])
            groups = ((1, 3), (0, 1))
        upstream, low, *partial = attend_backward_fast(
            groups,
            where,
            zero,
            upstream,
            received(near_ends, arrived),
            (h, m, na, q, k, v, o, lse, gains),
            tables,
            matrices[l],
            in_width,
            after=after,
        )
        if top:
            low, result_first, result_near_first = tie((low, result_first, result_near_first))
            held_parts = ([mine for mine, _ in grads], swapped)
            other_one, mine_one = partial
        else:
            partial, result_near = tie((partial, result_near))
    partial, one_arrived = tie((partial, one_arrived))
    sums[1] = one_total[:shard]
    for block in one_arrived:
        sums[1] = sums[1] + block.astype(jnp.float32)
    other_far, other_near, mine_far, mine_near = partial
    other_far, other_near = place.hop(other_far, swap=1), place.hop(other_near, swap=1)
    merged_far = merge_cores(mine_far, other_far, cut)
    came = [place.hop(tie(total[k], upstream), up=k) for k in (1, 2, 3)]
    merged_far, came[0] = tie((merged_far, came[0]))
    merged_near = merge_cores(mine_near, other_near, cut)
    far_first = fold_first(place, merged_far)
    joined = join_experts(where, tie(held_came, merged_far[0]), 1, layer_count, None)
    far_state = fold_sums(tie(far_first, joined[0]))
    near_first = fold_first(place, tie(merged_near, far_state[1], far_state[2]))
    near_ends = fold_end(place, fold_sums(near_first))
    far_ends = tie(fold_end(place, far_state), *came)
    far_total = add_pieces(*far_ends, axis=1)
    sums[0] = sum_down(place, far_total, add_pieces(*near_ends, axis=1))
    joined = join_experts(where, [total[0], *came], 0, layer_count, joined)
    last_block = down_hops(place, sum_blocks(tie(result_near, far_state[1]), (1,)))
    result = total_of(stored[-1][1][1], received(result_near, last_block + result_arrived))
    result = result.astype(jnp.bfloat16)
    sums = jnp.stack(sums)
    gain_sums = sums[:, :, in_width + model :]
    starts = (0, query.shape[2], query.shape[2] + key.shape[2], in_width, in_width + model)
    return (
        result,
        upstream,
        gain_sums[:, :, 0],
        gain_sums[:, :, 1],
        *[sums[:, :, a:b] for a, b in zip(starts, starts[1:])],
        *[jnp.transpose(grads, (0, 2, 1, 3)) for grads in joined],
    )


def solution(mesh):
    rows = P(AXES, None)
    layered = P(None, AXES, None)
    expert = P(None, "fsdp", "expert", None)
    gain = P(None, AXES)
    regular = mesh.shape["fsdp"] == 8 and mesh.shape["expert"] == 4
    return jax.shard_map(
        shards_fast if regular else shards,
        mesh=mesh,
        in_specs=(rows, rows, layered, layered, rows, gain, gain)
        + (layered,) * 4
        + (expert,) * 3,
        out_specs=(rows, rows, gain, gain) + (layered,) * 4 + (expert,) * 3,
        check_vma=False,
    )
```

```python
import functools
import math

import jax
import jax.numpy as jnp
from jax import lax
from jax.experimental import pallas as pl
from jax.experimental.pallas import tpu as pltpu
from jax.sharding import PartitionSpec as P

QUERY_HEADS = 24
KEY_VALUE_HEADS = 8
HEAD_DIMENSION = 64
CORES = 2

NORM_EPS = 1e-06
MASKED = -1000000000.0
AXES = ("fsdp", "expert")


class Place:
    def __init__(self):
        self.planes = lax.axis_size("fsdp") // CORES
        self.columns = lax.axis_size("expert")
        fsdp = lax.axis_index("fsdp")
        self.plane = fsdp // CORES
        self.core = fsdp % CORES
        self.column = lax.axis_index("expert")

    def hop(self, value, up=0, flip=0, swap=0):
        pairs = []
        for plane in range(self.planes):
            for core in range(CORES):
                for column in range(self.columns):
                    source = (plane * CORES + core) * self.columns + column
                    target = ((plane + up) % self.planes * CORES + (core ^ swap)) * self.columns
                    pairs.append((source, target + (column ^ flip)))
        return lax.ppermute(value, AXES, pairs)


def spread(place, block):
    if place.columns != 4:
        return [block] + [place.hop(block, flip=m) for m in range(1, place.columns)]
    half = block.shape[1] // 2
    one = place.hop(block, flip=1)
    two = place.hop(block, flip=2)
    head = place.hop(one[:, :half], flip=2)
    tail = place.hop(two[:, half:], flip=1)
    return [block, one, two, jnp.concatenate([head, tail], axis=1)]


def gather_tokens(place, block):
    own = block[None]
    others = jnp.stack([place.hop(block, up=k) for k in range(1, place.planes)])
    near = spread(place, own)
    far = spread(place, others)
    return [jnp.concatenate([a, b], axis=0) for a, b in zip(near, far)]


def fold(place, parts):
    wide = lambda value: value.astype(jnp.float32)
    if place.columns != 4:
        total = wide(parts[0])
        for m in range(1, place.columns):
            total = total + wide(place.hop(parts[m], flip=m))
        return total
    half = parts[0].shape[1] // 2
    head = place.hop(parts[3][:, :half], flip=2)
    tail = place.hop(parts[3][:, half:], flip=1)
    one_tail = place.hop(parts[1][:, half:], flip=1)
    two_head = place.hop(parts[2][:, :half], flip=2)
    one_head = place.hop((wide(parts[1][:, :half]) + wide(head)).astype(parts[1].dtype), flip=1)
    two_tail = place.hop((wide(parts[2][:, half:]) + wide(tail)).astype(parts[2].dtype), flip=2)
    upper = wide(parts[0][:, :half]) + wide(one_head) + wide(two_head)
    lower = wide(parts[0][:, half:]) + wide(one_tail) + wide(two_tail)
    return jnp.concatenate([upper, lower], axis=1)


def scatter_sums(place, parts):
    far = fold(place, [part[1:] for part in parts]).astype(parts[0].dtype)
    arrived = [place.hop(far[k - 1], up=-k) for k in range(1, place.planes)]
    total = fold(place, [part[:1] for part in parts])[0]
    for piece in arrived:
        total = total + piece.astype(jnp.float32)
    return total


def gate_table(routes, gates, expert_count):
    names = jnp.arange(expert_count, dtype=jnp.int32)
    chosen = routes[:, None, :, :] == names[None, :, None, None]
    return jnp.sum(jnp.where(chosen, gates[:, None, :, :], 0.0), axis=3)


def spread_gates(place, table):
    axis = table.ndim - 2
    owned = table.shape[axis] // place.columns
    found = []
    for m in range(place.columns):
        start = (place.column ^ m) * owned
        piece = lax.dynamic_slice_in_dim(table, start, owned, axis=axis)
        found.append(place.hop(piece, flip=m) if m else piece)
    return found


def gather_gates(place, routes, gates, expert_count):
    table = gate_table(routes, gates, expert_count)
    line = jnp.stack([table] + [place.hop(table, up=k) for k in range(1, place.planes)])
    return spread_gates(place, line)


def gather_experts(place, weights):
    rows, experts, hidden = weights[0].shape
    share = hidden // place.planes

    def cut(plane):
        pieces = [lax.dynamic_slice_in_dim(w, plane * share, share, axis=2) for w in weights]
        return jnp.stack([p.reshape(rows, experts * share) for p in pieces])

    own = [cut(place.plane)]
    for k in range(1, place.planes):
        own.append(place.hop(cut((place.plane + k) % place.planes), up=k))
    own = jnp.stack(own)
    sibling = place.hop(own, swap=1)
    both = jnp.concatenate([own, sibling])
    shard = jnp.arange(place.planes * CORES)
    index = ((shard % CORES) ^ place.core) * place.planes
    index = index + (place.plane - shard // CORES) % place.planes
    return [
        jnp.take(both[:, i], index, axis=0).reshape(-1, experts * share)
        for i in range(len(weights))
    ]


def scatter_experts(place, grads, experts):
    features, width = grads[0].shape
    rows = features // (place.planes * CORES)
    share = width // experts
    shape = (place.planes, CORES, rows, width)
    stacked = jnp.stack([g.reshape(shape) for g in grads], axis=1)
    mine = lax.dynamic_index_in_dim(stacked, place.core, axis=2, keepdims=False)
    others = lax.dynamic_index_in_dim(stacked, 1 - place.core, axis=2, keepdims=False)
    arrived = place.hop(others.astype(jnp.bfloat16), swap=1)
    total = (mine + arrived.astype(jnp.float32)).astype(jnp.bfloat16)
    pieces = [lax.dynamic_index_in_dim(total, place.plane, axis=0, keepdims=False)]
    for k in range(1, place.planes):
        target = (place.plane + k) % place.planes
        piece = lax.dynamic_index_in_dim(total, target, axis=0, keepdims=False)
        pieces.append(place.hop(piece, up=k))
    index = (place.plane - jnp.arange(place.planes)) % place.planes
    ordered = jnp.take(jnp.stack(pieces), index, axis=0)
    ordered = ordered.reshape(place.planes, len(grads), rows, experts, share)
    ordered = jnp.transpose(ordered, (1, 2, 3, 0, 4)).reshape(len(grads), rows, experts, -1)
    return [ordered[i].astype(jnp.float32) for i in range(len(grads))]


def positions(length_row, count_of_rows):
    ends = jnp.cumsum(length_row)
    token_order = jnp.arange(count_of_rows, dtype=jnp.int32)
    passed = token_order[:, None] >= ends[None, :]
    segment = jnp.sum(passed.astype(jnp.int32), axis=1)
    before = jnp.sum(jnp.where(passed, length_row[None, :], 0), axis=1)
    return (segment, token_order - before)


def rope_tables(seq_place, head_width):
    half_width = head_width // 2
    freq_table = jnp.exp(
        jnp.arange(half_width, dtype=jnp.float32) * (-2.0 * math.log(10000.0) / head_width)
    )
    angles = seq_place.astype(jnp.float32)[:, None] * freq_table[None, :]
    return (jnp.cos(angles), jnp.sin(angles))


def apply_rotation(vector, cosine_table, sine_table):
    half_width = vector.shape[-1] // 2
    former = vector[..., :half_width]
    latter = vector[..., half_width:]
    cos_wide = cosine_table[:, None, :]
    sin_wide = sine_table[:, None, :]
    return jnp.concatenate(
        [former * cos_wide - latter * sin_wide, latter * cos_wide + former * sin_wide], axis=-1
    )


def reverse_rotation(vector, cosine_table, sine_table):
    return apply_rotation(vector, cosine_table, -sine_table)


def rms_forward(residual, norm_gain):
    inverse = lax.rsqrt(jnp.mean(residual * residual, axis=-1, keepdims=True) + NORM_EPS)
    return (inverse, (residual * inverse * norm_gain).astype(jnp.bfloat16))


def rms_backward(residual, inverse, norm_gain, upstream):
    gain_grad = jnp.sum(upstream * residual * inverse, axis=0)
    scaled = upstream * norm_gain
    inner = jnp.mean(scaled * residual, axis=-1, keepdims=True)
    return (gain_grad, inverse * scaled - residual * inverse * inverse * inverse * inner)


def score_block(rotated_query, turned_k, allowed):
    scores = jnp.einsum(
        "qhgd,khd->hgqk", rotated_query, turned_k, preferred_element_type=jnp.float32
    ) * HEAD_DIMENSION ** (-0.5)
    return jnp.where(allowed, scores, MASKED)


def attend_forward(residual, allowed, tables, gain, matrices):
    w_in, w_output = matrices
    count_of_rows = residual.shape[0]
    query_width = QUERY_HEADS * HEAD_DIMENSION
    key_width = KEY_VALUE_HEADS * HEAD_DIMENSION
    inverse, normalized_input = rms_forward(residual, gain)
    projected = jnp.dot(normalized_input, w_in, preferred_element_type=jnp.float32)
    query_unrotated = projected[:, :query_width].reshape(count_of_rows, QUERY_HEADS, -1)
    key_unrotated = projected[:, query_width : query_width + key_width]
    key_unrotated = key_unrotated.reshape(count_of_rows, KEY_VALUE_HEADS, -1)
    value_rows = projected[:, query_width + key_width :].astype(jnp.bfloat16)
    value_rows = value_rows.reshape(count_of_rows, KEY_VALUE_HEADS, -1)
    rotated_query = (
        apply_rotation(query_unrotated, *tables)
        .astype(jnp.bfloat16)
        .reshape(count_of_rows, KEY_VALUE_HEADS, QUERY_HEADS // KEY_VALUE_HEADS, HEAD_DIMENSION)
    )
    turned_k = apply_rotation(key_unrotated, *tables).astype(jnp.bfloat16)
    scores = score_block(rotated_query, turned_k, allowed)
    row_top = jnp.max(scores, axis=-1, keepdims=True)
    exp_scores = jnp.exp(scores - row_top)
    row_total = jnp.sum(exp_scores, axis=-1, keepdims=True)
    attn_probs = (exp_scores / row_total).astype(jnp.bfloat16)
    log_total = row_top + jnp.log(row_total)
    mixed_heads = jnp.einsum(
        "hgqk,khd->qhgd", attn_probs, value_rows, preferred_element_type=jnp.float32
    )
    mixed_heads = mixed_heads.astype(jnp.bfloat16).reshape(count_of_rows, query_width)
    attn_out = jnp.dot(mixed_heads, w_output, preferred_element_type=jnp.float32)
    return (
        residual + attn_out,
        (inverse, normalized_input, rotated_query, turned_k, value_rows, log_total, mixed_heads),
    )


def attend_backward(residual, allowed, tables, gain, matrices, stash, upstream):
    w_in, w_output = matrices
    inverse, normalized_input, rotated_query, turned_k, value_rows, log_total, mixed_heads = stash
    count_of_rows = residual.shape[0]
    branch_grad = upstream.astype(jnp.bfloat16)
    grad_wo = jnp.einsum("td,te->de", mixed_heads, branch_grad, preferred_element_type=jnp.float32)
    mixed_gradient = jnp.einsum(
        "te,de->td", branch_grad, w_output, preferred_element_type=jnp.float32
    )
    mixed_gradient = mixed_gradient.astype(jnp.bfloat16).reshape(
        count_of_rows, KEY_VALUE_HEADS, QUERY_HEADS // KEY_VALUE_HEADS, HEAD_DIMENSION
    )
    attn_probs = jnp.exp(score_block(rotated_query, turned_k, allowed) - log_total)
    value_rows_gradient = jnp.einsum(
        "hgqk,qhgd->khd",
        attn_probs.astype(jnp.bfloat16),
        mixed_gradient,
        preferred_element_type=jnp.float32,
    )
    value_rows_gradient = value_rows_gradient.astype(jnp.bfloat16).reshape(count_of_rows, -1)
    grad_probs = jnp.einsum(
        "qhgd,khd->hgqk", mixed_gradient, value_rows, preferred_element_type=jnp.float32
    )
    grad_scores = attn_probs * (
        grad_probs - jnp.sum(attn_probs * grad_probs, axis=-1, keepdims=True)
    )
    grad_scores = grad_scores.astype(jnp.bfloat16)
    grad_tq = jnp.einsum(
        "hgqk,khd->qhgd", grad_scores, turned_k, preferred_element_type=jnp.float32
    ) * HEAD_DIMENSION ** (-0.5)
    turned_key_gradient = jnp.einsum(
        "hgqk,qhgd->khd", grad_scores, rotated_query, preferred_element_type=jnp.float32
    ) * HEAD_DIMENSION ** (-0.5)
    grad_query = reverse_rotation(
        grad_tq.reshape(count_of_rows, QUERY_HEADS, HEAD_DIMENSION), *tables
    )
    grad_query = grad_query.astype(jnp.bfloat16).reshape(count_of_rows, -1)
    grad_key = reverse_rotation(turned_key_gradient, *tables).astype(jnp.bfloat16)
    grad_key = grad_key.reshape(count_of_rows, -1)
    grad_in = jnp.concatenate([grad_query, grad_key, value_rows_gradient], axis=1)
    grad_w_in = jnp.einsum("td,te->de", normalized_input, grad_in, preferred_element_type=jnp.float32)
    grad_normed = jnp.einsum("te,de->td", grad_in, w_in, preferred_element_type=jnp.float32)
    gain_grad, residual_grad = rms_backward(residual, inverse, gain, grad_normed)
    return (upstream + residual_grad, gain_grad, grad_w_in, grad_wo)


def widen(gate_columns, share):
    return jnp.repeat(gate_columns, share, axis=1)


def experts_forward(place, middle, gain, gate_parts, weights):
    w_gate, w_up, w_down = weights
    share = w_gate.shape[1] // gate_parts[0].shape[1]
    model_width = middle.shape[1]
    inverse, normalized_input = rms_forward(middle, gain)
    chunks = gather_tokens(place, normalized_input)
    parts, kept = [], []
    for chunk, gate_columns in zip(chunks, gate_parts):
        rows = chunk.reshape(-1, model_width)
        gate_pre = jnp.dot(rows, w_gate, preferred_element_type=jnp.float32)
        up_pre = jnp.dot(rows, w_up, preferred_element_type=jnp.float32)
        weighed = gate_pre * jax.nn.sigmoid(gate_pre) * up_pre * widen(gate_columns, share)
        weighed = weighed.astype(jnp.bfloat16)
        produced = lax.dot_general(
            weighed, w_down, (((1,), (1,)), ((), ())), preferred_element_type=jnp.float32
        )
        parts.append(produced.astype(jnp.bfloat16).reshape(chunk.shape))
        kept.append((rows, gate_pre, up_pre, weighed))
    return (middle + scatter_sums(place, parts), (inverse, kept))


def experts_backward(place, middle, gain, gate_parts, weights, stash, upstream, chunks):
    w_gate, w_up, w_down = weights
    share = w_gate.shape[1] // gate_parts[0].shape[1]
    model_width = middle.shape[1]
    inverse, kept = stash
    parts, gate_grads, up_grads, row_grads = [], [], [], []
    for chunk, gate_columns, (rows, gate_pre, up_pre, weighed) in zip(chunks, gate_parts, kept):
        grads = chunk.reshape(-1, model_width)
        hidden_grad = jnp.dot(grads, w_down, preferred_element_type=jnp.float32)
        hidden_grad = hidden_grad * widen(gate_columns, share)
        gate_sig = jax.nn.sigmoid(gate_pre)
        gate_grad = hidden_grad * up_pre * gate_sig * (1.0 + gate_pre * (1.0 - gate_sig))
        gate_grad = gate_grad.astype(jnp.bfloat16)
        up_grad = (hidden_grad * gate_pre * gate_sig).astype(jnp.bfloat16)
        back = (((1,), (1,)), ((), ()))
        produced = lax.dot_general(gate_grad, w_gate, back, preferred_element_type=jnp.float32)
        produced = produced + lax.dot_general(
            up_grad, w_up, back, preferred_element_type=jnp.float32
        )
        parts.append(produced.astype(jnp.bfloat16).reshape(chunk.shape))
        gate_grads.append(gate_grad)
        up_grads.append(up_grad)
        row_grads.append(grads)
    normed_grad = scatter_sums(place, parts)
    rows = jnp.concatenate([entry[0] for entry in kept])
    weighed = jnp.concatenate([entry[3] for entry in kept])
    outer = (((0,), (0,)), ((), ()))
    weight_grads = [
        lax.dot_general(a, b, outer, preferred_element_type=jnp.float32)
        for a, b in (
            (rows, jnp.concatenate(gate_grads)),
            (rows, jnp.concatenate(up_grads)),
            (jnp.concatenate(row_grads), weighed),
        )
    ]
    gain_grad, middle_grad = rms_backward(middle, inverse, gain, normed_grad)
    return (upstream + middle_grad, gain_grad, weight_grads)


def shards(
    tokens,
    lengths,
    routes,
    gates,
    cotangent,
    norm_attn,
    norm_ffn,
    query,
    key,
    value,
    output,
    w_gate,
    w_up,
    w_down,
):
    place = Place()
    token_rows = tokens.shape[0]
    layer_count, _, experts, _ = w_gate.shape
    expert_count = experts * place.columns
    in_width = query.shape[2] + key.shape[2] + value.shape[2]
    segment, seq_place = positions(lengths[0], token_rows)
    tables = rope_tables(seq_place, HEAD_DIMENSION)
    token_order = jnp.arange(token_rows, dtype=jnp.int32)
    allowed = (segment[:, None] == segment[None, :]) & (
        token_order[:, None] >= token_order[None, :]
    )
    gains = jnp.concatenate([norm_attn, norm_ffn]).T
    packs = []
    for l in range(layer_count):
        pack = [query[l], key[l], value[l], output[l]]
        if l == 0:
            pack.append(jnp.pad(gains, ((0, 0), (0, 128 - gains.shape[1]))))
        packs.append(jnp.concatenate(pack, axis=1))
    full = lax.all_gather(packs[0], AXES, axis=0, tiled=True)
    gains = full[:, in_width + output.shape[2] :].T[: 2 * layer_count].astype(jnp.float32)
    gate_rows = gather_gates(place, routes, gates, expert_count)
    gate_parts = [
        [
            jnp.transpose(piece[:, l], (0, 2, 1)).reshape(-1, experts)
            for piece in gate_rows
        ]
        for l in range(layer_count)
    ]
    expert_weights = gather_experts(place, [w_gate[0], w_up[0], w_down[0]])
    last_grads = None

    residual = tokens.astype(jnp.float32)
    matrices, weights, stored = [], [], []
    for l in range(layer_count):
        matrices.append((full[:, :in_width], full[:, in_width : in_width + output.shape[2]]))
        weights.append(expert_weights)
        layer_input = residual
        middle, attn_stash = attend_forward(layer_input, allowed, tables, gains[l], matrices[l])
        if l + 1 < layer_count:
            held, pack, *shares = lax.optimization_barrier(
                (middle, packs[l + 1], w_gate[l + 1], w_up[l + 1], w_down[l + 1])
            )
            middle = held
            full = lax.all_gather(pack, AXES, axis=0, tiled=True)
            expert_weights = gather_experts(place, shares)
        residual, moe_stash = experts_forward(
            place, middle, gains[layer_count + l], gate_parts[l], weights[l]
        )
        if l + 2 == layer_count or layer_count == 1:
            held, last = lax.optimization_barrier((residual, cotangent))
            residual = held
            last_grads = gather_tokens(place, last)
        stored.append((layer_input, middle, attn_stash, moe_stash))
    result = residual.astype(jnp.bfloat16)

    upstream = cotangent.astype(jnp.float32)
    in_grads, out_grads = [None] * layer_count, [None] * layer_count
    gain_grads = [None] * (2 * layer_count)
    expert_grads = [None] * layer_count
    for l in reversed(range(layer_count)):
        layer_input, middle, attn_stash, moe_stash = stored[l]
        chunks = last_grads
        if l + 1 < layer_count:
            chunks = gather_tokens(place, upstream.astype(jnp.bfloat16))
        upstream, gain_grads[layer_count + l], weight_grads = experts_backward(
            place,
            middle,
            gains[layer_count + l],
            gate_parts[l],
            weights[l],
            moe_stash,
            upstream,
            chunks,
        )
        expert_grads[l] = scatter_experts(place, weight_grads, experts)
        upstream, gain_grads[l], grad_w_in, grad_wo = attend_backward(
            layer_input, allowed, tables, gains[l], matrices[l], attn_stash, upstream
        )
        summed = lax.psum_scatter(
            jnp.concatenate([grad_w_in, grad_wo], axis=1).astype(jnp.bfloat16),
            AXES,
            scatter_dimension=0,
            tiled=True,
        ).astype(jnp.float32)
        in_grads[l], out_grads[l] = summed[:, :in_width], summed[:, in_width:]
    gain_sums = lax.psum_scatter(jnp.stack(gain_grads), AXES, scatter_dimension=1, tiled=True)
    in_grads = jnp.stack(in_grads)
    key_start, value_start = query.shape[2], query.shape[2] + key.shape[2]
    return (
        result,
        upstream,
        gain_sums[:layer_count],
        gain_sums[layer_count:],
        in_grads[:, :, :key_start],
        in_grads[:, :, key_start:value_start],
        in_grads[:, :, value_start:],
        jnp.stack(out_grads),
        jnp.stack([entry[0] for entry in expert_grads]),
        jnp.stack([entry[1] for entry in expert_grads]),
        jnp.stack([entry[2] for entry in expert_grads]),
    )


HEADS_PER_TURN = 6
LANES = 128
EXTRA = 128
HALF = 64
MIB = 1 << 20
COST_PART = 16


def cost(flops):
    return pl.CostEstimate(flops=flops // COST_PART, bytes_accessed=0, transcendentals=0)


def any_spec():
    return pl.BlockSpec(memory_space=pl.ANY)


def whole_spec():
    return pl.BlockSpec(memory_space=pltpu.VMEM)


def scalar_spec():
    return pl.BlockSpec(memory_space=pltpu.SMEM)


def shape_of(*dims, dtype=jnp.bfloat16):
    return jax.ShapeDtypeStruct(dims, dtype)


class Copies:
    def __init__(self, semaphores, first=0):
        self.semaphores = semaphores
        self.used = first
        self.open = []

    def start(self, source, target):
        copy = pltpu.make_async_copy(source, target, self.semaphores.at[self.used])
        self.used += 1
        copy.start()
        self.open.append(copy)

    def wait(self):
        for copy in self.open:
            copy.wait()
        self.open = []


def shard_row(where, swapped, m, k, rows):
    plane = lax.rem(where[0] - k + 4, 4)
    fsdp = plane * CORES + (where[1] ^ swapped)
    return pl.multiple_of((fsdp * 4 + (where[2] ^ m)) * rows, 16)


MATRIX_PIECES = 10
MATRIX_COPIES = 40


def load_columns(copies, where, pieces, full, low, high):
    rows, cut = pieces[0].shape[0] // 4, pieces[3].shape[1]
    spans = ((0, 0, full.shape[1]), (1, 0, full.shape[1]), (2, 0, full.shape[1]), (3, 0, cut))
    spans += ((3, cut, full.shape[1]),)
    for swapped in range(CORES):
        for index, (m, first, last) in enumerate(spans):
            begin, end = max(low, first), min(high, last)
            if begin >= end:
                continue
            for k in range(4):
                row = shard_row(where, swapped, m, k, rows)
                copies.start(
                    pieces[swapped * 5 + index].at[
                        pl.ds(k * rows, rows), pl.ds(begin - first, end - begin)
                    ],
                    full.at[pl.ds(row, rows), pl.ds(begin, end - begin)],
                )


def half_swap(x):
    lane = lax.broadcasted_iota(jnp.int32, x.shape, 1)
    return jnp.where(lane % 64 < 32, pltpu.roll(x, 96, 1), pltpu.roll(x, 32, 1))


def both_sides(pair, side):
    lane = lax.broadcasted_iota(jnp.int32, pair.shape, 1)
    wide = pair.astype(jnp.float32)
    here = jnp.where(lane // 64 == side, wide, 0.0)
    there = pltpu.roll(here, 64, 1)
    here, there = here.astype(jnp.bfloat16), there.astype(jnp.bfloat16)
    return (here, there) if side == 0 else (there, here)


def merge_sides(even, odd, side):
    lane = lax.broadcasted_iota(jnp.int32, even.shape, 1)
    if side == 0:
        return jnp.where(lane < 64, even + pltpu.roll(odd, 64, 1), 0.0)
    return jnp.where(lane < 64, 0.0, odd + pltpu.roll(even, 64, 1))


def contract(a, b, dims):
    return lax.dot_general(a, b, (dims, ((), ())), preferred_element_type=jnp.float32)


PLAIN = ((1,), (0,))
ACROSS = ((1,), (1,))
OUTER = ((0,), (0,))


def read_sum(base, extra):
    total = base[...].astype(jnp.float32)
    for term in extra:
        total = total + term[pl.ds(0, total.shape[0]), :].astype(jnp.float32)
    return total


def attend_forward_kernel(terms, width, where, base, *refs):
    refs = list(refs)
    extra = [refs.pop(0) for _ in range(terms)]
    cosine, sine, allowed = refs[:3]
    pieces = refs[3 : 3 + MATRIX_PIECES]
    refs = refs[3 + MATRIX_PIECES :]
    h_out, m_out, nf_out, na_out, q_out, k_out, v_out, o_out, lse_out, gain_out = refs[:10]
    full, proj, mixed, semaphores = refs[10:]
    model = full.shape[0]
    in_width = width
    copies = Copies(semaphores)
    load_columns(copies, where, pieces, full, 0, in_width)
    load_columns(copies, where, pieces, full, in_width + model, full.shape[1])
    later = Copies(semaphores, copies.used)
    load_columns(later, where, pieces, full, in_width, in_width + model)
    h = read_sum(base, extra)
    h_out[...] = h
    inverse = lax.rsqrt(jnp.mean(h * h, axis=1, keepdims=True) + NORM_EPS)
    key_start = model
    value_start = model + (in_width - model) // 2
    copies.wait()
    gains = full[:, pl.ds(in_width + model, EXTRA)].astype(jnp.float32).T
    gain_out[...] = gains[:8]
    na_out[...] = (h * inverse * gains[0:1]).astype(jnp.bfloat16)
    step = 512

    @pl.loop(0, in_width // step)
    def _(i):
        columns = pl.ds(pl.multiple_of(i * step, step), step)
        proj[:, columns] = contract(na_out[...], full[:, columns], PLAIN)

    cos, sin = cosine[...], sine[...]

    @pl.loop(0, key_start // LANES)
    def _(i):
        columns = pl.ds(pl.multiple_of(i * LANES, LANES), LANES)
        x = proj[:, columns]
        q_out[:, columns] = (x * cos + half_swap(x) * sin).astype(jnp.bfloat16)

    @pl.loop(0, (value_start - key_start) // LANES)
    def _(i):
        start = pl.multiple_of(i * LANES, LANES)
        x = proj[:, pl.ds(key_start + start, LANES)]
        k_out[:, pl.ds(start, LANES)] = (x * cos + half_swap(x) * sin).astype(jnp.bfloat16)

    v_out[...] = proj[:, value_start:in_width].astype(jnp.bfloat16)
    lse_out[...] = jnp.zeros_like(lse_out)
    open_keys = allowed[...] > 0.5
    lane = lax.broadcasted_iota(jnp.int32, open_keys.shape, 1)

    @pl.loop(0, KEY_VALUE_HEADS // 2)
    def _(turn):
        pair = pl.ds(pl.multiple_of(turn * LANES, LANES), LANES)
        keys = [both_sides(k_out[:, pair], side) for side in range(2)]
        values = [both_sides(v_out[:, pair], side) for side in range(2)]
        lse = lse_out[...]
        for group in range(HEADS_PER_TURN // 2):
            columns = pl.ds(
                pl.multiple_of(turn * (HEADS_PER_TURN * 64) + group * LANES, LANES), LANES
            )
            total = jnp.zeros((h.shape[0], LANES), jnp.float32)
            for side in range(2):
                head = group * 2 + side
                scores = contract(q_out[:, columns], keys[head // 3][side], ACROSS)
                scores = jnp.where(open_keys, scores * HEAD_DIMENSION ** (-0.5), MASKED)
                top = jnp.max(scores, axis=1, keepdims=True)
                weights = jnp.exp(scores - top)
                row_total = jnp.sum(weights, axis=1, keepdims=True)
                probs = (weights / row_total).astype(jnp.bfloat16)
                lse = jnp.where(lane == turn * HEADS_PER_TURN + head, top + jnp.log(row_total), lse)
                total = total + contract(probs, values[head // 3][side], PLAIN)
            o_out[:, columns] = total.astype(jnp.bfloat16)
        lse_out[...] = lse

    later.wait()

    @pl.loop(0, model // step)
    def _(i):
        columns = pl.ds(pl.multiple_of(i * step, step), step)
        weights = full[:, pl.ds(pl.multiple_of(in_width + i * step, step), step)]
        mixed[:, columns] = contract(o_out[...], weights, PLAIN)

    m = h_out[...] + mixed[...]
    m_out[...] = m
    inverse = lax.rsqrt(jnp.mean(m * m, axis=1, keepdims=True) + NORM_EPS)
    nf_out[...] = (m * inverse * gain_out[1:2]).astype(jnp.bfloat16)


def attend_forward_fast(where, base, extra, tables, pieces, in_width, after=()):
    rows, model = base.shape
    bf, f32 = jnp.bfloat16, jnp.float32
    key_width = (in_width - model) // 2
    total = in_width + model + EXTRA
    shapes = [
        shape_of(rows, model, dtype=f32),
        shape_of(rows, model, dtype=f32),
        shape_of(rows, model),
        shape_of(rows, model),
        shape_of(rows, model),
        shape_of(rows, key_width),
        shape_of(rows, key_width),
        shape_of(rows, model),
        shape_of(rows, LANES, dtype=f32),
        shape_of(8, model, dtype=f32),
    ]

    def body(*refs):
        used = 2 + len(extra) + 3 + MATRIX_PIECES
        attend_forward_kernel(len(extra), in_width, *refs[:used], *refs[used + len(after) :])

    return pl.pallas_call(
        body,
        name="attend_forward",
        out_shape=shapes,
        in_specs=[scalar_spec()]
        + [whole_spec()] * (4 + len(extra))
        + [any_spec()] * (MATRIX_PIECES + len(after)),
        out_specs=[whole_spec()] * len(shapes),
        scratch_shapes=[
            pltpu.VMEM((model, total), bf),
            pltpu.VMEM((rows, in_width), f32),
            pltpu.VMEM((rows, model), f32),
            pltpu.SemaphoreType.DMA((3 * MATRIX_COPIES,)),
        ],
        compiler_params=pltpu.CompilerParams(vmem_limit_bytes=44 * MIB),
        cost_estimate=cost(2 * rows * model * total),
    )(where, base, *extra, *tables, *pieces, *after)


def attend_backward_kernel(groups, terms, width, where, base, upstream, *refs):
    refs = list(refs)
    extra = [refs.pop(0) for _ in range(terms)]
    h_in, m_in, na, q, k, v, o, lse_in, gains, cosine, sine, allowed = refs[:12]
    pieces = refs[12 : 12 + MATRIX_PIECES]
    outs, refs = refs[12 + MATRIX_PIECES : -6], refs[-6:]
    gh_out, gh_low = outs[:2]
    full, sums, mixed, grad_in, turned, semaphores = refs
    rows, model = h_in.shape
    in_width = width
    key_start = model
    value_start = model + (in_width - model) // 2
    shard = full.shape[0] // 32
    copies = Copies(semaphores)
    load_columns(copies, where, pieces, full, in_width, in_width + model)
    later = Copies(semaphores, copies.used)
    load_columns(later, where, pieces, full, 0, in_width)
    gnf = read_sum(base, extra)
    m = m_in[...]
    inverse = lax.rsqrt(jnp.mean(m * m, axis=1, keepdims=True) + NORM_EPS)
    gain_ffn = jnp.sum(gnf * m * inverse, axis=0, keepdims=True)
    scaled = gnf * gains[1:2]
    inner = jnp.mean(scaled * m, axis=1, keepdims=True)
    gm = upstream[...].astype(jnp.float32)
    gm = gm + inverse * scaled - m * (inverse * inverse * inverse) * inner
    gh_out[...] = gm
    gh_low[...] = gm.astype(jnp.bfloat16)
    copies.wait()
    step = 512

    @pl.loop(0, model // step)
    def _(i):
        row = pl.ds(pl.multiple_of(i * step, step), step)
        mixed[:, row] = contract(gh_low[...], full[row, in_width : in_width + model], ACROSS).astype(
            jnp.bfloat16
        )

    open_keys = allowed[...] > 0.5
    lane = lax.broadcasted_iota(jnp.int32, open_keys.shape, 1)
    cos, sin = cosine[...], sine[...]
    scale = HEAD_DIMENSION ** (-0.5)

    @pl.loop(0, KEY_VALUE_HEADS // 2)
    def _(turn):
        start = pl.multiple_of(turn * LANES, LANES)
        pair = pl.ds(start, LANES)
        keys = [both_sides(k[:, pair], side) for side in range(2)]
        values = [both_sides(v[:, pair], side) for side in range(2)]
        zero = jnp.zeros((rows, LANES), jnp.float32)
        grad_k = [[zero, zero], [zero, zero]]
        grad_v = [[zero, zero], [zero, zero]]
        lse = lse_in[...]
        for group in range(HEADS_PER_TURN // 2):
            columns = pl.ds(
                pl.multiple_of(turn * (HEADS_PER_TURN * 64) + group * LANES, LANES), LANES
            )
            grad_q = zero
            for side in range(2):
                head = group * 2 + side
                kv = head // 3
                top = jnp.sum(
                    jnp.where(lane == turn * HEADS_PER_TURN + head, lse, 0.0), axis=1, keepdims=True
                )
                scores = contract(q[:, columns], keys[kv][side], ACROSS) * scale
                probs = jnp.exp(jnp.where(open_keys, scores, MASKED) - top)
                go = mixed[:, columns]
                grad_v[kv][side] = grad_v[kv][side] + contract(
                    probs.astype(jnp.bfloat16), go, OUTER
                )
                grad_p = contract(go, values[kv][side], ACROSS)
                grad_s = probs * (grad_p - jnp.sum(probs * grad_p, axis=1, keepdims=True))
                grad_s = grad_s.astype(jnp.bfloat16)
                grad_q = grad_q + contract(grad_s, keys[kv][side], PLAIN)
                grad_k[kv][side] = grad_k[kv][side] + contract(grad_s, q[:, columns], OUTER)
            grad_q = grad_q * scale
            grad_in[:, columns] = (grad_q * cos - half_swap(grad_q) * sin).astype(jnp.bfloat16)
        key_grad = merge_sides(*grad_k[0], 0) + merge_sides(*grad_k[1], 1)
        key_grad = key_grad * scale
        key_grad = key_grad * cos - half_swap(key_grad) * sin
        value_grad = merge_sides(*grad_v[0], 0) + merge_sides(*grad_v[1], 1)
        grad_in[:, pl.ds(key_start + start, LANES)] = key_grad.astype(jnp.bfloat16)
        grad_in[:, pl.ds(value_start + start, LANES)] = value_grad.astype(jnp.bfloat16)

    band = 384

    @pl.loop(0, model // band)
    def _(i):
        start = pl.multiple_of(i * band, band)
        row = pl.ds(start, band)
        sums[row, in_width : in_width + model] = contract(o[:, row], gh_low[...], OUTER).astype(
            jnp.bfloat16
        )
        sums[row, :in_width] = contract(na[:, row], grad_in[...], OUTER).astype(jnp.bfloat16)

    def store_sums(low, width):
        at = 2
        for swapped in (1, 0):
            for first, count in groups:
                for m_index in range(4):
                    for n in range(count):
                        row = shard_row(where, swapped, m_index, first + n, shard)
                        place = pl.ds((m_index * count + n) * shard, shard)
                        columns = pl.ds(low, width)
                        later.start(
                            sums.at[pl.ds(row, shard), columns], outs[at].at[place, columns]
                        )
                at += 1

    later.wait()
    store_sums(0, in_width + model)
    turned[...] = jnp.zeros_like(turned)

    @pl.loop(0, in_width // step)
    def _(i):
        columns = pl.ds(pl.multiple_of(i * step, step), step)
        turned[...] += contract(grad_in[:, columns], full[:, columns], ACROSS)

    grad_na = turned[...]
    h = h_in[...]
    inverse = lax.rsqrt(jnp.mean(h * h, axis=1, keepdims=True) + NORM_EPS)
    gain_attn = jnp.sum(grad_na * h * inverse, axis=0, keepdims=True)
    scaled = grad_na * gains[0:1]
    inner = jnp.mean(scaled * h, axis=1, keepdims=True)
    both = jnp.concatenate([gain_attn, gain_ffn, jnp.zeros((EXTRA - 2, model), jnp.float32)], axis=0)
    sums[:, pl.ds(in_width + model, EXTRA)] = both.T.astype(jnp.bfloat16)
    store_sums(in_width + model, EXTRA)
    gh = gh_out[...] + inverse * scaled - h * (inverse * inverse * inverse) * inner
    gh_out[...] = gh
    gh_low[...] = gh.astype(jnp.bfloat16)
    later.wait()


def attend_backward_fast(
    groups, where, base, upstream, extra, stash, tables, pieces, in_width, after=()
):
    rows, model = upstream.shape
    bf, f32 = jnp.bfloat16, jnp.float32
    total = in_width + model + EXTRA
    shapes = [
        shape_of(rows, model, dtype=f32),
        shape_of(rows, model),
    ]
    shapes += [shape_of(model // 8 * count, total) for _, count in groups] * CORES

    def body(*refs):
        used = 3 + len(extra) + 12 + MATRIX_PIECES
        attend_backward_kernel(
            groups, len(extra), in_width, *refs[:used], *refs[used + len(after) :]
        )

    return pl.pallas_call(
        body,
        name="attend_backward",
        out_shape=shapes,
        in_specs=[scalar_spec()]
        + [whole_spec()] * (2 + len(extra) + 12)
        + [any_spec()] * (MATRIX_PIECES + len(after)),
        out_specs=[whole_spec()] * 2 + [any_spec()] * (len(shapes) - 2),
        scratch_shapes=[
            pltpu.VMEM((model, total), bf),
            pltpu.VMEM((model, total), bf),
            pltpu.VMEM((rows, model), bf),
            pltpu.VMEM((rows, in_width), bf),
            pltpu.VMEM((rows, model), f32),
            pltpu.SemaphoreType.DMA((2 * MATRIX_COPIES + 64,)),
        ],
        compiler_params=pltpu.CompilerParams(vmem_limit_bytes=56 * MIB),
        cost_estimate=cost(4 * rows * model * total),
    )(where, base, upstream, *extra, *stash, *tables, *pieces, *after)


SHARES = ((0, 0, 3), (1, 0, 3), (2, 0, 3), (3, 0, 3))
WEIGHT_PIECES = CORES * len(SHARES)


def load_experts(copies, where, pieces, targets):
    at = 0
    for swapped in range(CORES):
        for k, first, count in SHARES:
            piece = pieces[at]
            at += 1
            _, experts, rows, share = piece.shape
            fsdp = lax.rem(where[0] - k + 4, 4) * CORES + (where[1] ^ swapped)
            row = pl.ds(pl.multiple_of(fsdp * rows, 16), rows)
            for i, target in enumerate(targets[first : first + count]):
                for e in range(experts):
                    copies.start(piece.at[i, e], target.at[row, pl.ds(e * share, share)])


def load_weights(copies, where, weights, targets):
    if len(weights) > 1:
        load_experts(copies, where, weights, targets)
    else:
        rows = targets[0].shape[0] // 8
        for i, target in enumerate(targets):
            for n in range(8):
                row = pl.ds(n * rows, rows)
                copies.start(weights[0].at[i, row, :], target.at[row, :])


def widen_tile(columns, share, width):
    lane = lax.broadcasted_iota(jnp.int32, (columns.shape[0], width), 1)
    wide = jnp.broadcast_to(columns[:, 0:1], lane.shape)
    for e in range(1, width // share):
        wide = jnp.where(lane >= e * share, columns[:, e : e + 1], wide)
    return wide


def start_rows(copies, pieces, rows_ref):
    at = 0
    for piece in pieces:
        rows = piece.shape[0]
        copies.start(piece, rows_ref.at[pl.ds(at, rows), :])
        at += rows


class Pool:
    def __init__(self, semaphores, used=0):
        self.semaphores = semaphores
        self.used = used

    def copy(self, source, target):
        self.used += 1
        return pltpu.make_async_copy(source, target, self.semaphores.at[self.used - 1])


def rows_at(ref, first, count):
    return ref.at[pl.ds(first, count), :]


def tile_loads(pool, pieces, x):
    n = pieces[0].shape[0]
    found = [[pool.copy(pieces[m], rows_at(x, m * n, n))] for m in range(3)]
    half = n // 2
    last = [pool.copy(pieces[3 + i], rows_at(x, 3 * n + i * half, half)) for i in range(2)]
    return found + [last]


def tile_slices(pool, source, target, n):
    return [[pool.copy(rows_at(source, m * n, n), rows_at(target, m * n, n))] for m in range(4)]


def tile_parts(pool, y, parts):
    n = parts[0].shape[0]
    half = n // 2
    own, one_head, two_tail, to_one, to_two = parts

    def copy(first, count, part, at=0):
        return pool.copy(rows_at(y, first, count), rows_at(part, at, count))

    return [
        [copy(0, n, own)],
        [copy(n, half, one_head), copy(n + half, half, to_one)],
        [copy(2 * n, half, to_two), copy(2 * n + half, half, two_tail)],
        [copy(3 * n, half, to_two, half), copy(3 * n + half, half, to_one, half)],
    ]


def for_tile(i, groups, act):
    for m in range(4):

        @pl.when(i == m)
        def _():
            for group in groups:
                for copy in group[m]:
                    act(copy)


def finish(groups):
    for group in groups:
        for copies in group:
            for copy in copies:
                copy.wait()


def part_rows(n):
    return [n, n // 2, n // 2, n, n]


def experts_forward_kernel(share, count, where, gates, *refs):
    pieces, weights, refs = refs[:5], refs[5 : 5 + count], refs[5 + count :]
    parts, x_out, g_out, u_out = refs[:5], *refs[5:8]
    x, y, g, u, w_gate, w_up, w_down, semaphores = refs[-8:]
    laid = refs[8:-8]
    n = pieces[0].shape[0]
    pool = Pool(semaphores)
    loads = tile_loads(pool, pieces, x)
    for group in loads:
        for copy in group:
            copy.start()
    copies = Copies(semaphores, pool.used)
    load_weights(copies, where, weights, (w_gate, w_up, w_down))
    pool.used = copies.used
    pool.used = copies.used + 3
    kept = tile_slices(pool, x, x_out, n)
    stores = [
        tile_parts(pool, y, parts),
        tile_slices(pool, g, g_out, n),
        tile_slices(pool, u, u_out, n),
    ]
    width = w_gate.shape[1]
    copies.wait()
    for i, w in enumerate((w_gate, w_up, w_down)):
        if laid:
            copies.start(w, laid[0].at[i])

    @pl.loop(0, 4)
    def _(i):
        for_tile(i, [loads], lambda copy: copy.wait())
        for_tile(i, [kept], lambda copy: copy.start())
        row = pl.ds(pl.multiple_of(i * n, n), n)
        gate_pre = contract(x[row, :], w_gate[...], PLAIN)
        up_pre = contract(x[row, :], w_up[...], PLAIN)
        g[row, :] = gate_pre
        u[row, :] = up_pre
        wide = widen_tile(gates[row, :], share, width)
        weighed = (gate_pre * jax.nn.sigmoid(gate_pre) * up_pre * wide).astype(jnp.bfloat16)
        y[row, :] = contract(weighed, w_down[...], ACROSS).astype(jnp.bfloat16)
        for_tile(i, stores, lambda copy: copy.start())

    finish([kept, *stores])
    copies.wait()


def experts_forward_fast(experts, where, gates, pieces, weights, after=()):
    n, model = pieces[0].shape
    rows, count = 4 * n, len(weights)
    width = experts * weights[0].shape[3] if count > 1 else weights[0].shape[2]
    share = width // experts
    bf, f32 = jnp.bfloat16, jnp.float32
    shapes = [shape_of(r, model) for r in part_rows(n)]
    shapes += [shape_of(rows, model)] + [shape_of(rows, width, dtype=f32)] * 2
    if count > 1:
        shapes += [shape_of(3, model, width)]

    def body(*refs):
        used = 7 + count
        experts_forward_kernel(share, count, *refs[:used], *refs[used + len(after) :])

    return pl.pallas_call(
        body,
        name="experts_forward",
        out_shape=shapes,
        in_specs=[scalar_spec(), whole_spec()] + [any_spec()] * (5 + count + len(after)),
        out_specs=[any_spec()] * len(shapes),
        scratch_shapes=[
            pltpu.VMEM((rows, model), bf),
            pltpu.VMEM((rows, model), bf),
            pltpu.VMEM((rows, width), f32),
            pltpu.VMEM((rows, width), f32),
        ]
        + [pltpu.VMEM((model, width), bf)] * 3
        + [pltpu.SemaphoreType.DMA((24 * experts + 48,))],
        compiler_params=pltpu.CompilerParams(vmem_limit_bytes=48 * MIB),
        cost_estimate=cost(6 * rows * model * width),
    )(where, gates, *pieces, *weights, *after)


def experts_backward_kernel(share, where, gates, *refs):
    pieces, g_in, u_in = refs[:5], refs[5], refs[6]
    weights, refs = refs[7:8], refs[8:]
    parts, r_out, gg_out, gu_out, p_out = refs[:5], *refs[5:9]
    x, y, g, u, gg, gu, p, w_gate, w_up, w_down, semaphores = refs[9:]
    n = pieces[0].shape[0]
    pool = Pool(semaphores)
    loads = [
        tile_loads(pool, pieces, x),
        tile_slices(pool, g_in, g, n),
        tile_slices(pool, u_in, u, n),
    ]
    for group in loads[0]:
        for copy in group:
            copy.start()
    copies = Copies(semaphores, pool.used)
    load_weights(copies, where, weights, (w_gate, w_up, w_down))
    for loaded in loads[1:]:
        for group in loaded:
            for copy in group:
                copy.start()
    pool.used = copies.used
    kept = tile_slices(pool, x, r_out, n)
    stores = [
        tile_parts(pool, y, parts),
        tile_slices(pool, gg, gg_out, n),
        tile_slices(pool, gu, gu_out, n),
        tile_slices(pool, p, p_out, n),
    ]
    width = w_gate.shape[1]
    copies.wait()

    @pl.loop(0, 4)
    def _(i):
        for_tile(i, loads, lambda copy: copy.wait())
        for_tile(i, [kept], lambda copy: copy.start())
        row = pl.ds(pl.multiple_of(i * n, n), n)
        wide = widen_tile(gates[row, :], share, width)
        hidden_grad = contract(x[row, :], w_down[...], PLAIN) * wide
        gate_pre, up_pre = g[row, :], u[row, :]
        sig = jax.nn.sigmoid(gate_pre)
        active = gate_pre * sig
        p[row, :] = (active * up_pre * wide).astype(jnp.bfloat16)
        gate_grad = hidden_grad * up_pre * sig * (1.0 + gate_pre * (1.0 - sig))
        gg[row, :] = gate_grad.astype(jnp.bfloat16)
        gu[row, :] = (hidden_grad * active).astype(jnp.bfloat16)
        back = contract(gg[row, :], w_gate[...], ACROSS)
        back = back + contract(gu[row, :], w_up[...], ACROSS)
        y[row, :] = back.astype(jnp.bfloat16)
        for_tile(i, stores, lambda copy: copy.start())

    finish([kept, *stores])


def experts_backward_fast(experts, where, gates, pieces, stash, weights, after=()):
    n, model = gates.shape[0] // 4, pieces[0].shape[1]
    rows, width = 4 * n, weights[0].shape[2]
    share = width // experts
    bf, f32 = jnp.bfloat16, jnp.float32
    shapes = [shape_of(r, model) for r in part_rows(n)]
    shapes += [shape_of(rows, model)] + [shape_of(rows, width)] * 3

    def body(*refs):
        experts_backward_kernel(share, *refs[:10], *refs[10 + len(after) :])

    return pl.pallas_call(
        body,
        name="experts_backward",
        out_shape=shapes,
        in_specs=[scalar_spec(), whole_spec()] + [any_spec()] * (8 + len(after)),
        out_specs=[any_spec()] * len(shapes),
        scratch_shapes=[
            pltpu.VMEM((rows, model), bf),
            pltpu.VMEM((rows, model), bf),
            pltpu.VMEM((rows, width), f32),
            pltpu.VMEM((rows, width), f32),
            pltpu.VMEM((rows, width), bf),
            pltpu.VMEM((rows, width), bf),
            pltpu.VMEM((rows, width), bf),
        ]
        + [pltpu.VMEM((model, width), bf)] * 3
        + [pltpu.SemaphoreType.DMA((24 * experts + 48,))],
        compiler_params=pltpu.CompilerParams(vmem_limit_bytes=52 * MIB),
        cost_estimate=cost(6 * rows * model * width),
    )(where, gates, *pieces, *stash, *weights, *after)


def weight_grads_kernel(experts, where, *refs):
    sources, mine, other = refs[:4], refs[4], refs[5]
    x, g, out, semaphores = refs[6:]
    copies = Copies(semaphores)
    for target, near, far in zip((x, g), sources[:2], sources[2:]):
        start_rows(copies, (near, far), target)
    copies.wait()
    band = x.shape[1] // 4
    rows = band // CORES
    share = g.shape[1] // experts

    @pl.loop(0, 4)
    def _(z):
        columns = pl.ds(pl.multiple_of(z * band, band), band)
        k = lax.rem(z - where[0] + 4, 4)
        grads = contract(x[:, columns], g[...], OUTER).astype(jnp.bfloat16)
        for core in range(CORES):
            for e in range(experts):
                out[core, k, e] = grads[
                    core * rows : (core + 1) * rows, e * share : (e + 1) * share
                ]

    copies.start(out.at[1 - where[1]], other)
    copies.start(out.at[where[1]], mine)
    copies.wait()


def weight_grads_fast(where, near, far, experts, after=()):
    model, width = near[0].shape[1], near[1].shape[1]
    count = near[0].shape[0] + far[0].shape[0]
    rows, share = model // 8, width // experts
    bf = jnp.bfloat16

    def body(*refs):
        weight_grads_kernel(experts, *refs[:5], *refs[5 + len(after) :])

    return pl.pallas_call(
        body,
        name="weight_grads",
        out_shape=[shape_of(4, experts, rows, share)] * 2,
        in_specs=[scalar_spec()] + [any_spec()] * (4 + len(after)),
        out_specs=[any_spec()] * 2,
        scratch_shapes=[
            pltpu.VMEM((count, model), bf),
            pltpu.VMEM((count, width), bf),
            pltpu.VMEM((CORES, 4, experts, rows, share), bf),
            pltpu.SemaphoreType.DMA((6,)),
        ],
        compiler_params=pltpu.CompilerParams(vmem_limit_bytes=40 * MIB),
        cost_estimate=cost(2 * count * model * width),
    )(where, *near, *far, *after)


def cut_kernel(where, w_gate, w_up, w_down, *outs):
    share = outs[0].shape[3]
    matrices = (w_gate, w_up, w_down)
    for (k, first, count), out in zip(SHARES, outs):
        columns = pl.ds(pl.multiple_of(lax.rem(where[0] + k, 4) * share, share), share)
        for i in range(count):
            out[i, 0] = matrices[first + i][0, 0, :, columns]


def cut_experts(where, weights, layer):
    _, experts, rows, hidden = weights[0].shape
    share = hidden // 4
    return pl.pallas_call(
        cut_kernel,
        name="cut_experts",
        grid=(experts,),
        out_shape=[shape_of(count, experts, rows, share) for _, _, count in SHARES],
        in_specs=[scalar_spec()]
        + [pl.BlockSpec((1, 1, rows, hidden), lambda e: (layer, e, 0, 0))] * 3,
        out_specs=[
            pl.BlockSpec((count, 1, rows, share), lambda e: (0, e, 0, 0)) for _, _, count in SHARES
        ],
    )(where, *weights)


def merge_grads_kernel(*refs):
    mine, arrived, outs = refs[:3], refs[3:6], refs[6:]
    for i in range(3):
        for k, out in enumerate(outs):
            total = mine[i][k, 0].astype(jnp.float32) + arrived[i][k, 0].astype(jnp.float32)
            out[i, 0] = total.astype(jnp.bfloat16)


def merge_grads(mine, arrived):
    planes, experts, rows, share = mine[0].shape
    return pl.pallas_call(
        merge_grads_kernel,
        name="merge_grads",
        grid=(experts,),
        out_shape=[shape_of(3, experts, rows, share)] * planes,
        in_specs=[pl.BlockSpec((planes, 1, rows, share), lambda e: (0, e, 0, 0))] * 6,
        out_specs=[pl.BlockSpec((3, 1, rows, share), lambda e: (0, e, 0, 0))] * planes,
    )(*mine, *arrived)


def join_kernel(layer, where, *refs):
    pieces, outs = refs[:4], refs[-3:]
    i = pl.program_id(0)
    share = pieces[0].shape[3]
    for index, out in enumerate(outs):

        @pl.when(i == index)
        def _():
            for k, piece in enumerate(pieces):
                columns = pl.ds(pl.multiple_of(lax.rem(where[0] - k + 4, 4) * share, share), share)
                out[0, :, :, columns] = piece[0].astype(jnp.float32)


def join_experts(where, pieces, layer, layers, earlier=None):
    mats, experts, rows, share = pieces[0].shape
    shape = shape_of(layers, experts, rows, 4 * share, dtype=jnp.float32)
    given = [] if earlier is None else list(earlier)

    return pl.pallas_call(
        functools.partial(join_kernel, layer),
        name="join_experts",
        grid=(mats,),
        out_shape=[shape] * mats,
        in_specs=[scalar_spec()]
        + [pl.BlockSpec((1, experts, rows, share), lambda i: (i, 0, 0, 0))] * 4
        + [any_spec()] * len(given),
        out_specs=[pl.BlockSpec((1, experts, rows, 4 * share), lambda i: (layer, 0, 0, 0))] * mats,
        input_output_aliases={5 + j: j for j in range(len(given))},
        compiler_params=pltpu.CompilerParams(vmem_limit_bytes=40 * MIB),
    )(where, *pieces, *given)


def tie(value, *events):
    flat, tree = jax.tree.flatten(value)
    held = lax.optimization_barrier((*flat, *events))
    return jax.tree.unflatten(tree, held[: len(flat)])


def spread_first(place, block):
    return [block, place.hop(block, flip=1), place.hop(block, flip=2)]


def spread_last(place, first, axis=0, cut=None):
    block, one, two = first
    cut = cut or block.shape[axis] // 2
    head = place.hop(lax.slice_in_dim(one, 0, cut, axis=axis), flip=2)
    tail = place.hop(lax.slice_in_dim(two, cut, None, axis=axis), flip=1)
    return [block, one, two, head, tail]


def spread_pieces(place, block):
    return spread_last(place, spread_first(place, block))


def up_hops(place, block):
    return [place.hop(block, up=k) for k in range(1, 4)]


def add_low(a, b):
    return (a.astype(jnp.float32) + b.astype(jnp.float32)).astype(a.dtype)


def fold_first(place, parts):
    own, one_head, two_tail, to_one, to_two = parts
    return own, one_head, two_tail, place.hop(to_one, flip=1), place.hop(to_two, flip=2)


def fold_sums(first):
    own, one_head, two_tail, by_one, by_two = first
    half = one_head.shape[0]
    return own, add_low(one_head, by_two[half:]), add_low(two_tail, by_one[half:]), by_one, by_two


def fold_start(place, parts):
    return fold_sums(fold_first(place, parts))


def fold_end(place, state):
    own, one_head, two_tail, by_one, by_two = state
    return own, place.hop(one_head, flip=1), place.hop(two_tail, flip=2), by_one, by_two


def add_pieces(own, one_head, two_tail, by_one, by_two, axis=0):
    wide = lambda value: value.astype(jnp.float32)
    half = one_head.shape[0]
    one = jnp.concatenate([one_head, by_one[:half]], axis=axis)
    two = jnp.concatenate([by_two[:half], two_tail], axis=axis)
    return wide(own) + wide(one) + wide(two)


def blocks_kernel(sides, own, one_head, two_tail, by_one, by_two, *outs):
    half = one_head.shape[0]
    for side, out in zip(sides, outs):
        terms = (two_tail, by_one) if side else (one_head, by_two)
        total = own[side * half : (side + 1) * half, :].astype(jnp.float32)
        for term in terms:
            total = total + term[:half, :].astype(jnp.float32)
        out[...] = total.astype(jnp.bfloat16)


def sum_blocks(ends, sides):
    half, model = ends[1].shape
    return pl.pallas_call(
        functools.partial(blocks_kernel, sides),
        name="sum_blocks",
        out_shape=[shape_of(half, model)] * len(sides),
        in_specs=[whole_spec()] * 5,
        out_specs=[whole_spec()] * len(sides),
    )(*ends)


def down_hops(place, blocks, first=1):
    return [place.hop(block, up=-first - n) for n, block in enumerate(blocks)]


def total_of(base, extra):
    total = base.astype(jnp.float32)
    for term in extra:
        total = total + term[: base.shape[0]].astype(jnp.float32)
    return total


def received(near_ends, arrived):
    own, one_head, _, _, by_two = near_ends
    return [own, *arrived, one_head, by_two]


def merge_kernel(cut, mine, arrived, own, one_head, two_tail, to_one, to_two):
    m = pl.program_id(0)
    total = (mine[...].astype(jnp.float32) + arrived[...].astype(jnp.float32)).astype(jnp.bfloat16)
    rows = total.shape[0]

    @pl.when(m == 0)
    def _():
        own[...] = total

    @pl.when(m == 1)
    def _():
        one_head[...] = total[:, :cut]
        to_one[:rows, :] = total[:, cut:]

    @pl.when(m == 2)
    def _():
        to_two[:rows, :] = total[:, :cut]
        two_tail[...] = total[:, cut:]

    @pl.when(m == 3)
    def _():
        to_two[rows:, :] = total[:, :cut]
        to_one[rows:, :] = total[:, cut:]


def merge_cores(mine, arrived, cut):
    rows, width = mine.shape[0] // 4, mine.shape[1]
    outs = [(rows, width), (rows, cut), (rows, width - cut), (2 * rows, width - cut), (2 * rows, cut)]
    return pl.pallas_call(
        functools.partial(merge_kernel, cut),
        name="merge_cores",
        grid=(4,),
        out_shape=[shape_of(*out) for out in outs],
        in_specs=[pl.BlockSpec((rows, width), lambda m: (m, 0))] * 2,
        out_specs=[pl.BlockSpec(out, lambda m: (0, 0)) for out in outs],
        compiler_params=pltpu.CompilerParams(vmem_limit_bytes=40 * MIB),
    )(mine, arrived)


def pack_kernel(*refs):
    layers = refs[0].shape[0]
    for l in range(layers):
        out = refs[l - layers]
        at = 0
        for ref in refs[:-layers]:
            width = ref.shape[2]
            out[:, at : at + width] = ref[l]
            at += width


def pack_matrices(*arrays):
    width = sum(a.shape[2] for a in arrays)
    layers, rows, _ = arrays[0].shape
    return pl.pallas_call(
        pack_kernel,
        name="pack_matrices",
        out_shape=[shape_of(rows, width)] * layers,
        in_specs=[whole_spec()] * len(arrays),
        out_specs=[whole_spec()] * layers,
    )(*arrays)


def sum_down(place, total, own):
    rows = own.shape[0]
    total = total.astype(jnp.bfloat16)
    for block in down_hops(place, [total[k * rows : (k + 1) * rows] for k in range(3)]):
        own = own + block.astype(jnp.float32)
    return own


def tables_of(length_row, rows):
    order = jnp.arange(rows, dtype=jnp.int32)
    index = jnp.arange(length_row.shape[0], dtype=jnp.int32)
    ends = jnp.sum(jnp.where(index[:, None] <= index[None, :], length_row[:, None], 0), axis=0)
    passed = order[:, None] >= ends[None, :]
    segment = jnp.sum(passed.astype(jnp.int32), axis=1)
    begin = jnp.sum(jnp.where(passed, length_row[None, :], 0), axis=1)
    cosine, sine = rope_tables(order - begin, HEAD_DIMENSION)
    allowed = (segment[:, None] == segment[None, :]) & (order[:, None] >= order[None, :])
    return (
        jnp.concatenate([cosine] * 4, axis=1),
        jnp.concatenate([-sine, sine] * 2, axis=1),
        allowed.astype(jnp.float32),
    )


def gate_rows_of(found):
    order = jnp.transpose(jnp.stack(found), (2, 1, 0, 4, 3))
    order = jnp.pad(order, ((0, 0),) * 4 + ((0, 8 - order.shape[4]),))
    return [
        (layer[:, :2].reshape(-1, 8), layer[:, 2:].reshape(-1, 8)) for layer in order
    ]


def shards_fast(
    tokens,
    lengths,
    routes,
    gates,
    cotangent,
    norm_attn,
    norm_ffn,
    query,
    key,
    value,
    output,
    w_gate,
    w_up,
    w_down,
):
    place = Place()
    where = jnp.stack([place.plane, place.core, place.column]).astype(jnp.int32)
    rows, model = tokens.shape
    layer_count, _, experts, _ = w_gate.shape
    expert_count = experts * place.columns
    in_width = query.shape[2] + key.shape[2] + value.shape[2]
    gains = jnp.stack([norm_attn, norm_ffn], axis=2)
    gains = jnp.pad(gains, ((0, 0), (0, 0), (0, EXTRA - 2)))
    packs = pack_matrices(query, key, value, output, gains)
    cut = packs[0].shape[1] // 2 // 128 * 128
    weights = [jnp.transpose(w, (0, 2, 1, 3)) for w in (w_gate, w_up, w_down)]
    tables = tables_of(lengths[0], rows)

    def line_of(block):
        return jnp.concatenate([block] + up_hops(place, block))

    cuts = [cut_experts(where, weights, l) for l in range(layer_count)]
    table = gate_table(*tie((routes, gates), packs[0]), expert_count)
    found = jnp.stack(spread_gates(place, table))
    found = [found] + up_hops(place, found)
    line = jnp.concatenate([packs[0]] + tie(up_hops(place, packs[0]), *[cut[0] for cut in cuts], found[0]))
    first = spread_first(place, line)
    cuts[0] = tie(cuts[0], line)
    own_swaps = [place.hop(tie(cut[0], line), swap=1) for cut in cuts]
    one = place.hop(cuts[0][1], up=1)
    swapped = [place.hop(line, swap=1)]
    two = place.hop(tie(cuts[0][2], line), up=2)
    first = tie(first, one, two, swapped[0], *own_swaps)
    three = place.hop(tie(cuts[0][3], first[0]), up=3)
    swapped += [place.hop(piece, swap=1) for piece in first[1:]]
    last_two = tie(spread_last(place, first, axis=1, cut=cut)[3:], three, *swapped[1:])
    matrices = [[*first, *last_two, *swapped, *[place.hop(p, swap=1) for p in last_two]]]
    shares = [cuts[0][0], one, two, three]
    share_swaps = [own_swaps[0], place.hop(one, swap=1), place.hop(two, swap=1)]

    def run_forward(l, which, pieces, bank, after=()):
        return experts_forward_fast(experts, where, gate_rows[l][which], pieces, bank, after=after)

    def run_backward(l, which, pieces, stash, bank, after=()):
        return experts_backward_fast(
            experts, where, gate_rows[l][which], pieces, stash, bank, after=after
        )

    def pairs_of(block, *events):
        ups = up_hops(place, block)
        near = spread_first(place, jnp.concatenate([block, ups[0]]))
        return near, ups[1:]

    base, extra = tokens.astype(jnp.float32), []
    stored = []
    for l in range(layer_count):
        more = l + 1 < layer_count
        after = list(share_swaps)
        outs = attend_forward_fast(where, base, extra, tables, matrices[l], in_width, after=after)
        h, m, nf = outs[:3]
        nf, late, found = tie((nf, shares[len(share_swaps) :], found))
        if l == 0:
            gate_rows = gate_rows_of(found)
        share_swaps += [place.hop(piece, swap=1) for piece in late]
        bank_l = [*shares[: 4 - len(late)], *late, *share_swaps]
        near, far = pairs_of(nf)
        near = spread_last(place, near)
        far = spread_first(place, jnp.concatenate(tie(far, near[3], near[4])))
        line = up_hops(place, tie(packs[l + 1] if more else cotangent, far[0]))
        *y_near, laid = run_forward(l, 0, near, bank_l)
        bank_l = [laid]
        y_near, far, line[0], line[2] = tie((y_near, far, line[0], line[2]))
        far = spread_last(place, far)
        if more:
            near_first = fold_first(place, tie(y_near[:5], far[3], far[4]))
            y_far = run_forward(l, 1, far, bank_l, after=(y_near[0],))
            y_far, near_first, line[1] = tie((y_far, near_first, line[1]))
            one = place.hop(tie(cuts[l + 1][1], line[1]), up=1)
            far_first = fold_first(place, y_far[:5])
            near_ends = fold_end(place, fold_sums(near_first))
            far_first, one = tie((far_first, one))
            far_state = fold_sums(far_first)
            one_swap = place.hop(one, swap=1)
            far_ends, one_swap = tie((fold_end(place, far_state), one_swap), *near_ends[1:3])
            line = jnp.concatenate([packs[l + 1], *line])
            passing = spread_first(place, tie(line, far_ends[1], far_ends[2]))
            line_swap = place.hop(line, swap=1)
            arrived = down_hops(place, sum_blocks(near_ends, (1,)))
            blocks = sum_blocks(far_ends, (0, 1))
            arrived += down_hops(place, blocks, 2)
            passing = tie(passing, *arrived)
            two = place.hop(tie(cuts[l + 1][2], *arrived), up=2)
            swapped = [line_swap] + [place.hop(piece, swap=1) for piece in passing[1:]]
            last_two, two = tie((spread_last(place, passing, 1, cut)[3:], two), *swapped[1:])
            share_swaps = [own_swaps[l + 1], one_swap]
            ends = [place.hop(p, swap=1) for p in last_two]
            matrices.append([*passing, *last_two, *swapped, *ends])
            shares = [cuts[l + 1][0], one, two]
            shares.append(place.hop(tie(cuts[l + 1][3], last_two[0]), up=3))
            base, extra = m, received(near_ends, arrived)
        else:
            last_near = jnp.concatenate(tie([cotangent, line[0]], far[3], far[4]))
            last_near = spread_first(place, last_near)
            y_far = run_forward(l, 1, far, bank_l, after=(y_near[0],))
            y_far, last_near, line = tie((y_far, last_near, line))
            last_near = spread_last(place, last_near)
            last_far = spread_first(place, jnp.concatenate(tie(line[1:], *last_near[3:])))
        stored.append((h, outs, y_near, y_far, bank_l))

    upstream = cotangent
    zero = jnp.zeros((rows, model), jnp.bfloat16)
    sums = [None] * layer_count
    joined = None
    for l in reversed(range(layer_count)):
        h, outs, kept_near, kept_far, bank_l = stored[l]
        m, na, q, k, v, o, lse, gains = outs[1], *outs[3:]
        top = l + 1 == layer_count

        if top:
            b_near = run_backward(l, 0, last_near, kept_near[6:], bank_l, (y_far[0],))
            b_near, last_far = tie((b_near, last_far))
            far = spread_last(place, last_far)
            near_first = fold_first(place, tie(b_near[:5], far[3], far[4]))
            b_far = run_backward(l, 1, far, kept_far[6:], bank_l, (b_near[0],))
            b_far, near_first = tie((b_far, near_first))
            far_first = fold_first(place, b_far[:5])
        else:
            ups = up_hops(place, low)
            held = merge_grads(*held_parts)
            result_ends = fold_end(place, fold_sums(result_first))
            ups[0], held = tie((ups[0], held), *result_ends[1:3])
            near = jnp.concatenate([low, ups[0]])
            other_sum = place.hop(tie(other_one, near), swap=1)
            near = spread_last(place, spread_first(place, near))
            far = spread_first(place, jnp.concatenate(tie(ups[1:], near[3], near[4])))
            result_blocks = sum_blocks(result_ends, (0, 1))
            result_arrived = down_hops(place, tie(result_blocks, far[0]), 2)
            b_near = run_backward(l, 0, near, kept_near[6:], bank_l, (held[0],))
            b_near, far, result_arrived = tie((b_near, far, result_arrived))
            merged = merge_cores(mine_one, tie(other_sum, b_near[0]), cut)
            far = spread_last(place, far)
            came = [place.hop(tie(held[2][2:], b_near[0]), up=2)]
            merged_first = fold_first(place, tie(merged, far[3], far[4]))
            b_far = run_backward(l, 1, far, kept_far[6:], bank_l, (b_near[0],))
            b_far, merged_first, came[0] = tie((b_far, merged_first, came[0]))
            far_first = fold_first(place, b_far[:5])
            came.insert(0, place.hop(tie(held[1], b_far[0]), up=1))
            came.append(place.hop(tie(held[3], b_far[0]), up=3))

        def weight_grads(i, after, near=(kept_near, b_near), far=(kept_far, b_far)):
            pick = lambda kept, found: ((kept[5], found[6 + i]) if i < 2 else (found[5], found[8]))
            return weight_grads_fast(where, pick(*near), pick(*far), experts, after=after)

        grads = [weight_grads(0, (b_far[0],))]
        if not top:
            grads.append(weight_grads(1, (grads[0][0], came[0])))
        far_state = fold_sums(tie(far_first, grads[-1][0]))
        if not top:
            near_first = fold_first(place, tie(b_near[:5], far_state[1], far_state[2]))
        grads.append(weight_grads(len(grads), (far_state[1], far_state[2])))
        swapped = [place.hop(other, swap=1) for _, other in grads[:-1]]
        far_ends = fold_end(place, far_state)
        far_ends, swapped = tie((far_ends, swapped), grads[-1][0])
        swapped.append(place.hop(grads[-1][1], swap=1))
        if not top:
            far_ends, came = tie((far_ends, came))
        event = far_state if top else far_ends
        near_state = fold_sums(tie(near_first, event[1], event[2]))
        near_ends = fold_end(place, near_state)
        arrived = down_hops(place, sum_blocks(near_ends, (1,)))
        blocks = sum_blocks(far_ends, (0, 1))
        arrived += down_hops(place, blocks, 2)
        if top:
            grads.append(weight_grads(2, (blocks[0],)))
            early = jnp.stack([add_low(grads[n][0][2], swapped[n][2]) for n in range(2)])
            arrived, swapped, early = tie((arrived, swapped, early), grads[2][0])
            early = place.hop(tie(early, *arrived), up=2)
            swapped.append(place.hop(tie(grads[2][1], *arrived), swap=1))
        if top:
            result_first = fold_first(place, tie(kept_far[:5], *arrived))
            result_near_first = fold_first(place, tie(kept_near[:5], *arrived))
            after = ()
            groups = ((0, 4),)
        else:
            held_came = [held[0], came[0], jnp.concatenate([early, came[1]]), came[2]]
            total = merge_grads([mine for mine, _ in grads], swapped)
            merged_ends = fold_end(place, fold_sums(tie(merged_first, blocks[0], *near_ends[1:3])))
            one_total = add_pieces(*merged_ends, axis=1)
            shard = mine_one.shape[0] // 16
            low_total = one_total[shard:].astype(jnp.bfloat16)
            arrived = tie(arrived, total[0], low_total)
            low_total = tie(low_total, *arrived)
            one_arrived = down_hops(place, [low_total[n * shard :][:shard] for n in range(3)])
            result_near = fold_end(place, fold_sums(tie(result_near_first, *arrived)))
            after = (low_total, total[0])
            groups = ((1, 3), (0, 1))
        upstream, low, *partial = attend_backward_fast(
            groups,
            where,
            zero,
            upstream,
            received(near_ends, arrived),
            (h, m, na, q, k, v, o, lse, gains),
            tables,
            matrices[l],
            in_width,
            after=after,
        )
        if top:
            low, result_first, result_near_first, early = tie(
                (low, result_first, result_near_first, early)
            )
            held_parts = ([mine for mine, _ in grads], swapped)
            other_one, mine_one = partial
        else:
            partial, result_near = tie((partial, result_near))
    partial, one_arrived = tie((partial, one_arrived))
    sums[1] = one_total[:shard]
    for block in one_arrived:
        sums[1] = sums[1] + block.astype(jnp.float32)
    other_far, other_near, mine_far, mine_near = partial
    other_far, other_near = place.hop(other_far, swap=1), place.hop(other_near, swap=1)
    merged_far = merge_cores(mine_far, other_far, cut)
    came = [place.hop(tie(total[k], upstream), up=k) for k in (1, 2, 3)]
    merged_far, came[0] = tie((merged_far, came[0]))
    merged_near = merge_cores(mine_near, other_near, cut)
    far_first = fold_first(place, merged_far)
    joined = join_experts(where, tie(held_came, merged_far[0]), 1, layer_count, None)
    far_state = fold_sums(tie(far_first, joined[0]))
    near_first = fold_first(place, tie(merged_near, far_state[1], far_state[2]))
    near_ends = fold_end(place, fold_sums(near_first))
    far_ends = tie(fold_end(place, far_state), *came)
    far_total = add_pieces(*far_ends, axis=1)
    sums[0] = sum_down(place, far_total, add_pieces(*near_ends, axis=1))
    joined = join_experts(where, [total[0], *came], 0, layer_count, joined)
    last_block = down_hops(place, sum_blocks(tie(result_near, far_state[1]), (1,)))
    result = total_of(stored[-1][1][1], received(result_near, last_block + result_arrived))
    result = result.astype(jnp.bfloat16)
    sums = jnp.stack(sums)
    gain_sums = sums[:, :, in_width + model :]
    starts = (0, query.shape[2], query.shape[2] + key.shape[2], in_width, in_width + model)
    return (
        result,
        upstream,
        gain_sums[:, :, 0],
        gain_sums[:, :, 1],
        *[sums[:, :, a:b] for a, b in zip(starts, starts[1:])],
        *[jnp.transpose(grads, (0, 2, 1, 3)) for grads in joined],
    )


def solution(mesh):
    rows = P(AXES, None)
    layered = P(None, AXES, None)
    expert = P(None, "fsdp", "expert", None)
    gain = P(None, AXES)
    regular = mesh.shape["fsdp"] == 8 and mesh.shape["expert"] == 4
    return jax.shard_map(
        shards_fast if regular else shards,
        mesh=mesh,
        in_specs=(rows, rows, layered, layered, rows, gain, gain)
        + (layered,) * 4
        + (expert,) * 3,
        out_specs=(rows, rows, gain, gain) + (layered,) * 4 + (expert,) * 3,
        check_vma=False,
    )
```

```python
import functools
import math

import jax
import jax.numpy as jnp
from jax import lax
from jax.experimental import pallas as pl
from jax.experimental.pallas import tpu as pltpu
from jax.sharding import PartitionSpec as P

QUERY_HEADS = 24
KEY_VALUE_HEADS = 8
HEAD_DIMENSION = 64
CORES = 2

NORM_EPS = 1e-06
MASKED = -1000000000.0
AXES = ("fsdp", "expert")


class Place:
    def __init__(self):
        self.planes = lax.axis_size("fsdp") // CORES
        self.columns = lax.axis_size("expert")
        fsdp = lax.axis_index("fsdp")
        self.plane = fsdp // CORES
        self.core = fsdp % CORES
        self.column = lax.axis_index("expert")

    def hop(self, value, up=0, flip=0, swap=0):
        pairs = []
        for plane in range(self.planes):
            for core in range(CORES):
                for column in range(self.columns):
                    source = (plane * CORES + core) * self.columns + column
                    target = ((plane + up) % self.planes * CORES + (core ^ swap)) * self.columns
                    pairs.append((source, target + (column ^ flip)))
        return lax.ppermute(value, AXES, pairs)


def spread(place, block):
    if place.columns != 4:
        return [block] + [place.hop(block, flip=m) for m in range(1, place.columns)]
    half = block.shape[1] // 2
    one = place.hop(block, flip=1)
    two = place.hop(block, flip=2)
    head = place.hop(one[:, :half], flip=2)
    tail = place.hop(two[:, half:], flip=1)
    return [block, one, two, jnp.concatenate([head, tail], axis=1)]


def gather_tokens(place, block):
    own = block[None]
    others = jnp.stack([place.hop(block, up=k) for k in range(1, place.planes)])
    near = spread(place, own)
    far = spread(place, others)
    return [jnp.concatenate([a, b], axis=0) for a, b in zip(near, far)]


def fold(place, parts):
    wide = lambda value: value.astype(jnp.float32)
    if place.columns != 4:
        total = wide(parts[0])
        for m in range(1, place.columns):
            total = total + wide(place.hop(parts[m], flip=m))
        return total
    half = parts[0].shape[1] // 2
    head = place.hop(parts[3][:, :half], flip=2)
    tail = place.hop(parts[3][:, half:], flip=1)
    one_tail = place.hop(parts[1][:, half:], flip=1)
    two_head = place.hop(parts[2][:, :half], flip=2)
    one_head = place.hop((wide(parts[1][:, :half]) + wide(head)).astype(parts[1].dtype), flip=1)
    two_tail = place.hop((wide(parts[2][:, half:]) + wide(tail)).astype(parts[2].dtype), flip=2)
    upper = wide(parts[0][:, :half]) + wide(one_head) + wide(two_head)
    lower = wide(parts[0][:, half:]) + wide(one_tail) + wide(two_tail)
    return jnp.concatenate([upper, lower], axis=1)


def scatter_sums(place, parts):
    far = fold(place, [part[1:] for part in parts]).astype(parts[0].dtype)
    arrived = [place.hop(far[k - 1], up=-k) for k in range(1, place.planes)]
    total = fold(place, [part[:1] for part in parts])[0]
    for piece in arrived:
        total = total + piece.astype(jnp.float32)
    return total


def gate_table(routes, gates, expert_count):
    names = jnp.arange(expert_count, dtype=jnp.int32)
    chosen = routes[:, None, :, :] == names[None, :, None, None]
    return jnp.sum(jnp.where(chosen, gates[:, None, :, :], 0.0), axis=3)


def spread_gates(place, table):
    axis = table.ndim - 2
    owned = table.shape[axis] // place.columns
    found = []
    for m in range(place.columns):
        start = (place.column ^ m) * owned
        piece = lax.dynamic_slice_in_dim(table, start, owned, axis=axis)
        found.append(place.hop(piece, flip=m) if m else piece)
    return found


def gather_gates(place, routes, gates, expert_count):
    table = gate_table(routes, gates, expert_count)
    line = jnp.stack([table] + [place.hop(table, up=k) for k in range(1, place.planes)])
    return spread_gates(place, line)


def gather_experts(place, weights):
    rows, experts, hidden = weights[0].shape
    share = hidden // place.planes

    def cut(plane):
        pieces = [lax.dynamic_slice_in_dim(w, plane * share, share, axis=2) for w in weights]
        return jnp.stack([p.reshape(rows, experts * share) for p in pieces])

    own = [cut(place.plane)]
    for k in range(1, place.planes):
        own.append(place.hop(cut((place.plane + k) % place.planes), up=k))
    own = jnp.stack(own)
    sibling = place.hop(own, swap=1)
    both = jnp.concatenate([own, sibling])
    shard = jnp.arange(place.planes * CORES)
    index = ((shard % CORES) ^ place.core) * place.planes
    index = index + (place.plane - shard // CORES) % place.planes
    return [
        jnp.take(both[:, i], index, axis=0).reshape(-1, experts * share)
        for i in range(len(weights))
    ]


def scatter_experts(place, grads, experts):
    features, width = grads[0].shape
    rows = features // (place.planes * CORES)
    share = width // experts
    shape = (place.planes, CORES, rows, width)
    stacked = jnp.stack([g.reshape(shape) for g in grads], axis=1)
    mine = lax.dynamic_index_in_dim(stacked, place.core, axis=2, keepdims=False)
    others = lax.dynamic_index_in_dim(stacked, 1 - place.core, axis=2, keepdims=False)
    arrived = place.hop(others.astype(jnp.bfloat16), swap=1)
    total = (mine + arrived.astype(jnp.float32)).astype(jnp.bfloat16)
    pieces = [lax.dynamic_index_in_dim(total, place.plane, axis=0, keepdims=False)]
    for k in range(1, place.planes):
        target = (place.plane + k) % place.planes
        piece = lax.dynamic_index_in_dim(total, target, axis=0, keepdims=False)
        pieces.append(place.hop(piece, up=k))
    index = (place.plane - jnp.arange(place.planes)) % place.planes
    ordered = jnp.take(jnp.stack(pieces), index, axis=0)
    ordered = ordered.reshape(place.planes, len(grads), rows, experts, share)
    ordered = jnp.transpose(ordered, (1, 2, 3, 0, 4)).reshape(len(grads), rows, experts, -1)
    return [ordered[i].astype(jnp.float32) for i in range(len(grads))]


def positions(length_row, count_of_rows):
    ends = jnp.cumsum(length_row)
    token_order = jnp.arange(count_of_rows, dtype=jnp.int32)
    passed = token_order[:, None] >= ends[None, :]
    segment = jnp.sum(passed.astype(jnp.int32), axis=1)
    before = jnp.sum(jnp.where(passed, length_row[None, :], 0), axis=1)
    return (segment, token_order - before)


def rope_tables(seq_place, head_width):
    half_width = head_width // 2
    freq_table = jnp.exp(
        jnp.arange(half_width, dtype=jnp.float32) * (-2.0 * math.log(10000.0) / head_width)
    )
    angles = seq_place.astype(jnp.float32)[:, None] * freq_table[None, :]
    return (jnp.cos(angles), jnp.sin(angles))


def apply_rotation(vector, cosine_table, sine_table):
    half_width = vector.shape[-1] // 2
    former = vector[..., :half_width]
    latter = vector[..., half_width:]
    cos_wide = cosine_table[:, None, :]
    sin_wide = sine_table[:, None, :]
    return jnp.concatenate(
        [former * cos_wide - latter * sin_wide, latter * cos_wide + former * sin_wide], axis=-1
    )


def reverse_rotation(vector, cosine_table, sine_table):
    return apply_rotation(vector, cosine_table, -sine_table)


def rms_forward(residual, norm_gain):
    inverse = lax.rsqrt(jnp.mean(residual * residual, axis=-1, keepdims=True) + NORM_EPS)
    return (inverse, (residual * inverse * norm_gain).astype(jnp.bfloat16))


def rms_backward(residual, inverse, norm_gain, upstream):
    gain_grad = jnp.sum(upstream * residual * inverse, axis=0)
    scaled = upstream * norm_gain
    inner = jnp.mean(scaled * residual, axis=-1, keepdims=True)
    return (gain_grad, inverse * scaled - residual * inverse * inverse * inverse * inner)


def score_block(rotated_query, turned_k, allowed):
    scores = jnp.einsum(
        "qhgd,khd->hgqk", rotated_query, turned_k, preferred_element_type=jnp.float32
    ) * HEAD_DIMENSION ** (-0.5)
    return jnp.where(allowed, scores, MASKED)


def attend_forward(residual, allowed, tables, gain, matrices):
    w_in, w_output = matrices
    count_of_rows = residual.shape[0]
    query_width = QUERY_HEADS * HEAD_DIMENSION
    key_width = KEY_VALUE_HEADS * HEAD_DIMENSION
    inverse, normalized_input = rms_forward(residual, gain)
    projected = jnp.dot(normalized_input, w_in, preferred_element_type=jnp.float32)
    query_unrotated = projected[:, :query_width].reshape(count_of_rows, QUERY_HEADS, -1)
    key_unrotated = projected[:, query_width : query_width + key_width]
    key_unrotated = key_unrotated.reshape(count_of_rows, KEY_VALUE_HEADS, -1)
    value_rows = projected[:, query_width + key_width :].astype(jnp.bfloat16)
    value_rows = value_rows.reshape(count_of_rows, KEY_VALUE_HEADS, -1)
    rotated_query = (
        apply_rotation(query_unrotated, *tables)
        .astype(jnp.bfloat16)
        .reshape(count_of_rows, KEY_VALUE_HEADS, QUERY_HEADS // KEY_VALUE_HEADS, HEAD_DIMENSION)
    )
    turned_k = apply_rotation(key_unrotated, *tables).astype(jnp.bfloat16)
    scores = score_block(rotated_query, turned_k, allowed)
    row_top = jnp.max(scores, axis=-1, keepdims=True)
    exp_scores = jnp.exp(scores - row_top)
    row_total = jnp.sum(exp_scores, axis=-1, keepdims=True)
    attn_probs = (exp_scores / row_total).astype(jnp.bfloat16)
    log_total = row_top + jnp.log(row_total)
    mixed_heads = jnp.einsum(
        "hgqk,khd->qhgd", attn_probs, value_rows, preferred_element_type=jnp.float32
    )
    mixed_heads = mixed_heads.astype(jnp.bfloat16).reshape(count_of_rows, query_width)
    attn_out = jnp.dot(mixed_heads, w_output, preferred_element_type=jnp.float32)
    return (
        residual + attn_out,
        (inverse, normalized_input, rotated_query, turned_k, value_rows, log_total, mixed_heads),
    )


def attend_backward(residual, allowed, tables, gain, matrices, stash, upstream):
    w_in, w_output = matrices
    inverse, normalized_input, rotated_query, turned_k, value_rows, log_total, mixed_heads = stash
    count_of_rows = residual.shape[0]
    branch_grad = upstream.astype(jnp.bfloat16)
    grad_wo = jnp.einsum("td,te->de", mixed_heads, branch_grad, preferred_element_type=jnp.float32)
    mixed_gradient = jnp.einsum(
        "te,de->td", branch_grad, w_output, preferred_element_type=jnp.float32
    )
    mixed_gradient = mixed_gradient.astype(jnp.bfloat16).reshape(
        count_of_rows, KEY_VALUE_HEADS, QUERY_HEADS // KEY_VALUE_HEADS, HEAD_DIMENSION
    )
    attn_probs = jnp.exp(score_block(rotated_query, turned_k, allowed) - log_total)
    value_rows_gradient = jnp.einsum(
        "hgqk,qhgd->khd",
        attn_probs.astype(jnp.bfloat16),
        mixed_gradient,
        preferred_element_type=jnp.float32,
    )
    value_rows_gradient = value_rows_gradient.astype(jnp.bfloat16).reshape(count_of_rows, -1)
    grad_probs = jnp.einsum(
        "qhgd,khd->hgqk", mixed_gradient, value_rows, preferred_element_type=jnp.float32
    )
    grad_scores = attn_probs * (
        grad_probs - jnp.sum(attn_probs * grad_probs, axis=-1, keepdims=True)
    )
    grad_scores = grad_scores.astype(jnp.bfloat16)
    grad_tq = jnp.einsum(
        "hgqk,khd->qhgd", grad_scores, turned_k, preferred_element_type=jnp.float32
    ) * HEAD_DIMENSION ** (-0.5)
    turned_key_gradient = jnp.einsum(
        "hgqk,qhgd->khd", grad_scores, rotated_query, preferred_element_type=jnp.float32
    ) * HEAD_DIMENSION ** (-0.5)
    grad_query = reverse_rotation(
        grad_tq.reshape(count_of_rows, QUERY_HEADS, HEAD_DIMENSION), *tables
    )
    grad_query = grad_query.astype(jnp.bfloat16).reshape(count_of_rows, -1)
    grad_key = reverse_rotation(turned_key_gradient, *tables).astype(jnp.bfloat16)
    grad_key = grad_key.reshape(count_of_rows, -1)
    grad_in = jnp.concatenate([grad_query, grad_key, value_rows_gradient], axis=1)
    grad_w_in = jnp.einsum("td,te->de", normalized_input, grad_in, preferred_element_type=jnp.float32)
    grad_normed = jnp.einsum("te,de->td", grad_in, w_in, preferred_element_type=jnp.float32)
    gain_grad, residual_grad = rms_backward(residual, inverse, gain, grad_normed)
    return (upstream + residual_grad, gain_grad, grad_w_in, grad_wo)


def widen(gate_columns, share):
    return jnp.repeat(gate_columns, share, axis=1)


def experts_forward(place, middle, gain, gate_parts, weights):
    w_gate, w_up, w_down = weights
    share = w_gate.shape[1] // gate_parts[0].shape[1]
    model_width = middle.shape[1]
    inverse, normalized_input = rms_forward(middle, gain)
    chunks = gather_tokens(place, normalized_input)
    parts, kept = [], []
    for chunk, gate_columns in zip(chunks, gate_parts):
        rows = chunk.reshape(-1, model_width)
        gate_pre = jnp.dot(rows, w_gate, preferred_element_type=jnp.float32)
        up_pre = jnp.dot(rows, w_up, preferred_element_type=jnp.float32)
        weighed = gate_pre * jax.nn.sigmoid(gate_pre) * up_pre * widen(gate_columns, share)
        weighed = weighed.astype(jnp.bfloat16)
        produced = lax.dot_general(
            weighed, w_down, (((1,), (1,)), ((), ())), preferred_element_type=jnp.float32
        )
        parts.append(produced.astype(jnp.bfloat16).reshape(chunk.shape))
        kept.append((rows, gate_pre, up_pre, weighed))
    return (middle + scatter_sums(place, parts), (inverse, kept))


def experts_backward(place, middle, gain, gate_parts, weights, stash, upstream, chunks):
    w_gate, w_up, w_down = weights
    share = w_gate.shape[1] // gate_parts[0].shape[1]
    model_width = middle.shape[1]
    inverse, kept = stash
    parts, gate_grads, up_grads, row_grads = [], [], [], []
    for chunk, gate_columns, (rows, gate_pre, up_pre, weighed) in zip(chunks, gate_parts, kept):
        grads = chunk.reshape(-1, model_width)
        hidden_grad = jnp.dot(grads, w_down, preferred_element_type=jnp.float32)
        hidden_grad = hidden_grad * widen(gate_columns, share)
        gate_sig = jax.nn.sigmoid(gate_pre)
        gate_grad = hidden_grad * up_pre * gate_sig * (1.0 + gate_pre * (1.0 - gate_sig))
        gate_grad = gate_grad.astype(jnp.bfloat16)
        up_grad = (hidden_grad * gate_pre * gate_sig).astype(jnp.bfloat16)
        back = (((1,), (1,)), ((), ()))
        produced = lax.dot_general(gate_grad, w_gate, back, preferred_element_type=jnp.float32)
        produced = produced + lax.dot_general(
            up_grad, w_up, back, preferred_element_type=jnp.float32
        )
        parts.append(produced.astype(jnp.bfloat16).reshape(chunk.shape))
        gate_grads.append(gate_grad)
        up_grads.append(up_grad)
        row_grads.append(grads)
    normed_grad = scatter_sums(place, parts)
    rows = jnp.concatenate([entry[0] for entry in kept])
    weighed = jnp.concatenate([entry[3] for entry in kept])
    outer = (((0,), (0,)), ((), ()))
    weight_grads = [
        lax.dot_general(a, b, outer, preferred_element_type=jnp.float32)
        for a, b in (
            (rows, jnp.concatenate(gate_grads)),
            (rows, jnp.concatenate(up_grads)),
            (jnp.concatenate(row_grads), weighed),
        )
    ]
    gain_grad, middle_grad = rms_backward(middle, inverse, gain, normed_grad)
    return (upstream + middle_grad, gain_grad, weight_grads)


def shards(
    tokens,
    lengths,
    routes,
    gates,
    cotangent,
    norm_attn,
    norm_ffn,
    query,
    key,
    value,
    output,
    w_gate,
    w_up,
    w_down,
):
    place = Place()
    token_rows = tokens.shape[0]
    layer_count, _, experts, _ = w_gate.shape
    expert_count = experts * place.columns
    in_width = query.shape[2] + key.shape[2] + value.shape[2]
    segment, seq_place = positions(lengths[0], token_rows)
    tables = rope_tables(seq_place, HEAD_DIMENSION)
    token_order = jnp.arange(token_rows, dtype=jnp.int32)
    allowed = (segment[:, None] == segment[None, :]) & (
        token_order[:, None] >= token_order[None, :]
    )
    gains = jnp.concatenate([norm_attn, norm_ffn]).T
    packs = []
    for l in range(layer_count):
        pack = [query[l], key[l], value[l], output[l]]
        if l == 0:
            pack.append(jnp.pad(gains, ((0, 0), (0, 128 - gains.shape[1]))))
        packs.append(jnp.concatenate(pack, axis=1))
    full = lax.all_gather(packs[0], AXES, axis=0, tiled=True)
    gains = full[:, in_width + output.shape[2] :].T[: 2 * layer_count].astype(jnp.float32)
    gate_rows = gather_gates(place, routes, gates, expert_count)
    gate_parts = [
        [
            jnp.transpose(piece[:, l], (0, 2, 1)).reshape(-1, experts)
            for piece in gate_rows
        ]
        for l in range(layer_count)
    ]
    expert_weights = gather_experts(place, [w_gate[0], w_up[0], w_down[0]])
    last_grads = None

    residual = tokens.astype(jnp.float32)
    matrices, weights, stored = [], [], []
    for l in range(layer_count):
        matrices.append((full[:, :in_width], full[:, in_width : in_width + output.shape[2]]))
        weights.append(expert_weights)
        layer_input = residual
        middle, attn_stash = attend_forward(layer_input, allowed, tables, gains[l], matrices[l])
        if l + 1 < layer_count:
            held, pack, *shares = lax.optimization_barrier(
                (middle, packs[l + 1], w_gate[l + 1], w_up[l + 1], w_down[l + 1])
            )
            middle = held
            full = lax.all_gather(pack, AXES, axis=0, tiled=True)
            expert_weights = gather_experts(place, shares)
        residual, moe_stash = experts_forward(
            place, middle, gains[layer_count + l], gate_parts[l], weights[l]
        )
        if l + 2 == layer_count or layer_count == 1:
            held, last = lax.optimization_barrier((residual, cotangent))
            residual = held
            last_grads = gather_tokens(place, last)
        stored.append((layer_input, middle, attn_stash, moe_stash))
    result = residual.astype(jnp.bfloat16)

    upstream = cotangent.astype(jnp.float32)
    in_grads, out_grads = [None] * layer_count, [None] * layer_count
    gain_grads = [None] * (2 * layer_count)
    expert_grads = [None] * layer_count
    for l in reversed(range(layer_count)):
        layer_input, middle, attn_stash, moe_stash = stored[l]
        chunks = last_grads
        if l + 1 < layer_count:
            chunks = gather_tokens(place, upstream.astype(jnp.bfloat16))
        upstream, gain_grads[layer_count + l], weight_grads = experts_backward(
            place,
            middle,
            gains[layer_count + l],
            gate_parts[l],
            weights[l],
            moe_stash,
            upstream,
            chunks,
        )
        expert_grads[l] = scatter_experts(place, weight_grads, experts)
        upstream, gain_grads[l], grad_w_in, grad_wo = attend_backward(
            layer_input, allowed, tables, gains[l], matrices[l], attn_stash, upstream
        )
        summed = lax.psum_scatter(
            jnp.concatenate([grad_w_in, grad_wo], axis=1).astype(jnp.bfloat16),
            AXES,
            scatter_dimension=0,
            tiled=True,
        ).astype(jnp.float32)
        in_grads[l], out_grads[l] = summed[:, :in_width], summed[:, in_width:]
    gain_sums = lax.psum_scatter(jnp.stack(gain_grads), AXES, scatter_dimension=1, tiled=True)
    in_grads = jnp.stack(in_grads)
    key_start, value_start = query.shape[2], query.shape[2] + key.shape[2]
    return (
        result,
        upstream,
        gain_sums[:layer_count],
        gain_sums[layer_count:],
        in_grads[:, :, :key_start],
        in_grads[:, :, key_start:value_start],
        in_grads[:, :, value_start:],
        jnp.stack(out_grads),
        jnp.stack([entry[0] for entry in expert_grads]),
        jnp.stack([entry[1] for entry in expert_grads]),
        jnp.stack([entry[2] for entry in expert_grads]),
    )


HEADS_PER_TURN = 6
LANES = 128
EXTRA = 128
HALF = 64
MIB = 1 << 20
COST_PART = 16


def cost(flops):
    return pl.CostEstimate(flops=flops // COST_PART, bytes_accessed=0, transcendentals=0)


def any_spec():
    return pl.BlockSpec(memory_space=pl.ANY)


def whole_spec():
    return pl.BlockSpec(memory_space=pltpu.VMEM)


def scalar_spec():
    return pl.BlockSpec(memory_space=pltpu.SMEM)


def shape_of(*dims, dtype=jnp.bfloat16):
    return jax.ShapeDtypeStruct(dims, dtype)


class Copies:
    def __init__(self, semaphores, first=0):
        self.semaphores = semaphores
        self.used = first
        self.open = []

    def start(self, source, target):
        copy = pltpu.make_async_copy(source, target, self.semaphores.at[self.used])
        self.used += 1
        copy.start()
        self.open.append(copy)

    def wait(self):
        for copy in self.open:
            copy.wait()
        self.open = []


def shard_row(where, swapped, m, k, rows):
    plane = lax.rem(where[0] - k + 4, 4)
    fsdp = plane * CORES + (where[1] ^ swapped)
    return pl.multiple_of((fsdp * 4 + (where[2] ^ m)) * rows, 16)


MATRIX_PIECES = 10
MATRIX_COPIES = 40


def load_columns(copies, where, pieces, full, low, high):
    rows, cut = pieces[0].shape[0] // 4, pieces[3].shape[1]
    spans = ((0, 0, full.shape[1]), (1, 0, full.shape[1]), (2, 0, full.shape[1]), (3, 0, cut))
    spans += ((3, cut, full.shape[1]),)
    for swapped in range(CORES):
        for index, (m, first, last) in enumerate(spans):
            begin, end = max(low, first), min(high, last)
            if begin >= end:
                continue
            for k in range(4):
                row = shard_row(where, swapped, m, k, rows)
                copies.start(
                    pieces[swapped * 5 + index].at[
                        pl.ds(k * rows, rows), pl.ds(begin - first, end - begin)
                    ],
                    full.at[pl.ds(row, rows), pl.ds(begin, end - begin)],
                )


def half_swap(x):
    lane = lax.broadcasted_iota(jnp.int32, x.shape, 1)
    return jnp.where(lane % 64 < 32, pltpu.roll(x, 96, 1), pltpu.roll(x, 32, 1))


def both_sides(pair, side):
    lane = lax.broadcasted_iota(jnp.int32, pair.shape, 1)
    wide = pair.astype(jnp.float32)
    here = jnp.where(lane // 64 == side, wide, 0.0)
    there = pltpu.roll(here, 64, 1)
    here, there = here.astype(jnp.bfloat16), there.astype(jnp.bfloat16)
    return (here, there) if side == 0 else (there, here)


def merge_sides(even, odd, side):
    lane = lax.broadcasted_iota(jnp.int32, even.shape, 1)
    if side == 0:
        return jnp.where(lane < 64, even + pltpu.roll(odd, 64, 1), 0.0)
    return jnp.where(lane < 64, 0.0, odd + pltpu.roll(even, 64, 1))


def contract(a, b, dims):
    return lax.dot_general(a, b, (dims, ((), ())), preferred_element_type=jnp.float32)


PLAIN = ((1,), (0,))
ACROSS = ((1,), (1,))
OUTER = ((0,), (0,))


def read_sum(base, extra):
    total = base[...].astype(jnp.float32)
    for term in extra:
        total = total + term[pl.ds(0, total.shape[0]), :].astype(jnp.float32)
    return total


def attend_forward_kernel(terms, width, where, base, *refs):
    refs = list(refs)
    extra = [refs.pop(0) for _ in range(terms)]
    cosine, sine, allowed = refs[:3]
    pieces = refs[3 : 3 + MATRIX_PIECES]
    refs = refs[3 + MATRIX_PIECES :]
    h_out, m_out, nf_out, na_out, q_out, k_out, v_out, o_out, lse_out, gain_out = refs[:10]
    full, proj, mixed, semaphores = refs[10:]
    model = full.shape[0]
    in_width = width
    copies = Copies(semaphores)
    load_columns(copies, where, pieces, full, 0, in_width)
    load_columns(copies, where, pieces, full, in_width + model, full.shape[1])
    later = Copies(semaphores, copies.used)
    load_columns(later, where, pieces, full, in_width, in_width + model)
    h = read_sum(base, extra)
    h_out[...] = h
    inverse = lax.rsqrt(jnp.mean(h * h, axis=1, keepdims=True) + NORM_EPS)
    key_start = model
    value_start = model + (in_width - model) // 2
    copies.wait()
    gains = full[:, pl.ds(in_width + model, EXTRA)].astype(jnp.float32).T
    gain_out[...] = gains[:8]
    na_out[...] = (h * inverse * gains[0:1]).astype(jnp.bfloat16)
    step = 512

    @pl.loop(0, in_width // step)
    def _(i):
        columns = pl.ds(pl.multiple_of(i * step, step), step)
        proj[:, columns] = contract(na_out[...], full[:, columns], PLAIN)

    cos, sin = cosine[...], sine[...]

    @pl.loop(0, key_start // LANES)
    def _(i):
        columns = pl.ds(pl.multiple_of(i * LANES, LANES), LANES)
        x = proj[:, columns]
        q_out[:, columns] = (x * cos + half_swap(x) * sin).astype(jnp.bfloat16)

    @pl.loop(0, (value_start - key_start) // LANES)
    def _(i):
        start = pl.multiple_of(i * LANES, LANES)
        x = proj[:, pl.ds(key_start + start, LANES)]
        k_out[:, pl.ds(start, LANES)] = (x * cos + half_swap(x) * sin).astype(jnp.bfloat16)

    v_out[...] = proj[:, value_start:in_width].astype(jnp.bfloat16)
    lse_out[...] = jnp.zeros_like(lse_out)
    open_keys = allowed[...] > 0.5
    lane = lax.broadcasted_iota(jnp.int32, open_keys.shape, 1)

    @pl.loop(0, KEY_VALUE_HEADS // 2)
    def _(turn):
        pair = pl.ds(pl.multiple_of(turn * LANES, LANES), LANES)
        keys = [both_sides(k_out[:, pair], side) for side in range(2)]
        values = [both_sides(v_out[:, pair], side) for side in range(2)]
        lse = lse_out[...]
        for group in range(HEADS_PER_TURN // 2):
            columns = pl.ds(
                pl.multiple_of(turn * (HEADS_PER_TURN * 64) + group * LANES, LANES), LANES
            )
            total = jnp.zeros((h.shape[0], LANES), jnp.float32)
            for side in range(2):
                head = group * 2 + side
                scores = contract(q_out[:, columns], keys[head // 3][side], ACROSS)
                scores = jnp.where(open_keys, scores * HEAD_DIMENSION ** (-0.5), MASKED)
                top = jnp.max(scores, axis=1, keepdims=True)
                weights = jnp.exp(scores - top)
                row_total = jnp.sum(weights, axis=1, keepdims=True)
                probs = (weights / row_total).astype(jnp.bfloat16)
                lse = jnp.where(lane == turn * HEADS_PER_TURN + head, top + jnp.log(row_total), lse)
                total = total + contract(probs, values[head // 3][side], PLAIN)
            o_out[:, columns] = total.astype(jnp.bfloat16)
        lse_out[...] = lse

    later.wait()

    @pl.loop(0, model // step)
    def _(i):
        columns = pl.ds(pl.multiple_of(i * step, step), step)
        weights = full[:, pl.ds(pl.multiple_of(in_width + i * step, step), step)]
        mixed[:, columns] = contract(o_out[...], weights, PLAIN)

    m = h_out[...] + mixed[...]
    m_out[...] = m
    inverse = lax.rsqrt(jnp.mean(m * m, axis=1, keepdims=True) + NORM_EPS)
    nf_out[...] = (m * inverse * gain_out[1:2]).astype(jnp.bfloat16)


def attend_forward_fast(where, base, extra, tables, pieces, in_width, after=()):
    rows, model = base.shape
    bf, f32 = jnp.bfloat16, jnp.float32
    key_width = (in_width - model) // 2
    total = in_width + model + EXTRA
    shapes = [
        shape_of(rows, model, dtype=f32),
        shape_of(rows, model, dtype=f32),
        shape_of(rows, model),
        shape_of(rows, model),
        shape_of(rows, model),
        shape_of(rows, key_width),
        shape_of(rows, key_width),
        shape_of(rows, model),
        shape_of(rows, LANES, dtype=f32),
        shape_of(8, model, dtype=f32),
    ]

    def body(*refs):
        used = 2 + len(extra) + 3 + MATRIX_PIECES
        attend_forward_kernel(len(extra), in_width, *refs[:used], *refs[used + len(after) :])

    return pl.pallas_call(
        body,
        name="attend_forward",
        out_shape=shapes,
        in_specs=[scalar_spec()]
        + [whole_spec()] * (4 + len(extra))
        + [any_spec()] * (MATRIX_PIECES + len(after)),
        out_specs=[whole_spec()] * len(shapes),
        scratch_shapes=[
            pltpu.VMEM((model, total), bf),
            pltpu.VMEM((rows, in_width), f32),
            pltpu.VMEM((rows, model), f32),
            pltpu.SemaphoreType.DMA((3 * MATRIX_COPIES,)),
        ],
        compiler_params=pltpu.CompilerParams(vmem_limit_bytes=44 * MIB),
        cost_estimate=cost(2 * rows * model * total),
    )(where, base, *extra, *tables, *pieces, *after)


def attend_backward_kernel(groups, terms, width, where, base, upstream, *refs):
    refs = list(refs)
    extra = [refs.pop(0) for _ in range(terms)]
    h_in, m_in, na, q, k, v, o, lse_in, gains, cosine, sine, allowed = refs[:12]
    pieces = refs[12 : 12 + MATRIX_PIECES]
    outs, refs = refs[12 + MATRIX_PIECES : -6], refs[-6:]
    gh_out, gh_low = outs[:2]
    full, sums, mixed, grad_in, turned, semaphores = refs
    rows, model = h_in.shape
    in_width = width
    key_start = model
    value_start = model + (in_width - model) // 2
    shard = full.shape[0] // 32
    copies = Copies(semaphores)
    load_columns(copies, where, pieces, full, in_width, in_width + model)
    later = Copies(semaphores, copies.used)
    load_columns(later, where, pieces, full, 0, in_width)
    gnf = read_sum(base, extra)
    m = m_in[...]
    inverse = lax.rsqrt(jnp.mean(m * m, axis=1, keepdims=True) + NORM_EPS)
    gain_ffn = jnp.sum(gnf * m * inverse, axis=0, keepdims=True)
    scaled = gnf * gains[1:2]
    inner = jnp.mean(scaled * m, axis=1, keepdims=True)
    gm = upstream[...].astype(jnp.float32)
    gm = gm + inverse * scaled - m * (inverse * inverse * inverse) * inner
    gh_out[...] = gm
    gh_low[...] = gm.astype(jnp.bfloat16)
    copies.wait()
    step = 512

    @pl.loop(0, model // step)
    def _(i):
        row = pl.ds(pl.multiple_of(i * step, step), step)
        mixed[:, row] = contract(gh_low[...], full[row, in_width : in_width + model], ACROSS).astype(
            jnp.bfloat16
        )

    open_keys = allowed[...] > 0.5
    lane = lax.broadcasted_iota(jnp.int32, open_keys.shape, 1)
    cos, sin = cosine[...], sine[...]
    scale = HEAD_DIMENSION ** (-0.5)

    @pl.loop(0, KEY_VALUE_HEADS // 2)
    def _(turn):
        start = pl.multiple_of(turn * LANES, LANES)
        pair = pl.ds(start, LANES)
        keys = [both_sides(k[:, pair], side) for side in range(2)]
        values = [both_sides(v[:, pair], side) for side in range(2)]
        zero = jnp.zeros((rows, LANES), jnp.float32)
        grad_k = [[zero, zero], [zero, zero]]
        grad_v = [[zero, zero], [zero, zero]]
        lse = lse_in[...]
        for group in range(HEADS_PER_TURN // 2):
            columns = pl.ds(
                pl.multiple_of(turn * (HEADS_PER_TURN * 64) + group * LANES, LANES), LANES
            )
            grad_q = zero
            for side in range(2):
                head = group * 2 + side
                kv = head // 3
                top = jnp.sum(
                    jnp.where(lane == turn * HEADS_PER_TURN + head, lse, 0.0), axis=1, keepdims=True
                )
                scores = contract(q[:, columns], keys[kv][side], ACROSS) * scale
                probs = jnp.exp(jnp.where(open_keys, scores, MASKED) - top)
                go = mixed[:, columns]
                grad_v[kv][side] = grad_v[kv][side] + contract(
                    probs.astype(jnp.bfloat16), go, OUTER
                )
                grad_p = contract(go, values[kv][side], ACROSS)
                grad_s = probs * (grad_p - jnp.sum(probs * grad_p, axis=1, keepdims=True))
                grad_s = grad_s.astype(jnp.bfloat16)
                grad_q = grad_q + contract(grad_s, keys[kv][side], PLAIN)
                grad_k[kv][side] = grad_k[kv][side] + contract(grad_s, q[:, columns], OUTER)
            grad_q = grad_q * scale
            grad_in[:, columns] = (grad_q * cos - half_swap(grad_q) * sin).astype(jnp.bfloat16)
        key_grad = merge_sides(*grad_k[0], 0) + merge_sides(*grad_k[1], 1)
        key_grad = key_grad * scale
        key_grad = key_grad * cos - half_swap(key_grad) * sin
        value_grad = merge_sides(*grad_v[0], 0) + merge_sides(*grad_v[1], 1)
        grad_in[:, pl.ds(key_start + start, LANES)] = key_grad.astype(jnp.bfloat16)
        grad_in[:, pl.ds(value_start + start, LANES)] = value_grad.astype(jnp.bfloat16)

    band = 384

    @pl.loop(0, model // band)
    def _(i):
        start = pl.multiple_of(i * band, band)
        row = pl.ds(start, band)
        sums[row, in_width : in_width + model] = contract(o[:, row], gh_low[...], OUTER).astype(
            jnp.bfloat16
        )
        sums[row, :in_width] = contract(na[:, row], grad_in[...], OUTER).astype(jnp.bfloat16)

    def store_sums(low, width):
        at = 2
        for swapped in (1, 0):
            for first, count in groups:
                for m_index in range(4):
                    for n in range(count):
                        row = shard_row(where, swapped, m_index, first + n, shard)
                        place = pl.ds((m_index * count + n) * shard, shard)
                        columns = pl.ds(low, width)
                        later.start(
                            sums.at[pl.ds(row, shard), columns], outs[at].at[place, columns]
                        )
                at += 1

    later.wait()
    store_sums(0, in_width + model)
    turned[...] = jnp.zeros_like(turned)

    @pl.loop(0, in_width // step)
    def _(i):
        columns = pl.ds(pl.multiple_of(i * step, step), step)
        turned[...] += contract(grad_in[:, columns], full[:, columns], ACROSS)

    grad_na = turned[...]
    h = h_in[...]
    inverse = lax.rsqrt(jnp.mean(h * h, axis=1, keepdims=True) + NORM_EPS)
    gain_attn = jnp.sum(grad_na * h * inverse, axis=0, keepdims=True)
    scaled = grad_na * gains[0:1]
    inner = jnp.mean(scaled * h, axis=1, keepdims=True)
    both = jnp.concatenate([gain_attn, gain_ffn, jnp.zeros((EXTRA - 2, model), jnp.float32)], axis=0)
    sums[:, pl.ds(in_width + model, EXTRA)] = both.T.astype(jnp.bfloat16)
    store_sums(in_width + model, EXTRA)
    gh = gh_out[...] + inverse * scaled - h * (inverse * inverse * inverse) * inner
    gh_out[...] = gh
    gh_low[...] = gh.astype(jnp.bfloat16)
    later.wait()


def attend_backward_fast(
    groups, where, base, upstream, extra, stash, tables, pieces, in_width, after=()
):
    rows, model = upstream.shape
    bf, f32 = jnp.bfloat16, jnp.float32
    total = in_width + model + EXTRA
    shapes = [
        shape_of(rows, model, dtype=f32),
        shape_of(rows, model),
    ]
    shapes += [shape_of(model // 8 * count, total) for _, count in groups] * CORES

    def body(*refs):
        used = 3 + len(extra) + 12 + MATRIX_PIECES
        attend_backward_kernel(
            groups, len(extra), in_width, *refs[:used], *refs[used + len(after) :]
        )

    return pl.pallas_call(
        body,
        name="attend_backward",
        out_shape=shapes,
        in_specs=[scalar_spec()]
        + [whole_spec()] * (2 + len(extra) + 12)
        + [any_spec()] * (MATRIX_PIECES + len(after)),
        out_specs=[whole_spec()] * 2 + [any_spec()] * (len(shapes) - 2),
        scratch_shapes=[
            pltpu.VMEM((model, total), bf),
            pltpu.VMEM((model, total), bf),
            pltpu.VMEM((rows, model), bf),
            pltpu.VMEM((rows, in_width), bf),
            pltpu.VMEM((rows, model), f32),
            pltpu.SemaphoreType.DMA((2 * MATRIX_COPIES + 64,)),
        ],
        compiler_params=pltpu.CompilerParams(vmem_limit_bytes=56 * MIB),
        cost_estimate=cost(4 * rows * model * total),
    )(where, base, upstream, *extra, *stash, *tables, *pieces, *after)


SHARES = ((0, 0, 3), (1, 0, 3), (2, 0, 3), (3, 0, 3))
WEIGHT_PIECES = CORES * len(SHARES)


def load_experts(copies, where, pieces, targets):
    at = 0
    for swapped in range(CORES):
        for k, first, count in SHARES:
            piece = pieces[at]
            at += 1
            _, experts, rows, share = piece.shape
            fsdp = lax.rem(where[0] - k + 4, 4) * CORES + (where[1] ^ swapped)
            row = pl.ds(pl.multiple_of(fsdp * rows, 16), rows)
            for i, target in enumerate(targets[first : first + count]):
                for e in range(experts):
                    copies.start(piece.at[i, e], target.at[row, pl.ds(e * share, share)])


def load_weights(copies, where, weights, targets):
    if len(weights) > 1:
        load_experts(copies, where, weights, targets)
    else:
        rows = targets[0].shape[0] // 8
        for i, target in enumerate(targets):
            for n in range(8):
                row = pl.ds(n * rows, rows)
                copies.start(weights[0].at[i, row, :], target.at[row, :])


def widen_tile(columns, share, width):
    lane = lax.broadcasted_iota(jnp.int32, (columns.shape[0], width), 1)
    wide = jnp.broadcast_to(columns[:, 0:1], lane.shape)
    for e in range(1, width // share):
        wide = jnp.where(lane >= e * share, columns[:, e : e + 1], wide)
    return wide


def start_rows(copies, pieces, rows_ref):
    at = 0
    for piece in pieces:
        rows = piece.shape[0]
        copies.start(piece, rows_ref.at[pl.ds(at, rows), :])
        at += rows


class Pool:
    def __init__(self, semaphores, used=0):
        self.semaphores = semaphores
        self.used = used

    def copy(self, source, target):
        self.used += 1
        return pltpu.make_async_copy(source, target, self.semaphores.at[self.used - 1])


def rows_at(ref, first, count):
    return ref.at[pl.ds(first, count), :]


def tile_loads(pool, pieces, x):
    n = pieces[0].shape[0]
    found = [[pool.copy(pieces[m], rows_at(x, m * n, n))] for m in range(3)]
    half = n // 2
    last = [pool.copy(pieces[3 + i], rows_at(x, 3 * n + i * half, half)) for i in range(2)]
    return found + [last]


def tile_slices(pool, source, target, n):
    return [[pool.copy(rows_at(source, m * n, n), rows_at(target, m * n, n))] for m in range(4)]


def tile_parts(pool, y, parts):
    n = parts[0].shape[0]
    half = n // 2
    own, one_head, two_tail, to_one, to_two = parts

    def copy(first, count, part, at=0):
        return pool.copy(rows_at(y, first, count), rows_at(part, at, count))

    return [
        [copy(0, n, own)],
        [copy(n, half, one_head), copy(n + half, half, to_one)],
        [copy(2 * n, half, to_two), copy(2 * n + half, half, two_tail)],
        [copy(3 * n, half, to_two, half), copy(3 * n + half, half, to_one, half)],
    ]


def for_tile(i, groups, act):
    for m in range(4):

        @pl.when(i == m)
        def _():
            for group in groups:
                for copy in group[m]:
                    act(copy)


def finish(groups):
    for group in groups:
        for copies in group:
            for copy in copies:
                copy.wait()


def part_rows(n):
    return [n, n // 2, n // 2, n, n]


def experts_forward_kernel(share, count, where, gates, *refs):
    pieces, weights, refs = refs[:5], refs[5 : 5 + count], refs[5 + count :]
    parts, x_out, g_out, u_out = refs[:5], *refs[5:8]
    x, y, g, u, w_gate, w_up, w_down, semaphores = refs[-8:]
    laid = refs[8:-8]
    n = pieces[0].shape[0]
    pool = Pool(semaphores)
    loads = tile_loads(pool, pieces, x)
    for group in loads:
        for copy in group:
            copy.start()
    copies = Copies(semaphores, pool.used)
    load_weights(copies, where, weights, (w_gate, w_up, w_down))
    pool.used = copies.used
    pool.used = copies.used + 3
    kept = tile_slices(pool, x, x_out, n)
    stores = [
        tile_parts(pool, y, parts),
        tile_slices(pool, g, g_out, n),
        tile_slices(pool, u, u_out, n),
    ]
    width = w_gate.shape[1]
    copies.wait()
    for i, w in enumerate((w_gate, w_up, w_down)):
        if laid:
            copies.start(w, laid[0].at[i])

    @pl.loop(0, 4)
    def _(i):
        for_tile(i, [loads], lambda copy: copy.wait())
        for_tile(i, [kept], lambda copy: copy.start())
        row = pl.ds(pl.multiple_of(i * n, n), n)
        gate_pre = contract(x[row, :], w_gate[...], PLAIN)
        up_pre = contract(x[row, :], w_up[...], PLAIN)
        g[row, :] = gate_pre
        u[row, :] = up_pre
        wide = widen_tile(gates[row, :], share, width)
        weighed = (gate_pre * jax.nn.sigmoid(gate_pre) * up_pre * wide).astype(jnp.bfloat16)
        y[row, :] = contract(weighed, w_down[...], ACROSS).astype(jnp.bfloat16)
        for_tile(i, stores, lambda copy: copy.start())

    finish([kept, *stores])
    copies.wait()


def experts_forward_fast(experts, where, gates, pieces, weights, after=()):
    n, model = pieces[0].shape
    rows, count = 4 * n, len(weights)
    width = experts * weights[0].shape[3] if count > 1 else weights[0].shape[2]
    share = width // experts
    bf, f32 = jnp.bfloat16, jnp.float32
    shapes = [shape_of(r, model) for r in part_rows(n)]
    shapes += [shape_of(rows, model)] + [shape_of(rows, width, dtype=f32)] * 2
    if count > 1:
        shapes += [shape_of(3, model, width)]

    def body(*refs):
        used = 7 + count
        experts_forward_kernel(share, count, *refs[:used], *refs[used + len(after) :])

    return pl.pallas_call(
        body,
        name="experts_forward",
        out_shape=shapes,
        in_specs=[scalar_spec(), whole_spec()] + [any_spec()] * (5 + count + len(after)),
        out_specs=[any_spec()] * len(shapes),
        scratch_shapes=[
            pltpu.VMEM((rows, model), bf),
            pltpu.VMEM((rows, model), bf),
            pltpu.VMEM((rows, width), f32),
            pltpu.VMEM((rows, width), f32),
        ]
        + [pltpu.VMEM((model, width), bf)] * 3
        + [pltpu.SemaphoreType.DMA((24 * experts + 48,))],
        compiler_params=pltpu.CompilerParams(vmem_limit_bytes=48 * MIB),
        cost_estimate=cost(6 * rows * model * width),
    )(where, gates, *pieces, *weights, *after)


def experts_backward_kernel(share, where, gates, *refs):
    pieces, g_in, u_in = refs[:5], refs[5], refs[6]
    weights, refs = refs[7:8], refs[8:]
    parts, r_out, gg_out, gu_out, p_out = refs[:5], *refs[5:9]
    x, y, g, u, gg, gu, p, w_gate, w_up, w_down, semaphores = refs[9:]
    n = pieces[0].shape[0]
    pool = Pool(semaphores)
    loads = [
        tile_loads(pool, pieces, x),
        tile_slices(pool, g_in, g, n),
        tile_slices(pool, u_in, u, n),
    ]
    for group in loads[0]:
        for copy in group:
            copy.start()
    copies = Copies(semaphores, pool.used)
    load_weights(copies, where, weights, (w_gate, w_up, w_down))
    for loaded in loads[1:]:
        for group in loaded:
            for copy in group:
                copy.start()
    pool.used = copies.used
    kept = tile_slices(pool, x, r_out, n)
    stores = [
        tile_parts(pool, y, parts),
        tile_slices(pool, gg, gg_out, n),
        tile_slices(pool, gu, gu_out, n),
        tile_slices(pool, p, p_out, n),
    ]
    width = w_gate.shape[1]
    copies.wait()

    @pl.loop(0, 4)
    def _(i):
        for_tile(i, loads, lambda copy: copy.wait())
        for_tile(i, [kept], lambda copy: copy.start())
        row = pl.ds(pl.multiple_of(i * n, n), n)
        wide = widen_tile(gates[row, :], share, width)
        hidden_grad = contract(x[row, :], w_down[...], PLAIN) * wide
        gate_pre, up_pre = g[row, :], u[row, :]
        sig = jax.nn.sigmoid(gate_pre)
        active = gate_pre * sig
        p[row, :] = (active * up_pre * wide).astype(jnp.bfloat16)
        gate_grad = hidden_grad * up_pre * sig * (1.0 + gate_pre * (1.0 - sig))
        gg[row, :] = gate_grad.astype(jnp.bfloat16)
        gu[row, :] = (hidden_grad * active).astype(jnp.bfloat16)
        back = contract(gg[row, :], w_gate[...], ACROSS)
        back = back + contract(gu[row, :], w_up[...], ACROSS)
        y[row, :] = back.astype(jnp.bfloat16)
        for_tile(i, stores, lambda copy: copy.start())

    finish([kept, *stores])


def experts_backward_fast(experts, where, gates, pieces, stash, weights, after=()):
    n, model = gates.shape[0] // 4, pieces[0].shape[1]
    rows, width = 4 * n, weights[0].shape[2]
    share = width // experts
    bf, f32 = jnp.bfloat16, jnp.float32
    shapes = [shape_of(r, model) for r in part_rows(n)]
    shapes += [shape_of(rows, model)] + [shape_of(rows, width)] * 3

    def body(*refs):
        experts_backward_kernel(share, *refs[:10], *refs[10 + len(after) :])

    return pl.pallas_call(
        body,
        name="experts_backward",
        out_shape=shapes,
        in_specs=[scalar_spec(), whole_spec()] + [any_spec()] * (8 + len(after)),
        out_specs=[any_spec()] * len(shapes),
        scratch_shapes=[
            pltpu.VMEM((rows, model), bf),
            pltpu.VMEM((rows, model), bf),
            pltpu.VMEM((rows, width), f32),
            pltpu.VMEM((rows, width), f32),
            pltpu.VMEM((rows, width), bf),
            pltpu.VMEM((rows, width), bf),
            pltpu.VMEM((rows, width), bf),
        ]
        + [pltpu.VMEM((model, width), bf)] * 3
        + [pltpu.SemaphoreType.DMA((24 * experts + 48,))],
        compiler_params=pltpu.CompilerParams(vmem_limit_bytes=52 * MIB),
        cost_estimate=cost(6 * rows * model * width),
    )(where, gates, *pieces, *stash, *weights, *after)


def weight_grads_kernel(experts, where, *refs):
    sources, mine, other = refs[:4], refs[4], refs[5]
    x, g, out, semaphores = refs[6:]
    copies = Copies(semaphores)
    for target, near, far in zip((x, g), sources[:2], sources[2:]):
        start_rows(copies, (near, far), target)
    copies.wait()
    band = x.shape[1] // 4
    rows = band // CORES
    share = g.shape[1] // experts

    @pl.loop(0, 4)
    def _(z):
        columns = pl.ds(pl.multiple_of(z * band, band), band)
        k = lax.rem(z - where[0] + 4, 4)
        grads = contract(x[:, columns], g[...], OUTER).astype(jnp.bfloat16)
        for core in range(CORES):
            for e in range(experts):
                out[core, k, e] = grads[
                    core * rows : (core + 1) * rows, e * share : (e + 1) * share
                ]

    copies.start(out.at[1 - where[1]], other)
    copies.start(out.at[where[1]], mine)
    copies.wait()


def weight_grads_fast(where, near, far, experts, after=()):
    model, width = near[0].shape[1], near[1].shape[1]
    count = near[0].shape[0] + far[0].shape[0]
    rows, share = model // 8, width // experts
    bf = jnp.bfloat16

    def body(*refs):
        weight_grads_kernel(experts, *refs[:5], *refs[5 + len(after) :])

    return pl.pallas_call(
        body,
        name="weight_grads",
        out_shape=[shape_of(4, experts, rows, share)] * 2,
        in_specs=[scalar_spec()] + [any_spec()] * (4 + len(after)),
        out_specs=[any_spec()] * 2,
        scratch_shapes=[
            pltpu.VMEM((count, model), bf),
            pltpu.VMEM((count, width), bf),
            pltpu.VMEM((CORES, 4, experts, rows, share), bf),
            pltpu.SemaphoreType.DMA((6,)),
        ],
        compiler_params=pltpu.CompilerParams(vmem_limit_bytes=40 * MIB),
        cost_estimate=cost(2 * count * model * width),
    )(where, *near, *far, *after)


def cut_kernel(where, w_gate, w_up, w_down, *outs):
    share = outs[0].shape[3]
    matrices = (w_gate, w_up, w_down)
    for (k, first, count), out in zip(SHARES, outs):
        columns = pl.ds(pl.multiple_of(lax.rem(where[0] + k, 4) * share, share), share)
        for i in range(count):
            out[i, 0] = matrices[first + i][0, 0, :, columns]


def cut_experts(where, weights, layer):
    _, experts, rows, hidden = weights[0].shape
    share = hidden // 4
    return pl.pallas_call(
        cut_kernel,
        name="cut_experts",
        grid=(experts,),
        out_shape=[shape_of(count, experts, rows, share) for _, _, count in SHARES],
        in_specs=[scalar_spec()]
        + [pl.BlockSpec((1, 1, rows, hidden), lambda e: (layer, e, 0, 0))] * 3,
        out_specs=[
            pl.BlockSpec((count, 1, rows, share), lambda e: (0, e, 0, 0)) for _, _, count in SHARES
        ],
    )(where, *weights)


def merge_grads_kernel(*refs):
    mine, arrived, outs = refs[:3], refs[3:6], refs[6:]
    for i in range(3):
        for k, out in enumerate(outs):
            total = mine[i][k, 0].astype(jnp.float32) + arrived[i][k, 0].astype(jnp.float32)
            out[i, 0] = total.astype(jnp.bfloat16)


def merge_grads(mine, arrived):
    planes, experts, rows, share = mine[0].shape
    return pl.pallas_call(
        merge_grads_kernel,
        name="merge_grads",
        grid=(experts,),
        out_shape=[shape_of(3, experts, rows, share)] * planes,
        in_specs=[pl.BlockSpec((planes, 1, rows, share), lambda e: (0, e, 0, 0))] * 6,
        out_specs=[pl.BlockSpec((3, 1, rows, share), lambda e: (0, e, 0, 0))] * planes,
    )(*mine, *arrived)


def join_kernel(layer, where, *refs):
    pieces, outs = refs[:4], refs[-3:]
    i = pl.program_id(0)
    share = pieces[0].shape[3]
    for index, out in enumerate(outs):

        @pl.when(i == index)
        def _():
            for k, piece in enumerate(pieces):
                columns = pl.ds(pl.multiple_of(lax.rem(where[0] - k + 4, 4) * share, share), share)
                out[0, :, :, columns] = piece[0].astype(jnp.float32)


def join_experts(where, pieces, layer, layers, earlier=None):
    mats, experts, rows, share = pieces[0].shape
    shape = shape_of(layers, experts, rows, 4 * share, dtype=jnp.float32)
    given = [] if earlier is None else list(earlier)

    return pl.pallas_call(
        functools.partial(join_kernel, layer),
        name="join_experts",
        grid=(mats,),
        out_shape=[shape] * mats,
        in_specs=[scalar_spec()]
        + [pl.BlockSpec((1, experts, rows, share), lambda i: (i, 0, 0, 0))] * 4
        + [any_spec()] * len(given),
        out_specs=[pl.BlockSpec((1, experts, rows, 4 * share), lambda i: (layer, 0, 0, 0))] * mats,
        input_output_aliases={5 + j: j for j in range(len(given))},
        compiler_params=pltpu.CompilerParams(vmem_limit_bytes=40 * MIB),
    )(where, *pieces, *given)


def tie(value, *events):
    flat, tree = jax.tree.flatten(value)
    held = lax.optimization_barrier((*flat, *events))
    return jax.tree.unflatten(tree, held[: len(flat)])


def spread_first(place, block):
    return [block, place.hop(block, flip=1), place.hop(block, flip=2)]


def spread_last(place, first, axis=0, cut=None):
    block, one, two = first
    cut = cut or block.shape[axis] // 2
    head = place.hop(lax.slice_in_dim(one, 0, cut, axis=axis), flip=2)
    tail = place.hop(lax.slice_in_dim(two, cut, None, axis=axis), flip=1)
    return [block, one, two, head, tail]


def spread_pieces(place, block):
    return spread_last(place, spread_first(place, block))


def up_hops(place, block):
    return [place.hop(block, up=k) for k in range(1, 4)]


def add_low(a, b):
    return (a.astype(jnp.float32) + b.astype(jnp.float32)).astype(a.dtype)


def fold_first(place, parts):
    own, one_head, two_tail, to_one, to_two = parts
    return own, one_head, two_tail, place.hop(to_one, flip=1), place.hop(to_two, flip=2)


def fold_sums(first):
    own, one_head, two_tail, by_one, by_two = first
    half = one_head.shape[0]
    return own, add_low(one_head, by_two[half:]), add_low(two_tail, by_one[half:]), by_one, by_two


def fold_start(place, parts):
    return fold_sums(fold_first(place, parts))


def fold_end(place, state):
    own, one_head, two_tail, by_one, by_two = state
    return own, place.hop(one_head, flip=1), place.hop(two_tail, flip=2), by_one, by_two


def add_pieces(own, one_head, two_tail, by_one, by_two, axis=0):
    wide = lambda value: value.astype(jnp.float32)
    half = one_head.shape[0]
    one = jnp.concatenate([one_head, by_one[:half]], axis=axis)
    two = jnp.concatenate([by_two[:half], two_tail], axis=axis)
    return wide(own) + wide(one) + wide(two)


def blocks_kernel(sides, own, one_head, two_tail, by_one, by_two, *outs):
    half = one_head.shape[0]
    for side, out in zip(sides, outs):
        terms = (two_tail, by_one) if side else (one_head, by_two)
        total = own[side * half : (side + 1) * half, :].astype(jnp.float32)
        for term in terms:
            total = total + term[:half, :].astype(jnp.float32)
        out[...] = total.astype(jnp.bfloat16)


def sum_blocks(ends, sides):
    half, model = ends[1].shape
    return pl.pallas_call(
        functools.partial(blocks_kernel, sides),
        name="sum_blocks",
        out_shape=[shape_of(half, model)] * len(sides),
        in_specs=[whole_spec()] * 5,
        out_specs=[whole_spec()] * len(sides),
    )(*ends)


def down_hops(place, blocks, first=1):
    return [place.hop(block, up=-first - n) for n, block in enumerate(blocks)]


def total_of(base, extra):
    total = base.astype(jnp.float32)
    for term in extra:
        total = total + term[: base.shape[0]].astype(jnp.float32)
    return total


def received(near_ends, arrived):
    own, one_head, _, _, by_two = near_ends
    return [own, *arrived, one_head, by_two]


def merge_kernel(cut, mine, arrived, own, one_head, two_tail, to_one, to_two):
    m = pl.program_id(0)
    total = (mine[...].astype(jnp.float32) + arrived[...].astype(jnp.float32)).astype(jnp.bfloat16)
    rows = total.shape[0]

    @pl.when(m == 0)
    def _():
        own[...] = total

    @pl.when(m == 1)
    def _():
        one_head[...] = total[:, :cut]
        to_one[:rows, :] = total[:, cut:]

    @pl.when(m == 2)
    def _():
        to_two[:rows, :] = total[:, :cut]
        two_tail[...] = total[:, cut:]

    @pl.when(m == 3)
    def _():
        to_two[rows:, :] = total[:, :cut]
        to_one[rows:, :] = total[:, cut:]


def merge_cores(mine, arrived, cut):
    rows, width = mine.shape[0] // 4, mine.shape[1]
    outs = [(rows, width), (rows, cut), (rows, width - cut), (2 * rows, width - cut), (2 * rows, cut)]
    return pl.pallas_call(
        functools.partial(merge_kernel, cut),
        name="merge_cores",
        grid=(4,),
        out_shape=[shape_of(*out) for out in outs],
        in_specs=[pl.BlockSpec((rows, width), lambda m: (m, 0))] * 2,
        out_specs=[pl.BlockSpec(out, lambda m: (0, 0)) for out in outs],
        compiler_params=pltpu.CompilerParams(vmem_limit_bytes=40 * MIB),
    )(mine, arrived)


def pack_kernel(*refs):
    layers = refs[0].shape[0]
    for l in range(layers):
        out = refs[l - layers]
        at = 0
        for ref in refs[:-layers]:
            width = ref.shape[2]
            out[:, at : at + width] = ref[l]
            at += width


def pack_matrices(*arrays):
    width = sum(a.shape[2] for a in arrays)
    layers, rows, _ = arrays[0].shape
    return pl.pallas_call(
        pack_kernel,
        name="pack_matrices",
        out_shape=[shape_of(rows, width)] * layers,
        in_specs=[whole_spec()] * len(arrays),
        out_specs=[whole_spec()] * layers,
    )(*arrays)


def tables_of(length_row, rows):
    order = jnp.arange(rows, dtype=jnp.int32)
    index = jnp.arange(length_row.shape[0], dtype=jnp.int32)
    ends = jnp.sum(jnp.where(index[:, None] <= index[None, :], length_row[:, None], 0), axis=0)
    passed = order[:, None] >= ends[None, :]
    segment = jnp.sum(passed.astype(jnp.int32), axis=1)
    begin = jnp.sum(jnp.where(passed, length_row[None, :], 0), axis=1)
    cosine, sine = rope_tables(order - begin, HEAD_DIMENSION)
    allowed = (segment[:, None] == segment[None, :]) & (order[:, None] >= order[None, :])
    return (
        jnp.concatenate([cosine] * 4, axis=1),
        jnp.concatenate([-sine, sine] * 2, axis=1),
        allowed.astype(jnp.float32),
    )


def gate_rows_of(found):
    order = jnp.transpose(jnp.stack(found), (2, 1, 0, 4, 3))
    order = jnp.pad(order, ((0, 0),) * 4 + ((0, 8 - order.shape[4]),))
    return [
        (layer[:, :2].reshape(-1, 8), layer[:, 2:].reshape(-1, 8)) for layer in order
    ]


def shards_fast(
    tokens,
    lengths,
    routes,
    gates,
    cotangent,
    norm_attn,
    norm_ffn,
    query,
    key,
    value,
    output,
    w_gate,
    w_up,
    w_down,
):
    place = Place()
    where = jnp.stack([place.plane, place.core, place.column]).astype(jnp.int32)
    rows, model = tokens.shape
    layer_count, _, experts, _ = w_gate.shape
    expert_count = experts * place.columns
    in_width = query.shape[2] + key.shape[2] + value.shape[2]
    gains = jnp.stack([norm_attn, norm_ffn], axis=2)
    gains = jnp.pad(gains, ((0, 0), (0, 0), (0, EXTRA - 2)))
    packs = pack_matrices(query, key, value, output, gains)
    cut = packs[0].shape[1] // 2 // 128 * 128
    weights = [jnp.transpose(w, (0, 2, 1, 3)) for w in (w_gate, w_up, w_down)]
    tables = tables_of(lengths[0], rows)

    def line_of(block):
        return jnp.concatenate([block] + up_hops(place, block))

    cuts = [cut_experts(where, weights, l) for l in range(layer_count)]
    table = gate_table(*tie((routes, gates), packs[0]), expert_count)
    found = jnp.stack(spread_gates(place, table))
    found = [found] + up_hops(place, found)
    line = jnp.concatenate([packs[0]] + tie(up_hops(place, packs[0]), *[cut[0] for cut in cuts], found[0]))
    first = spread_first(place, line)
    cuts[0] = tie(cuts[0], line)
    own_swaps = [place.hop(tie(cut[0], line), swap=1) for cut in cuts]
    one = place.hop(cuts[0][1], up=1)
    swapped = [place.hop(line, swap=1)]
    two = place.hop(tie(cuts[0][2], line), up=2)
    first = tie(first, one, two, swapped[0], *own_swaps)
    three = place.hop(tie(cuts[0][3], first[0]), up=3)
    swapped += [place.hop(piece, swap=1) for piece in first[1:]]
    last_two = tie(spread_last(place, first, axis=1, cut=cut)[3:], three, *swapped[1:])
    matrices = [[*first, *last_two, *swapped, *[place.hop(p, swap=1) for p in last_two]]]
    shares = [cuts[0][0], one, two, three]
    share_swaps = [own_swaps[0], place.hop(one, swap=1), place.hop(two, swap=1)]

    def run_forward(l, which, pieces, bank, after=()):
        return experts_forward_fast(experts, where, gate_rows[l][which], pieces, bank, after=after)

    def run_backward(l, which, pieces, stash, bank, after=()):
        return experts_backward_fast(
            experts, where, gate_rows[l][which], pieces, stash, bank, after=after
        )

    def pairs_of(block, *events):
        ups = up_hops(place, block)
        near = spread_first(place, jnp.concatenate([block, ups[0]]))
        return near, ups[1:]

    base, extra = tokens.astype(jnp.float32), []
    stored = []
    for l in range(layer_count):
        more = l + 1 < layer_count
        after = list(share_swaps)
        outs = attend_forward_fast(where, base, extra, tables, matrices[l], in_width, after=after)
        h, m, nf = outs[:3]
        nf, late, found = tie((nf, shares[len(share_swaps) :], found))
        if l == 0:
            gate_rows = gate_rows_of(found)
        share_swaps += [place.hop(piece, swap=1) for piece in late]
        bank_l = [*shares[: 4 - len(late)], *late, *share_swaps]
        near, far = pairs_of(nf)
        near = spread_last(place, near)
        far = spread_first(place, jnp.concatenate(tie(far, near[3], near[4])))
        line = up_hops(place, tie(packs[l + 1] if more else cotangent, far[0]))
        *y_near, laid = run_forward(l, 0, near, bank_l)
        bank_l = [laid]
        y_near, far, line[0], line[2] = tie((y_near, far, line[0], line[2]))
        far = spread_last(place, far)
        if more:
            near_first = fold_first(place, tie(y_near[:5], far[3], far[4]))
            y_far = run_forward(l, 1, far, bank_l, after=(y_near[0],))
            y_far, near_first, line[1] = tie((y_far, near_first, line[1]))
            one = place.hop(tie(cuts[l + 1][1], line[1]), up=1)
            far_first = fold_first(place, y_far[:5])
            near_ends = fold_end(place, fold_sums(near_first))
            far_first, one = tie((far_first, one))
            far_state = fold_sums(far_first)
            one_swap = place.hop(one, swap=1)
            far_ends, one_swap = tie((fold_end(place, far_state), one_swap), *near_ends[1:3])
            line = jnp.concatenate([packs[l + 1], *line])
            passing = spread_first(place, tie(line, far_ends[1], far_ends[2]))
            line_swap = place.hop(line, swap=1)
            arrived = down_hops(place, sum_blocks(near_ends, (1,)))
            blocks = sum_blocks(far_ends, (0, 1))
            arrived += down_hops(place, blocks, 2)
            passing = tie(passing, *arrived)
            two = place.hop(tie(cuts[l + 1][2], *arrived), up=2)
            swapped = [line_swap] + [place.hop(piece, swap=1) for piece in passing[1:]]
            last_two, two = tie((spread_last(place, passing, 1, cut)[3:], two), *swapped[1:])
            share_swaps = [own_swaps[l + 1], one_swap]
            ends = [place.hop(p, swap=1) for p in last_two]
            matrices.append([*passing, *last_two, *swapped, *ends])
            shares = [cuts[l + 1][0], one, two]
            shares.append(place.hop(tie(cuts[l + 1][3], last_two[0]), up=3))
            base, extra = m, received(near_ends, arrived)
        else:
            last_near = jnp.concatenate(tie([cotangent, line[0]], far[3], far[4]))
            last_near = spread_first(place, last_near)
            y_far = run_forward(l, 1, far, bank_l, after=(y_near[0],))
            y_far, last_near, line = tie((y_far, last_near, line))
            last_near = spread_last(place, last_near)
            last_far = spread_first(place, jnp.concatenate(tie(line[1:], *last_near[3:])))
        stored.append((h, outs, y_near, y_far, bank_l))

    upstream = cotangent
    zero = jnp.zeros((rows, model), jnp.bfloat16)
    sums = [None] * layer_count
    joined = None
    for l in reversed(range(layer_count)):
        h, outs, kept_near, kept_far, bank_l = stored[l]
        m, na, q, k, v, o, lse, gains = outs[1], *outs[3:]
        top = l + 1 == layer_count

        if top:
            b_near = run_backward(l, 0, last_near, kept_near[6:], bank_l, (y_far[0],))
            b_near, last_far = tie((b_near, last_far))
            far = spread_last(place, last_far)
            near_first = fold_first(place, tie(b_near[:5], far[3], far[4]))
            b_far = run_backward(l, 1, far, kept_far[6:], bank_l, (b_near[0],))
            b_far, near_first = tie((b_far, near_first))
            far_first = fold_first(place, b_far[:5])
        else:
            ups = up_hops(place, low)
            held = merge_grads(*held_parts)
            result_ends = fold_end(place, fold_sums(result_first))
            ups[0], held = tie((ups[0], held), *result_ends[1:3])
            near = jnp.concatenate([low, ups[0]])
            other_sum = place.hop(tie(other_one, near), swap=1)
            near = spread_last(place, spread_first(place, near))
            far = spread_first(place, jnp.concatenate(tie(ups[1:], near[3], near[4])))
            result_blocks = sum_blocks(result_ends, (0, 1))
            result_arrived = down_hops(place, tie(result_blocks, far[0]), 2)
            b_near = run_backward(l, 0, near, kept_near[6:], bank_l, (held[0],))
            b_near, far, result_arrived = tie((b_near, far, result_arrived))
            merged = merge_cores(mine_one, tie(other_sum, b_near[0]), cut)
            far = spread_last(place, far)
            came = [place.hop(tie(held[2][2:], b_near[0]), up=2)]
            merged_first = fold_first(place, tie(merged, far[3], far[4]))
            b_far = run_backward(l, 1, far, kept_far[6:], bank_l, (b_near[0],))
            b_far, merged_first, came[0] = tie((b_far, merged_first, came[0]))
            far_first = fold_first(place, b_far[:5])
            came.insert(0, place.hop(tie(held[1], b_far[0]), up=1))
            came.append(place.hop(tie(held[3], b_far[0]), up=3))

        def weight_grads(i, after, near=(kept_near, b_near), far=(kept_far, b_far)):
            pick = lambda kept, found: ((kept[5], found[6 + i]) if i < 2 else (found[5], found[8]))
            return weight_grads_fast(where, pick(*near), pick(*far), experts, after=after)

        grads = [weight_grads(0, (b_far[0],))]
        if not top:
            grads.append(weight_grads(1, (grads[0][0], came[0])))
        far_state = fold_sums(tie(far_first, grads[-1][0]))
        if not top:
            near_first = fold_first(place, tie(b_near[:5], far_state[1], far_state[2]))
        grads.append(weight_grads(len(grads), (far_state[1], far_state[2])))
        swapped = [place.hop(other, swap=1) for _, other in grads[:-1]]
        far_ends = fold_end(place, far_state)
        far_ends, swapped = tie((far_ends, swapped), grads[-1][0])
        swapped.append(place.hop(grads[-1][1], swap=1))
        if not top:
            far_ends, came = tie((far_ends, came))
        event = far_state if top else far_ends
        near_state = fold_sums(tie(near_first, event[1], event[2]))
        near_ends = fold_end(place, near_state)
        arrived = down_hops(place, sum_blocks(near_ends, (1,)))
        blocks = sum_blocks(far_ends, (0, 1))
        arrived += down_hops(place, blocks, 2)
        if top:
            grads.append(weight_grads(2, (blocks[0],)))
            early = jnp.stack([add_low(grads[n][0][2], swapped[n][2]) for n in range(2)])
            arrived, swapped, early = tie((arrived, swapped, early), grads[2][0])
            early = place.hop(tie(early, *arrived), up=2)
            swapped.append(place.hop(tie(grads[2][1], *arrived), swap=1))
        if top:
            result_first = fold_first(place, tie(kept_far[:5], *arrived))
            result_near_first = fold_first(place, tie(kept_near[:5], *arrived))
            after = ()
            groups = ((0, 4),)
        else:
            held_came = [held[0], came[0], jnp.concatenate([early, came[1]]), came[2]]
            total = merge_grads([mine for mine, _ in grads], swapped)
            merged_ends = fold_end(place, fold_sums(tie(merged_first, blocks[0], *near_ends[1:3])))
            one_total = add_pieces(*merged_ends, axis=1)
            shard = mine_one.shape[0] // 16
            low_total = one_total[shard:].astype(jnp.bfloat16)
            arrived = tie(arrived, total[0], low_total)
            low_total = tie(low_total, *arrived)
            one_arrived = down_hops(place, [low_total[n * shard :][:shard] for n in range(3)])
            result_near = fold_end(place, fold_sums(tie(result_near_first, *arrived)))
            after = (low_total, total[0])
            groups = ((1, 3), (0, 1))
        upstream, low, *partial = attend_backward_fast(
            groups,
            where,
            zero,
            upstream,
            received(near_ends, arrived),
            (h, m, na, q, k, v, o, lse, gains),
            tables,
            matrices[l],
            in_width,
            after=after,
        )
        if top:
            low, result_first, result_near_first, early = tie(
                (low, result_first, result_near_first, early)
            )
            held_parts = ([mine for mine, _ in grads], swapped)
            other_one, mine_one = partial
        else:
            partial, result_near = tie((partial, result_near))
    partial, one_arrived = tie((partial, one_arrived))
    sums[1] = one_total[:shard]
    for block in one_arrived:
        sums[1] = sums[1] + block.astype(jnp.float32)
    other_far, other_near, mine_far, mine_near = partial
    other_far, other_near = place.hop(other_far, swap=1), place.hop(other_near, swap=1)
    merged_far = merge_cores(mine_far, other_far, cut)
    came = [place.hop(tie(total[k], upstream), up=k) for k in (1, 2, 3)]
    merged_far, came[0] = tie((merged_far, came[0]))
    merged_near = merge_cores(mine_near, other_near, cut)
    far_first = fold_first(place, merged_far)
    joined = join_experts(where, tie(held_came, merged_far[0]), 1, layer_count, None)
    far_state = fold_sums(tie(far_first, joined[0]))
    near_first = fold_first(place, tie(merged_near, far_state[1], far_state[2]))
    far_ends = tie(fold_end(place, far_state), *came)
    near_ends = fold_end(place, fold_sums(tie(near_first, *far_ends[1:3])))
    far_total = add_pieces(*far_ends, axis=1).astype(jnp.bfloat16)
    far_blocks = down_hops(place, [far_total[n * shard :][:shard] for n in range(3)])
    sums[0] = add_pieces(*near_ends, axis=1)
    for block in far_blocks:
        sums[0] = sums[0] + block.astype(jnp.float32)
    held_came = tie([total[0], *came], near_ends[1], near_ends[2])
    joined = join_experts(where, held_came, 0, layer_count, joined)
    last_block = down_hops(place, sum_blocks(tie(result_near, far_state[1]), (1,)))
    result = total_of(stored[-1][1][1], received(result_near, last_block + result_arrived))
    result = result.astype(jnp.bfloat16)
    sums = jnp.stack(sums)
    gain_sums = sums[:, :, in_width + model :]
    starts = (0, query.shape[2], query.shape[2] + key.shape[2], in_width, in_width + model)
    return (
        result,
        upstream,
        gain_sums[:, :, 0],
        gain_sums[:, :, 1],
        *[sums[:, :, a:b] for a, b in zip(starts, starts[1:])],
        *[jnp.transpose(grads, (0, 2, 1, 3)) for grads in joined],
    )


def solution(mesh):
    rows = P(AXES, None)
    layered = P(None, AXES, None)
    expert = P(None, "fsdp", "expert", None)
    gain = P(None, AXES)
    regular = mesh.shape["fsdp"] == 8 and mesh.shape["expert"] == 4
    return jax.shard_map(
        shards_fast if regular else shards,
        mesh=mesh,
        in_specs=(rows, rows, layered, layered, rows, gain, gain)
        + (layered,) * 4
        + (expert,) * 3,
        out_specs=(rows, rows, gain, gain) + (layered,) * 4 + (expert,) * 3,
        check_vma=False,
    )
```
